32 devices in a mesh: ctx: 16 (over z, x, core), fsdp: 2 (over y).
Axes of the slice: x: 2, y: 2, z: 4, core: 2. Of those that a mesh axis runs over, the one named last changes fastest.
Arguments:
- inputs: bfloat16 [2, 2048, 1280], P('fsdp', 'ctx'), may hold values from -6 to 6
- norm1_gain: bfloat16 [1280], P('fsdp'), may hold values from 0.099609375 to 1.8984375
- w_query: bfloat16 [1280, 1280], P('fsdp'), may hold values from -0.15625 to 0.15625
- w_key: bfloat16 [1280, 1280], P('fsdp'), may hold values from -0.15625 to 0.15625
- w_value: bfloat16 [1280, 1280], P('fsdp'), may hold values from -0.15625 to 0.15625
- w_output: bfloat16 [1280, 1280], P('fsdp'), may hold values from -0.625 to 0.625
- norm2_gain: bfloat16 [1280], P('fsdp'), may hold values from 0.099609375 to 1.8984375
- router: bfloat16 [1280, 16], P('fsdp'), may hold values from -0.083984375 to 0.083984375
- shared_gate_up_weight: bfloat16 [1280, 1792], P('fsdp'), may hold values from -0.15625 to 0.15625
- shared_down_weight: bfloat16 [896, 1280], P('fsdp'), may hold values from -0.1875 to 0.1875
- expert_in: bfloat16 [16, 1280, 1792], P('ctx', 'fsdp'), may hold values from -0.15625 to 0.15625
- expert_out: bfloat16 [16, 896, 1280], P('ctx', 'fsdp'), may hold values from -0.1875 to 0.1875
- picks: int32 [2, 2048, 7], P('fsdp', 'ctx'), may hold values from 0 to 15, all different within a row
- fill_order: int32 [2, 16, 896], P('fsdp', 'ctx'), may hold values from 0 to 895, each once within a row
- grad_out: bfloat16 [2, 2048, 1280], P('fsdp', 'ctx'), may hold values from -6 to 6
Outputs:
- layer_out: bfloat16 [2, 2048, 1280], P('fsdp', 'ctx')
- grad_inputs: float32 [2, 2048, 1280], P('fsdp', 'ctx')
- grad_norm1: float32 [1280], P('fsdp')
- grad_query: float32 [1280, 1280], P('fsdp')
- grad_key: float32 [1280, 1280], P('fsdp')
- grad_value: float32 [1280, 1280], P('fsdp')
- grad_output: float32 [1280, 1280], P('fsdp')
- grad_norm2: float32 [1280], P('fsdp')
- grad_router: float32 [1280, 16], P('fsdp')
- grad_shared_in: float32 [1280, 1792], P('fsdp')
- grad_shared_out: float32 [896, 1280], P('fsdp')
- grad_expert_in: float32 [16, 1280, 1792], P('ctx', 'fsdp')
- grad_expert_out: float32 [16, 896, 1280], P('ctx', 'fsdp')
The draws below stay inside these ranges and needn't reach their ends.
Inputs may be any that keep to these rules, and one draw needn't show every extreme that they name: Each token's 7 picks name different experts, and every expert is picked by some token. `fill_order`: for each sequence and run c, the 896 entries are a permutation; entry t * 7 + k belongs to token c * 128 + t and its k-th pick.
All inputs are finite; a program needn't handle non-finite values.
Results may differ from the reference program's by a relative error of at most 0.018.
Values may be sent and summed in bfloat16 or wider, within the bound.
No kernel may reach another device: no remote copies, remote signals or barrier semaphores. Data moves between devices by JAX's collectives and lax.ppermute only.
A program may use at most 320 MiB of HBM per device.

```python
import math
import jax
import jax.numpy as jnp
from jax import lax

D = 1280
HEADS = 10
HEAD_DIM = 128
EXP_HID = 896
TOP = 7
BLOCK = 256
TOK_DEV = 128
EXPERTS = 16
CAPACITY = 56
SEQ_LEN = 2048
SEQS = 2
N_CTX = 16


def shard_levels(key, shape, split, low, largest):
    factor_of, own = 1.0, jax.random.fold_in(key, 6)
    for axis_at, shards_of in split:
        steps = jnp.exp(jax.random.uniform(jax.random.fold_in(own, axis_at), (shards_of,), jnp.float32, low / len(split), largest / len(split)))
        factor_of = factor_of * jnp.repeat(steps, shape[axis_at] // shards_of).reshape([-1 if axis == axis_at else 1 for axis in range(len(shape))])
    return factor_of


def picks_of(stream_key, rows, amount, top, lift):
    order = jax.random.permutation(jax.random.fold_in(stream_key, 1), amount)
    pull = order
    for power in range(3):
        pull = pull * pull // amount
    pull = pull * lift // amount
    chance = jax.random.randint(jax.random.fold_in(stream_key, 2), (rows, amount), 0, 4096) + pull
    fixed_rows = jax.random.permutation(jax.random.fold_in(stream_key, 3), rows)[jnp.arange(amount) % rows]
    chance = jnp.where(jnp.arange(rows)[:, None] == fixed_rows[None, :], 1 << 14, chance)
    score = chance * amount + jnp.arange(amount)
    return lax.top_k(score.astype(jnp.int32), top)[1].astype(jnp.int32)


def scatter_about(key, dims, spread, limit, pieces=(), kind=jnp.bfloat16):
    drawn = jax.random.normal(key, dims, jnp.float32) * spread
    if len(pieces) > 0:
        drawn = shard_levels(key, dims, pieces, -0.22, 0.18) * drawn
    return jnp.clip(drawn, min=-limit, max=limit).astype(kind)


def setup_inputs(seed: int = 0) -> dict:
    streams_of = jax.random.split(jax.random.key(seed), 16)
    return {
        "inputs": scatter_about(streams_of[0], (SEQS, SEQ_LEN, D), 1.0, 6.0, ((0, 2), (1, 16))),
        "norm1_gain": jnp.clip(1.0 + 0.18 * jax.random.normal(streams_of[1], (D,), jnp.float32), 0.099609375, 1.8984375).astype(jnp.bfloat16),
        "w_query": scatter_about(streams_of[2], (D, D), D ** -0.5, 0.15625, ((0, 2),)),
        "w_key": scatter_about(streams_of[3], (D, D), D ** -0.5, 0.15625, ((0, 2),)),
        "w_value": scatter_about(streams_of[4], (D, D), D ** -0.5, 0.15625, ((0, 2),)),
        "w_output": scatter_about(streams_of[5], (D, D), (D // 16) ** -0.5, 0.625, ((0, 2),)),
        "norm2_gain": jnp.clip(1.0 + 0.18 * jax.random.normal(streams_of[6], (D,), jnp.float32), 0.099609375, 1.8984375).astype(jnp.bfloat16),
        "router": scatter_about(streams_of[7], (D, EXPERTS), 0.014, 0.083984375, ((0, 2),)),
        "shared_gate_up_weight": scatter_about(streams_of[8], (D, 2 * EXP_HID), D ** -0.5, 0.15625, ((0, 2),)),
        "shared_down_weight": scatter_about(streams_of[9], (EXP_HID, D), EXP_HID ** -0.5, 0.1875, ((0, 2),)),
        "expert_in": scatter_about(streams_of[10], (EXPERTS, D, 2 * EXP_HID), D ** -0.5, 0.15625, ((0, 16), (1, 2))),
        "expert_out": scatter_about(streams_of[11], (EXPERTS, EXP_HID, D), EXP_HID ** -0.5, 0.1875, ((0, 16), (1, 2))),
        "picks": picks_of(streams_of[12], SEQS * SEQ_LEN, EXPERTS, TOP, 3584).reshape((SEQS, SEQ_LEN, TOP)),
        "fill_order": jax.vmap(lambda own: jax.random.permutation(own, TOK_DEV * TOP))(jax.random.split(streams_of[13], SEQS * N_CTX)).reshape((SEQS, N_CTX, TOK_DEV * TOP)).astype(jnp.int32),
        "grad_out": scatter_about(streams_of[14], (SEQS, SEQ_LEN, D), 1.0, 6.0, ((0, 2), (1, 16))),
    }


top_score_value = lax.Precision.HIGHEST
epsilon = 1e-06
masked_score = -1000000000.0

@jax.custom_vjp
def low(v):
    return lax.optimization_barrier(v.astype(jnp.bfloat16)).astype(jnp.float32)

@jax.custom_vjp
def lower_precision_back(v):
    return v

def low_keep(v):
    return (low(v), None)

def low_pass(kept, grad):
    return (grad,)

def back_keep(v):
    return (v, None)

def back_low(kept, grad):
    return (low(grad),)
low.defvjp(low_keep, low_pass)
lower_precision_back.defvjp(back_keep, back_low)

def rms_scale(values):
    return lax.rsqrt(lax.optimization_barrier(jnp.mean(values * values, axis=-1, keepdims=True)) + epsilon)

def rotary_tables(positions, width):
    half = width // 2
    freqs = jnp.exp(-math.log(10000.0) * jnp.arange(half, dtype=jnp.float32) * 2.0 / width)
    angles = positions.astype(jnp.float32)[:, None] * freqs[None, :]
    cosine = jnp.concatenate([jnp.cos(angles), jnp.cos(angles)], axis=-1)
    sine = jnp.concatenate([jnp.sin(angles), jnp.sin(angles)], axis=-1)
    return (cosine, sine)

def rotate(values, cosine, sine):
    half = values.shape[-1] // 2
    turned = jnp.concatenate([-values[..., half:], values[..., :half]], axis=-1)
    return values * cosine[:, None, :] + turned * sine[:, None, :]

def slot_plan(span_picks, span_order, experts, capacity):
    top_count = span_picks.shape[-1]
    chosen = span_picks.reshape(-1)
    pairs = chosen.shape[0]
    sequence = jnp.argsort(span_order)
    ordered = chosen[sequence]
    onehot = (ordered[:, None] == jnp.arange(experts, dtype=jnp.int32)[None, :]).astype(jnp.int32)
    before = jnp.cumsum(onehot, axis=0) - onehot
    slots = lax.optimization_barrier(jnp.sum(before * onehot, axis=1))[span_order]
    kept = slots < capacity
    target = jnp.where(kept, chosen * capacity + slots, experts * capacity).astype(jnp.int32)
    pair_ids = jnp.arange(pairs, dtype=jnp.int32)
    pair_of_slot = jnp.zeros((experts * capacity,), jnp.int32).at[target].set(pair_ids, mode='drop')
    filled = jnp.zeros((experts * capacity,), jnp.int32).at[target].set(1, mode='drop')
    return (target, kept, pair_of_slot // top_count, pair_of_slot, filled)

def attend(query_rows, key_rows, value_rows, score_scale):
    length = query_rows.shape[0]
    groups = length // TOK_DEV
    key_groups = key_rows.reshape(groups, TOK_DEV, HEADS, HEAD_DIM)
    value_groups = value_rows.reshape(groups, TOK_DEV, HEADS, HEAD_DIM)
    key_block = (jnp.arange(length, dtype=jnp.int32) // BLOCK).reshape(groups, TOK_DEV)

    def one_block(block_args):
        query_part, start = block_args
        raw = lower_precision_back(jnp.einsum('qhd,nkhd->qhnk', query_part, key_groups, precision=top_score_value))
        query_block = (start + jnp.arange(512, dtype=jnp.int32)) // BLOCK
        allowed = key_block[None, None, :, :] <= query_block[:, None, None, None]
        scores = jnp.where(allowed, raw * score_scale, masked_score)
        peak = lax.optimization_barrier(jnp.max(scores, axis=-1))
        weights = jnp.exp(scores - peak[..., None])
        total = lax.optimization_barrier(jnp.sum(weights, axis=-1))
        partial_value = lower_precision_back(jnp.einsum('qhnk,nkhd->qhnd', low(weights), value_groups, precision=top_score_value))
        top_peak = lax.optimization_barrier(jnp.max(peak, axis=-1))
        factor = jnp.exp(peak - top_peak[..., None])
        numer = lax.optimization_barrier(jnp.sum(factor[..., None] * partial_value, axis=2))
        denom = lax.optimization_barrier(jnp.sum(factor * total, axis=2))
        return numer / denom[..., None]
    blocks = query_rows.reshape(length // 512, 512, HEADS, HEAD_DIM)
    starts = jnp.arange(length // 512, dtype=jnp.int32) * 512
    result = lax.map(jax.checkpoint(one_block), (blocks, starts))
    return result.reshape(length, HEADS, HEAD_DIM)

def expert_apply(expert_args):
    rows_in, weight_in, weight_out = expert_args
    projected = lower_precision_back(jnp.dot(rows_in, weight_in, precision=top_score_value))
    hidden = low(jax.nn.silu(projected[:, :EXP_HID]) * projected[:, EXP_HID:])
    return low(lower_precision_back(jnp.dot(hidden, weight_out, precision=top_score_value)))

def mixture(second_normalized, picks, fill_order, router, shared_gate_up_weight, shared_down_weight, expert_in, expert_out):
    router_scores = lower_precision_back(jnp.einsum('inu,ub->inb', second_normalized, router, precision=top_score_value))
    onehot = (picks[..., None] == jnp.arange(EXPERTS, dtype=jnp.int32)).astype(jnp.float32)
    selected = jnp.einsum('slke,sle->slk', onehot, router_scores, precision=top_score_value)
    gates = jax.nn.softmax(selected, axis=-1)
    shared_expert_projected = lower_precision_back(jnp.einsum('hxy,yc->hxc', second_normalized, shared_gate_up_weight, precision=top_score_value))
    shared_expert_hidden = low(jax.nn.silu(shared_expert_projected[..., :EXP_HID]) * shared_expert_projected[..., EXP_HID:])
    shared_expert_output = jnp.einsum('ynb,bz->ynz', shared_expert_hidden, shared_down_weight, precision=top_score_value)
    runs = SEQS * N_CTX
    run_rows = second_normalized.reshape(runs, TOK_DEV, D)
    run_picks = picks.reshape(runs, TOK_DEV, TOP)
    run_order = fill_order.reshape(runs, TOK_DEV * TOP)
    target, kept, token_of_slot, pair_of_slot, filled = jax.vmap(lambda span_picks, span_order: slot_plan(span_picks, span_order, EXPERTS, CAPACITY))(run_picks, run_order)
    gathered = jax.vmap(lambda source, index: source[index])(run_rows, token_of_slot)
    dispatched = lower_precision_back(jnp.where(filled[..., None] > 0, gathered, 0.0))
    per_expert = dispatched.reshape(runs, EXPERTS, CAPACITY, D).transpose(1, 0, 2, 3).reshape(EXPERTS, runs * CAPACITY, D)
    produced = lax.map(jax.checkpoint(expert_apply), (per_expert, expert_in, expert_out))
    produced = produced.reshape(EXPERTS, runs, CAPACITY, D).transpose(1, 0, 2, 3).reshape(runs, EXPERTS * CAPACITY, D)
    clipped = jnp.minimum(target, EXPERTS * CAPACITY - 1)
    chosen_experts = jax.vmap(lambda source, index: source[index])(produced, clipped).reshape(SEQS, SEQ_LEN, TOP, D)
    token_expert_weight = gates * kept.reshape(SEQS, SEQ_LEN, TOP).astype(jnp.float32)
    routed_output = jnp.einsum('cgn,cgnj->cgj', token_expert_weight, chosen_experts, precision=top_score_value)
    return shared_expert_output + routed_output

def layer(inputs, norm1_gain, w_query, w_key, w_value, w_output, norm2_gain, router, shared_gate_up_weight, shared_down_weight, expert_in, expert_out, picks, fill_order):
    score_scale = 1.0 / math.sqrt(HEAD_DIM)
    normed1 = low(inputs * rms_scale(inputs) * norm1_gain)
    cosine, sine = rotary_tables(jnp.arange(SEQ_LEN, dtype=jnp.int32), HEAD_DIM)
    mixed_all = []
    for which in range(SEQS):
        rows_in = normed1[which]
        query_proj = lower_precision_back(jnp.dot(rows_in, w_query, precision=top_score_value)).reshape(SEQ_LEN, HEADS, HEAD_DIM)
        key_proj = lower_precision_back(jnp.dot(rows_in, w_key, precision=top_score_value)).reshape(SEQ_LEN, HEADS, HEAD_DIM)
        query_rows = low(rotate(query_proj, cosine, sine))
        key_rows = low(rotate(key_proj, cosine, sine))
        value_rows = low(lower_precision_back(jnp.dot(rows_in, w_value, precision=top_score_value))).reshape(SEQ_LEN, HEADS, HEAD_DIM)
        context = attend(query_rows, key_rows, value_rows, score_scale)
        attended = low(lower_precision_back(context.reshape(SEQ_LEN, D)))
        mixed_all.append(lower_precision_back(jnp.dot(attended, w_output, precision=top_score_value)))
    second = inputs + jnp.stack(mixed_all)
    second_normalized = low(second * rms_scale(second) * norm2_gain)
    return second + mixture(second_normalized, picks, fill_order, router, shared_gate_up_weight, shared_down_weight, expert_in, expert_out)

def reference(inputs, norm1_gain, w_query, w_key, w_value, w_output, norm2_gain, router, shared_gate_up_weight, shared_down_weight, expert_in, expert_out, picks, fill_order, grad_out):
    floats = [array.astype(jnp.float32) for array in (inputs, norm1_gain, w_query, w_key, w_value, w_output, norm2_gain, router, shared_gate_up_weight, shared_down_weight, expert_in, expert_out)]

    def forward(*values):
        return layer(*values, picks, fill_order)
    result, pullback = jax.vjp(forward, *floats)
    grads = pullback(grad_out.astype(jnp.float32))
    return (result.astype(jnp.bfloat16), grads[0], grads[1], grads[2], grads[3], grads[4], grads[5], grads[6], grads[7], grads[8], grads[9], grads[10], grads[11])
```

```python
import functools
import math

import jax
import jax.numpy as jnp
from jax import lax
from jax.experimental import pallas as pl
from jax.experimental.pallas import tpu as pltpu
from jax.sharding import PartitionSpec as P

HEADS = 10
HEAD_DIM = 128
EXP_HID = 896
TOP = 7
BLOCK = 256
TILE = 512

epsilon = 1e-06
masked_score = -1000000000.0
score_scale = 1.0 / math.sqrt(HEAD_DIM)
exact = lax.Precision.HIGHEST
f32 = jnp.float32
bf16 = jnp.bfloat16


def dot(a, b):
    return jnp.dot(a, b, preferred_element_type=f32)


def dot_nt(a, b):
    return lax.dot_general(a, b, (((1,), (1,)), ((), ())), preferred_element_type=f32)


def dot_tn(a, b):
    return lax.dot_general(a, b, (((0,), (0,)), ((), ())), preferred_element_type=f32)


def rms_scale(values):
    return lax.rsqrt(jnp.mean(values * values, axis=-1, keepdims=True) + epsilon)


def rotary_tables(positions, width):
    half = width // 2
    freqs = jnp.exp(-math.log(10000.0) * jnp.arange(half, dtype=f32) * 2.0 / width)
    angles = positions.astype(f32)[:, None] * freqs[None, :]
    cosine = jnp.concatenate([jnp.cos(angles), jnp.cos(angles)], axis=-1)
    sine = jnp.concatenate([jnp.sin(angles), jnp.sin(angles)], axis=-1)
    return (cosine, sine)


def rotate(values, cosine, sine):
    half = values.shape[-1] // 2
    turned = jnp.concatenate([-values[..., half:], values[..., :half]], axis=-1)
    return values * cosine + turned * sine


def rotate_back(grads, cosine, sine):
    half = grads.shape[-1] // 2
    scaled = grads * sine
    return grads * cosine + jnp.concatenate([scaled[..., half:], -scaled[..., :half]], axis=-1)


def allowed_tile(rows, columns):
    key_block = lax.broadcasted_iota(jnp.int32, (rows, columns), 0) // BLOCK
    query_block = lax.broadcasted_iota(jnp.int32, (rows, columns), 1) // BLOCK
    return key_block <= query_block


def attend_kernel(q_ref, k_ref, v_ref, context_ref, lse_ref, score_ref):
    tile = q_ref.shape[0]
    here = pl.program_id(0)
    queries = q_ref[...]

    def raw_scores(j):
        keys = k_ref[pl.ds(pl.multiple_of(j * tile, tile), tile), :]
        return dot_nt(keys, queries) * score_scale

    def fold(j, scores, peak):
        score_ref[pl.ds(pl.multiple_of(j * tile, tile), tile), :] = scores
        return jnp.maximum(peak, jnp.max(scores.reshape(tile // 8, 8, tile), axis=0))

    diagonal = jnp.where(allowed_tile(tile, tile), raw_scores(here), masked_score)
    peak = fold(here, diagonal, jnp.full((8, tile), masked_score, f32))
    peak = lax.fori_loop(0, here, lambda j, p: fold(j, raw_scores(j), p), peak)
    top = jnp.max(peak, axis=0, keepdims=True)

    def gather(j, carry):
        total, numer = carry
        window = pl.ds(pl.multiple_of(j * tile, tile), tile)
        weights = jnp.exp(score_ref[window, :] - top)
        total = total + jnp.sum(weights.reshape(tile // 8, 8, tile), axis=0)
        return total, numer + dot_tn(v_ref[window, :], weights.astype(bf16))

    zero = (jnp.zeros((8, tile), f32), jnp.zeros((HEAD_DIM, tile), f32))
    total, numer = lax.fori_loop(0, here + 1, gather, zero)
    total = jnp.sum(total, axis=0, keepdims=True)
    context_ref[...] = (numer / total).T
    lse_ref[...] = top + jnp.log(total)


def attend(query, key, value):
    length = query.shape[0]
    tile = min(TILE, length)
    whole = pl.BlockSpec((length, HEAD_DIM), lambda i: (0, 0))
    part = pl.BlockSpec((tile, HEAD_DIM), lambda i: (i, 0))
    return pl.pallas_call(
        attend_kernel,
        grid=(length // tile,),
        in_specs=[part, whole, whole],
        out_specs=[part, pl.BlockSpec((1, tile), lambda i: (0, i))],
        out_shape=[
            jax.ShapeDtypeStruct((length, HEAD_DIM), f32),
            jax.ShapeDtypeStruct((1, length), f32),
        ],
        scratch_shapes=[pltpu.VMEM((length, tile), f32)],
        name="attend",
        cost_estimate=pl.CostEstimate(
            flops=2 * length * length * HEAD_DIM,
            bytes_accessed=12 * length * HEAD_DIM,
            transcendentals=length * length // 2,
        ),
    )(query, key, value)


def attend_back_kernel(
    q_ref, grad_ref, lse_ref, delta_ref, k_ref, v_ref, dq_ref, dk_ref, dv_ref
):
    tile = k_ref.shape[0]
    here = pl.program_id(0)
    keys = k_ref[...]
    values = v_ref[...]

    @pl.when(here == 0)
    def _():
        dq_ref[...] = jnp.zeros_like(dq_ref)

    def visit(i, masked):
        window = pl.ds(pl.multiple_of(i * tile, tile), tile)
        queries = q_ref[window, :]
        grads = grad_ref[window, :]
        weights = jnp.exp(dot_nt(keys, queries) * score_scale - lse_ref[:, window])
        if masked:
            weights = jnp.where(allowed_tile(tile, tile), weights, 0.0)
        grad_weights = dot_nt(values, grads)
        grad_raw = (weights * (grad_weights - delta_ref[:, window]) * score_scale).astype(bf16)
        dq_ref[window, :] += dot_tn(grad_raw, keys)
        return dot(grad_raw, queries), dot(weights.astype(bf16), grads)

    dk, dv = visit(here, True)
    dk_ref[...] = dk
    dv_ref[...] = dv

    def step(i, carry):
        more_k, more_v = visit(i, False)
        dk_ref[...] += more_k
        dv_ref[...] += more_v
        return carry

    lax.fori_loop(here + 1, pl.num_programs(0), step, 0)


def attend_back(query, key, value, grad, lse, delta):
    length = query.shape[0]
    tile = min(TILE, length)
    whole = pl.BlockSpec((length, HEAD_DIM), lambda i: (0, 0))
    row = pl.BlockSpec((1, length), lambda i: (0, 0))
    part = pl.BlockSpec((tile, HEAD_DIM), lambda i: (i, 0))
    return pl.pallas_call(
        attend_back_kernel,
        grid=(length // tile,),
        in_specs=[whole, whole, row, row, part, part],
        out_specs=[whole, part, part],
        out_shape=[jax.ShapeDtypeStruct((length, HEAD_DIM), f32)] * 3,
        name="attend_back",
        cost_estimate=pl.CostEstimate(
            flops=5 * length * length * HEAD_DIM,
            bytes_accessed=20 * length * HEAD_DIM,
            transcendentals=length * length // 2,
        ),
    )(query, grad, lse, delta, key, value)


def swiglu_back(grad_hidden, gate_part, up_part):
    sigmoid = jax.nn.sigmoid(gate_part)
    grad_gate = grad_hidden * up_part * sigmoid * (1.0 + gate_part * (1.0 - sigmoid))
    grad_up = grad_hidden * jax.nn.silu(gate_part)
    return jnp.concatenate([grad_gate, grad_up], axis=-1).astype(bf16)


def slot_table(span_picks, span_order, experts):
    tokens = span_picks.shape[0]
    order = span_order.reshape(tokens, TOP)
    onehot = span_picks[:, :, None] == jnp.arange(experts, dtype=jnp.int32)
    picked = jnp.any(onehot, axis=1)
    rank_key = jnp.sum(jnp.where(onehot, order[:, :, None], 0), axis=1)
    rank_key = jnp.where(picked, rank_key, tokens * TOP)
    before = rank_key[:, None, :] < rank_key[None, :, :]
    slots = jnp.sum(before.astype(jnp.int32), axis=0)
    return jnp.where(picked, slots, tokens * TOP)


def on_device(
    inputs,
    norm1_gain,
    w_query,
    w_key,
    w_value,
    w_output,
    norm2_gain,
    router,
    shared_gate_up_weight,
    shared_down_weight,
    expert_in,
    expert_out,
    picks,
    fill_order,
    grad_out,
):
    spans = lax.axis_size("ctx")
    here = lax.axis_index("ctx")
    side = lax.axis_index("fsdp")
    tokens, width = inputs.shape[1:]
    half = width // 2
    length = spans * tokens
    experts = spans * expert_in.shape[0]
    capacity = tokens * TOP // experts
    head = jnp.minimum(here, HEADS - 1)
    share = shared_down_weight.shape[0] // spans

    def across(value):
        return lax.ppermute(value, "fsdp", [(0, 1), (1, 0)])

    def ordered(own, other, axis):
        return jnp.where(
            side == 0,
            jnp.concatenate([own, other], axis=axis),
            jnp.concatenate([other, own], axis=axis),
        )

    def both(own, axis=0):
        return ordered(own, across(own), axis)

    def everyone(value):
        return lax.all_gather(value, "ctx", axis=0, tiled=True)

    def columns(value, start, count):
        return lax.dynamic_slice_in_dim(value, start, count, 1)

    def rows(value, start, count):
        return lax.dynamic_slice_in_dim(value, start, count, 0)

    def halves(value, axis=0):
        size = value.shape[axis] // 2
        mine = lax.dynamic_slice_in_dim(value, side * size, size, axis)
        theirs = lax.dynamic_slice_in_dim(value, (1 - side) * size, size, axis)
        return mine, theirs

    def reduced(value, axis=0):
        mine, theirs = halves(value, axis)
        return mine + across(theirs.astype(bf16)).astype(f32)

    x_all = everyone(inputs[0])
    g_all = everyone(grad_out[0])

    table = everyone(slot_table(picks[0], fill_order[0, 0], experts))
    head_parts = [columns(w, head * HEAD_DIM, HEAD_DIM) for w in (w_query, w_key, w_value)]
    small = jnp.concatenate(
        head_parts + [router, norm1_gain[:, None], norm2_gain[:, None]], axis=1
    )
    small = both(small)
    head_w = small[:, : 3 * HEAD_DIM]
    router_w = small[:, 3 * HEAD_DIM : 3 * HEAD_DIM + experts]
    gain_one = small[:, 3 * HEAD_DIM + experts].astype(f32)
    gain_two = small[:, 3 * HEAD_DIM + experts + 1].astype(f32)
    output_w = both(w_output)
    starts = [part * EXP_HID + block * (EXP_HID // 2) for part in (0, 1) for block in (0, 1)]
    shared_in = both(
        jnp.concatenate(
            [columns(shared_gate_up_weight, s + here * share, share) for s in starts], axis=1
        )
    )
    shared_out = both(rows(shared_down_weight, here * share, share))
    expert_in_w = both(expert_in[0])
    expert_out_w = both(expert_out[0])
    query_other, key_other, value_other = (across(w) for w in (w_query, w_key, w_value))

    cosine, sine = rotary_tables(jnp.arange(length, dtype=jnp.int32), HEAD_DIM)

    resid_all = x_all.astype(f32)
    normed1_all = (resid_all * rms_scale(resid_all) * gain_one).astype(bf16)
    projected = dot(normed1_all, head_w)
    query = rotate(projected[:, :HEAD_DIM], cosine, sine).astype(bf16)
    key = rotate(projected[:, HEAD_DIM : 2 * HEAD_DIM], cosine, sine).astype(bf16)
    value = projected[:, 2 * HEAD_DIM :].astype(bf16)
    context, lse = attend(query, key, value)
    attended_head = context.astype(bf16)

    def to_tokens(rows_of_head):
        sent = rows_of_head.reshape(spans, tokens, -1)
        got = lax.all_to_all(sent, "ctx", split_axis=0, concat_axis=0, tiled=True)
        return got[:HEADS]

    def by_token(got):
        return jnp.swapaxes(got, 0, 1).reshape(tokens, -1)

    attended = by_token(to_tokens(attended_head))
    resid = inputs[0].astype(f32)
    second = resid + dot(attended, output_w)
    scale_two = rms_scale(second)
    normed2 = (second * scale_two * gain_two).astype(bf16)
    normed2_all = everyone(normed2)

    logits = dot(normed2_all, router_w)
    picked = table < tokens * TOP
    peak = jnp.max(jnp.where(picked, logits, masked_score), axis=-1, keepdims=True)
    chances = jnp.where(picked, jnp.exp(logits - peak), 0.0)
    gates = chances / jnp.sum(chances, axis=-1, keepdims=True)
    expert_ids = lax.broadcasted_iota(jnp.int32, (length, experts), 1)
    own_slot = jnp.sum(jnp.where(expert_ids == here, table, 0), axis=1).reshape(spans, tokens)
    own_gate = jnp.sum(jnp.where(expert_ids == here, gates, 0.0), axis=1).reshape(spans, tokens)
    takes = own_slot[:, None, :] == jnp.arange(capacity, dtype=jnp.int32)[None, :, None]
    select = takes.astype(bf16)
    slot_gate = jnp.sum(jnp.where(takes, own_gate[:, None, :], 0.0), axis=2).reshape(-1, 1)

    def to_slots(value):
        picked_rows = jnp.einsum(
            "rst,rtd->rsd",
            select,
            value.reshape(spans, tokens, width),
            preferred_element_type=bf16,
        )
        return picked_rows.reshape(spans * capacity, width)

    def from_slots(value):
        back = jnp.einsum(
            "rst,rsd->rtd",
            select,
            value.reshape(spans, capacity, width),
            preferred_element_type=f32,
        )
        return back.reshape(length, width)

    dispatched = to_slots(normed2_all)
    grad_slots = to_slots(g_all)
    projected_e = dot(dispatched, expert_in_w)
    gate_e, up_e = projected_e[:, :EXP_HID], projected_e[:, EXP_HID:]
    expert_hidden = (jax.nn.silu(gate_e) * up_e).astype(bf16)
    expert_result = dot(expert_hidden, expert_out_w).astype(bf16)
    grad_slots_f = grad_slots.astype(f32)
    grad_result = (grad_slots_f * slot_gate).astype(bf16)
    slot_dot = jnp.sum(grad_slots_f * expert_result.astype(f32), axis=1).reshape(spans, capacity)
    gate_dot = jnp.sum(jnp.where(takes, slot_dot[:, :, None], 0.0), axis=1)
    gate_grads = lax.all_to_all(
        gate_dot[:, None, :], "ctx", split_axis=0, concat_axis=0, tiled=True
    )[:, 0, :].T

    shared_proj = dot(normed2_all, shared_in)
    shared_gate, shared_up = shared_proj[:, : 2 * share], shared_proj[:, 2 * share :]
    shared_hidden = (jax.nn.silu(shared_gate) * shared_up).astype(bf16)
    out_part = from_slots(expert_result) * own_gate.reshape(-1, 1) + dot(shared_hidden, shared_out)

    grad_ehidden = dot_nt(grad_result, expert_out_w)
    grad_eproj = swiglu_back(grad_ehidden, gate_e, up_e)
    grad_dispatched = dot_nt(grad_eproj, expert_in_w).astype(bf16)
    grad_shidden = dot_nt(g_all, shared_out)
    grad_sproj = swiglu_back(grad_shidden, shared_gate, shared_up)
    grad_part = from_slots(grad_dispatched) + dot_nt(grad_sproj, shared_in)
    scatter = functools.partial(lax.psum_scatter, axis_name="ctx", scatter_dimension=0, tiled=True)
    grad_normed2 = scatter(grad_part.astype(bf16)).astype(f32)

    grad_expert_out = reduced(dot_tn(expert_hidden, grad_result))
    grad_expert_in = reduced(dot_tn(dispatched, grad_eproj))
    grad_shared_in = reduced(dot_tn(normed2_all, grad_sproj)).astype(bf16)
    grad_shared_out = reduced(dot_tn(shared_hidden, g_all)).astype(bf16)

    own_gates = rows(gates, here * tokens, tokens)
    grad_sel = own_gates * (gate_grads - jnp.sum(own_gates * gate_grads, axis=-1, keepdims=True))
    grad_logits = grad_sel.astype(bf16)
    grad_normed2 = grad_normed2 + dot_nt(grad_logits, router_w)
    norm2_part = jnp.sum(grad_normed2 * second * scale_two, axis=0)
    hat = grad_normed2 * gain_two
    cubed = scale_two * scale_two * scale_two
    grad_second = (
        grad_out[0].astype(f32)
        + scale_two * hat
        - second * cubed * jnp.mean(hat * second, axis=-1, keepdims=True)
    )
    grad_mixed = grad_second.astype(bf16)
    grad_context = dot_nt(grad_mixed, output_w).astype(bf16)

    grad_context_head = jnp.swapaxes(grad_context.reshape(tokens, HEADS, HEAD_DIM), 0, 1)
    grad_context_head = jnp.pad(grad_context_head, ((0, spans - HEADS), (0, 0), (0, 0)))
    grad_context_head = lax.all_to_all(
        grad_context_head, "ctx", split_axis=0, concat_axis=0, tiled=True
    ).reshape(length, HEAD_DIM)

    high = norm2_part.astype(bf16)
    low = (norm2_part - high.astype(f32)).astype(bf16)
    extra_rows = jnp.zeros((16, width), bf16).at[0].set(high).at[1].set(low)
    extra_columns = jnp.pad(grad_logits, ((0, 16), (0, HEAD_DIM - experts)))
    carried = jnp.concatenate(
        [jnp.concatenate([grad_mixed, extra_rows], axis=0), extra_columns], axis=1
    )
    carried = everyone(carried).reshape(spans, tokens + 16, width + HEAD_DIM)
    grad_mixed_all = carried[:, :tokens, :width].reshape(length, width)
    grad_logits_all = carried[:, :tokens, width : width + experts].reshape(length, experts)
    norm2_all = jnp.sum(carried[:, tokens : tokens + 2, :width].astype(f32), axis=(0, 1))
    grad_norm2 = reduced_f32 = None
    mine, theirs = halves(norm2_all)
    grad_norm2 = mine + across(theirs)
    grad_router = dot_tn(normed2_all, grad_logits_all)
    mine, theirs = halves(grad_router)
    grad_router = mine + across(theirs)
    grad_output = dot_tn(attended_head, grad_mixed_all).astype(bf16)
    grad_output = (grad_output.astype(f32) + across(grad_output).astype(f32)).astype(bf16)

    delta = jnp.sum(grad_context_head.astype(f32) * context, axis=-1).reshape(1, length)
    grad_q, grad_k, grad_v = attend_back(query, key, value, grad_context_head, lse, delta)
    grad_heads = jnp.concatenate(
        [rotate_back(grad_q, cosine, sine), rotate_back(grad_k, cosine, sine), grad_v], axis=1
    ).astype(bf16)
    grad_head_w = reduced(dot_tn(normed1_all, grad_heads)).astype(bf16)

    got = to_tokens(grad_heads)
    pieces = [
        by_token(got[:, :, i * HEAD_DIM : (i + 1) * HEAD_DIM]) for i in range(3)
    ]
    own_part = sum(dot_nt(p, w) for p, w in zip(pieces, (w_query, w_key, w_value)))
    other_part = sum(dot_nt(p, w) for p, w in zip(pieces, (query_other, key_other, value_other)))
    grad_normed1 = ordered(own_part, other_part, 1)
    scale_one = rms_scale(resid)
    hat = grad_normed1 * gain_one
    cubed = scale_one * scale_one * scale_one
    grad_inputs = (
        grad_second
        + scale_one * hat
        - resid * cubed * jnp.mean(hat * resid, axis=-1, keepdims=True)
    )

    def replicated(value):
        return everyone(value[None])

    grads_qkv = replicated(grad_head_w)[:HEADS].reshape(HEADS, half, 3, HEAD_DIM)
    grad_query, grad_key, grad_value = (
        jnp.swapaxes(grads_qkv[:, :, i], 0, 1).reshape(half, width).astype(f32) for i in range(3)
    )
    gain_products = (
        grad_query * w_query.astype(f32)
        + grad_key * w_key.astype(f32)
        + grad_value * w_value.astype(f32)
    )
    grad_norm1 = jnp.sum(gain_products, axis=1) / norm1_gain.astype(f32)
    side_heads = HEADS // 2
    grad_output = rows(replicated(grad_output), side * side_heads, side_heads)
    grad_output = grad_output.reshape(half, width).astype(f32)
    grad_shared_in = replicated(grad_shared_in).reshape(spans, half, 4, share)
    grad_shared_in = jnp.transpose(grad_shared_in, (1, 2, 0, 3)).reshape(half, 2 * EXP_HID)
    grad_shared_out = everyone(grad_shared_out)
    layer_out = second + scatter(out_part.astype(bf16)).astype(f32)
    return (
        layer_out.astype(bf16)[None],
        grad_inputs[None],
        grad_norm1,
        grad_query,
        grad_key,
        grad_value,
        grad_output,
        grad_norm2,
        grad_router,
        grad_shared_in.astype(f32),
        grad_shared_out.astype(f32),
        grad_expert_in[None],
        grad_expert_out[None],
    )


def solution(mesh):
    placed = (
        P("fsdp", "ctx", None),
        P("fsdp"),
        P("fsdp", None),
        P("fsdp", None),
        P("fsdp", None),
        P("fsdp", None),
        P("fsdp"),
        P("fsdp", None),
        P("fsdp", None),
        P("fsdp", None),
        P("ctx", "fsdp", None),
        P("ctx", "fsdp", None),
        P("fsdp", "ctx", None),
        P("fsdp", "ctx", None),
        P("fsdp", "ctx", None),
    )
    return jax.shard_map(
        on_device,
        mesh=mesh,
        in_specs=placed,
        out_specs=(
            P("fsdp", "ctx", None),
            P("fsdp", "ctx", None),
            P("fsdp"),
            P("fsdp", None),
            P("fsdp", None),
            P("fsdp", None),
            P("fsdp", None),
            P("fsdp"),
            P("fsdp", None),
            P("fsdp", None),
            P("fsdp", None),
            P("ctx", "fsdp", None),
            P("ctx", "fsdp", None),
        ),
        check_vma=False,
    )
```

```python
import functools
import math

import jax
import jax.numpy as jnp
from jax import lax
from jax.experimental import pallas as pl
from jax.experimental.layout import Layout, with_layout_constraint
from jax.experimental.pallas import tpu as pltpu
from jax.sharding import PartitionSpec as P

HEADS = 10
HEAD_DIM = 128
EXP_HID = 896
TOP = 7
BLOCK = 256
TILE = 512

epsilon = 1e-06
masked_score = -1000000000.0
score_scale = 1.0 / math.sqrt(HEAD_DIM)
exact = lax.Precision.HIGHEST
f32 = jnp.float32
bf16 = jnp.bfloat16


def dot(a, b):
    return jnp.dot(a, b, preferred_element_type=f32)


def dot_nt(a, b):
    return lax.dot_general(a, b, (((1,), (1,)), ((), ())), preferred_element_type=f32)


def dot_tn(a, b):
    return lax.dot_general(a, b, (((0,), (0,)), ((), ())), preferred_element_type=f32)


def rms_scale(values):
    return lax.rsqrt(jnp.mean(values * values, axis=-1, keepdims=True) + epsilon)


def rotary_tables(positions, width):
    half = width // 2
    freqs = jnp.exp(-math.log(10000.0) * jnp.arange(half, dtype=f32) * 2.0 / width)
    angles = positions.astype(f32)[:, None] * freqs[None, :]
    cosine = jnp.concatenate([jnp.cos(angles), jnp.cos(angles)], axis=-1)
    sine = jnp.concatenate([jnp.sin(angles), jnp.sin(angles)], axis=-1)
    return (cosine, sine)


def allowed_tile(rows, columns):
    key_block = lax.broadcasted_iota(jnp.int32, (rows, columns), 0) // BLOCK
    query_block = lax.broadcasted_iota(jnp.int32, (rows, columns), 1) // BLOCK
    return key_block <= query_block


def ring_of(spans):
    if spans != 16:
        return list(range(spans))
    chips = [0, 2, 4, 6, 7, 5, 3, 1]
    return [2 * chip + core for chip in chips for core in (0, 1)]


def pieces(j, tile, length, ring):
    if ring:
        starts = (j * BLOCK, length - BLOCK - j * BLOCK)
        return [pl.ds(pl.multiple_of(at, BLOCK), BLOCK) for at in starts]
    return [pl.ds(pl.multiple_of(j * tile, tile), tile)]


def load(ref, windows, columns=slice(None)):
    parts = [ref[window, columns] for window in windows]
    return parts[0] if len(parts) == 1 else jnp.concatenate(parts, axis=0)


def store(ref, windows, value, columns=slice(None)):
    size = value.shape[0] // len(windows)
    for i, window in enumerate(windows):
        ref[window, columns] = value[i * size : (i + 1) * size]


def attend_kernel(
    ring, q_ref, k_ref, v_ref, context_ref, lse_ref, low_ref, low_ring_ref, score_ref
):
    length = k_ref.shape[0]
    tile = context_ref.shape[0]
    here = pl.program_id(0)
    queries = load(q_ref, pieces(here, tile, length, ring))

    def raw_scores(j):
        return dot_nt(load(k_ref, pieces(j, tile, length, ring)), queries) * score_scale

    def fold(j, scores, peak):
        score_ref[pl.ds(pl.multiple_of(j * tile, tile), tile), :] = scores
        return jnp.maximum(peak, jnp.max(scores.reshape(tile // 8, 8, tile), axis=0))

    diagonal = jnp.where(allowed_tile(tile, tile), raw_scores(here), masked_score)
    peak = fold(here, diagonal, jnp.full((8, tile), masked_score, f32))
    peak = lax.fori_loop(0, here, lambda j, p: fold(j, raw_scores(j), p), peak)
    top = jnp.max(peak, axis=0, keepdims=True)

    def gather(j, carry):
        total, numer = carry
        weights = jnp.exp(score_ref[pl.ds(pl.multiple_of(j * tile, tile), tile), :] - top)
        total = total + jnp.sum(weights.reshape(tile // 8, 8, tile), axis=0)
        values = load(v_ref, pieces(j, tile, length, ring))
        return total, numer + dot_tn(values, weights.astype(bf16))

    zero = (jnp.zeros((8, tile), f32), jnp.zeros((HEAD_DIM, tile), f32))
    total, numer = lax.fori_loop(0, here + 1, gather, zero)
    total = jnp.sum(total, axis=0, keepdims=True)
    context = (numer / total).T
    context_ref[...] = context
    low_ref[...] = context.astype(bf16)
    store(low_ring_ref, pieces(here, tile, length, ring), context.astype(bf16))
    lse_ref[...] = top + jnp.log(total)


def attend(query, key, value, ring):
    length = query.shape[0]
    tile = min(TILE, length)
    whole = pl.BlockSpec((length, HEAD_DIM), lambda i: (0, 0))
    part = pl.BlockSpec((tile, HEAD_DIM), lambda i: (i, 0))
    return pl.pallas_call(
        functools.partial(attend_kernel, ring),
        grid=(length // tile,),
        in_specs=[whole] * 3,
        out_specs=[part, pl.BlockSpec((1, tile), lambda i: (0, i)), part, whole],
        out_shape=[
            jax.ShapeDtypeStruct((length, HEAD_DIM), f32),
            jax.ShapeDtypeStruct((1, length), f32),
            jax.ShapeDtypeStruct((length, HEAD_DIM), bf16),
            jax.ShapeDtypeStruct((length, HEAD_DIM), bf16),
        ],
        scratch_shapes=[pltpu.VMEM((length, tile), f32)],
        name="attend",
        cost_estimate=pl.CostEstimate(
            flops=2 * length * length * HEAD_DIM,
            bytes_accessed=12 * length * HEAD_DIM,
            transcendentals=length * length // 2,
        ),
    )(query, key, value)


def attend_back_kernel(
    ring,
    q_ref,
    k_ref,
    v_ref,
    grad_ref,
    context_ref,
    lse_ref,
    cos_ref,
    sin_ref,
    out_ref,
    out_ring_ref,
    dq_ref,
    delta_ref,
    dk_ref,
    dv_ref,
):
    length = q_ref.shape[0]
    tile = dk_ref.shape[0]
    steps = length // tile
    here = pl.program_id(0)

    def natural(i):
        return pl.ds(pl.multiple_of(i * tile, tile), tile)

    @pl.when(here == 0)
    def _():
        def prepare(i, carry):
            window = natural(i)
            dq_ref[window, :] = jnp.zeros((tile, HEAD_DIM), f32)
            product = grad_ref[window, :].astype(f32) * context_ref[window, :]
            ones = jnp.ones((8, HEAD_DIM), f32)
            delta = lax.dot_general(
                ones, product, (((1,), (1,)), ((), ())), precision=exact, preferred_element_type=f32
            )
            delta_ref[:, window] = delta
            return carry

        lax.fori_loop(0, steps, prepare, 0)

    keys = load(k_ref, pieces(here, tile, length, ring))
    values = load(v_ref, pieces(here, tile, length, ring))

    def visit(i, masked):
        window = natural(i)
        queries = load(q_ref, pieces(i, tile, length, ring))
        grads = grad_ref[window, :]
        weights = jnp.exp(dot_nt(keys, queries) * score_scale - lse_ref[:, window])
        if masked:
            weights = jnp.where(allowed_tile(tile, tile), weights, 0.0)
        grad_weights = dot_nt(values, grads)
        grad_raw = (weights * (grad_weights - delta_ref[0:1, window]) * score_scale).astype(bf16)
        dq_ref[window, :] += dot_tn(grad_raw, keys)
        return dot(grad_raw, queries), dot(weights.astype(bf16), grads)

    dk, dv = visit(here, True)
    dk_ref[...] = dk
    dv_ref[...] = dv

    def step(i, carry):
        more_k, more_v = visit(i, False)
        dk_ref[...] += more_k
        dv_ref[...] += more_v
        return carry

    lax.fori_loop(here + 1, steps, step, 0)

    def write(i, part, value):
        at = slice(part * HEAD_DIM, (part + 1) * HEAD_DIM)
        out_ref[natural(i), at] = value
        store(out_ring_ref, pieces(i, tile, length, ring), value, at)

    def turned_back(i, value):
        windows = pieces(i, tile, length, ring)
        scaled = pltpu.roll(value * load(sin_ref, windows), HEAD_DIM // 2, 1)
        return (value * load(cos_ref, windows) + scaled).astype(bf16)

    write(here, 1, turned_back(here, dk_ref[...]))
    write(here, 2, dv_ref[...].astype(bf16))

    @pl.when(here == steps - 1)
    def _():
        def finish(i, carry):
            write(i, 0, turned_back(i, dq_ref[natural(i), :]))
            return carry

        lax.fori_loop(0, steps, finish, 0)


def attend_back(query, key, value, grad, context, lse, cosine, sine, ring):
    length = query.shape[0]
    tile = min(TILE, length)
    memory = pl.BlockSpec(memory_space=pltpu.VMEM)
    return pl.pallas_call(
        functools.partial(attend_back_kernel, ring),
        grid=(length // tile,),
        in_specs=[memory] * 8,
        out_specs=[memory] * 2,
        out_shape=[jax.ShapeDtypeStruct((length, 3 * HEAD_DIM), bf16)] * 2,
        scratch_shapes=[
            pltpu.VMEM((length, HEAD_DIM), f32),
            pltpu.VMEM((8, length), f32),
            pltpu.VMEM((tile, HEAD_DIM), f32),
            pltpu.VMEM((tile, HEAD_DIM), f32),
        ],
        name="attend_back",
        cost_estimate=pl.CostEstimate(
            flops=5 * length * length * HEAD_DIM,
            bytes_accessed=20 * length * HEAD_DIM,
            transcendentals=length * length // 2,
        ),
    )(query, key, value, grad, context, lse, cosine, sine)


def head_pairs(side, count):
    first = side * count
    return [(first + i, count - first + i, slice(i * HEAD_DIM, (i + 1) * HEAD_DIM)) for i in range(count)]


def mix_kernel(side_ref, got_ref, own_ref, other_ref, x_ref, gain_ref, second_ref, low_ref, scale_ref):
    second = x_ref[...].astype(f32)
    for mine, theirs, at in head_pairs(side_ref[0], HEADS // 2):
        attended = jnp.concatenate([got_ref[mine], got_ref[theirs]], axis=1)
        weight = jnp.concatenate([own_ref[at, :], other_ref[at, :]], axis=0)
        second += dot(attended, weight)
    scale = rms_scale(second)
    second_ref[...] = second
    scale_ref[...] = scale
    low_ref[...] = (second * scale * gain_ref[...]).astype(bf16)


def mix(side, got, own, other, x, gain):
    smem = pl.BlockSpec(memory_space=pltpu.SMEM)
    memory = pl.BlockSpec(memory_space=pltpu.VMEM)
    return pl.pallas_call(
        mix_kernel,
        in_specs=[smem] + [memory] * 5,
        out_specs=[memory] * 3,
        out_shape=[
            jax.ShapeDtypeStruct(x.shape, f32),
            jax.ShapeDtypeStruct(x.shape, bf16),
            jax.ShapeDtypeStruct((x.shape[0], 1), f32),
        ],
        name="mix",
    )(side.reshape(1), got, own, other, x, gain)


def mix_back_kernel(
    side_ref,
    sums_ref,
    gates_ref,
    gate_grads_ref,
    router_ref,
    second_ref,
    scale_ref,
    gain_ref,
    g_ref,
    own_ref,
    other_ref,
    carried_ref,
    grad_second_ref,
    context_ref,
    out_ref,
):
    tokens, width = second_ref.shape
    second = second_ref[...]
    scale = scale_ref[...]
    gain = gain_ref[...]
    gates = gates_ref[...]
    gate_grads = gate_grads_ref[...]
    out_ref[...] = (second + sums_ref[:, width:].astype(f32)).astype(bf16)
    weighted = gates * gate_grads
    grad_sel = weighted - gates * jnp.sum(weighted, axis=-1, keepdims=True)
    grad_logits = grad_sel.astype(bf16)
    grad_normed = sums_ref[:, :width].astype(f32) + dot_nt(grad_logits, router_ref[...])
    gain_part = jnp.sum(grad_normed * second * scale, axis=0, keepdims=True)
    hat = grad_normed * gain
    mean = jnp.mean(hat * second, axis=-1, keepdims=True)
    grad_second = g_ref[...].astype(f32) + scale * hat - second * (scale * scale * scale) * mean
    grad_second_ref[...] = grad_second
    grad_mixed = grad_second.astype(bf16)
    carried_ref[:tokens, :width] = grad_mixed
    carried_ref[:tokens, width:] = grad_logits
    high = gain_part.astype(bf16)
    rest = (gain_part - high.astype(f32)).astype(bf16)
    spare = carried_ref.shape[0] - tokens
    row = lax.broadcasted_iota(jnp.int32, (spare, width), 0)
    packed = jnp.where(row == 0, high.astype(f32), jnp.where(row == 1, rest.astype(f32), 0.0))
    carried_ref[tokens:, :width] = packed.astype(bf16)
    carried_ref[tokens:, width:] = jnp.zeros((spare, HEAD_DIM), bf16)
    for mine, theirs, at in head_pairs(side_ref[0], HEADS // 2):
        weight = jnp.concatenate([own_ref[at, :], other_ref[at, :]], axis=0)
        grad_context = dot_nt(grad_mixed, weight).astype(bf16)
        context_ref[mine] = grad_context[:, :HEAD_DIM]
        context_ref[theirs] = grad_context[:, HEAD_DIM:]
    for h in range(HEADS, context_ref.shape[0]):
        context_ref[h] = jnp.zeros((tokens, HEAD_DIM), bf16)


def mix_back(side, sums, gates, gate_grads, router, second, scale, gain, g, own, other, spans):
    tokens, width = second.shape
    smem = pl.BlockSpec(memory_space=pltpu.SMEM)
    memory = pl.BlockSpec(memory_space=pltpu.VMEM)
    return pl.pallas_call(
        mix_back_kernel,
        in_specs=[smem] + [memory] * 10,
        out_specs=[memory] * 4,
        out_shape=[
            jax.ShapeDtypeStruct((tokens + 16, width + HEAD_DIM), bf16),
            jax.ShapeDtypeStruct((tokens, width), f32),
            jax.ShapeDtypeStruct((spans, tokens, HEAD_DIM), bf16),
            jax.ShapeDtypeStruct((tokens, width), bf16),
        ],
        name="mix_back",
    )(side.reshape(1), sums, gates, gate_grads, router, second, scale, gain, g, own, other)


def inputs_back_kernel(
    side_ref,
    core_ref,
    got_ref,
    wq_ref,
    wk_ref,
    wv_ref,
    near_ref,
    far_ref,
    x_ref,
    gain_ref,
    grad_second_ref,
    out_ref,
):
    tokens, width = x_ref.shape
    half = width // 2
    count = HEADS // 2
    own_part = jnp.zeros((tokens, half), f32)
    other_part = jnp.zeros((tokens, half), f32)
    first = core_ref[0] * count
    for i, weight in enumerate((wq_ref, wk_ref, wv_ref)):
        at = slice(i * HEAD_DIM, (i + 1) * HEAD_DIM)
        for h in range(0, HEADS, 2):
            grads = jnp.concatenate([got_ref[h, :, at], got_ref[h + 1, :, at]], axis=1)
            own_part += dot_nt(grads, weight[:, h * HEAD_DIM : (h + 2) * HEAD_DIM])
        rows = slice(i * half, (i + 1) * half)
        for h in range(count):
            window = slice(h * HEAD_DIM, (h + 1) * HEAD_DIM)
            grads = jnp.concatenate(
                [got_ref[first + h, :, at], got_ref[count - first + h, :, at]], axis=1
            )
            weights = jnp.concatenate([near_ref[rows, window], far_ref[rows, window]], axis=1)
            other_part += dot_nt(grads, weights)
    grad_normed = jnp.where(
        side_ref[0] == 0,
        jnp.concatenate([own_part, other_part], axis=1),
        jnp.concatenate([other_part, own_part], axis=1),
    )
    resid = x_ref[...].astype(f32)
    scale = rms_scale(resid)
    hat = grad_normed * gain_ref[...]
    mean = jnp.mean(hat * resid, axis=-1, keepdims=True)
    out_ref[...] = grad_second_ref[...] + scale * hat - resid * (scale * scale * scale) * mean


def inputs_back(side, core, got, w_query, w_key, w_value, near, far, x, gain, grad_second):
    smem = pl.BlockSpec(memory_space=pltpu.SMEM)
    memory = pl.BlockSpec(memory_space=pltpu.VMEM)
    return pl.pallas_call(
        inputs_back_kernel,
        in_specs=[smem] * 2 + [memory] * 9,
        out_specs=memory,
        out_shape=jax.ShapeDtypeStruct(x.shape, f32),
        name="inputs_back",
    )(
        side.reshape(1),
        core.reshape(1),
        got,
        w_query,
        w_key,
        w_value,
        near,
        far,
        x,
        gain,
        grad_second,
    )


def place_heads_kernel(got_ref, wq_ref, wk_ref, wv_ref, gain_ref, q_ref, k_ref, v_ref, n_ref, sum_ref):
    here = pl.program_id(0)

    @pl.when(here == 0)
    def _():
        sum_ref[...] = jnp.zeros_like(sum_ref)

    start = got_ref.shape[2] - 3 * HEAD_DIM
    for i, (weight, out) in enumerate(((wq_ref, q_ref), (wk_ref, k_ref), (wv_ref, v_ref))):
        at = start + i * HEAD_DIM
        grad = got_ref[0, :, at : at + HEAD_DIM].astype(f32)
        out[...] = grad
        sum_ref[...] += grad * weight[...].astype(f32)

    @pl.when(here == pl.num_programs(0) - 1)
    def _():
        n_ref[...] = jnp.sum(sum_ref[...], axis=1, keepdims=True) / gain_ref[...]


def ring_position(index, spans):
    if spans != 16:
        return index
    chip, core = index // 2, index % 2
    level, column = chip // 2, chip % 2
    return (level + column * (7 - 2 * level)) * 2 + core


def place_heads(got, w_query, w_key, w_value, gain):
    spans, half, packed = got.shape
    part = pl.BlockSpec((half, HEAD_DIM), lambda h: (0, h))
    column = pl.BlockSpec((half, 1), lambda h: (0, 0))
    return pl.pallas_call(
        place_heads_kernel,
        grid=(HEADS,),
        in_specs=[
            pl.BlockSpec((1, half, packed), lambda h: (ring_position(h, spans), 0, 0)),
            part,
            part,
            part,
            column,
        ],
        out_specs=[part, part, part, column],
        out_shape=[jax.ShapeDtypeStruct(w_query.shape, f32)] * 3
        + [jax.ShapeDtypeStruct((half, 1), f32)],
        scratch_shapes=[pltpu.VMEM((half, HEAD_DIM), f32)],
        name="place_heads",
    )(got, w_query, w_key, w_value, gain)


def place_output_kernel(side_ref, got_ref, out_ref):
    wide = got_ref.shape[2]
    for block in range(out_ref.shape[1] // wide):
        rows = got_ref[0, block * HEAD_DIM : (block + 1) * HEAD_DIM, :]
        out_ref[:, block * wide : (block + 1) * wide] = rows.astype(f32)


def place_output(got, side, width):
    spans, half = got.shape[:2]
    wide = HEAD_DIM * width // half
    heads = HEADS // 2
    return pl.pallas_call(
        place_output_kernel,
        grid_spec=pltpu.PrefetchScalarGridSpec(
            num_scalar_prefetch=1,
            grid=(heads,),
            in_specs=[
                pl.BlockSpec(
                    (1, half, wide), lambda h, s: (ring_position(s[0] * heads + h, spans), 0, 0)
                )
            ],
            out_specs=pl.BlockSpec((HEAD_DIM, width), lambda h, s: (h, 0)),
        ),
        out_shape=jax.ShapeDtypeStruct((heads * HEAD_DIM, width), f32),
        name="place_output",
    )(side.reshape(1), got)


def place_shared_kernel(side_ref, got_ref, in_ref, out_ref, rows_ref):
    spans = got_ref.shape[0]
    units = got_ref.shape[1] // 4
    half = got_ref.shape[2]
    hidden = spans * units
    for part in range(2):
        for c in range(spans):
            piece = got_ref[ring_position(c, spans), part * units : (part + 1) * units, :]
            rows_ref[c * units : (c + 1) * units, :] = piece.astype(f32)
        for at in range(0, hidden, HEAD_DIM):
            in_ref[:, part * hidden + at : part * hidden + at + HEAD_DIM] = rows_ref[
                at : at + HEAD_DIM, :
            ].T
    first = side_ref[0] * (spans // 2)
    for c in range(spans // 2):
        for part in range(2):
            spot = ring_position(first + c, spans)
            piece = got_ref[spot, (2 + part) * units : (3 + part) * units, :]
            out_ref[c * units : (c + 1) * units, part * half : (part + 1) * half] = piece.astype(f32)


def place_shared(got, side):
    spans, quad, half = got.shape
    hidden = spans * quad // 4
    memory = pl.BlockSpec(memory_space=pltpu.VMEM)
    return pl.pallas_call(
        place_shared_kernel,
        in_specs=[pl.BlockSpec(memory_space=pltpu.SMEM), memory],
        out_specs=[memory, memory],
        out_shape=[
            jax.ShapeDtypeStruct((half, 2 * hidden), f32),
            jax.ShapeDtypeStruct((hidden // 2, 2 * half), f32),
        ],
        scratch_shapes=[pltpu.VMEM((hidden, half), f32)],
        name="place_shared",
    )(side.reshape(1), got)


def after(value, *others):
    return lax.optimization_barrier((value, *others))[0]


def tied(*values):
    return lax.optimization_barrier(values)


def swiglu_back(grad_hidden, gate_part, up_part):
    sigmoid = jax.nn.sigmoid(gate_part)
    grad_gate = grad_hidden * up_part * sigmoid * (1.0 + gate_part * (1.0 - sigmoid))
    grad_up = grad_hidden * jax.nn.silu(gate_part)
    return grad_gate.astype(bf16), grad_up.astype(bf16)


def slot_table(span_picks, span_order, experts):
    tokens = span_picks.shape[0]
    order = span_order.reshape(tokens, TOP)
    onehot = span_picks[:, :, None] == jnp.arange(experts, dtype=jnp.int32)
    picked = jnp.any(onehot, axis=1)
    rank_key = jnp.sum(jnp.where(onehot, order[:, :, None], 0), axis=1)
    rank_key = jnp.where(picked, rank_key, tokens * TOP)
    before = rank_key[:, None, :] < rank_key[None, :, :]
    slots = jnp.sum(before.astype(jnp.int32), axis=0)
    return jnp.where(picked, slots, tokens * TOP)


def on_device(
    inputs,
    norm1_gain,
    w_query,
    w_key,
    w_value,
    w_output,
    norm2_gain,
    router,
    shared_gate_up_weight,
    shared_down_weight,
    expert_in,
    expert_out,
    picks,
    fill_order,
    grad_out,
):
    spans = lax.axis_size("ctx")
    here = lax.axis_index("ctx")
    side = lax.axis_index("fsdp")
    core = here % 2
    tokens, width = inputs.shape[1:]
    half = width // 2
    length = spans * tokens
    experts = spans * expert_in.shape[0]
    capacity = tokens * TOP // experts
    head = jnp.minimum(here, HEADS - 1)
    units = EXP_HID // spans
    ring = ring_of(spans)
    is_ring = spans == 16
    groups = [ring] if is_ring else None
    swap_core = [(i, i ^ 1) for i in range(spans)]

    def across(value):
        return lax.ppermute(value, "fsdp", [(0, 1), (1, 0)])

    def ordered(own, other, axis):
        return jnp.where(
            side == 0,
            jnp.concatenate([own, other], axis=axis),
            jnp.concatenate([other, own], axis=axis),
        )

    def everyone(value):
        return lax.all_gather(value, "ctx", axis=0, tiled=True, axis_index_groups=groups)

    def columns(value, start, count):
        return lax.dynamic_slice_in_dim(value, start, count, 1)

    def rows(value, start, count):
        return lax.dynamic_slice_in_dim(value, start, count, 0)

    def halves(value, axis=0):
        size = value.shape[axis] // 2
        mine = lax.dynamic_slice_in_dim(value, side * size, size, axis)
        theirs = lax.dynamic_slice_in_dim(value, (1 - side) * size, size, axis)
        return mine, theirs

    def reduced(value, axis=0):
        mine, theirs = halves(value, axis)
        return mine + across(theirs.astype(bf16)).astype(f32)

    def swapped(value):
        return lax.all_to_all(value, "ctx", split_axis=0, concat_axis=0, tiled=True)

    def row_major(value):
        return with_layout_constraint(value, Layout(tuple(range(value.ndim))))

    x = inputs[0]
    g = grad_out[0]
    x_all = everyone(x)
    table = everyone(slot_table(picks[0], fill_order[0, 0], experts))
    head_parts = [columns(w, head * HEAD_DIM, HEAD_DIM) for w in (w_query, w_key, w_value)]
    small = jnp.concatenate(
        head_parts + [router, norm1_gain[:, None], norm2_gain[:, None]], axis=1
    )
    small_other = across(small)
    output_other = across(w_output)
    shared_in_own = jnp.concatenate(
        [columns(shared_gate_up_weight, at + here * units, units) for at in (0, EXP_HID)], axis=1
    )
    shared_rows = shared_down_weight.shape[0]
    shared_out_own = rows(shared_down_weight, here * units % shared_rows, units)
    ring_blocks = jnp.asarray(ring, jnp.int32)[:, None] * tokens
    positions = (ring_blocks + jnp.arange(tokens, dtype=jnp.int32)[None, :]).reshape(length)
    cosine, sine = rotary_tables(positions, HEAD_DIM)
    lane = lax.broadcasted_iota(jnp.int32, (length, HEAD_DIM), 1)
    sine = jnp.where(lane < HEAD_DIM // 2, -sine, sine)
    x_all, table, cosine, sine, small_other, output_other = tied(
        x_all, table, cosine, sine, small_other, output_other
    )
    small = ordered(small, small_other, 0)
    head_w = small[:, : 3 * HEAD_DIM]
    router_w = small[:, 3 * HEAD_DIM : 3 * HEAD_DIM + experts]
    gain_one = small[:, 3 * HEAD_DIM + experts].astype(f32).reshape(1, width)
    gain_two = small[:, 3 * HEAD_DIM + experts + 1].astype(f32).reshape(1, width)
    g_all = everyone(after(g, x_all))
    own_gate_w, own_up_w = expert_in[0, :, :EXP_HID], expert_in[0, :, EXP_HID:]
    gate_other = across(after(own_gate_w, x_all))
    up_other = across(after(own_up_w, x_all))

    resid_all = x_all.astype(f32)
    normed1_all = (resid_all * rms_scale(resid_all) * gain_one).astype(bf16)
    projected = dot(normed1_all, head_w)

    def rotate(values):
        turned = jnp.concatenate(
            [values[:, HEAD_DIM // 2 :], values[:, : HEAD_DIM // 2]], axis=1
        )
        return (values * cosine + turned * sine).astype(bf16)

    query = rotate(projected[:, :HEAD_DIM])
    key = rotate(projected[:, HEAD_DIM : 2 * HEAD_DIM])
    value = projected[:, 2 * HEAD_DIM :].astype(bf16)
    context, lse, attended, attended_ring = attend(query, key, value, is_ring)
    attended, gate_other = tied(attended, gate_other)
    down_other = across(after(expert_out[0], attended))
    shared_in_other = across(after(shared_in_own, attended))
    shared_out_other = across(after(shared_out_own, attended))
    got = swapped(attended.reshape(spans, tokens, HEAD_DIM))
    got, up_other = tied(got, up_other)
    second, normed2, scale_two = mix(side, got, w_output, output_other, x, gain_two)
    normed2_all = everyone(normed2)
    normed2_all, down_other, shared_in_other, shared_out_other = tied(
        normed2_all, down_other, shared_in_other, shared_out_other
    )
    shared_in = ordered(shared_in_own, shared_in_other, 0)
    shared_out = jnp.where(
        here * units // shared_rows == side, shared_out_own, shared_out_other
    )
    gate_w = ordered(own_gate_w, gate_other, 0)
    up_w = ordered(own_up_w, up_other, 0)
    down_w = ordered(expert_out[0], down_other, 0)
    dense = [columns(after(w, normed2_all), core * half, half) for w in (w_query, w_key, w_value)]
    near = [across(w) for w in dense]

    shared_proj = dot(normed2_all, shared_in)
    shared_gate, shared_up = shared_proj[:, :units], shared_proj[:, units:]
    shared_hidden = (jax.nn.silu(shared_gate) * shared_up).astype(bf16)
    grad_shidden = dot_nt(g_all, shared_out)
    grad_sproj = jnp.concatenate(swiglu_back(grad_shidden, shared_gate, shared_up), axis=1)
    grad_shared_in = reduced(dot_tn(grad_sproj, normed2_all), 1).astype(bf16)
    grad_shared_out = dot_tn(shared_hidden, g_all).astype(bf16)
    grad_shared_out = grad_shared_out.astype(f32) + across(grad_shared_out).astype(f32)
    grad_shared_out = grad_shared_out.astype(bf16)
    shared_grads = jnp.concatenate(
        [grad_shared_in, grad_shared_out[:, :half], grad_shared_out[:, half:]], axis=0
    )

    logits = dot(normed2_all, router_w)
    picked = table < tokens * TOP
    peak = jnp.max(jnp.where(picked, logits, masked_score), axis=-1, keepdims=True)
    chances = jnp.where(picked, jnp.exp(logits - peak), 0.0)
    gates = chances / jnp.sum(chances, axis=-1, keepdims=True)
    expert_ids = lax.broadcasted_iota(jnp.int32, (length, experts), 1)
    own_slot = jnp.sum(jnp.where(expert_ids == here, table, 0), axis=1).reshape(spans, tokens)
    own_gate = jnp.sum(jnp.where(expert_ids == here, gates, 0.0), axis=1).reshape(spans, tokens)
    takes = own_slot[:, None, :] == jnp.arange(capacity, dtype=jnp.int32)[None, :, None]
    select = takes.astype(bf16)
    slot_gate = jnp.sum(jnp.where(takes, own_gate[:, None, :], 0.0), axis=2).reshape(-1, 1)

    def to_slots(value):
        picked_rows = jnp.einsum(
            "rst,rtd->rsd",
            select,
            value.reshape(spans, tokens, width),
            preferred_element_type=bf16,
        )
        return picked_rows.reshape(spans * capacity, width)

    def from_slots(value):
        back = jnp.einsum(
            "rst,rsd->rtd",
            select,
            value.reshape(spans, capacity, width),
            preferred_element_type=f32,
        )
        return back.reshape(length, width)

    dispatched = to_slots(normed2_all)
    grad_slots = to_slots(g_all)
    gate_e, up_e = dot(dispatched, gate_w), dot(dispatched, up_w)
    expert_hidden = (jax.nn.silu(gate_e) * up_e).astype(bf16)
    expert_hidden, shared_grads, near[0] = tied(expert_hidden, shared_grads, near[0])
    shared_grads = everyone(row_major(shared_grads)[None])
    expert_result = dot(expert_hidden, down_w).astype(bf16)
    grad_slots_f = grad_slots.astype(f32)
    grad_result = (grad_slots_f * slot_gate).astype(bf16)
    slot_dot = jnp.sum(grad_slots_f * expert_result.astype(f32), axis=1).reshape(spans, capacity)
    gate_dot = jnp.sum(jnp.where(takes, slot_dot[:, :, None], 0.0), axis=1)
    out_part = from_slots(expert_result) * own_gate.reshape(-1, 1) + dot(shared_hidden, shared_out)
    grad_ehidden = dot_nt(grad_result, down_w)
    grad_gate, grad_up = swiglu_back(grad_ehidden, gate_e, up_e)
    grad_gate, near[1] = tied(grad_gate, near[1])
    grad_dispatched = (dot_nt(grad_gate, gate_w) + dot_nt(grad_up, up_w)).astype(bf16)
    grad_part = from_slots(grad_dispatched) + dot_nt(grad_sproj, shared_in)
    parts = jnp.concatenate([grad_part.astype(bf16), out_part.astype(bf16)], axis=1)
    parts, near[2] = tied(row_major(parts), near[2])
    sums = lax.psum_scatter(
        parts, "ctx", scatter_dimension=0, tiled=True, axis_index_groups=groups
    )
    spots = [ring_position(i, spans) for i in range(spans)]
    gate_dot = jnp.concatenate([gate_dot[i : i + 1] for i in spots], axis=0)
    gate_grads = swapped(after(gate_dot, parts)[:, None, :])[:, 0, :].T

    near = jnp.concatenate(near, axis=0)
    far = lax.ppermute(near, "ctx", swap_core)
    own_down, down_theirs = halves(dot_tn(expert_hidden, grad_result))
    own_gate_grad, gate_theirs = halves(dot_tn(dispatched, grad_gate))
    own_up_grad, up_theirs = halves(dot_tn(dispatched, grad_up))
    down_theirs = across(after(down_theirs.astype(bf16), parts))
    sums, gate_theirs, up_theirs, down_theirs = tied(
        sums, gate_theirs.astype(bf16), up_theirs.astype(bf16), down_theirs
    )
    gate_theirs, up_theirs = across(gate_theirs), across(up_theirs)

    own_gates = rows(gates, ring_position(here, spans) * tokens, tokens)
    padded = ((0, 0), (0, HEAD_DIM - experts))
    carried, grad_second, grad_context, layer_out = mix_back(
        side,
        sums,
        jnp.pad(own_gates, padded),
        jnp.pad(gate_grads, padded),
        jnp.pad(router_w, padded),
        second,
        scale_two,
        gain_two,
        g,
        w_output,
        output_other,
        spans,
    )
    grad_context = swapped(grad_context).reshape(length, HEAD_DIM)
    grad_context, gate_theirs = tied(grad_context, gate_theirs)
    carried = everyone(carried).reshape(spans, tokens + 16, width + HEAD_DIM)
    grad_heads, grad_heads_ring = attend_back(
        query, key, value, grad_context, context, lse, cosine, sine, is_ring
    )
    grad_heads, grad_heads_ring, up_theirs = tied(grad_heads, grad_heads_ring, up_theirs)
    grad_mixed_all = carried[:, :tokens, :width].reshape(length, width)
    grad_logits_all = carried[:, :tokens, width : width + experts].reshape(length, experts)
    norm2_all = jnp.sum(carried[:, tokens : tokens + 2, :width].astype(f32), axis=(0, 1))
    mine, theirs = halves(norm2_all)
    grad_norm2 = mine + across(theirs)
    mine, theirs = halves(dot_tn(normed2_all, grad_logits_all))
    grad_router = mine + across(theirs)
    grad_output = dot_tn(attended_ring, grad_mixed_all).astype(bf16)
    grad_output = (grad_output.astype(f32) + across(grad_output).astype(f32)).astype(bf16)
    grad_head_w = reduced(dot_tn(normed1_all, grad_heads_ring)).astype(bf16)
    wide = HEAD_DIM * width // half
    output_blocks = [grad_output[:, i : i + wide] for i in range(0, width, wide)]
    head_grads = jnp.concatenate([jnp.concatenate(output_blocks, axis=0), grad_head_w], axis=1)
    head_grads = everyone(row_major(head_grads)[None])

    got = swapped(grad_heads.reshape(spans, tokens, 3 * HEAD_DIM))
    grad_inputs = inputs_back(
        side, core, got, w_query, w_key, w_value, near, far, x, gain_one, grad_second
    )
    grad_query, grad_key, grad_value, grad_norm1 = place_heads(
        head_grads, w_query, w_key, w_value, norm1_gain[:, None].astype(f32)
    )
    grad_output = place_output(head_grads, side, width)
    grad_expert_in = jnp.concatenate(
        [own_gate_grad + gate_theirs.astype(f32), own_up_grad + up_theirs.astype(f32)], axis=1
    )
    grad_shared_in, grad_shared_out = place_shared(shared_grads, side)
    return (
        layer_out[None],
        grad_inputs[None],
        grad_norm1[:, 0],
        grad_query,
        grad_key,
        grad_value,
        grad_output,
        grad_norm2,
        grad_router,
        grad_shared_in,
        grad_shared_out,
        grad_expert_in[None],
        (own_down + down_theirs.astype(f32))[None],
    )


def solution(mesh):
    placed = (
        P("fsdp", "ctx", None),
        P("fsdp"),
        P("fsdp", None),
        P("fsdp", None),
        P("fsdp", None),
        P("fsdp", None),
        P("fsdp"),
        P("fsdp", None),
        P("fsdp", None),
        P("fsdp", None),
        P("ctx", "fsdp", None),
        P("ctx", "fsdp", None),
        P("fsdp", "ctx", None),
        P("fsdp", "ctx", None),
        P("fsdp", "ctx", None),
    )
    return jax.shard_map(
        on_device,
        mesh=mesh,
        in_specs=placed,
        out_specs=(
            P("fsdp", "ctx", None),
            P("fsdp", "ctx", None),
            P("fsdp"),
            P("fsdp", None),
            P("fsdp", None),
            P("fsdp", None),
            P("fsdp", None),
            P("fsdp"),
            P("fsdp", None),
            P("fsdp", None),
            P("fsdp", None),
            P("ctx", "fsdp", None),
            P("ctx", "fsdp", None),
        ),
        check_vma=False,
    )
```

```python
import functools
import math

import jax
import jax.numpy as jnp
from jax import lax
from jax.experimental import pallas as pl
from jax.experimental.layout import Layout, with_layout_constraint
from jax.experimental.pallas import tpu as pltpu
from jax.sharding import PartitionSpec as P

HEADS = 10
HEAD_DIM = 128
EXP_HID = 896
TOP = 7
BLOCK = 256
TILE = 512

epsilon = 1e-06
masked_score = -1000000000.0
score_scale = 1.0 / math.sqrt(HEAD_DIM)
exact = lax.Precision.HIGHEST
f32 = jnp.float32
bf16 = jnp.bfloat16


def dot(a, b):
    return jnp.dot(a, b, preferred_element_type=f32)


def dot_nt(a, b):
    return lax.dot_general(a, b, (((1,), (1,)), ((), ())), preferred_element_type=f32)


def dot_tn(a, b):
    return lax.dot_general(a, b, (((0,), (0,)), ((), ())), preferred_element_type=f32)


def rms_scale(values):
    return lax.rsqrt(jnp.mean(values * values, axis=-1, keepdims=True) + epsilon)


def rotary_tables(positions, width):
    half = width // 2
    freqs = jnp.exp(-math.log(10000.0) * jnp.arange(half, dtype=f32) * 2.0 / width)
    angles = positions.astype(f32)[:, None] * freqs[None, :]
    cosine = jnp.concatenate([jnp.cos(angles), jnp.cos(angles)], axis=-1)
    sine = jnp.concatenate([jnp.sin(angles), jnp.sin(angles)], axis=-1)
    return (cosine, sine)


def allowed_tile(rows, columns):
    key_block = lax.broadcasted_iota(jnp.int32, (rows, columns), 0) // BLOCK
    query_block = lax.broadcasted_iota(jnp.int32, (rows, columns), 1) // BLOCK
    return key_block <= query_block


def ring_of(spans):
    if spans != 16:
        return list(range(spans))
    chips = [0, 2, 4, 6, 7, 5, 3, 1]
    return [2 * chip + core for chip in chips for core in (0, 1)]


def pieces(j, tile, length, ring):
    if ring:
        starts = (j * BLOCK, length - BLOCK - j * BLOCK)
        return [pl.ds(pl.multiple_of(at, BLOCK), BLOCK) for at in starts]
    return [pl.ds(pl.multiple_of(j * tile, tile), tile)]


def load(ref, windows, columns=slice(None)):
    parts = [ref[window, columns] for window in windows]
    return parts[0] if len(parts) == 1 else jnp.concatenate(parts, axis=0)


def store(ref, windows, value, columns=slice(None)):
    size = value.shape[0] // len(windows)
    for i, window in enumerate(windows):
        ref[window, columns] = value[i * size : (i + 1) * size]


def attend_kernel(
    ring, q_ref, k_ref, v_ref, context_ref, lse_ref, low_ref, score_ref
):
    length = k_ref.shape[0]
    tile = context_ref.shape[0]
    here = pl.program_id(0)
    queries = load(q_ref, pieces(here, tile, length, ring))

    def raw_scores(j):
        return dot_nt(load(k_ref, pieces(j, tile, length, ring)), queries) * score_scale

    def fold(j, scores, peak):
        score_ref[pl.ds(pl.multiple_of(j * tile, tile), tile), :] = scores
        return jnp.maximum(peak, jnp.max(scores.reshape(tile // 8, 8, tile), axis=0))

    diagonal = jnp.where(allowed_tile(tile, tile), raw_scores(here), masked_score)
    peak = fold(here, diagonal, jnp.full((8, tile), masked_score, f32))
    peak = lax.fori_loop(0, here, lambda j, p: fold(j, raw_scores(j), p), peak)
    top = jnp.max(peak, axis=0, keepdims=True)

    def gather(j, carry):
        total, numer = carry
        weights = jnp.exp(score_ref[pl.ds(pl.multiple_of(j * tile, tile), tile), :] - top)
        total = total + jnp.sum(weights.reshape(tile // 8, 8, tile), axis=0)
        values = load(v_ref, pieces(j, tile, length, ring))
        return total, numer + dot_tn(values, weights.astype(bf16))

    zero = (jnp.zeros((8, tile), f32), jnp.zeros((HEAD_DIM, tile), f32))
    total, numer = lax.fori_loop(0, here + 1, gather, zero)
    total = jnp.sum(total, axis=0, keepdims=True)
    context = (numer / total).T
    context_ref[...] = context
    low_ref[...] = context.astype(bf16)
    lse_ref[...] = top + jnp.log(total)


def attend(query, key, value, ring):
    length = query.shape[0]
    tile = min(TILE, length)
    whole = pl.BlockSpec((length, HEAD_DIM), lambda i: (0, 0))
    part = pl.BlockSpec((tile, HEAD_DIM), lambda i: (i, 0))
    return pl.pallas_call(
        functools.partial(attend_kernel, ring),
        grid=(length // tile,),
        in_specs=[whole] * 3,
        out_specs=[part, pl.BlockSpec((1, tile), lambda i: (0, i)), part],
        out_shape=[
            jax.ShapeDtypeStruct((length, HEAD_DIM), f32),
            jax.ShapeDtypeStruct((1, length), f32),
            jax.ShapeDtypeStruct((length, HEAD_DIM), bf16),
        ],
        scratch_shapes=[pltpu.VMEM((length, tile), f32)],
        name="attend",
        cost_estimate=pl.CostEstimate(
            flops=2 * length * length * HEAD_DIM,
            bytes_accessed=12 * length * HEAD_DIM,
            transcendentals=length * length // 2,
        ),
    )(query, key, value)


def attend_back_kernel(
    ring,
    q_ref,
    k_ref,
    v_ref,
    grad_ref,
    context_ref,
    lse_ref,
    cos_ref,
    sin_ref,
    out_ref,
    out_ring_ref,
    dq_ref,
    delta_ref,
    dk_ref,
    dv_ref,
):
    length = q_ref.shape[0]
    tile = dk_ref.shape[0]
    steps = length // tile
    here = pl.program_id(0)

    def natural(i):
        return pl.ds(pl.multiple_of(i * tile, tile), tile)

    tokens = grad_ref.shape[1] - 16
    blocks = tile // tokens

    def arrived(i):
        parts = [grad_ref[i * blocks + b, :tokens, :HEAD_DIM] for b in range(blocks)]
        return jnp.concatenate(parts, axis=0)

    @pl.when(here == 0)
    def _():
        def prepare(i, carry):
            window = natural(i)
            dq_ref[window, :] = jnp.zeros((tile, HEAD_DIM), f32)
            product = arrived(i).astype(f32) * context_ref[window, :]
            ones = jnp.ones((8, HEAD_DIM), f32)
            delta = lax.dot_general(
                ones, product, (((1,), (1,)), ((), ())), precision=exact, preferred_element_type=f32
            )
            delta_ref[:, window] = delta
            return carry

        lax.fori_loop(0, steps, prepare, 0)

    keys = load(k_ref, pieces(here, tile, length, ring))
    values = load(v_ref, pieces(here, tile, length, ring))

    def visit(i, masked):
        window = natural(i)
        queries = load(q_ref, pieces(i, tile, length, ring))
        grads = arrived(i)
        weights = jnp.exp(dot_nt(keys, queries) * score_scale - lse_ref[:, window])
        if masked:
            weights = jnp.where(allowed_tile(tile, tile), weights, 0.0)
        grad_weights = dot_nt(values, grads)
        grad_raw = (weights * (grad_weights - delta_ref[0:1, window]) * score_scale).astype(bf16)
        dq_ref[window, :] += dot_tn(grad_raw, keys)
        return dot(grad_raw, queries), dot(weights.astype(bf16), grads)

    dk, dv = visit(here, True)
    dk_ref[...] = dk
    dv_ref[...] = dv

    def step(i, carry):
        more_k, more_v = visit(i, False)
        dk_ref[...] += more_k
        dv_ref[...] += more_v
        return carry

    lax.fori_loop(here + 1, steps, step, 0)

    def write(i, part, value):
        at = slice(part * HEAD_DIM, (part + 1) * HEAD_DIM)
        out_ref[natural(i), at] = value
        store(out_ring_ref, pieces(i, tile, length, ring), value, at)

    def turned_back(i, value):
        windows = pieces(i, tile, length, ring)
        scaled = pltpu.roll(value * load(sin_ref, windows), HEAD_DIM // 2, 1)
        return (value * load(cos_ref, windows) + scaled).astype(bf16)

    write(here, 1, turned_back(here, dk_ref[...]))
    write(here, 2, dv_ref[...].astype(bf16))

    @pl.when(here == steps - 1)
    def _():
        def finish(i, carry):
            write(i, 0, turned_back(i, dq_ref[natural(i), :]))
            return carry

        lax.fori_loop(0, steps, finish, 0)


def attend_back(query, key, value, grad, context, lse, cosine, sine, ring):
    length = query.shape[0]
    tile = min(TILE, length)
    memory = pl.BlockSpec(memory_space=pltpu.VMEM)
    return pl.pallas_call(
        functools.partial(attend_back_kernel, ring),
        grid=(length // tile,),
        in_specs=[memory] * 8,
        out_specs=[memory] * 2,
        out_shape=[jax.ShapeDtypeStruct((length, 3 * HEAD_DIM), bf16)] * 2,
        scratch_shapes=[
            pltpu.VMEM((length, HEAD_DIM), f32),
            pltpu.VMEM((8, length), f32),
            pltpu.VMEM((tile, HEAD_DIM), f32),
            pltpu.VMEM((tile, HEAD_DIM), f32),
        ],
        name="attend_back",
        cost_estimate=pl.CostEstimate(
            flops=5 * length * length * HEAD_DIM,
            bytes_accessed=20 * length * HEAD_DIM,
            transcendentals=length * length // 2,
        ),
    )(query, key, value, grad, context, lse, cosine, sine)


def project_kernel(
    side_ref, x_ref, gain_ref, own_ref, other_ref, cos_ref, sin_ref, normed_ref, q_ref, k_ref, v_ref
):
    own, other = own_ref[...], other_ref[...]
    weight = jnp.where(
        side_ref[0] == 0,
        jnp.concatenate([own, other], axis=0),
        jnp.concatenate([other, own], axis=0),
    )
    resid = x_ref[...].astype(f32)
    normed = (resid * rms_scale(resid) * gain_ref[...]).astype(bf16)
    normed_ref[...] = normed
    projected = dot(normed, weight)
    for out, at in ((q_ref, 0), (k_ref, HEAD_DIM)):
        part = projected[:, at : at + HEAD_DIM]
        turned = pltpu.roll(part, HEAD_DIM // 2, 1)
        out[...] = (part * cos_ref[...] + turned * sin_ref[...]).astype(bf16)
    v_ref[...] = projected[:, 2 * HEAD_DIM :].astype(bf16)


def project(side, x, gain, own, other, cosine, sine):
    length, width = x.shape
    tile = min(TILE, length)
    part = pl.BlockSpec((tile, HEAD_DIM), lambda i: (i, 0))
    wide = pl.BlockSpec((tile, width), lambda i: (i, 0))
    return pl.pallas_call(
        project_kernel,
        grid=(length // tile,),
        in_specs=[
            pl.BlockSpec(memory_space=pltpu.SMEM),
            wide,
            pl.BlockSpec((1, width), lambda i: (0, 0)),
            pl.BlockSpec(own.shape, lambda i: (0, 0)),
            pl.BlockSpec(own.shape, lambda i: (0, 0)),
            part,
            part,
        ],
        out_specs=[wide, part, part, part],
        out_shape=[jax.ShapeDtypeStruct((length, width), bf16)]
        + [jax.ShapeDtypeStruct((length, HEAD_DIM), bf16)] * 3,
        name="project",
        cost_estimate=pl.CostEstimate(
            flops=6 * length * width * HEAD_DIM,
            bytes_accessed=4 * length * width,
            transcendentals=0,
        ),
    )(side.reshape(1), x, gain, own, other, cosine, sine)


def head_pairs(side, spans):
    ring = ring_of(spans)
    count = HEADS // 2
    pairs = []
    for i in range(count):
        low, high = ring[i], ring[count + i]
        mine = jnp.where(side == 0, low, high)
        theirs = jnp.where(side == 0, high, low)
        pairs.append((mine, theirs, slice(i * HEAD_DIM, (i + 1) * HEAD_DIM)))
    return pairs


def mix_kernel(
    experts,
    spot_ref,
    got_ref,
    own_ref,
    near_ref,
    far_ref,
    x_ref,
    gain_ref,
    router_ref,
    table_ref,
    second_ref,
    low_ref,
    scale_ref,
    gates_ref,
    attended_ref,
):
    ring = ring_of(got_ref.shape[0])
    for h in range(HEADS):
        attended_ref[:, h * HEAD_DIM : (h + 1) * HEAD_DIM] = got_ref[ring[h]]
    second = x_ref[...].astype(f32)
    tokens, width = second.shape
    half = near_ref.shape[1]
    near = jnp.zeros((tokens, half), f32)
    far = near
    for mine, theirs, at in head_pairs(spot_ref[0], got_ref.shape[0]):
        second += dot(got_ref[mine], own_ref[at, :])
        near += dot(got_ref[theirs], near_ref[at, :])
        far += dot(got_ref[theirs], far_ref[at, :])
    second += jnp.where(
        spot_ref[1] == 0,
        jnp.concatenate([near, far], axis=1),
        jnp.concatenate([far, near], axis=1),
    )
    scale = rms_scale(second)
    second_ref[...] = second
    scale_ref[...] = scale
    normed = (second * scale * gain_ref[...]).astype(bf16)
    logits = dot_nt(normed, router_ref[...])
    picked = table_ref[...] < tokens
    peak = jnp.max(jnp.where(picked, logits, masked_score), axis=-1, keepdims=True)
    chances = jnp.where(picked, jnp.exp(logits - peak), 0.0)
    gates = chances / jnp.sum(chances, axis=-1, keepdims=True)
    gates_ref[...] = gates
    high = gates.astype(bf16).astype(f32)
    rest = pltpu.roll(gates - high, experts, 1)
    low_ref[:, :width] = normed
    low_ref[:, width:] = (high + rest).astype(bf16)


def mix(spot, got, own, near, far, x, gain, router, table, experts):
    smem = pl.BlockSpec(memory_space=pltpu.SMEM)
    memory = pl.BlockSpec(memory_space=pltpu.VMEM)
    tokens, width = x.shape
    spare = table.shape[1]
    return pl.pallas_call(
        functools.partial(mix_kernel, experts),
        in_specs=[smem] + [memory] * 8,
        out_specs=[memory] * 5,
        out_shape=[
            jax.ShapeDtypeStruct(x.shape, f32),
            jax.ShapeDtypeStruct((tokens, width + spare), bf16),
            jax.ShapeDtypeStruct((tokens, 1), f32),
            jax.ShapeDtypeStruct((tokens, spare), f32),
            jax.ShapeDtypeStruct(x.shape, bf16),
        ],
        name="mix",
    )(spot, got, own, near, far, x, gain, router, table)


def mix_back_kernel(
    spot_ref,
    sums_ref,
    gates_ref,
    gate_grads_ref,
    router_ref,
    second_ref,
    scale_ref,
    gain_ref,
    g_ref,
    own_ref,
    near_ref,
    far_ref,
    send_ref,
    grad_second_ref,
    out_ref,
):
    tokens, width = second_ref.shape
    second = second_ref[...]
    scale = scale_ref[...]
    gain = gain_ref[...]
    gates = gates_ref[...]
    gate_grads = gate_grads_ref[...]
    out_ref[...] = (second + sums_ref[:, width:].astype(f32)).astype(bf16)
    weighted = gates * gate_grads
    grad_sel = weighted - gates * jnp.sum(weighted, axis=-1, keepdims=True)
    grad_logits = grad_sel.astype(bf16)
    grad_normed = sums_ref[:, :width].astype(f32) + dot(grad_logits, router_ref[...])
    gain_part = jnp.sum(grad_normed * second * scale, axis=0, keepdims=True)
    hat = grad_normed * gain
    mean = jnp.mean(hat * second, axis=-1, keepdims=True)
    grad_second = g_ref[...].astype(f32) + scale * hat - second * (scale * scale * scale) * mean
    grad_second_ref[...] = grad_second
    grad_mixed = grad_second.astype(bf16)
    spans = send_ref.shape[0]
    cut = width // spans
    lane = lax.broadcasted_iota(jnp.int32, (1, HEAD_DIM), 1)
    high = gain_part.astype(bf16).astype(f32)
    row = lax.broadcasted_iota(jnp.int32, (16, width), 0)
    gain_rows = jnp.where(row == 0, high, jnp.where(row == 1, gain_part - high, 0.0))
    shifted = pltpu.roll(grad_logits.astype(f32), cut, 1)
    for c in range(spans):
        start = min(c * cut // HEAD_DIM * HEAD_DIM, width - 2 * HEAD_DIM)
        shift = (start - c * cut) % (2 * HEAD_DIM)
        for value, rest, out_rows in (
            (grad_second, shifted, slice(0, tokens)),
            (gain_rows, 0.0, slice(tokens, tokens + 16)),
        ):
            window = pltpu.roll(value[:, start : start + 2 * HEAD_DIM], shift, 1)[:, :HEAD_DIM]
            window = jnp.where(lane < cut, window, 0.0) + rest
            send_ref[c, out_rows, HEAD_DIM:] = window.astype(bf16)
        send_ref[c, tokens:, :HEAD_DIM] = jnp.zeros((16, HEAD_DIM), bf16)
    left, right = grad_mixed[:, : width // 2], grad_mixed[:, width // 2 :]
    at_near = jnp.where(spot_ref[1] == 0, left, right)
    at_far = jnp.where(spot_ref[1] == 0, right, left)
    for mine, theirs, at in head_pairs(spot_ref[0], spans):
        send_ref[mine, :tokens, :HEAD_DIM] = dot_nt(grad_mixed, own_ref[at, :]).astype(bf16)
        other = dot_nt(at_near, near_ref[at, :]) + dot_nt(at_far, far_ref[at, :])
        send_ref[theirs, :tokens, :HEAD_DIM] = other.astype(bf16)
    for h in ring_of(spans)[HEADS:]:
        send_ref[h, :tokens, :HEAD_DIM] = jnp.zeros((tokens, HEAD_DIM), bf16)


def mix_back(spot, sums, gates, gate_grads, router, second, scale, gain, g, own, near, far, spans):
    tokens, width = second.shape
    smem = pl.BlockSpec(memory_space=pltpu.SMEM)
    memory = pl.BlockSpec(memory_space=pltpu.VMEM)
    return pl.pallas_call(
        mix_back_kernel,
        in_specs=[smem] + [memory] * 11,
        out_specs=[memory] * 3,
        out_shape=[
            jax.ShapeDtypeStruct((spans, tokens + 16, 2 * HEAD_DIM), bf16),
            jax.ShapeDtypeStruct((tokens, width), f32),
            jax.ShapeDtypeStruct((tokens, width), bf16),
        ],
        name="mix_back",
    )(spot, sums, gates, gate_grads, router, second, scale, gain, g, own, near, far)


def inputs_back_kernel(
    side_ref,
    core_ref,
    got_ref,
    wq_ref,
    wk_ref,
    wv_ref,
    near_ref,
    far_ref,
    x_ref,
    gain_ref,
    grad_second_ref,
    out_ref,
):
    tokens, width = x_ref.shape
    half = width // 2
    count = HEADS // 2
    own_part = jnp.zeros((tokens, half), f32)
    other_part = jnp.zeros((tokens, half), f32)
    ring = ring_of(got_ref.shape[0])
    for i, weight in enumerate((wq_ref, wk_ref, wv_ref)):
        at = slice(i * HEAD_DIM, (i + 1) * HEAD_DIM)
        for h in range(0, HEADS, 2):
            grads = jnp.concatenate([got_ref[ring[h], :, at], got_ref[ring[h + 1], :, at]], axis=1)
            own_part += dot_nt(grads, weight[:, h * HEAD_DIM : (h + 2) * HEAD_DIM])
        rows = slice(i * half, (i + 1) * half)
        for h in range(count):
            window = slice(h * HEAD_DIM, (h + 1) * HEAD_DIM)
            low, high = ring[h], ring[count + h]
            mine = jnp.where(core_ref[0] == 0, low, high)
            theirs = jnp.where(core_ref[0] == 0, high, low)
            grads = jnp.concatenate([got_ref[mine, :, at], got_ref[theirs, :, at]], axis=1)
            weights = jnp.concatenate([near_ref[rows, window], far_ref[rows, window]], axis=1)
            other_part += dot_nt(grads, weights)
    grad_normed = jnp.where(
        side_ref[0] == 0,
        jnp.concatenate([own_part, other_part], axis=1),
        jnp.concatenate([other_part, own_part], axis=1),
    )
    resid = x_ref[...].astype(f32)
    scale = rms_scale(resid)
    hat = grad_normed * gain_ref[...]
    mean = jnp.mean(hat * resid, axis=-1, keepdims=True)
    out_ref[...] = grad_second_ref[...] + scale * hat - resid * (scale * scale * scale) * mean


def inputs_back(side, core, got, w_query, w_key, w_value, near, far, x, gain, grad_second):
    smem = pl.BlockSpec(memory_space=pltpu.SMEM)
    memory = pl.BlockSpec(memory_space=pltpu.VMEM)
    return pl.pallas_call(
        inputs_back_kernel,
        in_specs=[smem] * 2 + [memory] * 9,
        out_specs=memory,
        out_shape=jax.ShapeDtypeStruct(x.shape, f32),
        name="inputs_back",
    )(
        side.reshape(1),
        core.reshape(1),
        got,
        w_query,
        w_key,
        w_value,
        near,
        far,
        x,
        gain,
        grad_second,
    )


def place_heads_kernel(
    cut, heads_ref, rest_ref, gain_ref, q_ref, k_ref, v_ref, output_ref, norm_ref
):
    for h in range(HEADS):
        at = slice(h * HEAD_DIM, (h + 1) * HEAD_DIM)
        for i, out in enumerate((q_ref, k_ref, v_ref)):
            out[:, at] = heads_ref[h, :, i * HEAD_DIM : (i + 1) * HEAD_DIM].astype(f32)
    sums = jnp.zeros((rest_ref.shape[1], 2), f32)
    for h in range(HEADS):
        sums += rest_ref[h, :, cut : cut + 2].astype(f32)
    norm_ref[...] = jnp.sum(sums, axis=1, keepdims=True) / gain_ref[...]
    spans = rest_ref.shape[0]
    for c in range(spans):
        piece = rest_ref[ring_position(c, spans), :, :cut].astype(f32)
        output_ref[:, c * cut : (c + 1) * cut] = piece


def ring_position(index, spans):
    if spans != 16:
        return index
    chip, core = index // 2, index % 2
    level, column = chip // 2, chip % 2
    return (level + column * (7 - 2 * level)) * 2 + core


def place_heads(got, gain, width):
    spans, _, packed = got.shape
    half = width // 2
    cut = width // spans
    block = half // 8
    part = pl.BlockSpec((block, width), lambda r: (r, 0))
    column = pl.BlockSpec((block, 1), lambda r: (r, 0))
    return pl.pallas_call(
        functools.partial(place_heads_kernel, cut),
        grid=(8,),
        in_specs=[
            pl.BlockSpec((HEADS, block, 3 * HEAD_DIM), lambda r: (0, r, 0)),
            pl.BlockSpec((spans, block, HEAD_DIM), lambda r: (0, r, 3)),
            column,
        ],
        out_specs=[part] * 4 + [column],
        out_shape=[jax.ShapeDtypeStruct((half, width), f32)] * 4
        + [jax.ShapeDtypeStruct((half, 1), f32)],
        name="place_heads",
    )(got, got, gain)


def place_shared_kernel(side_ref, got_ref, in_ref, out_ref, rows_ref):
    spans = got_ref.shape[0]
    units = got_ref.shape[1] // 4
    half = got_ref.shape[2]
    hidden = spans * units
    for part in range(2):
        for c in range(spans):
            piece = got_ref[ring_position(c, spans), part * units : (part + 1) * units, :]
            rows_ref[c * units : (c + 1) * units, :] = piece.astype(f32)
        for at in range(0, hidden, HEAD_DIM):
            in_ref[:, part * hidden + at : part * hidden + at + HEAD_DIM] = rows_ref[
                at : at + HEAD_DIM, :
            ].T
    first = side_ref[0] * (spans // 2)
    for c in range(spans // 2):
        for part in range(2):
            spot = ring_position(first + c, spans)
            piece = got_ref[spot, (2 + part) * units : (3 + part) * units, :]
            out_ref[c * units : (c + 1) * units, part * half : (part + 1) * half] = piece.astype(f32)


def place_shared(got, side):
    spans, quad, half = got.shape
    hidden = spans * quad // 4
    memory = pl.BlockSpec(memory_space=pltpu.VMEM)
    return pl.pallas_call(
        place_shared_kernel,
        in_specs=[pl.BlockSpec(memory_space=pltpu.SMEM), memory],
        out_specs=[memory, memory],
        out_shape=[
            jax.ShapeDtypeStruct((half, 2 * hidden), f32),
            jax.ShapeDtypeStruct((hidden // 2, 2 * half), f32),
        ],
        scratch_shapes=[pltpu.VMEM((hidden, half), f32)],
        name="place_shared",
    )(side.reshape(1), got)


def after(value, *others):
    return lax.optimization_barrier((value, *others))[0]


def tied(*values):
    return lax.optimization_barrier(values)


def one_hot_rows(lanes, *targets):
    row = lax.broadcasted_iota(jnp.int32, (8, lanes), 0)
    lane = lax.broadcasted_iota(jnp.int32, (8, lanes), 1)
    rows = jnp.zeros((8, lanes), f32)
    for i, target in enumerate(targets):
        rows = jnp.where((row == i) & (lane == target), 1.0, rows)
    return rows.astype(bf16)


def slot_keys(shape, axis, capacity):
    index = lax.broadcasted_iota(jnp.int32, shape, axis)
    return (index % capacity + 1024 * (index // capacity)).astype(f32)


def run_keys(shape, axis, tokens):
    return (1024 * (lax.broadcasted_iota(jnp.int32, shape, axis) // tokens)).astype(f32)


def pick_slots_kernel(capacity, tokens, here_ref, g_ref, out_ref):
    many = g_ref.shape[0]
    width = out_ref.shape[1]
    extras = g_ref[:, width:]
    rows = one_hot_rows(extras.shape[1], here_ref[0])
    slots = dot_nt(rows, extras)[0:1] + run_keys((1, many), 1, tokens)
    takes = slot_keys((out_ref.shape[0], 1), 0, capacity) == slots
    select = jnp.where(takes, 1.0, 0.0).astype(bf16)
    out_ref[...] = dot(select, g_ref[:, :width]).astype(bf16)


def pick_slots(here, g_wide, width, capacity, tokens):
    length, wide = g_wide.shape
    runs = min(8, 224 // capacity)
    steps = length // (runs * tokens)
    return pl.pallas_call(
        functools.partial(pick_slots_kernel, capacity, tokens),
        grid=(steps,),
        in_specs=[
            pl.BlockSpec(memory_space=pltpu.SMEM),
            pl.BlockSpec((runs * tokens, wide), lambda i: (i, 0)),
        ],
        out_specs=pl.BlockSpec((runs * capacity, width), lambda i: (i, 0)),
        out_shape=jax.ShapeDtypeStruct((steps * runs * capacity, width), bf16),
        name="pick_slots",
        cost_estimate=pl.CostEstimate(
            flops=2 * length * runs * capacity * width,
            bytes_accessed=3 * length * wide,
            transcendentals=0,
        ),
    )(here.reshape(1), g_wide)


def sigmoid(value):
    return 1.0 / (1.0 + jnp.exp(-value))


def experts_kernel(
    capacity,
    tokens,
    experts,
    here_ref,
    normed_ref,
    g_ref,
    grad_slots_ref,
    in_ref,
    down_ref,
    shared_in_ref,
    shared_out_ref,
    dispatched_ref,
    hidden_ref,
    grad_result_ref,
    grad_proj_ref,
    shared_hidden_ref,
    shared_grad_ref,
    parts_ref,
    gate_dot_ref,
):
    many, slots = normed_ref.shape[0], dispatched_ref.shape[0]
    width = dispatched_ref.shape[1]
    here = here_ref[0]
    normed = normed_ref[:, :width]
    g = g_ref[:, :width]
    spare = normed_ref.shape[1] - width
    gate_rows = dot_nt(one_hot_rows(spare, here, experts + here), normed_ref[:, width:])
    gate_row = gate_rows[0:1] + gate_rows[1:2]
    slot_pick = one_hot_rows(spare, here)
    slot_row = dot_nt(slot_pick, g_ref[:, width:])[0:1] + run_keys((1, many), 1, tokens)
    slot_column = dot_nt(g_ref[:, width:], slot_pick)[:, 0:1] + run_keys((many, 1), 0, tokens)
    takes = slot_keys((slots, 1), 0, capacity) == slot_row
    select = jnp.where(takes, 1.0, 0.0).astype(bf16)
    back = jnp.where(slot_column == slot_keys((1, slots), 1, capacity), 1.0, 0.0).astype(bf16)
    slot_gate = jnp.sum(jnp.where(takes, gate_row, 0.0), axis=1, keepdims=True)

    dispatched = dot(select, normed).astype(bf16)
    dispatched_ref[...] = dispatched
    grad_slots = grad_slots_ref[...].astype(f32)
    grad_result = (grad_slots * slot_gate).astype(bf16)
    grad_result_ref[...] = grad_result

    projected = dot(dispatched, in_ref[...])
    gate, up = projected[:, :EXP_HID], projected[:, EXP_HID:]
    chance = sigmoid(gate)
    silu = gate * chance
    hidden = (silu * up).astype(bf16)
    hidden_ref[...] = hidden
    grad_hidden = dot_nt(grad_result, down_ref[...])
    grad_proj_ref[:, :EXP_HID] = (
        grad_hidden * up * chance * (1.0 + gate * (1.0 - chance))
    ).astype(bf16)
    grad_proj_ref[:, EXP_HID:] = (grad_hidden * silu).astype(bf16)
    result = dot(hidden, down_ref[...]).astype(bf16).astype(f32)
    slot_dot = jnp.sum(grad_slots * result, axis=1, keepdims=True)
    gate_dot = jnp.sum(jnp.where(takes, slot_dot, 0.0), axis=0, keepdims=True)
    gate_dot_ref[...] = jnp.broadcast_to(gate_dot, gate_dot_ref.shape)
    scaled = (result * slot_gate).astype(bf16)
    grad_dispatched = dot_nt(grad_proj_ref[...], in_ref[...]).astype(bf16)

    lanes = shared_out_ref.shape[0]
    shared = dot(normed, shared_in_ref[...])
    shared_gate, shared_up = shared[:, :lanes], shared[:, lanes:]
    shared_chance = sigmoid(shared_gate)
    shared_silu = shared_gate * shared_chance
    shared_hidden = (shared_silu * shared_up).astype(bf16)
    shared_hidden_ref[...] = shared_hidden
    grad_shared = dot_nt(g, shared_out_ref[...])
    shared_grad_ref[:, :lanes] = (
        grad_shared * shared_up * shared_chance * (1.0 + shared_gate * (1.0 - shared_chance))
    ).astype(bf16)
    shared_grad_ref[:, lanes:] = (grad_shared * shared_silu).astype(bf16)
    parts_ref[:, :width] = (
        dot(back, grad_dispatched) + dot_nt(shared_grad_ref[...], shared_in_ref[...])
    ).astype(bf16)
    parts_ref[:, width:] = (
        dot(back, scaled) + dot(shared_hidden, shared_out_ref[...])
    ).astype(bf16)


def run_experts(
    here, normed_wide, g_wide, grad_slots, weight_in, down, shared_in, shared_out, tokens, capacity
):
    length, wide = normed_wide.shape
    width = down.shape[1]
    experts = length // tokens
    runs = min(8, 224 // capacity)
    steps = length // (runs * tokens)
    many, slots = runs * tokens, runs * capacity
    lanes = shared_out.shape[0]

    def block(rows, columns):
        return pl.BlockSpec((rows, columns), lambda i: (i, 0))

    def fixed(value):
        return pl.BlockSpec(value.shape, lambda i: (0, 0), pipeline_mode=pl.Buffered(1))

    def shape(rows, columns, kind=bf16):
        return jax.ShapeDtypeStruct((rows, columns), kind)

    return pl.pallas_call(
        functools.partial(experts_kernel, capacity, tokens, experts),
        grid=(steps,),
        in_specs=[
            pl.BlockSpec(memory_space=pltpu.SMEM),
            block(many, wide),
            block(many, wide),
            block(slots, width),
            fixed(weight_in),
            fixed(down),
            fixed(shared_in),
            fixed(shared_out),
        ],
        out_specs=[
            block(slots, width),
            block(slots, EXP_HID),
            block(slots, width),
            block(slots, 2 * EXP_HID),
            block(many, lanes),
            block(many, 2 * lanes),
            block(many, 2 * width),
            pl.BlockSpec((8, many), lambda i: (0, i)),
        ],
        out_shape=[
            shape(steps * slots, width),
            shape(steps * slots, EXP_HID),
            shape(steps * slots, width),
            shape(steps * slots, 2 * EXP_HID),
            shape(length, lanes),
            shape(length, 2 * lanes),
            shape(length, 2 * width),
            shape(8, length, f32),
        ],
        name="experts",
        cost_estimate=pl.CostEstimate(
            flops=20 * 10**9, bytes_accessed=40 * 10**6, transcendentals=2 * 10**6
        ),
    )(here.reshape(1), normed_wide, g_wide, grad_slots, weight_in, down, shared_in, shared_out)


def slot_table(span_picks, span_order, experts):
    tokens = span_picks.shape[0]
    order = span_order.reshape(tokens, TOP)
    onehot = span_picks[:, :, None] == jnp.arange(experts, dtype=jnp.int32)
    picked = jnp.any(onehot, axis=1)
    rank_key = jnp.sum(jnp.where(onehot, order[:, :, None], 0), axis=1)
    rank_key = jnp.where(picked, rank_key, tokens * TOP)
    before = rank_key[:, None, :] < rank_key[None, :, :]
    slots = jnp.sum(before.astype(jnp.int32), axis=0)
    return jnp.where(picked, slots, 2 * tokens)


def on_device(
    inputs,
    norm1_gain,
    w_query,
    w_key,
    w_value,
    w_output,
    norm2_gain,
    router,
    shared_gate_up_weight,
    shared_down_weight,
    expert_in,
    expert_out,
    picks,
    fill_order,
    grad_out,
):
    spans = lax.axis_size("ctx")
    here = lax.axis_index("ctx")
    side = lax.axis_index("fsdp")
    core = here % 2
    tokens, width = inputs.shape[1:]
    half = width // 2
    length = spans * tokens
    experts = spans * expert_in.shape[0]
    capacity = tokens * TOP // experts
    head = jnp.minimum(ring_position(here, spans), HEADS - 1)
    units = EXP_HID // spans
    ring = ring_of(spans)
    is_ring = spans == 16
    groups = [ring] if is_ring else None
    swap_core = [(i, i ^ 1) for i in range(spans)]

    def across(value):
        return lax.ppermute(value, "fsdp", [(0, 1), (1, 0)])

    def ordered(own, other, axis):
        return jnp.where(
            side == 0,
            jnp.concatenate([own, other], axis=axis),
            jnp.concatenate([other, own], axis=axis),
        )

    def everyone(value):
        return lax.all_gather(value, "ctx", axis=0, tiled=True, axis_index_groups=groups)

    def columns(value, start, count):
        return lax.dynamic_slice_in_dim(value, start, count, 1)

    def rows(value, start, count):
        return lax.dynamic_slice_in_dim(value, start, count, 0)

    def halves(value, axis=0):
        size = value.shape[axis] // 2
        mine = lax.dynamic_slice_in_dim(value, side * size, size, axis)
        theirs = lax.dynamic_slice_in_dim(value, (1 - side) * size, size, axis)
        return mine, theirs

    def reduced(value, axis=0):
        mine, theirs = halves(value, axis)
        return mine + across(theirs.astype(bf16)).astype(f32)

    def swapped(value):
        return lax.all_to_all(value, "ctx", split_axis=0, concat_axis=0, tiled=True)

    def row_major(value):
        return with_layout_constraint(value, Layout(tuple(range(value.ndim))))

    x = inputs[0]
    g = grad_out[0]
    x_all = everyone(x)
    spare = -(-2 * experts // HEAD_DIM) * HEAD_DIM
    own_table = slot_table(picks[0], fill_order[0, 0], experts)
    own_table = jnp.pad(
        own_table.astype(f32), ((0, 0), (0, spare - experts)), constant_values=2.0 * tokens
    )
    g_wide = jnp.concatenate([g, own_table.astype(bf16)], axis=1)
    head_own = jnp.concatenate(
        [columns(w, head * HEAD_DIM, HEAD_DIM) for w in (w_query, w_key, w_value)], axis=1
    )
    head_other = across(head_own)
    small = jnp.concatenate([router.T, norm1_gain[None], norm2_gain[None]], axis=0)
    small_other = across(small)
    output_near = across(columns(w_output, core * half, half))
    lanes = -(-units // HEAD_DIM) * HEAD_DIM
    shared_in_own = jnp.concatenate(
        [
            jnp.pad(
                columns(shared_gate_up_weight, at + here * units, units),
                ((0, 0), (0, lanes - units)),
            )
            for at in (0, EXP_HID)
        ],
        axis=1,
    )
    shared_rows = shared_down_weight.shape[0]
    shared_out_own = rows(shared_down_weight, here * units % shared_rows, units)
    ring_blocks = jnp.asarray(ring, jnp.int32)[:, None] * tokens
    positions = (ring_blocks + jnp.arange(tokens, dtype=jnp.int32)[None, :]).reshape(length)
    cosine, sine = rotary_tables(positions, HEAD_DIM)
    lane = lax.broadcasted_iota(jnp.int32, (length, HEAD_DIM), 1)
    sine = jnp.where(lane < HEAD_DIM // 2, -sine, sine)
    small = ordered(small, small_other, 1)
    router_w = small[:experts]
    gain_one = small[experts : experts + 1].astype(f32)
    gain_two = small[experts + 1 :].astype(f32)
    quarter = half // 8
    chunks = [expert_in[0, :quarter], expert_in[0, quarter:]]
    head_other, *chunks = tied(head_other, *chunks)
    chunks = [across(chunk) for chunk in chunks]
    x_all, cosine, sine, head_other, gain_one, output_near, chunks[0] = tied(
        x_all, cosine, sine, head_other, gain_one, output_near, chunks[0]
    )
    output_far = lax.ppermute(output_near, "ctx", swap_core)
    g_wide_all = everyone(after(g_wide, x_all))
    g_all = g_wide_all[:, :width]
    table = g_wide_all[:, width : width + experts]

    normed1_all, query, key, value = project(
        side, x_all, gain_one, head_own, head_other, cosine, sine
    )
    context, lse, attended = attend(query, key, value, is_ring)
    attended, output_far = tied(attended, output_far)
    down_other = across(after(expert_out[0], attended))
    shared_in_other = across(after(shared_in_own, attended))
    shared_out_other = across(after(shared_out_own, attended))
    got = swapped(attended.reshape(spans, tokens, HEAD_DIM))
    got, chunks[1] = tied(got, chunks[1])
    spot = jnp.stack([side, core]).astype(jnp.int32)
    router_pad = jnp.pad(router_w, ((0, spare - experts), (0, 0)))
    second, normed2_wide, scale_two, own_gates, attended = mix(
        spot,
        got,
        w_output,
        output_near,
        output_far,
        x,
        gain_two,
        router_pad,
        own_table,
        experts,
    )
    normed2_wide, g_wide_all = tied(normed2_wide, g_wide_all)
    normed2_wide = everyone(normed2_wide)
    grad_slots = pick_slots(here, g_wide_all, width, capacity, tokens)
    down_w = ordered(expert_out[0], down_other, 0)
    expert_w = ordered(expert_in[0], jnp.concatenate(chunks, axis=0), 0)
    shared_in = ordered(shared_in_own, shared_in_other, 0)
    shared_out = jnp.where(
        here * units // shared_rows == side, shared_out_own, shared_out_other
    )
    shared_out = jnp.pad(shared_out, ((0, lanes - units), (0, 0)))
    normed2_wide, grad_slots, down_w, expert_w, shared_in, shared_out = tied(
        normed2_wide, grad_slots, down_w, expert_w, shared_in, shared_out
    )
    normed2_all = normed2_wide[:, :width]
    attended_all = everyone(after(attended, normed2_wide))
    dense = [
        columns(after(w, normed2_wide), core * half, half) for w in (w_query, w_key, w_value)
    ]
    dense = jnp.concatenate(dense, axis=0)
    near = [across(dense[: dense.shape[0] // 2]), across(dense[dense.shape[0] // 2 :])]
    spots = [ring_position(i, spans) for i in range(spans)]
    (
        dispatched,
        expert_hidden,
        grad_result,
        grad_proj,
        shared_hidden,
        grad_sproj,
        parts,
        gate_dot,
    ) = run_experts(
        here,
        normed2_wide,
        g_wide_all,
        grad_slots,
        expert_w,
        down_w,
        shared_in,
        shared_out,
        tokens,
        capacity,
    )
    parts, near[0], attended_all = tied(parts, near[0], attended_all)
    sums = lax.psum_scatter(
        parts, "ctx", scatter_dimension=0, tiled=True, axis_index_groups=groups
    )
    gate_dot = gate_dot[0].reshape(spans, tokens)
    grad_shared_in = dot_tn(grad_sproj, normed2_all)
    grad_shared_in = jnp.concatenate(
        [grad_shared_in[:units], grad_shared_in[lanes : lanes + units]], axis=0
    )
    grad_shared_in = reduced(grad_shared_in, 1).astype(bf16)
    grad_shared_out = dot_tn(shared_hidden, g_all)[:units].astype(bf16)
    grad_shared_out = grad_shared_out.astype(f32) + across(grad_shared_out).astype(f32)
    grad_shared_out = grad_shared_out.astype(bf16)
    shared_grads = jnp.concatenate(
        [grad_shared_in, grad_shared_out[:, :half], grad_shared_out[:, half:]], axis=0
    )
    gate_dot = jnp.concatenate([gate_dot[i : i + 1] for i in spots], axis=0)
    gate_grads = swapped(after(gate_dot, parts)[:, None, :])[:, 0, :].T

    near = jnp.concatenate(near, axis=0)
    far = lax.ppermute(near, "ctx", swap_core)
    own_down, down_theirs = halves(dot_tn(expert_hidden, grad_result))
    own_gate_grad, gate_theirs = halves(dot_tn(dispatched, grad_proj[:, :EXP_HID]))
    own_up_grad, up_theirs = halves(dot_tn(dispatched, grad_proj[:, EXP_HID:]))
    down_theirs = across(after(down_theirs.astype(bf16), parts))
    sums, gate_theirs, up_theirs, down_theirs, near, far, shared_grads, gate_grads = tied(
        sums,
        gate_theirs.astype(bf16),
        up_theirs.astype(bf16),
        down_theirs,
        near,
        far,
        row_major(shared_grads),
        gate_grads,
    )
    shared_grads = everyone(shared_grads[None])
    gate_theirs, up_theirs = across(gate_theirs), across(up_theirs)

    sent, grad_second, layer_out = mix_back(
        spot,
        sums,
        own_gates,
        jnp.pad(gate_grads, ((0, 0), (0, spare - experts))),
        router_pad,
        second,
        scale_two,
        gain_two,
        g,
        w_output,
        output_near,
        output_far,
        spans,
    )
    arrived = swapped(sent)
    arrived, gate_theirs = tied(arrived, gate_theirs)
    grad_heads, grad_heads_ring = attend_back(
        query, key, value, arrived, context, lse, cosine, sine, is_ring
    )
    cut = width // spans
    extras = jnp.concatenate([arrived[i, :tokens, HEAD_DIM:] for i in ring], axis=0)
    gain_rows = arrived[:, tokens : tokens + 2, HEAD_DIM : HEAD_DIM + cut].astype(f32)
    gain_rows = jnp.sum(gain_rows, axis=(0, 1))
    gain_rows = jnp.pad(gain_rows.reshape(1, cut), ((0, 15), (0, HEAD_DIM - cut)))
    grad_router = dot_tn(normed2_all, extras)[:, cut : cut + experts]
    mine, theirs = halves(grad_router)
    grad_router = mine + across(theirs)
    mine, theirs = halves(dot_tn(attended_all, extras))
    gain_high = gain_rows.astype(bf16)
    gain_low = jnp.roll((gain_rows - gain_high.astype(f32)).astype(bf16), 1, axis=0)
    theirs = jnp.concatenate([theirs.astype(bf16), gain_high + gain_low], axis=0)
    theirs = across(theirs).astype(f32)
    grad_output = mine + theirs[:half]
    gain_rows = gain_rows[:1] + theirs[half : half + 1] + theirs[half + 1 : half + 2]
    gain_high = gain_rows.astype(bf16)
    gain_low = (gain_rows - gain_high.astype(f32)).astype(bf16)
    gain_rows = jnp.pad(
        jnp.concatenate([gain_high, gain_low], axis=0), ((0, 14), (3 * HEAD_DIM, 0))
    )
    grad_head_w = reduced(dot_tn(normed1_all, grad_heads_ring)).astype(bf16)
    part = jnp.sum(grad_head_w.astype(f32) * head_own.astype(f32), axis=1, keepdims=True)
    part_high = part.astype(bf16).astype(f32)
    lane = lax.broadcasted_iota(jnp.int32, (half, HEAD_DIM), 1)
    grad_output = jnp.where(lane < cut, grad_output, 0.0)
    grad_output = jnp.where(lane == cut, part_high, grad_output)
    grad_output = jnp.where(lane == cut + 1, part - part_high, grad_output)
    head_grads = jnp.concatenate([grad_head_w, grad_output.astype(bf16)], axis=1)
    head_grads = jnp.concatenate([head_grads, gain_rows], axis=0)
    got = swapped(grad_heads.reshape(spans, tokens, 3 * HEAD_DIM))
    head_grads, got = tied(row_major(head_grads), got)
    head_grads = everyone(head_grads[None])

    grad_inputs = inputs_back(
        side, core, got, w_query, w_key, w_value, near, far, x, gain_one, grad_second
    )
    grad_inputs, up_theirs = tied(grad_inputs, up_theirs)
    grad_query, grad_key, grad_value, grad_output, grad_norm1 = place_heads(
        head_grads, norm1_gain[:, None].astype(f32), width
    )
    norm2_rows = head_grads[:, half : half + 2, 3 * HEAD_DIM : 3 * HEAD_DIM + cut]
    norm2_rows = jnp.sum(norm2_rows.astype(f32), axis=1)
    norm2_rows = jnp.concatenate([norm2_rows[i] for i in spots], axis=0)
    grad_norm2 = lax.dynamic_slice_in_dim(norm2_rows, side * half, half)
    grad_expert_in = jnp.concatenate(
        [own_gate_grad + gate_theirs.astype(f32), own_up_grad + up_theirs.astype(f32)], axis=1
    )
    grad_shared_in, grad_shared_out = place_shared(shared_grads, side)
    return (
        layer_out[None],
        grad_inputs[None],
        grad_norm1[:, 0],
        grad_query,
        grad_key,
        grad_value,
        grad_output,
        grad_norm2,
        grad_router,
        grad_shared_in,
        grad_shared_out,
        grad_expert_in[None],
        (own_down + down_theirs.astype(f32))[None],
    )


def solution(mesh):
    placed = (
        P("fsdp", "ctx", None),
        P("fsdp"),
        P("fsdp", None),
        P("fsdp", None),
        P("fsdp", None),
        P("fsdp", None),
        P("fsdp"),
        P("fsdp", None),
        P("fsdp", None),
        P("fsdp", None),
        P("ctx", "fsdp", None),
        P("ctx", "fsdp", None),
        P("fsdp", "ctx", None),
        P("fsdp", "ctx", None),
        P("fsdp", "ctx", None),
    )
    return jax.shard_map(
        on_device,
        mesh=mesh,
        in_specs=placed,
        out_specs=(
            P("fsdp", "ctx", None),
            P("fsdp", "ctx", None),
            P("fsdp"),
            P("fsdp", None),
            P("fsdp", None),
            P("fsdp", None),
            P("fsdp", None),
            P("fsdp"),
            P("fsdp", None),
            P("fsdp", None),
            P("fsdp", None),
            P("ctx", "fsdp", None),
            P("ctx", "fsdp", None),
        ),
        check_vma=False,
    )
```

```python
import functools
import math

import jax
import jax.numpy as jnp
from jax import lax
from jax.experimental import pallas as pl
from jax.experimental.layout import Layout, with_layout_constraint
from jax.experimental.pallas import tpu as pltpu
from jax.sharding import PartitionSpec as P

HEADS = 10
HEAD_DIM = 128
EXP_HID = 896
TOP = 7
BLOCK = 256
TILE = 512

epsilon = 1e-06
masked_score = -1000000000.0
score_scale = 1.0 / math.sqrt(HEAD_DIM)
exact = lax.Precision.HIGHEST
f32 = jnp.float32
bf16 = jnp.bfloat16


def dot(a, b):
    return jnp.dot(a, b, preferred_element_type=f32)


def dot_nt(a, b):
    return lax.dot_general(a, b, (((1,), (1,)), ((), ())), preferred_element_type=f32)


def dot_tn(a, b):
    return lax.dot_general(a, b, (((0,), (0,)), ((), ())), preferred_element_type=f32)


def rms_scale(values):
    return lax.rsqrt(jnp.mean(values * values, axis=-1, keepdims=True) + epsilon)


def rotary_tables(positions, width):
    half = width // 2
    freqs = jnp.exp(-math.log(10000.0) * jnp.arange(half, dtype=f32) * 2.0 / width)
    angles = positions.astype(f32)[:, None] * freqs[None, :]
    cosine = jnp.concatenate([jnp.cos(angles), jnp.cos(angles)], axis=-1)
    sine = jnp.concatenate([jnp.sin(angles), jnp.sin(angles)], axis=-1)
    return (cosine, sine)


def allowed_tile(rows, columns):
    key_block = lax.broadcasted_iota(jnp.int32, (rows, columns), 0) // BLOCK
    query_block = lax.broadcasted_iota(jnp.int32, (rows, columns), 1) // BLOCK
    return key_block <= query_block


def ring_of(spans):
    if spans != 16:
        return list(range(spans))
    chips = [0, 2, 4, 6, 7, 5, 3, 1]
    return [2 * chip + core for chip in chips for core in (0, 1)]


def pieces(j, tile, length, ring):
    if ring:
        starts = (j * BLOCK, length - BLOCK - j * BLOCK)
        return [pl.ds(pl.multiple_of(at, BLOCK), BLOCK) for at in starts]
    return [pl.ds(pl.multiple_of(j * tile, tile), tile)]


def load(ref, windows, columns=slice(None)):
    parts = [ref[window, columns] for window in windows]
    return parts[0] if len(parts) == 1 else jnp.concatenate(parts, axis=0)


def store(ref, windows, value, columns=slice(None)):
    size = value.shape[0] // len(windows)
    for i, window in enumerate(windows):
        ref[window, columns] = value[i * size : (i + 1) * size]


def attend_kernel(
    ring, q_ref, k_ref, v_ref, context_ref, lse_ref, low_ref, score_ref
):
    length = k_ref.shape[0]
    tile = context_ref.shape[0]
    here = pl.program_id(0)
    queries = load(q_ref, pieces(here, tile, length, ring))

    def raw_scores(j):
        return dot_nt(load(k_ref, pieces(j, tile, length, ring)), queries) * score_scale

    def fold(j, scores, peak):
        score_ref[pl.ds(pl.multiple_of(j * tile, tile), tile), :] = scores
        return jnp.maximum(peak, jnp.max(scores.reshape(tile // 8, 8, tile), axis=0))

    diagonal = jnp.where(allowed_tile(tile, tile), raw_scores(here), masked_score)
    peak = fold(here, diagonal, jnp.full((8, tile), masked_score, f32))
    peak = lax.fori_loop(0, here, lambda j, p: fold(j, raw_scores(j), p), peak)
    top = jnp.max(peak, axis=0, keepdims=True)

    def gather(j, carry):
        total, numer = carry
        weights = jnp.exp(score_ref[pl.ds(pl.multiple_of(j * tile, tile), tile), :] - top)
        total = total + jnp.sum(weights.reshape(tile // 8, 8, tile), axis=0)
        values = load(v_ref, pieces(j, tile, length, ring))
        return total, numer + dot_tn(values, weights.astype(bf16))

    zero = (jnp.zeros((8, tile), f32), jnp.zeros((HEAD_DIM, tile), f32))
    total, numer = lax.fori_loop(0, here + 1, gather, zero)
    total = jnp.sum(total, axis=0, keepdims=True)
    context = (numer / total).T
    context_ref[...] = context
    low_ref[...] = context.astype(bf16)
    lse_ref[...] = top + jnp.log(total)


def attend(query, key, value, ring):
    length = query.shape[0]
    tile = min(TILE, length)
    whole = pl.BlockSpec((length, HEAD_DIM), lambda i: (0, 0))
    part = pl.BlockSpec((tile, HEAD_DIM), lambda i: (i, 0))
    return pl.pallas_call(
        functools.partial(attend_kernel, ring),
        grid=(length // tile,),
        in_specs=[whole] * 3,
        out_specs=[part, pl.BlockSpec((1, tile), lambda i: (0, i)), part],
        out_shape=[
            jax.ShapeDtypeStruct((length, HEAD_DIM), f32),
            jax.ShapeDtypeStruct((1, length), f32),
            jax.ShapeDtypeStruct((length, HEAD_DIM), bf16),
        ],
        scratch_shapes=[pltpu.VMEM((length, tile), f32)],
        name="attend",
        cost_estimate=pl.CostEstimate(
            flops=2 * length * length * HEAD_DIM,
            bytes_accessed=12 * length * HEAD_DIM,
            transcendentals=length * length // 2,
        ),
    )(query, key, value)


def attend_back_kernel(
    ring,
    q_ref,
    k_ref,
    v_ref,
    grad_ref,
    context_ref,
    lse_ref,
    cos_ref,
    sin_ref,
    out_ref,
    out_ring_ref,
    dq_ref,
    delta_ref,
    dk_ref,
    dv_ref,
):
    length = q_ref.shape[0]
    tile = dk_ref.shape[0]
    steps = length // tile
    here = pl.program_id(0)

    def natural(i):
        return pl.ds(pl.multiple_of(i * tile, tile), tile)

    @pl.when(here == 0)
    def _():
        def prepare(i, carry):
            window = natural(i)
            dq_ref[window, :] = jnp.zeros((tile, HEAD_DIM), f32)
            product = grad_ref[window, :].astype(f32) * context_ref[window, :]
            ones = jnp.ones((8, HEAD_DIM), f32)
            delta = lax.dot_general(
                ones, product, (((1,), (1,)), ((), ())), precision=exact, preferred_element_type=f32
            )
            delta_ref[:, window] = delta
            return carry

        lax.fori_loop(0, steps, prepare, 0)

    keys = load(k_ref, pieces(here, tile, length, ring))
    values = load(v_ref, pieces(here, tile, length, ring))

    def visit(i, masked):
        window = natural(i)
        queries = load(q_ref, pieces(i, tile, length, ring))
        grads = grad_ref[window, :]
        weights = jnp.exp(dot_nt(keys, queries) * score_scale - lse_ref[:, window])
        if masked:
            weights = jnp.where(allowed_tile(tile, tile), weights, 0.0)
        grad_weights = dot_nt(values, grads)
        grad_raw = (weights * (grad_weights - delta_ref[0:1, window]) * score_scale).astype(bf16)
        dq_ref[window, :] += dot_tn(grad_raw, keys)
        return dot(grad_raw, queries), dot(weights.astype(bf16), grads)

    dk, dv = visit(here, True)
    dk_ref[...] = dk
    dv_ref[...] = dv

    def step(i, carry):
        more_k, more_v = visit(i, False)
        dk_ref[...] += more_k
        dv_ref[...] += more_v
        return carry

    lax.fori_loop(here + 1, steps, step, 0)

    def write(i, part, value):
        at = slice(part * HEAD_DIM, (part + 1) * HEAD_DIM)
        out_ref[natural(i), at] = value
        store(out_ring_ref, pieces(i, tile, length, ring), value, at)

    def turned_back(i, value):
        windows = pieces(i, tile, length, ring)
        scaled = pltpu.roll(value * load(sin_ref, windows), HEAD_DIM // 2, 1)
        return (value * load(cos_ref, windows) + scaled).astype(bf16)

    write(here, 1, turned_back(here, dk_ref[...]))
    write(here, 2, dv_ref[...].astype(bf16))

    @pl.when(here == steps - 1)
    def _():
        def finish(i, carry):
            write(i, 0, turned_back(i, dq_ref[natural(i), :]))
            return carry

        lax.fori_loop(0, steps, finish, 0)


def attend_back(query, key, value, grad, context, lse, cosine, sine, ring):
    length = query.shape[0]
    tile = min(TILE, length)
    memory = pl.BlockSpec(memory_space=pltpu.VMEM)
    return pl.pallas_call(
        functools.partial(attend_back_kernel, ring),
        grid=(length // tile,),
        in_specs=[memory] * 8,
        out_specs=[memory] * 2,
        out_shape=[jax.ShapeDtypeStruct((length, 3 * HEAD_DIM), bf16)] * 2,
        scratch_shapes=[
            pltpu.VMEM((length, HEAD_DIM), f32),
            pltpu.VMEM((8, length), f32),
            pltpu.VMEM((tile, HEAD_DIM), f32),
            pltpu.VMEM((tile, HEAD_DIM), f32),
        ],
        name="attend_back",
        cost_estimate=pl.CostEstimate(
            flops=5 * length * length * HEAD_DIM,
            bytes_accessed=20 * length * HEAD_DIM,
            transcendentals=length * length // 2,
        ),
    )(query, key, value, grad, context, lse, cosine, sine)


def project_kernel(
    side_ref, x_ref, gain_ref, own_ref, other_ref, cos_ref, sin_ref, normed_ref, q_ref, k_ref, v_ref
):
    own, other = own_ref[...], other_ref[...]
    weight = jnp.where(
        side_ref[0] == 0,
        jnp.concatenate([own, other], axis=0),
        jnp.concatenate([other, own], axis=0),
    )
    resid = x_ref[...].astype(f32)
    normed = (resid * rms_scale(resid) * gain_ref[...]).astype(bf16)
    normed_ref[...] = normed
    projected = dot(normed, weight)
    for out, at in ((q_ref, 0), (k_ref, HEAD_DIM)):
        part = projected[:, at : at + HEAD_DIM]
        turned = pltpu.roll(part, HEAD_DIM // 2, 1)
        out[...] = (part * cos_ref[...] + turned * sin_ref[...]).astype(bf16)
    v_ref[...] = projected[:, 2 * HEAD_DIM :].astype(bf16)


def project(side, x, gain, own, other, cosine, sine):
    length, width = x.shape
    tile = min(TILE, length)
    part = pl.BlockSpec((tile, HEAD_DIM), lambda i: (i, 0))
    wide = pl.BlockSpec((tile, width), lambda i: (i, 0))
    return pl.pallas_call(
        project_kernel,
        grid=(length // tile,),
        in_specs=[
            pl.BlockSpec(memory_space=pltpu.SMEM),
            wide,
            pl.BlockSpec((1, width), lambda i: (0, 0)),
            pl.BlockSpec(own.shape, lambda i: (0, 0)),
            pl.BlockSpec(own.shape, lambda i: (0, 0)),
            part,
            part,
        ],
        out_specs=[wide, part, part, part],
        out_shape=[jax.ShapeDtypeStruct((length, width), bf16)]
        + [jax.ShapeDtypeStruct((length, HEAD_DIM), bf16)] * 3,
        name="project",
        cost_estimate=pl.CostEstimate(
            flops=6 * length * width * HEAD_DIM,
            bytes_accessed=4 * length * width,
            transcendentals=0,
        ),
    )(side.reshape(1), x, gain, own, other, cosine, sine)


def head_pairs(side, spans):
    ring = ring_of(spans)
    count = HEADS // 2
    pairs = []
    for i in range(count):
        low, high = ring[i], ring[count + i]
        mine = jnp.where(side == 0, low, high)
        theirs = jnp.where(side == 0, high, low)
        pairs.append((mine, theirs, slice(i * HEAD_DIM, (i + 1) * HEAD_DIM)))
    return pairs


def mix_kernel(
    experts,
    spot_ref,
    got_ref,
    own_ref,
    near_ref,
    far_ref,
    x_ref,
    gain_ref,
    router_ref,
    table_ref,
    second_ref,
    low_ref,
    scale_ref,
    gates_ref,
    attended_ref,
):
    ring = ring_of(got_ref.shape[0])
    for h in range(HEADS):
        attended_ref[:, h * HEAD_DIM : (h + 1) * HEAD_DIM] = got_ref[ring[h]]
    second = x_ref[...].astype(f32)
    tokens, width = second.shape
    half = near_ref.shape[1]
    near = jnp.zeros((tokens, half), f32)
    far = near
    for mine, theirs, at in head_pairs(spot_ref[0], got_ref.shape[0]):
        second += dot(got_ref[mine], own_ref[at, :])
        near += dot(got_ref[theirs], near_ref[at, :])
        far += dot(got_ref[theirs], far_ref[at, :])
    second += jnp.where(
        spot_ref[1] == 0,
        jnp.concatenate([near, far], axis=1),
        jnp.concatenate([far, near], axis=1),
    )
    scale = rms_scale(second)
    second_ref[...] = second
    scale_ref[...] = scale
    normed = (second * scale * gain_ref[...]).astype(bf16)
    logits = dot_nt(normed, router_ref[...])
    picked = table_ref[...] < tokens
    peak = jnp.max(jnp.where(picked, logits, masked_score), axis=-1, keepdims=True)
    chances = jnp.where(picked, jnp.exp(logits - peak), 0.0)
    gates = chances / jnp.sum(chances, axis=-1, keepdims=True)
    gates_ref[...] = gates
    high = gates.astype(bf16).astype(f32)
    rest = pltpu.roll(gates - high, experts, 1)
    low_ref[:, :width] = normed
    low_ref[:, width:] = (high + rest).astype(bf16)


def mix(spot, got, own, near, far, x, gain, router, table, experts):
    smem = pl.BlockSpec(memory_space=pltpu.SMEM)
    memory = pl.BlockSpec(memory_space=pltpu.VMEM)
    tokens, width = x.shape
    spare = table.shape[1]
    return pl.pallas_call(
        functools.partial(mix_kernel, experts),
        in_specs=[smem] + [memory] * 8,
        out_specs=[memory] * 5,
        out_shape=[
            jax.ShapeDtypeStruct(x.shape, f32),
            jax.ShapeDtypeStruct((tokens, width + spare), bf16),
            jax.ShapeDtypeStruct((tokens, 1), f32),
            jax.ShapeDtypeStruct((tokens, spare), f32),
            jax.ShapeDtypeStruct(x.shape, bf16),
        ],
        name="mix",
    )(spot, got, own, near, far, x, gain, router, table)


def mix_back_kernel(
    spot_ref,
    sums_ref,
    gates_ref,
    gate_grads_ref,
    router_ref,
    second_ref,
    scale_ref,
    gain_ref,
    g_ref,
    own_ref,
    near_ref,
    far_ref,
    send_ref,
    cuts_ref,
    grad_second_ref,
    out_ref,
):
    tokens, width = second_ref.shape
    second = second_ref[...]
    scale = scale_ref[...]
    gain = gain_ref[...]
    gates = gates_ref[...]
    gate_grads = gate_grads_ref[...]
    out_ref[...] = (second + sums_ref[:, width:].astype(f32)).astype(bf16)
    weighted = gates * gate_grads
    grad_sel = weighted - gates * jnp.sum(weighted, axis=-1, keepdims=True)
    grad_logits = grad_sel.astype(bf16)
    grad_normed = sums_ref[:, :width].astype(f32) + dot(grad_logits, router_ref[...])
    gain_part = jnp.sum(grad_normed * second * scale, axis=0, keepdims=True)
    hat = grad_normed * gain
    mean = jnp.mean(hat * second, axis=-1, keepdims=True)
    grad_second = g_ref[...].astype(f32) + scale * hat - second * (scale * scale * scale) * mean
    grad_second_ref[...] = grad_second
    grad_mixed = grad_second.astype(bf16)
    spans = send_ref.shape[0]
    cut = width // spans
    lane = lax.broadcasted_iota(jnp.int32, (1, HEAD_DIM), 1)
    high = gain_part.astype(bf16).astype(f32)
    row = lax.broadcasted_iota(jnp.int32, (16, width), 0)
    gain_rows = jnp.where(row == 0, high, jnp.where(row == 1, gain_part - high, 0.0))
    shifted = pltpu.roll(grad_logits.astype(f32), cut, 1)
    for k, c in enumerate(ring_of(spans)):
        start = min(c * cut // HEAD_DIM * HEAD_DIM, width - 2 * HEAD_DIM)
        shift = (start - c * cut) % (2 * HEAD_DIM)
        for value, rest, out_rows in (
            (grad_second, shifted, slice(0, tokens)),
            (gain_rows, 0.0, slice(tokens, tokens + 16)),
        ):
            window = pltpu.roll(value[:, start : start + 2 * HEAD_DIM], shift, 1)[:, :HEAD_DIM]
            window = jnp.where(lane < cut, window, 0.0) + rest
            cuts_ref[k, out_rows, :] = window.astype(bf16)
    left, right = grad_mixed[:, : width // 2], grad_mixed[:, width // 2 :]
    at_near = jnp.where(spot_ref[1] == 0, left, right)
    at_far = jnp.where(spot_ref[1] == 0, right, left)
    for mine, theirs, at in head_pairs(spot_ref[0], spans):
        send_ref[mine] = dot_nt(grad_mixed, own_ref[at, :]).astype(bf16)
        other = dot_nt(at_near, near_ref[at, :]) + dot_nt(at_far, far_ref[at, :])
        send_ref[theirs] = other.astype(bf16)
    for h in ring_of(spans)[HEADS:]:
        send_ref[h] = jnp.zeros((tokens, HEAD_DIM), bf16)


def mix_back(spot, sums, gates, gate_grads, router, second, scale, gain, g, own, near, far, spans):
    tokens, width = second.shape
    smem = pl.BlockSpec(memory_space=pltpu.SMEM)
    memory = pl.BlockSpec(memory_space=pltpu.VMEM)
    return pl.pallas_call(
        mix_back_kernel,
        in_specs=[smem] + [memory] * 11,
        out_specs=[memory] * 4,
        out_shape=[
            jax.ShapeDtypeStruct((spans, tokens, HEAD_DIM), bf16),
            jax.ShapeDtypeStruct((spans, tokens + 16, HEAD_DIM), bf16),
            jax.ShapeDtypeStruct((tokens, width), f32),
            jax.ShapeDtypeStruct((tokens, width), bf16),
        ],
        name="mix_back",
    )(spot, sums, gates, gate_grads, router, second, scale, gain, g, own, near, far)


def inputs_back_kernel(
    side_ref,
    core_ref,
    got_ref,
    wq_ref,
    wk_ref,
    wv_ref,
    near_ref,
    far_ref,
    x_ref,
    gain_ref,
    grad_second_ref,
    out_ref,
):
    tokens, width = x_ref.shape
    half = width // 2
    count = HEADS // 2
    own_part = jnp.zeros((tokens, half), f32)
    other_part = jnp.zeros((tokens, half), f32)
    ring = ring_of(got_ref.shape[0])
    for i, weight in enumerate((wq_ref, wk_ref, wv_ref)):
        at = slice(i * HEAD_DIM, (i + 1) * HEAD_DIM)
        for h in range(0, HEADS, 2):
            grads = jnp.concatenate([got_ref[ring[h], :, at], got_ref[ring[h + 1], :, at]], axis=1)
            own_part += dot_nt(grads, weight[:, h * HEAD_DIM : (h + 2) * HEAD_DIM])
        rows = slice(i * half, (i + 1) * half)
        for h in range(count):
            window = slice(h * HEAD_DIM, (h + 1) * HEAD_DIM)
            low, high = ring[h], ring[count + h]
            mine = jnp.where(core_ref[0] == 0, low, high)
            theirs = jnp.where(core_ref[0] == 0, high, low)
            grads = jnp.concatenate([got_ref[mine, :, at], got_ref[theirs, :, at]], axis=1)
            weights = jnp.concatenate([near_ref[rows, window], far_ref[rows, window]], axis=1)
            other_part += dot_nt(grads, weights)
    grad_normed = jnp.where(
        side_ref[0] == 0,
        jnp.concatenate([own_part, other_part], axis=1),
        jnp.concatenate([other_part, own_part], axis=1),
    )
    resid = x_ref[...].astype(f32)
    scale = rms_scale(resid)
    hat = grad_normed * gain_ref[...]
    mean = jnp.mean(hat * resid, axis=-1, keepdims=True)
    out_ref[...] = grad_second_ref[...] + scale * hat - resid * (scale * scale * scale) * mean


def inputs_back(side, core, got, w_query, w_key, w_value, near, far, x, gain, grad_second):
    smem = pl.BlockSpec(memory_space=pltpu.SMEM)
    memory = pl.BlockSpec(memory_space=pltpu.VMEM)
    return pl.pallas_call(
        inputs_back_kernel,
        in_specs=[smem] * 2 + [memory] * 9,
        out_specs=memory,
        out_shape=jax.ShapeDtypeStruct(x.shape, f32),
        name="inputs_back",
    )(
        side.reshape(1),
        core.reshape(1),
        got,
        w_query,
        w_key,
        w_value,
        near,
        far,
        x,
        gain,
        grad_second,
    )


def place_heads_kernel(
    cut,
    side_ref,
    heads_ref,
    rest_ref,
    gain_rows_ref,
    gain_ref,
    q_ref,
    k_ref,
    v_ref,
    output_ref,
    norm_ref,
    norm2_ref,
):
    for h in range(HEADS):
        at = slice(h * HEAD_DIM, (h + 1) * HEAD_DIM)
        for i, out in enumerate((q_ref, k_ref, v_ref)):
            out[:, at] = heads_ref[h, :, i * HEAD_DIM : (i + 1) * HEAD_DIM].astype(f32)
    sums = rest_ref[0].astype(f32)
    for h in range(1, HEADS):
        sums += rest_ref[h].astype(f32)
    lane = lax.broadcasted_iota(jnp.int32, (8, HEAD_DIM), 1)
    pair = jnp.where((lane == cut) | (lane == cut + 1), 1.0, 0.0)
    row = lax.dot_general(
        pair, sums, (((1,), (1,)), ((), ())), precision=exact, preferred_element_type=f32
    )
    norm_ref[0] = row[0:1] / gain_ref[0]
    spans = rest_ref.shape[0]

    @pl.when(pl.program_id(0) == 0)
    def _():
        for i in range(spans // 2):
            low, high = ring_position(i, spans), ring_position(spans // 2 + i, spans)
            rows = gain_rows_ref[jnp.where(side_ref[0] == 0, low, high)].astype(f32)
            norm2_ref[i : i + 1, :] = rows[0:1] + rows[1:2]

    for c in range(spans):
        piece = rest_ref[ring_position(c, spans), :, :cut].astype(f32)
        output_ref[:, c * cut : (c + 1) * cut] = piece


def ring_position(index, spans):
    if spans != 16:
        return index
    chip, core = index // 2, index % 2
    level, column = chip // 2, chip % 2
    return (level + column * (7 - 2 * level)) * 2 + core


def place_heads(side, got, gain, width):
    spans, _, packed = got.shape
    half = width // 2
    cut = width // spans
    block = half // 8
    part = pl.BlockSpec((block, width), lambda r: (r, 0))
    column = pl.BlockSpec((1, 1, block), lambda r: (r, 0, 0))
    return pl.pallas_call(
        functools.partial(place_heads_kernel, cut),
        grid=(8,),
        in_specs=[
            pl.BlockSpec(memory_space=pltpu.SMEM),
            pl.BlockSpec((HEADS, block, 3 * HEAD_DIM), lambda r: (0, r, 0)),
            pl.BlockSpec((spans, block, HEAD_DIM), lambda r: (0, r, 3)),
            pl.BlockSpec((spans, 16, HEAD_DIM), lambda r: (0, half // 16, 3)),
            column,
        ],
        out_specs=[part] * 4
        + [column, pl.BlockSpec((spans // 2, HEAD_DIM), lambda r: (0, 0))],
        out_shape=[jax.ShapeDtypeStruct((half, width), f32)] * 4
        + [
            jax.ShapeDtypeStruct((8, 1, block), f32),
            jax.ShapeDtypeStruct((spans // 2, HEAD_DIM), f32),
        ],
        name="place_heads",
    )(side.reshape(1), got, got, got, gain.reshape(8, 1, block))


def place_shared_kernel(side_ref, got_ref, in_ref, out_ref, rows_ref):
    spans = got_ref.shape[0]
    units = got_ref.shape[1] // 4
    half = got_ref.shape[2]
    hidden = spans * units
    for part in range(2):
        for c in range(spans):
            piece = got_ref[ring_position(c, spans), part * units : (part + 1) * units, :]
            rows_ref[c * units : (c + 1) * units, :] = piece.astype(f32)
        for at in range(0, hidden, HEAD_DIM):
            in_ref[:, part * hidden + at : part * hidden + at + HEAD_DIM] = rows_ref[
                at : at + HEAD_DIM, :
            ].T
    first = side_ref[0] * (spans // 2)
    for c in range(spans // 2):
        for part in range(2):
            spot = ring_position(first + c, spans)
            piece = got_ref[spot, (2 + part) * units : (3 + part) * units, :]
            out_ref[c * units : (c + 1) * units, part * half : (part + 1) * half] = piece.astype(f32)


def place_shared(got, side):
    spans, quad, half = got.shape
    hidden = spans * quad // 4
    memory = pl.BlockSpec(memory_space=pltpu.VMEM)
    return pl.pallas_call(
        place_shared_kernel,
        in_specs=[pl.BlockSpec(memory_space=pltpu.SMEM), memory],
        out_specs=[memory, memory],
        out_shape=[
            jax.ShapeDtypeStruct((half, 2 * hidden), f32),
            jax.ShapeDtypeStruct((hidden // 2, 2 * half), f32),
        ],
        scratch_shapes=[pltpu.VMEM((hidden, half), f32)],
        name="place_shared",
    )(side.reshape(1), got)


def after(value, *others):
    return lax.optimization_barrier((value, *others))[0]


def tied(*values):
    return lax.optimization_barrier(values)


def one_hot_rows(lanes, *targets):
    row = lax.broadcasted_iota(jnp.int32, (8, lanes), 0)
    lane = lax.broadcasted_iota(jnp.int32, (8, lanes), 1)
    rows = jnp.zeros((8, lanes), f32)
    for i, target in enumerate(targets):
        rows = jnp.where((row == i) & (lane == target), 1.0, rows)
    return rows.astype(bf16)


def slot_keys(shape, axis, capacity):
    index = lax.broadcasted_iota(jnp.int32, shape, axis)
    return (index % capacity + 1024 * (index // capacity)).astype(f32)


def run_keys(shape, axis, tokens):
    return (1024 * (lax.broadcasted_iota(jnp.int32, shape, axis) // tokens)).astype(f32)


def pick_slots_kernel(capacity, tokens, here_ref, g_ref, out_ref):
    many = g_ref.shape[0]
    width = out_ref.shape[1]
    extras = g_ref[:, width:]
    rows = one_hot_rows(extras.shape[1], here_ref[0])
    slots = dot_nt(rows, extras)[0:1] + run_keys((1, many), 1, tokens)
    takes = slot_keys((out_ref.shape[0], 1), 0, capacity) == slots
    select = jnp.where(takes, 1.0, 0.0).astype(bf16)
    out_ref[...] = dot(select, g_ref[:, :width]).astype(bf16)


def pick_slots(here, g_wide, width, capacity, tokens):
    length, wide = g_wide.shape
    runs = min(8, 224 // capacity)
    steps = length // (runs * tokens)
    return pl.pallas_call(
        functools.partial(pick_slots_kernel, capacity, tokens),
        grid=(steps,),
        in_specs=[
            pl.BlockSpec(memory_space=pltpu.SMEM),
            pl.BlockSpec((runs * tokens, wide), lambda i: (i, 0)),
        ],
        out_specs=pl.BlockSpec((runs * capacity, width), lambda i: (i, 0)),
        out_shape=jax.ShapeDtypeStruct((steps * runs * capacity, width), bf16),
        name="pick_slots",
        cost_estimate=pl.CostEstimate(
            flops=2 * length * runs * capacity * width,
            bytes_accessed=3 * length * wide,
            transcendentals=0,
        ),
    )(here.reshape(1), g_wide)


def sigmoid(value):
    return 1.0 / (1.0 + jnp.exp(-value))


def experts_kernel(
    capacity,
    tokens,
    experts,
    here_ref,
    normed_ref,
    g_ref,
    grad_slots_ref,
    own_in_ref,
    first_in_ref,
    rest_in_ref,
    own_down_ref,
    other_down_ref,
    own_shared_in_ref,
    other_shared_in_ref,
    own_shared_out_ref,
    other_shared_out_ref,
    dispatched_ref,
    hidden_ref,
    grad_result_ref,
    grad_proj_ref,
    shared_hidden_ref,
    shared_grad_ref,
    parts_ref,
    gate_dot_ref,
    in_ref,
    down_ref,
    shared_in_ref,
    shared_out_ref,
):
    @pl.when(pl.program_id(0) == 0)
    def _():
        side = here_ref[1]
        rows = own_in_ref.shape[0]
        first = first_in_ref.shape[0]
        at = (1 - side) * rows
        in_ref[pl.ds(pl.multiple_of(side * rows, 64), rows), :] = own_in_ref[...]
        in_ref[pl.ds(pl.multiple_of(at, 16), first), :] = first_in_ref[...]
        in_ref[pl.ds(pl.multiple_of(at + first, 16), rows - first), :] = rest_in_ref[...]
        rows = own_down_ref.shape[0]
        down_ref[pl.ds(pl.multiple_of(side * rows, 64), rows), :] = own_down_ref[...]
        down_ref[pl.ds(pl.multiple_of((1 - side) * rows, 64), rows), :] = other_down_ref[...]
        rows = own_shared_in_ref.shape[0]
        units = own_shared_out_ref.shape[0]
        shared_in_ref[...] = jnp.zeros_like(shared_in_ref)
        shared_out_ref[...] = jnp.zeros_like(shared_out_ref)
        for place, ref in ((side, own_shared_in_ref), (1 - side, other_shared_in_ref)):
            window = pl.ds(pl.multiple_of(place * rows, 64), rows)
            shared_in_ref[window, :units] = ref[:, :units]
            shared_in_ref[window, HEAD_DIM : HEAD_DIM + units] = ref[:, units:]
        shared_out_ref[:units, :] = jnp.where(
            here_ref[2] == side, own_shared_out_ref[...], other_shared_out_ref[...]
        )

    many, slots = normed_ref.shape[0], dispatched_ref.shape[0]
    width = dispatched_ref.shape[1]
    here = here_ref[0]
    normed = normed_ref[:, :width]
    g = g_ref[:, :width]
    spare = normed_ref.shape[1] - width
    gate_rows = dot_nt(one_hot_rows(spare, here, experts + here), normed_ref[:, width:])
    gate_row = gate_rows[0:1] + gate_rows[1:2]
    slot_pick = one_hot_rows(spare, here)
    slot_row = dot_nt(slot_pick, g_ref[:, width:])[0:1] + run_keys((1, many), 1, tokens)
    slot_column = dot_nt(g_ref[:, width:], slot_pick)[:, 0:1] + run_keys((many, 1), 0, tokens)
    takes = slot_keys((slots, 1), 0, capacity) == slot_row
    select = jnp.where(takes, 1.0, 0.0).astype(bf16)
    back = jnp.where(slot_column == slot_keys((1, slots), 1, capacity), 1.0, 0.0).astype(bf16)
    slot_gate = jnp.sum(jnp.where(takes, gate_row, 0.0), axis=1, keepdims=True)

    dispatched = dot(select, normed).astype(bf16)
    dispatched_ref[...] = dispatched
    grad_slots = grad_slots_ref[...].astype(f32)
    grad_result = (grad_slots * slot_gate).astype(bf16)
    grad_result_ref[...] = grad_result

    projected = dot(dispatched, in_ref[...])
    gate, up = projected[:, :EXP_HID], projected[:, EXP_HID:]
    chance = sigmoid(gate)
    silu = gate * chance
    hidden = (silu * up).astype(bf16)
    hidden_ref[...] = hidden
    grad_hidden = dot_nt(grad_result, down_ref[...])
    grad_proj_ref[:, :EXP_HID] = (
        grad_hidden * up * chance * (1.0 + gate * (1.0 - chance))
    ).astype(bf16)
    grad_proj_ref[:, EXP_HID:] = (grad_hidden * silu).astype(bf16)
    result = dot(hidden, down_ref[...]).astype(bf16).astype(f32)
    slot_dot = jnp.sum(grad_slots * result, axis=1, keepdims=True)
    gate_dot = jnp.sum(jnp.where(takes, slot_dot, 0.0), axis=0, keepdims=True)
    gate_dot_ref[...] = jnp.broadcast_to(gate_dot, gate_dot_ref.shape)
    scaled = (result * slot_gate).astype(bf16)
    grad_dispatched = dot_nt(grad_proj_ref[...], in_ref[...]).astype(bf16)

    lanes = shared_out_ref.shape[0]
    shared = dot(normed, shared_in_ref[...])
    shared_gate, shared_up = shared[:, :lanes], shared[:, lanes:]
    shared_chance = sigmoid(shared_gate)
    shared_silu = shared_gate * shared_chance
    shared_hidden = (shared_silu * shared_up).astype(bf16)
    shared_hidden_ref[...] = shared_hidden
    grad_shared = dot_nt(g, shared_out_ref[...])
    shared_grad_ref[:, :lanes] = (
        grad_shared * shared_up * shared_chance * (1.0 + shared_gate * (1.0 - shared_chance))
    ).astype(bf16)
    shared_grad_ref[:, lanes:] = (grad_shared * shared_silu).astype(bf16)
    parts_ref[:, :width] = (
        dot(back, grad_dispatched) + dot_nt(shared_grad_ref[...], shared_in_ref[...])
    ).astype(bf16)
    parts_ref[:, width:] = (
        dot(back, scaled) + dot(shared_hidden, shared_out_ref[...])
    ).astype(bf16)


def run_experts(
    places, normed_wide, g_wide, grad_slots, weights, tokens, capacity
):
    length, wide = normed_wide.shape
    width = grad_slots.shape[1]
    experts = length // tokens
    runs = min(8, 224 // capacity)
    steps = length // (runs * tokens)
    many, slots = runs * tokens, runs * capacity
    lanes = HEAD_DIM

    def block(rows, columns):
        return pl.BlockSpec((rows, columns), lambda i: (i, 0))

    def fixed(value):
        return pl.BlockSpec(value.shape, lambda i: (0, 0), pipeline_mode=pl.Buffered(1))

    def shape(rows, columns, kind=bf16):
        return jax.ShapeDtypeStruct((rows, columns), kind)

    return pl.pallas_call(
        functools.partial(experts_kernel, capacity, tokens, experts),
        grid=(steps,),
        in_specs=[
            pl.BlockSpec(memory_space=pltpu.SMEM),
            block(many, wide),
            block(many, wide),
            block(slots, width),
            *[fixed(weight) for weight in weights],
        ],
        out_specs=[
            block(slots, width),
            block(slots, EXP_HID),
            block(slots, width),
            block(slots, 2 * EXP_HID),
            block(many, lanes),
            block(many, 2 * lanes),
            block(many, 2 * width),
            pl.BlockSpec((8, many), lambda i: (0, i)),
        ],
        out_shape=[
            shape(steps * slots, width),
            shape(steps * slots, EXP_HID),
            shape(steps * slots, width),
            shape(steps * slots, 2 * EXP_HID),
            shape(length, lanes),
            shape(length, 2 * lanes),
            shape(length, 2 * width),
            shape(8, length, f32),
        ],
        scratch_shapes=[
            pltpu.VMEM((width, 2 * EXP_HID), bf16),
            pltpu.VMEM((EXP_HID, width), bf16),
            pltpu.VMEM((width, 2 * lanes), bf16),
            pltpu.VMEM((lanes, width), bf16),
        ],
        name="experts",
        cost_estimate=pl.CostEstimate(
            flops=20 * 10**9, bytes_accessed=40 * 10**6, transcendentals=2 * 10**6
        ),
    )(
        places,
        normed_wide,
        g_wide,
        grad_slots,
        *weights,
    )


def slot_table(span_picks, span_order, experts):
    tokens = span_picks.shape[0]
    order = span_order.reshape(tokens, TOP)
    onehot = span_picks[:, :, None] == jnp.arange(experts, dtype=jnp.int32)
    picked = jnp.any(onehot, axis=1)
    rank_key = jnp.sum(jnp.where(onehot, order[:, :, None], 0), axis=1)
    rank_key = jnp.where(picked, rank_key, tokens * TOP)
    before = rank_key[:, None, :] < rank_key[None, :, :]
    slots = jnp.sum(before.astype(jnp.int32), axis=0)
    return jnp.where(picked, slots, 2 * tokens)


def on_device(
    inputs,
    norm1_gain,
    w_query,
    w_key,
    w_value,
    w_output,
    norm2_gain,
    router,
    shared_gate_up_weight,
    shared_down_weight,
    expert_in,
    expert_out,
    picks,
    fill_order,
    grad_out,
):
    spans = lax.axis_size("ctx")
    here = lax.axis_index("ctx")
    side = lax.axis_index("fsdp")
    core = here % 2
    tokens, width = inputs.shape[1:]
    half = width // 2
    length = spans * tokens
    experts = spans * expert_in.shape[0]
    capacity = tokens * TOP // experts
    head = jnp.minimum(ring_position(here, spans), HEADS - 1)
    units = EXP_HID // spans
    ring = ring_of(spans)
    is_ring = spans == 16
    groups = [ring] if is_ring else None
    swap_core = [(i, i ^ 1) for i in range(spans)]

    def across(value):
        return lax.ppermute(value, "fsdp", [(0, 1), (1, 0)])

    def ordered(own, other, axis):
        return jnp.where(
            side == 0,
            jnp.concatenate([own, other], axis=axis),
            jnp.concatenate([other, own], axis=axis),
        )

    def everyone(value):
        return lax.all_gather(value, "ctx", axis=0, tiled=True, axis_index_groups=groups)

    def columns(value, start, count):
        return lax.dynamic_slice_in_dim(value, start, count, 1)

    def rows(value, start, count):
        return lax.dynamic_slice_in_dim(value, start, count, 0)

    def halves(value, axis=0):
        size = value.shape[axis] // 2
        mine = lax.dynamic_slice_in_dim(value, side * size, size, axis)
        theirs = lax.dynamic_slice_in_dim(value, (1 - side) * size, size, axis)
        return mine, theirs

    def reduced(value, axis=0):
        mine, theirs = halves(value, axis)
        return mine + across(theirs.astype(bf16)).astype(f32)

    def swapped(value):
        return lax.all_to_all(value, "ctx", split_axis=0, concat_axis=0, tiled=True)

    def row_major(value):
        return with_layout_constraint(value, Layout(tuple(range(value.ndim))))

    x = inputs[0]
    g = grad_out[0]
    x_all = everyone(x)
    spare = -(-2 * experts // HEAD_DIM) * HEAD_DIM
    own_table = slot_table(picks[0], fill_order[0, 0], experts)
    own_table = jnp.pad(
        own_table.astype(f32), ((0, 0), (0, spare - experts)), constant_values=2.0 * tokens
    )
    g_wide = jnp.concatenate([g, own_table.astype(bf16)], axis=1)
    head_own = jnp.concatenate(
        [columns(w, head * HEAD_DIM, HEAD_DIM) for w in (w_query, w_key, w_value)], axis=1
    )
    head_other = across(head_own)
    small = jnp.concatenate([router.T, norm1_gain[None], norm2_gain[None]], axis=0)
    small_other = across(small)
    output_near = across(columns(w_output, core * half, half))
    lanes = HEAD_DIM
    shared_in_own = jnp.concatenate(
        [columns(shared_gate_up_weight, at + here * units, units) for at in (0, EXP_HID)], axis=1
    )
    shared_rows = shared_down_weight.shape[0]
    shared_out_own = rows(shared_down_weight, here * units % shared_rows, units)
    ring_blocks = jnp.asarray(ring, jnp.int32)[:, None] * tokens
    positions = (ring_blocks + jnp.arange(tokens, dtype=jnp.int32)[None, :]).reshape(length)
    cosine, sine = rotary_tables(positions, HEAD_DIM)
    lane = lax.broadcasted_iota(jnp.int32, (length, HEAD_DIM), 1)
    sine = jnp.where(lane < HEAD_DIM // 2, -sine, sine)
    small = ordered(small, small_other, 1)
    router_w = small[:experts]
    gain_one = small[experts : experts + 1].astype(f32)
    gain_two = small[experts + 1 :].astype(f32)
    quarter = half // 8
    chunks = [expert_in[0, :quarter], expert_in[0, quarter:]]
    head_other, *chunks = tied(head_other, *chunks)
    chunks = [across(chunk) for chunk in chunks]
    x_all, cosine, sine, head_other, gain_one, output_near, chunks[0] = tied(
        x_all, cosine, sine, head_other, gain_one, output_near, chunks[0]
    )
    output_far = lax.ppermute(output_near, "ctx", swap_core)
    g_wide_all = everyone(after(g_wide, x_all))
    g_all = g_wide_all[:, :width]
    table = g_wide_all[:, width : width + experts]

    normed1_all, query, key, value = project(
        side, x_all, gain_one, head_own, head_other, cosine, sine
    )
    context, lse, attended = attend(query, key, value, is_ring)
    attended, output_far = tied(attended, output_far)
    down_other = across(after(expert_out[0], attended))
    got = swapped(attended.reshape(spans, tokens, HEAD_DIM))
    got, chunks[1] = tied(got, chunks[1])
    spot = jnp.stack([side, core]).astype(jnp.int32)
    router_pad = jnp.pad(router_w, ((0, spare - experts), (0, 0)))
    second, normed2_wide, scale_two, own_gates, attended = mix(
        spot,
        got,
        w_output,
        output_near,
        output_far,
        x,
        gain_two,
        router_pad,
        own_table,
        experts,
    )
    normed2_wide, g_wide_all = tied(normed2_wide, g_wide_all)
    normed2_wide = everyone(normed2_wide)
    grad_slots = pick_slots(here, g_wide_all, width, capacity, tokens)
    shared_in_other = across(after(shared_in_own, grad_slots))
    shared_out_other = across(after(shared_out_own, grad_slots))
    normed2_wide, grad_slots, down_other, shared_in_other, shared_out_other = tied(
        normed2_wide, grad_slots, down_other, shared_in_other, shared_out_other
    )
    normed2_all = normed2_wide[:, :width]
    attended_all = everyone(after(attended, normed2_wide))
    dense = [
        columns(after(w, grad_slots), core * half, half) for w in (w_query, w_key, w_value)
    ]
    dense = jnp.concatenate(dense, axis=0)
    near = [across(dense[: dense.shape[0] // 2]), across(dense[dense.shape[0] // 2 :])]
    spots = [ring_position(i, spans) for i in range(spans)]
    (
        dispatched,
        expert_hidden,
        grad_result,
        grad_proj,
        shared_hidden,
        grad_sproj,
        parts,
        gate_dot,
    ) = run_experts(
        jnp.stack([here, side, here * units // shared_rows]).astype(jnp.int32),
        normed2_wide,
        g_wide_all,
        grad_slots,
        (
            expert_in[0],
            chunks[0],
            chunks[1],
            expert_out[0],
            down_other,
            shared_in_own,
            shared_in_other,
            shared_out_own,
            shared_out_other,
        ),
        tokens,
        capacity,
    )
    parts, near[0], attended_all = tied(parts, near[0], attended_all)
    sums = lax.psum_scatter(
        parts, "ctx", scatter_dimension=0, tiled=True, axis_index_groups=groups
    )
    gate_dot = gate_dot[0].reshape(spans, tokens)
    grad_shared_in = dot_tn(grad_sproj, normed2_all)
    grad_shared_in = jnp.concatenate(
        [grad_shared_in[:units], grad_shared_in[lanes : lanes + units]], axis=0
    )
    grad_shared_in = reduced(grad_shared_in, 1).astype(bf16)
    grad_shared_out = dot_tn(shared_hidden, g_all)[:units].astype(bf16)
    grad_shared_out = grad_shared_out.astype(f32) + across(grad_shared_out).astype(f32)
    grad_shared_out = grad_shared_out.astype(bf16)
    shared_grads = jnp.concatenate(
        [grad_shared_in, grad_shared_out[:, :half], grad_shared_out[:, half:]], axis=0
    )
    gate_dot = jnp.concatenate([gate_dot[i : i + 1] for i in spots], axis=0)
    gate_grads = swapped(after(gate_dot, parts)[:, None, :])[:, 0, :].T

    own_down, down_theirs = halves(dot_tn(expert_hidden, grad_result))
    own_in, in_theirs = halves(dot_tn(dispatched, grad_proj))
    in_theirs = in_theirs.astype(bf16)
    down_theirs = across(after(down_theirs.astype(bf16), parts))
    sums, in_theirs, shared_grads, gate_grads = tied(
        sums,
        in_theirs,
        row_major(shared_grads),
        gate_grads,
    )
    in_upper = across(in_theirs[: half // 2])

    sent, cuts, grad_second, layer_out = mix_back(
        spot,
        sums,
        own_gates,
        jnp.pad(gate_grads, ((0, 0), (0, spare - experts))),
        router_pad,
        second,
        scale_two,
        gain_two,
        g,
        w_output,
        output_near,
        output_far,
        spans,
    )
    arrived = swapped(sent).reshape(length, HEAD_DIM)
    arrived, shared_grads, cuts, near[1], down_theirs = tied(
        arrived, shared_grads, cuts, near[1], down_theirs
    )
    cuts = lax.all_to_all(
        cuts, "ctx", split_axis=0, concat_axis=0, tiled=True, axis_index_groups=groups
    )
    extras = cuts[:, :tokens].reshape(length, HEAD_DIM)
    shared_grads = everyone(shared_grads[None])
    grad_heads, grad_heads_ring = attend_back(
        query, key, value, arrived, context, lse, cosine, sine, is_ring
    )
    grad_heads, grad_heads_ring, in_upper = tied(grad_heads, grad_heads_ring, in_upper)
    cut = width // spans
    gain_rows = cuts[:, tokens : tokens + 2, :cut].astype(f32)
    gain_rows = jnp.sum(gain_rows, axis=(0, 1))
    gain_rows = jnp.pad(gain_rows.reshape(1, cut), ((0, 15), (0, HEAD_DIM - cut)))
    grad_router = dot_tn(normed2_all, extras)[:, cut : cut + experts]
    mine, theirs = halves(grad_router)
    grad_router = mine + across(theirs)
    mine, theirs = halves(dot_tn(attended_all, extras))
    gain_high = gain_rows.astype(bf16)
    gain_low = jnp.roll((gain_rows - gain_high.astype(f32)).astype(bf16), 1, axis=0)
    theirs = jnp.concatenate([theirs.astype(bf16), gain_high + gain_low], axis=0)
    grad_heads_ring, theirs = tied(grad_heads_ring, theirs)
    theirs = across(theirs).astype(f32)
    grad_output = mine + theirs[:half]
    gain_rows = gain_rows[:1] + theirs[half : half + 1] + theirs[half + 1 : half + 2]
    gain_high = gain_rows.astype(bf16)
    gain_low = (gain_rows - gain_high.astype(f32)).astype(bf16)
    gain_rows = jnp.pad(
        jnp.concatenate([gain_high, gain_low], axis=0), ((0, 14), (3 * HEAD_DIM, 0))
    )
    head_mine, head_theirs = halves(dot_tn(normed1_all, grad_heads_ring))
    head_theirs = head_theirs.astype(bf16)
    got = swapped(grad_heads.reshape(spans, tokens, 3 * HEAD_DIM))
    grad_head_w = (head_mine + across(head_theirs).astype(f32)).astype(bf16)
    part = jnp.sum(grad_head_w.astype(f32) * head_own.astype(f32), axis=1, keepdims=True)
    part_high = part.astype(bf16).astype(f32)
    lane = lax.broadcasted_iota(jnp.int32, (half, HEAD_DIM), 1)
    grad_output = jnp.where(lane < cut, grad_output, 0.0)
    grad_output = jnp.where(lane == cut, part_high, grad_output)
    grad_output = jnp.where(lane == cut + 1, part - part_high, grad_output)
    head_grads = jnp.concatenate([grad_head_w, grad_output.astype(bf16)], axis=1)
    head_grads = jnp.concatenate([head_grads, gain_rows], axis=0)
    in_lower = across(after(in_theirs[half // 2 :], head_grads))
    head_grads, got = tied(row_major(head_grads), got)
    head_grads = everyone(head_grads[None])
    near = jnp.concatenate(near, axis=0)
    far = lax.ppermute(near, "ctx", swap_core)

    grad_inputs = inputs_back(
        side, core, got, w_query, w_key, w_value, near, far, x, gain_one, grad_second
    )
    grad_inputs, in_lower = tied(grad_inputs, in_lower)
    grad_query, grad_key, grad_value, grad_output, grad_norm1, grad_norm2 = place_heads(
        side, head_grads, norm1_gain.astype(f32), width
    )
    grad_expert_in = jnp.concatenate(
        [
            own_in[: half // 2] + in_upper.astype(f32),
            own_in[half // 2 :] + in_lower.astype(f32),
        ],
        axis=0,
    )
    grad_shared_in, grad_shared_out = place_shared(shared_grads, side)
    return (
        layer_out[None],
        grad_inputs[None],
        grad_norm1.reshape(half),
        grad_query,
        grad_key,
        grad_value,
        grad_output,
        grad_norm2[:, :cut].reshape(half),
        grad_router,
        grad_shared_in,
        grad_shared_out,
        grad_expert_in[None],
        (own_down + down_theirs.astype(f32))[None],
    )


def solution(mesh):
    placed = (
        P("fsdp", "ctx", None),
        P("fsdp"),
        P("fsdp", None),
        P("fsdp", None),
        P("fsdp", None),
        P("fsdp", None),
        P("fsdp"),
        P("fsdp", None),
        P("fsdp", None),
        P("fsdp", None),
        P("ctx", "fsdp", None),
        P("ctx", "fsdp", None),
        P("fsdp", "ctx", None),
        P("fsdp", "ctx", None),
        P("fsdp", "ctx", None),
    )
    return jax.shard_map(
        on_device,
        mesh=mesh,
        in_specs=placed,
        out_specs=(
            P("fsdp", "ctx", None),
            P("fsdp", "ctx", None),
            P("fsdp"),
            P("fsdp", None),
            P("fsdp", None),
            P("fsdp", None),
            P("fsdp", None),
            P("fsdp"),
            P("fsdp", None),
            P("fsdp", None),
            P("fsdp", None),
            P("ctx", "fsdp", None),
            P("ctx", "fsdp", None),
        ),
        check_vma=False,
    )
```

```python
import functools
import math

import jax
import jax.numpy as jnp
from jax import lax
from jax.experimental import pallas as pl
from jax.experimental.layout import Layout, with_layout_constraint
from jax.experimental.pallas import tpu as pltpu
from jax.sharding import PartitionSpec as P

HEADS = 10
HEAD_DIM = 128
EXP_HID = 896
TOP = 7
BLOCK = 256
TILE = 512

epsilon = 1e-06
masked_score = -1000000000.0
score_scale = 1.0 / math.sqrt(HEAD_DIM)
exact = lax.Precision.HIGHEST
f32 = jnp.float32
bf16 = jnp.bfloat16


def dot(a, b):
    return jnp.dot(a, b, preferred_element_type=f32)


def dot_nt(a, b):
    return lax.dot_general(a, b, (((1,), (1,)), ((), ())), preferred_element_type=f32)


def dot_tn(a, b):
    return lax.dot_general(a, b, (((0,), (0,)), ((), ())), preferred_element_type=f32)


def rms_scale(values):
    return lax.rsqrt(jnp.mean(values * values, axis=-1, keepdims=True) + epsilon)


def rotary_tables(starts, count, width):
    half = width // 2
    freqs = jnp.exp(-math.log(10000.0) * jnp.arange(half, dtype=f32) * 2.0 / width)
    first = starts.astype(f32)[:, None] * freqs[None, :]
    second = jnp.arange(count, dtype=f32)[:, None] * freqs[None, :]
    angles = jnp.concatenate([first, second], axis=0)
    cosine, sine = lax.optimization_barrier((jnp.cos(angles), jnp.sin(angles)))
    spans = starts.shape[0]
    cos_a, sin_a = cosine[:spans, None], sine[:spans, None]
    cos_b, sin_b = cosine[None, spans:], sine[None, spans:]
    cosine = (cos_a * cos_b - sin_a * sin_b).reshape(spans * count, half)
    sine = (sin_a * cos_b + cos_a * sin_b).reshape(spans * count, half)
    return (
        jnp.concatenate([cosine, cosine], axis=1),
        jnp.concatenate([-sine, sine], axis=1),
    )


def allowed_tile(rows, columns):
    key_block = lax.broadcasted_iota(jnp.int32, (rows, columns), 0) // BLOCK
    query_block = lax.broadcasted_iota(jnp.int32, (rows, columns), 1) // BLOCK
    return key_block <= query_block


def ring_of(spans):
    if spans != 16:
        return list(range(spans))
    chips = [0, 2, 4, 6, 7, 5, 3, 1]
    return [2 * chip + core for chip in chips for core in (0, 1)]


def pieces(j, tile, length, ring):
    if ring:
        starts = (j * BLOCK, length - BLOCK - j * BLOCK)
        return [pl.ds(pl.multiple_of(at, BLOCK), BLOCK) for at in starts]
    return [pl.ds(pl.multiple_of(j * tile, tile), tile)]


def load(ref, windows, columns=slice(None)):
    parts = [ref[window, columns] for window in windows]
    return parts[0] if len(parts) == 1 else jnp.concatenate(parts, axis=0)


def store(ref, windows, value, columns=slice(None)):
    size = value.shape[0] // len(windows)
    for i, window in enumerate(windows):
        ref[window, columns] = value[i * size : (i + 1) * size]


def attend_kernel(
    ring, q_ref, k_ref, v_ref, context_ref, lse_ref, low_ref, score_ref
):
    length = k_ref.shape[0]
    tile = context_ref.shape[0]
    here = pl.program_id(0)
    queries = load(q_ref, pieces(here, tile, length, ring))

    def raw_scores(j):
        return dot_nt(load(k_ref, pieces(j, tile, length, ring)), queries) * score_scale

    def fold(j, scores, peak):
        score_ref[pl.ds(pl.multiple_of(j * tile, tile), tile), :] = scores
        return jnp.maximum(peak, jnp.max(scores.reshape(tile // 8, 8, tile), axis=0))

    diagonal = jnp.where(allowed_tile(tile, tile), raw_scores(here), masked_score)
    peak = fold(here, diagonal, jnp.full((8, tile), masked_score, f32))
    peak = lax.fori_loop(0, here, lambda j, p: fold(j, raw_scores(j), p), peak)
    top = jnp.max(peak, axis=0, keepdims=True)

    def gather(j, carry):
        total, numer = carry
        weights = jnp.exp(score_ref[pl.ds(pl.multiple_of(j * tile, tile), tile), :] - top)
        total = total + jnp.sum(weights.reshape(tile // 8, 8, tile), axis=0)
        values = load(v_ref, pieces(j, tile, length, ring))
        return total, numer + dot_tn(values, weights.astype(bf16))

    zero = (jnp.zeros((8, tile), f32), jnp.zeros((HEAD_DIM, tile), f32))
    total, numer = lax.fori_loop(0, here + 1, gather, zero)
    total = jnp.sum(total, axis=0, keepdims=True)
    context = (numer / total).T
    context_ref[...] = context
    low_ref[...] = context.astype(bf16)
    lse_ref[...] = top + jnp.log(total)


def attend(query, key, value, ring):
    length = query.shape[0]
    tile = min(TILE, length)
    whole = pl.BlockSpec((length, HEAD_DIM), lambda i: (0, 0))
    part = pl.BlockSpec((tile, HEAD_DIM), lambda i: (i, 0))
    return pl.pallas_call(
        functools.partial(attend_kernel, ring),
        grid=(length // tile,),
        in_specs=[whole] * 3,
        out_specs=[part, pl.BlockSpec((1, tile), lambda i: (0, i)), part],
        out_shape=[
            jax.ShapeDtypeStruct((length, HEAD_DIM), f32),
            jax.ShapeDtypeStruct((1, length), f32),
            jax.ShapeDtypeStruct((length, HEAD_DIM), bf16),
        ],
        scratch_shapes=[pltpu.VMEM((length, tile), f32)],
        name="attend",
        cost_estimate=pl.CostEstimate(
            flops=2 * length * length * HEAD_DIM,
            bytes_accessed=12 * length * HEAD_DIM,
            transcendentals=length * length // 2,
        ),
    )(query, key, value)


def attend_back_kernel(
    ring,
    q_ref,
    k_ref,
    v_ref,
    grad_ref,
    context_ref,
    lse_ref,
    cos_ref,
    sin_ref,
    out_ref,
    out_ring_ref,
    dq_ref,
    delta_ref,
    dk_ref,
    dv_ref,
):
    length = q_ref.shape[0]
    tile = dk_ref.shape[0]
    steps = length // tile
    here = pl.program_id(0)

    def natural(i):
        return pl.ds(pl.multiple_of(i * tile, tile), tile)

    @pl.when(here == 0)
    def _():
        def prepare(i, carry):
            window = natural(i)
            dq_ref[window, :] = jnp.zeros((tile, HEAD_DIM), f32)
            product = grad_ref[window, :].astype(f32) * context_ref[window, :]
            ones = jnp.ones((8, HEAD_DIM), f32)
            delta = lax.dot_general(
                ones, product, (((1,), (1,)), ((), ())), precision=exact, preferred_element_type=f32
            )
            delta_ref[:, window] = delta
            return carry

        lax.fori_loop(0, steps, prepare, 0)

    keys = load(k_ref, pieces(here, tile, length, ring))
    values = load(v_ref, pieces(here, tile, length, ring))

    dk_ref[...] = jnp.zeros_like(dk_ref)
    dv_ref[...] = jnp.zeros_like(dv_ref)

    def visit(i, carry):
        window = natural(i)
        queries = load(q_ref, pieces(i, tile, length, ring))
        grads = grad_ref[window, :]
        weights = jnp.exp(dot_nt(keys, queries) * score_scale - lse_ref[:, window])
        later = jnp.where(i > here, weights[BLOCK:, :BLOCK], 0.0)
        later = jnp.concatenate([later, weights[BLOCK:, BLOCK:]], axis=1)
        weights = jnp.concatenate([weights[:BLOCK], later], axis=0)
        grad_weights = dot_nt(values, grads)
        grad_raw = (weights * (grad_weights - delta_ref[0:1, window]) * score_scale).astype(bf16)
        dq_ref[window, :] += dot_tn(grad_raw, keys)
        dk_ref[...] += dot(grad_raw, queries)
        dv_ref[...] += dot(weights.astype(bf16), grads)
        return carry

    lax.fori_loop(here, steps, visit, 0)

    def write(i, part, value):
        at = slice(part * HEAD_DIM, (part + 1) * HEAD_DIM)
        out_ref[natural(i), at] = value
        store(out_ring_ref, pieces(i, tile, length, ring), value, at)

    def turned_back(i, value):
        windows = pieces(i, tile, length, ring)
        scaled = pltpu.roll(value * load(sin_ref, windows), HEAD_DIM // 2, 1)
        return (value * load(cos_ref, windows) + scaled).astype(bf16)

    write(here, 1, turned_back(here, dk_ref[...]))
    write(here, 2, dv_ref[...].astype(bf16))

    @pl.when(here == steps - 1)
    def _():
        def finish(i, carry):
            write(i, 0, turned_back(i, dq_ref[natural(i), :]))
            return carry

        lax.fori_loop(0, steps, finish, 0)


def attend_back(query, key, value, grad, context, lse, cosine, sine, ring):
    length = query.shape[0]
    tile = min(TILE, length)
    memory = pl.BlockSpec(memory_space=pltpu.VMEM)
    return pl.pallas_call(
        functools.partial(attend_back_kernel, ring),
        grid=(length // tile,),
        in_specs=[memory] * 8,
        out_specs=[memory] * 2,
        out_shape=[jax.ShapeDtypeStruct((length, 3 * HEAD_DIM), bf16)] * 2,
        scratch_shapes=[
            pltpu.VMEM((length, HEAD_DIM), f32),
            pltpu.VMEM((8, length), f32),
            pltpu.VMEM((tile, HEAD_DIM), f32),
            pltpu.VMEM((tile, HEAD_DIM), f32),
        ],
        name="attend_back",
        cost_estimate=pl.CostEstimate(
            flops=5 * length * length * HEAD_DIM,
            bytes_accessed=20 * length * HEAD_DIM,
            transcendentals=length * length // 2,
        ),
    )(query, key, value, grad, context, lse, cosine, sine)


def project_kernel(
    side_ref, x_ref, gain_ref, own_ref, other_ref, cos_ref, sin_ref, normed_ref, q_ref, k_ref, v_ref
):
    own, other = own_ref[...], other_ref[...]
    weight = jnp.where(
        side_ref[0] == 0,
        jnp.concatenate([own, other], axis=0),
        jnp.concatenate([other, own], axis=0),
    )
    resid = x_ref[...].astype(f32)
    normed = (resid * rms_scale(resid) * gain_ref[...]).astype(bf16)
    normed_ref[...] = normed
    projected = dot(normed, weight)
    for out, at in ((q_ref, 0), (k_ref, HEAD_DIM)):
        part = projected[:, at : at + HEAD_DIM]
        turned = pltpu.roll(part, HEAD_DIM // 2, 1)
        out[...] = (part * cos_ref[...] + turned * sin_ref[...]).astype(bf16)
    v_ref[...] = projected[:, 2 * HEAD_DIM :].astype(bf16)


def project(side, x, gain, own, other, cosine, sine):
    length, width = x.shape
    tile = min(TILE // 2, length)
    part = pl.BlockSpec((tile, HEAD_DIM), lambda i: (i, 0))
    wide = pl.BlockSpec((tile, width), lambda i: (i, 0))
    return pl.pallas_call(
        project_kernel,
        grid=(length // tile,),
        in_specs=[
            pl.BlockSpec(memory_space=pltpu.SMEM),
            wide,
            pl.BlockSpec((1, width), lambda i: (0, 0)),
            pl.BlockSpec(own.shape, lambda i: (0, 0)),
            pl.BlockSpec(own.shape, lambda i: (0, 0)),
            part,
            part,
        ],
        out_specs=[wide, part, part, part],
        out_shape=[jax.ShapeDtypeStruct((length, width), bf16)]
        + [jax.ShapeDtypeStruct((length, HEAD_DIM), bf16)] * 3,
        name="project",
        cost_estimate=pl.CostEstimate(
            flops=6 * length * width * HEAD_DIM,
            bytes_accessed=4 * length * width,
            transcendentals=0,
        ),
    )(side.reshape(1), x, gain, own, other, cosine, sine)


def home(head, spans):
    if spans != 16:
        return head
    chip, core = head // 2, head % 2
    return 2 * jnp.where(chip < 4, 2 * chip, 15 - 2 * chip) + core


def head_pair(side, spans, i):
    count = HEADS // 2
    low, high = home(i, spans), home(count + i, spans)
    mine = jnp.where(side == 0, low, high)
    theirs = jnp.where(side == 0, high, low)
    return mine, theirs, pl.ds(pl.multiple_of(i * HEAD_DIM, HEAD_DIM), HEAD_DIM)


def mix_kernel(
    experts,
    spot_ref,
    got_ref,
    own_ref,
    near_ref,
    far_ref,
    x_ref,
    gain_ref,
    router_ref,
    table_ref,
    second_ref,
    low_ref,
    scale_ref,
    gates_ref,
    attended_ref,
    near_sum_ref,
    far_sum_ref,
):
    ring = ring_of(got_ref.shape[0])
    for h in range(HEADS):
        attended_ref[:, h * HEAD_DIM : (h + 1) * HEAD_DIM] = got_ref[ring[h]]
    second = x_ref[...].astype(f32)
    tokens, width = second.shape
    half = near_ref.shape[1]
    second_ref[...] = second
    near_sum_ref[...] = jnp.zeros((tokens, half), f32)
    far_sum_ref[...] = jnp.zeros((tokens, half), f32)

    def visit(i, carry):
        mine, theirs, at = head_pair(spot_ref[0], got_ref.shape[0], i)
        second_ref[...] += dot(got_ref[mine], own_ref[at, :])
        near_sum_ref[...] += dot(got_ref[theirs], near_ref[at, :])
        far_sum_ref[...] += dot(got_ref[theirs], far_ref[at, :])
        return carry

    lax.fori_loop(0, HEADS // 2, visit, 0)
    second, near, far = second_ref[...], near_sum_ref[...], far_sum_ref[...]
    second += jnp.where(
        spot_ref[1] == 0,
        jnp.concatenate([near, far], axis=1),
        jnp.concatenate([far, near], axis=1),
    )
    scale = rms_scale(second)
    second_ref[...] = second
    scale_ref[...] = scale
    normed = (second * scale * gain_ref[...]).astype(bf16)
    logits = dot_nt(normed, router_ref[...])
    picked = table_ref[...] < tokens
    peak = jnp.max(jnp.where(picked, logits, masked_score), axis=-1, keepdims=True)
    chances = jnp.where(picked, jnp.exp(logits - peak), 0.0)
    gates = chances / jnp.sum(chances, axis=-1, keepdims=True)
    gates_ref[...] = gates
    high = gates.astype(bf16).astype(f32)
    rest = pltpu.roll(gates - high, experts, 1)
    low_ref[:, :width] = normed
    low_ref[:, width:] = (high + rest).astype(bf16)


def mix(spot, got, own, near, far, x, gain, router, table, experts):
    smem = pl.BlockSpec(memory_space=pltpu.SMEM)
    memory = pl.BlockSpec(memory_space=pltpu.VMEM)
    tokens, width = x.shape
    spare = table.shape[1]
    return pl.pallas_call(
        functools.partial(mix_kernel, experts),
        in_specs=[smem] + [memory] * 8,
        out_specs=[memory] * 5,
        out_shape=[
            jax.ShapeDtypeStruct(x.shape, f32),
            jax.ShapeDtypeStruct((tokens, width + spare), bf16),
            jax.ShapeDtypeStruct((tokens, 1), f32),
            jax.ShapeDtypeStruct((tokens, spare), f32),
            jax.ShapeDtypeStruct(x.shape, bf16),
        ],
        scratch_shapes=[pltpu.VMEM((tokens, width // 2), f32)] * 2,
        name="mix",
    )(spot, got, own, near, far, x, gain, router, table)


def mix_back_kernel(
    spot_ref,
    sums_ref,
    gates_ref,
    gate_grads_ref,
    router_ref,
    second_ref,
    scale_ref,
    gain_ref,
    g_ref,
    own_ref,
    near_ref,
    far_ref,
    send_ref,
    cuts_ref,
    grad_second_ref,
    out_ref,
):
    tokens, width = second_ref.shape
    second = second_ref[...]
    scale = scale_ref[...]
    gain = gain_ref[...]
    gates = gates_ref[...]
    gate_grads = gate_grads_ref[...]
    out_ref[...] = (second + sums_ref[:, width:].astype(f32)).astype(bf16)
    weighted = gates * gate_grads
    grad_sel = weighted - gates * jnp.sum(weighted, axis=-1, keepdims=True)
    grad_logits = grad_sel.astype(bf16)
    grad_normed = sums_ref[:, :width].astype(f32) + dot(grad_logits, router_ref[...])
    gain_part = jnp.sum(grad_normed * second * scale, axis=0, keepdims=True)
    hat = grad_normed * gain
    mean = jnp.mean(hat * second, axis=-1, keepdims=True)
    grad_second = g_ref[...].astype(f32) + scale * hat - second * (scale * scale * scale) * mean
    grad_second_ref[...] = grad_second
    grad_mixed = grad_second.astype(bf16)
    spans = send_ref.shape[0]
    cut = width // spans
    lane = lax.broadcasted_iota(jnp.int32, (1, HEAD_DIM), 1)
    high = gain_part.astype(bf16).astype(f32)
    row = lax.broadcasted_iota(jnp.int32, (16, width), 0)
    gain_rows = jnp.where(row == 0, high, jnp.where(row == 1, gain_part - high, 0.0))
    shifted = pltpu.roll(grad_logits.astype(f32), cut, 1)
    for k, c in enumerate(ring_of(spans)):
        start = min(c * cut // HEAD_DIM * HEAD_DIM, width - 2 * HEAD_DIM)
        shift = (start - c * cut) % (2 * HEAD_DIM)
        for value, rest, out_rows in (
            (grad_second, shifted, slice(0, tokens)),
            (gain_rows, 0.0, slice(tokens, tokens + 16)),
        ):
            window = pltpu.roll(value[:, start : start + 2 * HEAD_DIM], shift, 1)[:, :HEAD_DIM]
            window = jnp.where(lane < cut, window, 0.0) + rest
            cuts_ref[k, out_rows, :] = window.astype(bf16)
    left, right = grad_mixed[:, : width // 2], grad_mixed[:, width // 2 :]
    at_near = jnp.where(spot_ref[1] == 0, left, right)
    at_far = jnp.where(spot_ref[1] == 0, right, left)
    def visit(i, carry):
        mine, theirs, at = head_pair(spot_ref[0], spans, i)
        send_ref[mine] = dot_nt(grad_mixed, own_ref[at, :]).astype(bf16)
        other = dot_nt(at_near, near_ref[at, :]) + dot_nt(at_far, far_ref[at, :])
        send_ref[theirs] = other.astype(bf16)
        return carry

    lax.fori_loop(0, HEADS // 2, visit, 0)
    for h in ring_of(spans)[HEADS:]:
        send_ref[h] = jnp.zeros((tokens, HEAD_DIM), bf16)


def mix_back(spot, sums, gates, gate_grads, router, second, scale, gain, g, own, near, far, spans):
    tokens, width = second.shape
    smem = pl.BlockSpec(memory_space=pltpu.SMEM)
    memory = pl.BlockSpec(memory_space=pltpu.VMEM)
    return pl.pallas_call(
        mix_back_kernel,
        in_specs=[smem] + [memory] * 11,
        out_specs=[memory] * 4,
        out_shape=[
            jax.ShapeDtypeStruct((spans, tokens, HEAD_DIM), bf16),
            jax.ShapeDtypeStruct((spans, tokens + 16, HEAD_DIM), bf16),
            jax.ShapeDtypeStruct((tokens, width), f32),
            jax.ShapeDtypeStruct((tokens, width), bf16),
        ],
        name="mix_back",
    )(spot, sums, gates, gate_grads, router, second, scale, gain, g, own, near, far)


def inputs_back_kernel(
    side_ref,
    core_ref,
    got_ref,
    wq_ref,
    wk_ref,
    wv_ref,
    near_ref,
    far_ref,
    x_ref,
    gain_ref,
    grad_second_ref,
    out_ref,
    own_sum_ref,
    other_sum_ref,
):
    tokens, width = x_ref.shape
    half = width // 2
    count = HEADS // 2
    own_sum_ref[...] = jnp.zeros((tokens, half), f32)
    other_sum_ref[...] = jnp.zeros((tokens, half), f32)
    spans = got_ref.shape[0]

    def visit(h, carry):
        low, high = home(h, spans), home(count + h, spans)
        mine = jnp.where(core_ref[0] == 0, low, high)
        theirs = jnp.where(core_ref[0] == 0, high, low)
        window = pl.ds(pl.multiple_of(h * HEAD_DIM, HEAD_DIM), HEAD_DIM)
        upper = pl.ds(pl.multiple_of((count + h) * HEAD_DIM, HEAD_DIM), HEAD_DIM)
        for i, weight in enumerate((wq_ref, wk_ref, wv_ref)):
            at = slice(i * HEAD_DIM, (i + 1) * HEAD_DIM)
            rows = slice(i * half, (i + 1) * half)
            grads = jnp.concatenate([got_ref[low, :, at], got_ref[high, :, at]], axis=1)
            weights = jnp.concatenate([weight[:, window], weight[:, upper]], axis=1)
            own_sum_ref[...] += dot_nt(grads, weights)
            grads = jnp.concatenate([got_ref[mine, :, at], got_ref[theirs, :, at]], axis=1)
            weights = jnp.concatenate([near_ref[rows, window], far_ref[rows, window]], axis=1)
            other_sum_ref[...] += dot_nt(grads, weights)
        return carry

    lax.fori_loop(0, count, visit, 0)
    own_part, other_part = own_sum_ref[...], other_sum_ref[...]
    grad_normed = jnp.where(
        side_ref[0] == 0,
        jnp.concatenate([own_part, other_part], axis=1),
        jnp.concatenate([other_part, own_part], axis=1),
    )
    resid = x_ref[...].astype(f32)
    scale = rms_scale(resid)
    hat = grad_normed * gain_ref[...]
    mean = jnp.mean(hat * resid, axis=-1, keepdims=True)
    out_ref[...] = grad_second_ref[...] + scale * hat - resid * (scale * scale * scale) * mean


def inputs_back(side, core, got, w_query, w_key, w_value, near, far, x, gain, grad_second):
    smem = pl.BlockSpec(memory_space=pltpu.SMEM)
    memory = pl.BlockSpec(memory_space=pltpu.VMEM)
    return pl.pallas_call(
        inputs_back_kernel,
        in_specs=[smem] * 2 + [memory] * 9,
        out_specs=memory,
        out_shape=jax.ShapeDtypeStruct(x.shape, f32),
        scratch_shapes=[pltpu.VMEM((x.shape[0], x.shape[1] // 2), f32)] * 2,
        name="inputs_back",
    )(
        side.reshape(1),
        core.reshape(1),
        got,
        w_query,
        w_key,
        w_value,
        near,
        far,
        x,
        gain,
        grad_second,
    )


def place_heads_kernel(
    cut,
    side_ref,
    heads_ref,
    rest_ref,
    gain_rows_ref,
    gain_ref,
    q_ref,
    k_ref,
    v_ref,
    output_ref,
    norm_ref,
    norm2_ref,
):
    for h in range(HEADS):
        at = slice(h * HEAD_DIM, (h + 1) * HEAD_DIM)
        for i, out in enumerate((q_ref, k_ref, v_ref)):
            out[:, at] = heads_ref[h, :, i * HEAD_DIM : (i + 1) * HEAD_DIM].astype(f32)
    sums = rest_ref[0].astype(f32)
    for h in range(1, HEADS):
        sums += rest_ref[h].astype(f32)
    lane = lax.broadcasted_iota(jnp.int32, (8, HEAD_DIM), 1)
    pair = jnp.where((lane == cut) | (lane == cut + 1), 1.0, 0.0)
    row = lax.dot_general(
        pair, sums, (((1,), (1,)), ((), ())), precision=exact, preferred_element_type=f32
    )
    block = rest_ref.shape[1]
    for i in range(norm_ref.shape[1] // block):

        @pl.when(pl.program_id(0) == i)
        def _(at=slice(i * block, (i + 1) * block)):
            norm_ref[:, at] = row[0:1] / gain_ref[:, at]

    spans = rest_ref.shape[0]

    @pl.when(pl.program_id(0) == 0)
    def _():
        for i in range(spans // 2):
            low, high = ring_position(i, spans), ring_position(spans // 2 + i, spans)
            rows = gain_rows_ref[jnp.where(side_ref[0] == 0, low, high)].astype(f32)
            norm2_ref[:, i * cut : (i + 1) * cut] = (rows[0:1] + rows[1:2])[:, :cut]

    for c in range(spans):
        piece = rest_ref[ring_position(c, spans), :, :cut].astype(f32)
        output_ref[:, c * cut : (c + 1) * cut] = piece


def ring_position(index, spans):
    if spans != 16:
        return index
    chip, core = index // 2, index % 2
    level, column = chip // 2, chip % 2
    return (level + column * (7 - 2 * level)) * 2 + core


def place_heads(side, got, gain, width):
    spans, _, packed = got.shape
    half = width // 2
    cut = width // spans
    block = half // 8
    part = pl.BlockSpec((block, width), lambda r: (r, 0))
    line = pl.BlockSpec((1, half), lambda r: (0, 0))
    return pl.pallas_call(
        functools.partial(place_heads_kernel, cut),
        grid=(8,),
        in_specs=[
            pl.BlockSpec(memory_space=pltpu.SMEM),
            pl.BlockSpec((HEADS, block, 3 * HEAD_DIM), lambda r: (0, r, 0)),
            pl.BlockSpec((spans, block, HEAD_DIM), lambda r: (0, r, 3)),
            pl.BlockSpec((spans, 16, HEAD_DIM), lambda r: (0, half // 16, 3)),
            line,
        ],
        out_specs=[part] * 4 + [line] * 2,
        out_shape=[jax.ShapeDtypeStruct((half, width), f32)] * 4
        + [jax.ShapeDtypeStruct((1, half), f32)] * 2,
        name="place_heads",
    )(side.reshape(1), got, got, got, gain.reshape(1, half))


def place_shared_kernel(side_ref, got_ref, in_ref, out_ref, rows_ref):
    spans = got_ref.shape[0]
    units = got_ref.shape[1] // 4
    half = got_ref.shape[2]
    hidden = spans * units

    for part in range(2):
        for c in range(spans):
            spot = ring_position(c, spans)
            piece = got_ref[spot, part * units : (part + 1) * units, :]
            rows_ref[c * units : (c + 1) * units, :] = piece.astype(f32)

        def turn(i, carry):
            window = pl.ds(pl.multiple_of(i * HEAD_DIM, HEAD_DIM), HEAD_DIM)
            at = pl.ds(pl.multiple_of(part * hidden + i * HEAD_DIM, HEAD_DIM), HEAD_DIM)
            in_ref[:, at] = rows_ref[window, :].T
            return carry

        lax.fori_loop(0, hidden // HEAD_DIM, turn, 0)
    first = side_ref[0] * (spans // 2)
    for c in range(spans // 2):
        spot = ring_position(first + c, spans)
        for part in range(2):
            piece = got_ref[spot, (2 + part) * units : (3 + part) * units, :]
            out_ref[c * units : (c + 1) * units, part * half : (part + 1) * half] = piece.astype(f32)


def place_shared(got, side):
    spans, quad, half = got.shape
    hidden = spans * quad // 4
    memory = pl.BlockSpec(memory_space=pltpu.VMEM)
    return pl.pallas_call(
        place_shared_kernel,
        in_specs=[pl.BlockSpec(memory_space=pltpu.SMEM), memory],
        out_specs=[memory, memory],
        out_shape=[
            jax.ShapeDtypeStruct((half, 2 * hidden), f32),
            jax.ShapeDtypeStruct((hidden // 2, 2 * half), f32),
        ],
        scratch_shapes=[pltpu.VMEM((hidden, half), f32)],
        name="place_shared",
    )(side.reshape(1), got)


def after(value, *others):
    return lax.optimization_barrier((value, *others))[0]


def tied(*values):
    return lax.optimization_barrier(values)


def one_hot_rows(lanes, *targets):
    row = lax.broadcasted_iota(jnp.int32, (8, lanes), 0)
    lane = lax.broadcasted_iota(jnp.int32, (8, lanes), 1)
    rows = jnp.zeros((8, lanes), f32)
    for i, target in enumerate(targets):
        rows = jnp.where((row == i) & (lane == target), 1.0, rows)
    return rows.astype(bf16)


def slot_keys(shape, axis, capacity):
    index = lax.broadcasted_iota(jnp.int32, shape, axis)
    return (index % capacity + 1024 * (index // capacity)).astype(f32)


def run_keys(shape, axis, tokens):
    return (1024 * (lax.broadcasted_iota(jnp.int32, shape, axis) // tokens)).astype(f32)


def group_runs(capacity):
    return min(8, 224 // capacity)


def pick_slots_kernel(capacity, tokens, here_ref, g_ref, out_ref):
    many = g_ref.shape[0]
    width = out_ref.shape[1]
    extras = g_ref[:, width:]
    rows = one_hot_rows(extras.shape[1], here_ref[0])
    slots = dot_nt(rows, extras)[0:1] + run_keys((1, many), 1, tokens)
    takes = slot_keys((out_ref.shape[0], 1), 0, capacity) == slots
    select = jnp.where(takes, 1.0, 0.0).astype(bf16)
    out_ref[...] = dot(select, g_ref[:, :width]).astype(bf16)


def pick_slots(here, g_wide, width, capacity, tokens):
    length, wide = g_wide.shape
    runs = group_runs(capacity)
    steps = length // (runs * tokens)
    return pl.pallas_call(
        functools.partial(pick_slots_kernel, capacity, tokens),
        grid=(steps,),
        in_specs=[
            pl.BlockSpec(memory_space=pltpu.SMEM),
            pl.BlockSpec((runs * tokens, wide), lambda i: (i, 0)),
        ],
        out_specs=pl.BlockSpec((runs * capacity, width), lambda i: (i, 0)),
        out_shape=jax.ShapeDtypeStruct((steps * runs * capacity, width), bf16),
        name="pick_slots",
        cost_estimate=pl.CostEstimate(
            flops=2 * length * runs * capacity * width,
            bytes_accessed=3 * length * wide,
            transcendentals=0,
        ),
    )(here.reshape(1), g_wide)


def sigmoid(value):
    return 1.0 / (1.0 + jnp.exp(-value))


def experts_kernel(
    capacity,
    tokens,
    experts,
    here_ref,
    normed_ref,
    g_ref,
    grad_slots_ref,
    own_in_ref,
    first_in_ref,
    rest_in_ref,
    own_down_ref,
    other_down_ref,
    own_shared_in_ref,
    other_shared_in_ref,
    own_shared_out_ref,
    other_shared_out_ref,
    dispatched_ref,
    hidden_ref,
    grad_result_ref,
    grad_proj_ref,
    shared_hidden_ref,
    shared_grad_ref,
    parts_ref,
    gate_dot_ref,
    in_ref,
    down_ref,
    shared_in_ref,
    shared_out_ref,
    grad_dispatched_ref,
    scaled_ref,
):
    @pl.when(pl.program_id(0) == 0)
    def _():
        side = here_ref[1]
        rows = own_in_ref.shape[0]
        first = first_in_ref.shape[0]
        at = (1 - side) * rows
        in_ref[pl.ds(pl.multiple_of(side * rows, 64), rows), :] = own_in_ref[...]
        in_ref[pl.ds(pl.multiple_of(at, 16), first), :] = first_in_ref[...]
        in_ref[pl.ds(pl.multiple_of(at + first, 16), rows - first), :] = rest_in_ref[...]
        rows = own_down_ref.shape[0]
        down_ref[pl.ds(pl.multiple_of(side * rows, 64), rows), :] = own_down_ref[...]
        down_ref[pl.ds(pl.multiple_of((1 - side) * rows, 64), rows), :] = other_down_ref[...]
        rows = own_shared_in_ref.shape[0]
        units = own_shared_out_ref.shape[0]
        shared_in_ref[...] = jnp.zeros_like(shared_in_ref)
        shared_out_ref[...] = jnp.zeros_like(shared_out_ref)
        for place, ref in ((side, own_shared_in_ref), (1 - side, other_shared_in_ref)):
            window = pl.ds(pl.multiple_of(place * rows, 64), rows)
            shared_in_ref[window, :units] = ref[:, :units]
            shared_in_ref[window, HEAD_DIM : HEAD_DIM + units] = ref[:, units:]
        shared_out_ref[:units, :] = jnp.where(
            here_ref[2] == side, own_shared_out_ref[...], other_shared_out_ref[...]
        )

    many, slots = normed_ref.shape[0], dispatched_ref.shape[0]
    width = dispatched_ref.shape[1]
    here = here_ref[0]
    spare = normed_ref.shape[1] - width
    gate_rows = dot_nt(one_hot_rows(spare, here, experts + here), normed_ref[:, width:])
    gate_row = gate_rows[0:1] + gate_rows[1:2]
    slot_pick = one_hot_rows(spare, here)
    group = group_runs(capacity)
    chunk, picks = group * tokens, group * capacity
    takes = []
    for at in range(0, many, chunk):
        extras = g_ref[at : at + chunk, width:]
        slot_row = dot_nt(slot_pick, extras)[0:1] + run_keys((1, chunk), 1, tokens)
        hit = slot_keys((picks, 1), 0, capacity) == slot_row
        takes.append(hit)
        select = jnp.where(hit, 1.0, 0.0).astype(bf16)
        at_slots = slice(at // tokens * capacity, (at // tokens + group) * capacity)
        dispatched_ref[at_slots, :] = dot(select, normed_ref[at : at + chunk, :width]).astype(bf16)
    slot_gate = jnp.concatenate(
        [
            jnp.sum(
                jnp.where(hit, gate_row[:, i * chunk : (i + 1) * chunk], 0.0), axis=1, keepdims=True
            )
            for i, hit in enumerate(takes)
        ],
        axis=0,
    )
    dispatched = dispatched_ref[...]
    grad_slots = grad_slots_ref[...].astype(f32)
    grad_result = (grad_slots * slot_gate).astype(bf16)
    grad_result_ref[...] = grad_result

    projected = dot(dispatched, in_ref[...])
    gate, up = projected[:, :EXP_HID], projected[:, EXP_HID:]
    chance = sigmoid(gate)
    silu = gate * chance
    hidden = (silu * up).astype(bf16)
    hidden_ref[...] = hidden
    grad_hidden = dot_nt(grad_result, down_ref[...])
    grad_proj_ref[:, :EXP_HID] = (
        grad_hidden * up * chance * (1.0 + gate * (1.0 - chance))
    ).astype(bf16)
    grad_proj_ref[:, EXP_HID:] = (grad_hidden * silu).astype(bf16)
    result = dot(hidden, down_ref[...]).astype(bf16).astype(f32)
    slot_dot = jnp.sum(grad_slots * result, axis=1, keepdims=True)
    for i, hit in enumerate(takes):
        dots = slot_dot[i * picks : (i + 1) * picks]
        gate_dot = jnp.sum(jnp.where(hit, dots, 0.0), axis=0, keepdims=True)
        gate_dot_ref[:, i * chunk : (i + 1) * chunk] = jnp.broadcast_to(gate_dot, (8, chunk))
    scaled = (result * slot_gate).astype(bf16)
    grad_dispatched = dot_nt(grad_proj_ref[...], in_ref[...]).astype(bf16)

    grad_dispatched_ref[...] = grad_dispatched
    scaled_ref[...] = scaled
    lanes = shared_out_ref.shape[0]
    size = min(2 * HEAD_DIM, chunk)

    def visit(i, carry):
        at = pl.ds(pl.multiple_of(i * size, size), size)
        which = i * size // chunk
        filled = pl.ds(pl.multiple_of(which * picks, 16), picks)
        shared = dot(normed_ref[at, :width], shared_in_ref[...])
        shared_gate, shared_up = shared[:, :lanes], shared[:, lanes:]
        shared_chance = sigmoid(shared_gate)
        shared_silu = shared_gate * shared_chance
        shared_hidden = (shared_silu * shared_up).astype(bf16)
        shared_hidden_ref[at, :] = shared_hidden
        grad_shared = dot_nt(g_ref[at, :width], shared_out_ref[...])
        slope = shared_chance * (1.0 + shared_gate * (1.0 - shared_chance))
        shared_grad = jnp.concatenate(
            [(grad_shared * shared_up * slope).astype(bf16), (grad_shared * shared_silu).astype(bf16)],
            axis=1,
        )
        shared_grad_ref[at, :] = shared_grad
        slot_column = dot_nt(g_ref[at, width:], slot_pick)[:, 0:1]
        run = (i * size - which * chunk + lax.broadcasted_iota(jnp.int32, (size, 1), 0)) // tokens
        key = slot_column + (1024 * run).astype(f32)
        back = jnp.where(key == slot_keys((1, picks), 1, capacity), 1.0, 0.0).astype(bf16)
        parts_ref[at, :width] = (
            dot(back, grad_dispatched_ref[filled, :]) + dot_nt(shared_grad, shared_in_ref[...])
        ).astype(bf16)
        parts_ref[at, width:] = (
            dot(back, scaled_ref[filled, :]) + dot(shared_hidden, shared_out_ref[...])
        ).astype(bf16)
        return carry

    lax.fori_loop(0, many // size, visit, 0)


def run_experts(
    places, normed_wide, g_wide, grad_slots, weights, tokens, capacity
):
    length, wide = normed_wide.shape
    width = grad_slots.shape[1]
    experts = length // tokens
    runs = group_runs(capacity)
    steps = length // (runs * tokens)
    many, slots = runs * tokens, runs * capacity
    lanes = HEAD_DIM

    def block(rows, columns):
        return pl.BlockSpec((rows, columns), lambda i: (i, 0))

    def fixed(value):
        return pl.BlockSpec(value.shape, lambda i: (0, 0), pipeline_mode=pl.Buffered(1))

    def shape(rows, columns, kind=bf16):
        return jax.ShapeDtypeStruct((rows, columns), kind)

    return pl.pallas_call(
        functools.partial(experts_kernel, capacity, tokens, experts),
        grid=(steps,),
        in_specs=[
            pl.BlockSpec(memory_space=pltpu.SMEM),
            block(many, wide),
            block(many, wide),
            block(slots, width),
            *[fixed(weight) for weight in weights],
        ],
        out_specs=[
            block(slots, width),
            block(slots, EXP_HID),
            block(slots, width),
            block(slots, 2 * EXP_HID),
            block(many, lanes),
            block(many, 2 * lanes),
            block(many, 2 * width),
            pl.BlockSpec((8, many), lambda i: (0, i)),
        ],
        out_shape=[
            shape(steps * slots, width),
            shape(steps * slots, EXP_HID),
            shape(steps * slots, width),
            shape(steps * slots, 2 * EXP_HID),
            shape(length, lanes),
            shape(length, 2 * lanes),
            shape(length, 2 * width),
            shape(8, length, f32),
        ],
        scratch_shapes=[
            pltpu.VMEM((width, 2 * EXP_HID), bf16),
            pltpu.VMEM((EXP_HID, width), bf16),
            pltpu.VMEM((width, 2 * lanes), bf16),
            pltpu.VMEM((lanes, width), bf16),
            pltpu.VMEM((slots, width), bf16),
            pltpu.VMEM((slots, width), bf16),
        ],
        name="experts",
        cost_estimate=pl.CostEstimate(
            flops=20 * 10**9, bytes_accessed=40 * 10**6, transcendentals=2 * 10**6
        ),
    )(
        places,
        normed_wide,
        g_wide,
        grad_slots,
        *weights,
    )


def slot_grads_kernel(side_ref, left_ref, right_ref, own_ref, other_ref, turned_ref):
    @pl.when(pl.program_id(0) == 0)
    def _():
        turned_ref[...] = left_ref[...].T

    rows = own_ref.shape[0]
    size = rows // 5 if rows % 80 == 0 else rows // 4
    side = side_ref[0]

    def visit(i, carry):
        def part(place):
            at = pl.ds(pl.multiple_of(place * rows + i * size, 16), size)
            return dot(turned_ref[at, :], right_ref[...])

        at = pl.ds(pl.multiple_of(i * size, 16), size)
        own_ref[at, :] = part(side)
        other_ref[at, :] = part(1 - side).astype(bf16)
        return carry

    lax.fori_loop(0, rows // size, visit, 0)


def slot_grads(side, left, right):
    slots, tall = left.shape
    wide = right.shape[1]
    block = pl.BlockSpec((tall // 2, 2 * HEAD_DIM), lambda i: (0, i))
    return pl.pallas_call(
        slot_grads_kernel,
        grid=(wide // (2 * HEAD_DIM),),
        in_specs=[
            pl.BlockSpec(memory_space=pltpu.SMEM),
            pl.BlockSpec((slots, tall), lambda i: (0, 0), pipeline_mode=pl.Buffered(1)),
            pl.BlockSpec((slots, 2 * HEAD_DIM), lambda i: (0, i)),
        ],
        out_specs=[block, block],
        out_shape=[
            jax.ShapeDtypeStruct((tall // 2, wide), f32),
            jax.ShapeDtypeStruct((tall // 2, wide), bf16),
        ],
        scratch_shapes=[pltpu.VMEM((tall, slots), bf16)],
        name="slot_grads",
        cost_estimate=pl.CostEstimate(
            flops=2 * slots * tall * wide,
            bytes_accessed=2 * slots * (tall + wide) + 3 * tall * wide,
            transcendentals=0,
        ),
    )(side.reshape(1), left, right)


def turned_product_kernel(side_ref, left_ref, right_ref, out_ref, sum_ref):
    step = pl.program_id(0)

    @pl.when(step == 0)
    def _():
        sum_ref[...] = jnp.zeros_like(sum_ref)

    sum_ref[...] += dot_tn(right_ref[...], left_ref[...])

    @pl.when(step == pl.num_programs(0) - 1)
    def _():
        count = out_ref.shape[0] // HEAD_DIM
        near = count // 2

        def turn(i, carry):
            window = pl.ds(pl.multiple_of(i * HEAD_DIM, HEAD_DIM), HEAD_DIM)
            place = jnp.where(i // near == side_ref[0], 0, near) + i % near
            at = pl.ds(pl.multiple_of(place * HEAD_DIM, HEAD_DIM), HEAD_DIM)
            out_ref[at, :] = sum_ref[:, window].T
            return carry

        lax.fori_loop(0, count, turn, 0)


def turned_product(side, left, right, wide):
    length, lanes = right.shape
    tile = 2 * HEAD_DIM
    return pl.pallas_call(
        turned_product_kernel,
        grid=(length // tile,),
        in_specs=[
            pl.BlockSpec(memory_space=pltpu.SMEM),
            pl.BlockSpec((tile, wide), lambda i: (i, 0)),
            pl.BlockSpec((tile, lanes), lambda i: (i, 0)),
        ],
        out_specs=pl.BlockSpec((wide, lanes), lambda i: (0, 0)),
        out_shape=jax.ShapeDtypeStruct((wide, lanes), f32),
        scratch_shapes=[pltpu.VMEM((lanes, wide), f32)],
        name="turned_product",
        cost_estimate=pl.CostEstimate(
            flops=2 * length * lanes * wide,
            bytes_accessed=2 * length * wide,
            transcendentals=0,
        ),
    )(side.reshape(1), left, right)


def slot_table(span_picks, span_order, experts):
    tokens = span_picks.shape[0]
    order = span_order.reshape(tokens, TOP)
    onehot = span_picks[:, :, None] == jnp.arange(experts, dtype=jnp.int32)
    picked = jnp.any(onehot, axis=1)
    rank_key = jnp.sum(jnp.where(onehot, order[:, :, None], 0), axis=1)
    rank_key = jnp.where(picked, rank_key, tokens * TOP)
    before = rank_key[:, None, :] < rank_key[None, :, :]
    slots = jnp.sum(before.astype(jnp.int32), axis=0)
    return jnp.where(picked, slots, 2 * tokens)


def on_device(
    inputs,
    norm1_gain,
    w_query,
    w_key,
    w_value,
    w_output,
    norm2_gain,
    router,
    shared_gate_up_weight,
    shared_down_weight,
    expert_in,
    expert_out,
    picks,
    fill_order,
    grad_out,
):
    spans = lax.axis_size("ctx")
    here = lax.axis_index("ctx")
    side = lax.axis_index("fsdp")
    core = here % 2
    tokens, width = inputs.shape[1:]
    half = width // 2
    length = spans * tokens
    experts = spans * expert_in.shape[0]
    capacity = tokens * TOP // experts
    head = jnp.minimum(ring_position(here, spans), HEADS - 1)
    units = EXP_HID // spans
    ring = ring_of(spans)
    is_ring = spans == 16
    groups = [ring] if is_ring else None
    swap_core = [(i, i ^ 1) for i in range(spans)]

    def across(value):
        return lax.ppermute(value, "fsdp", [(0, 1), (1, 0)])

    def ordered(own, other, axis):
        return jnp.where(
            side == 0,
            jnp.concatenate([own, other], axis=axis),
            jnp.concatenate([other, own], axis=axis),
        )

    def everyone(value):
        return lax.all_gather(value, "ctx", axis=0, tiled=True, axis_index_groups=groups)

    def columns(value, start, count):
        return lax.dynamic_slice_in_dim(value, start, count, 1)

    def rows(value, start, count):
        return lax.dynamic_slice_in_dim(value, start, count, 0)

    def halves(value, axis=0):
        size = value.shape[axis] // 2
        mine = lax.dynamic_slice_in_dim(value, side * size, size, axis)
        theirs = lax.dynamic_slice_in_dim(value, (1 - side) * size, size, axis)
        return mine, theirs

    def reduced(value, axis=0):
        mine, theirs = halves(value, axis)
        return mine + across(theirs.astype(bf16)).astype(f32)

    def swapped(value):
        return lax.all_to_all(value, "ctx", split_axis=0, concat_axis=0, tiled=True)

    def row_major(value):
        return with_layout_constraint(value, Layout(tuple(range(value.ndim))))

    x = inputs[0]
    g = grad_out[0]
    x_all = everyone(x)
    spare = -(-2 * experts // HEAD_DIM) * HEAD_DIM
    own_table = slot_table(picks[0], fill_order[0, 0], experts)
    own_table = jnp.pad(
        own_table.astype(f32), ((0, 0), (0, spare - experts)), constant_values=2.0 * tokens
    )
    g_wide = jnp.concatenate([g, own_table.astype(bf16)], axis=1)
    head_own = jnp.concatenate(
        [columns(w, head * HEAD_DIM, HEAD_DIM) for w in (w_query, w_key, w_value)], axis=1
    )
    head_other = across(head_own)
    small = jnp.concatenate([router.T, norm1_gain[None], norm2_gain[None]], axis=0)
    small_other = across(small)
    output_near = across(columns(w_output, core * half, half))
    lanes = HEAD_DIM
    shared_in_own = jnp.concatenate(
        [columns(shared_gate_up_weight, at + here * units, units) for at in (0, EXP_HID)], axis=1
    )
    shared_rows = shared_down_weight.shape[0]
    shared_out_own = rows(shared_down_weight, here * units % shared_rows, units)
    cosine, sine = rotary_tables(jnp.asarray(ring, jnp.int32) * tokens, tokens, HEAD_DIM)
    small = ordered(small, small_other, 1)
    router_w = small[:experts]
    gain_one = small[experts : experts + 1].astype(f32)
    gain_two = small[experts + 1 :].astype(f32)
    quarter = half // 8
    chunks = [expert_in[0, :quarter], expert_in[0, quarter:]]
    head_other, *chunks = tied(head_other, *chunks)
    chunks = [across(chunk) for chunk in chunks]
    x_all, cosine, sine, head_other, gain_one, output_near, chunks[0] = tied(
        x_all, cosine, sine, head_other, gain_one, output_near, chunks[0]
    )
    output_far = lax.ppermute(output_near, "ctx", swap_core)
    g_wide_all = everyone(after(g_wide, x_all))
    g_all = g_wide_all[:, :width]
    table = g_wide_all[:, width : width + experts]

    normed1_all, query, key, value = project(
        side, x_all, gain_one, head_own, head_other, cosine, sine
    )
    context, lse, attended = attend(query, key, value, is_ring)
    attended, output_far = tied(attended, output_far)
    down_other = across(after(expert_out[0], attended))
    got = swapped(attended.reshape(spans, tokens, HEAD_DIM))
    got, chunks[1] = tied(got, chunks[1])
    spot = jnp.stack([side, core]).astype(jnp.int32)
    router_pad = jnp.pad(router_w, ((0, spare - experts), (0, 0)))
    second, normed2_wide, scale_two, own_gates, attended = mix(
        spot,
        got,
        w_output,
        output_near,
        output_far,
        x,
        gain_two,
        router_pad,
        own_table,
        experts,
    )
    normed2_wide, g_wide_all = tied(normed2_wide, g_wide_all)
    normed2_wide = everyone(normed2_wide)
    grad_slots = pick_slots(here, g_wide_all, width, capacity, tokens)
    shared_in_other = across(after(shared_in_own, grad_slots))
    shared_out_other = across(after(shared_out_own, grad_slots))
    normed2_wide, grad_slots, down_other, shared_in_other, shared_out_other = tied(
        normed2_wide, grad_slots, down_other, shared_in_other, shared_out_other
    )
    normed2_all = normed2_wide[:, :width]
    attended_all = everyone(after(attended, normed2_wide))
    dense = [
        columns(after(w, grad_slots), core * half, half) for w in (w_query, w_key, w_value)
    ]
    dense = jnp.concatenate(dense, axis=0)
    near = [across(dense[: dense.shape[0] // 2]), across(dense[dense.shape[0] // 2 :])]
    spots = [ring_position(i, spans) for i in range(spans)]
    (
        dispatched,
        expert_hidden,
        grad_result,
        grad_proj,
        shared_hidden,
        grad_sproj,
        parts,
        gate_dot,
    ) = run_experts(
        jnp.stack([here, side, here * units // shared_rows]).astype(jnp.int32),
        normed2_wide,
        g_wide_all,
        grad_slots,
        (
            expert_in[0],
            chunks[0],
            chunks[1],
            expert_out[0],
            down_other,
            shared_in_own,
            shared_in_other,
            shared_out_own,
            shared_out_other,
        ),
        tokens,
        capacity,
    )
    parts, near[0], attended_all = tied(parts, near[0], attended_all)
    sums = lax.psum_scatter(
        parts, "ctx", scatter_dimension=0, tiled=True, axis_index_groups=groups
    )
    gate_dot = gate_dot[0].reshape(spans, tokens)
    grad_shared_in = dot_tn(grad_sproj, normed2_all)
    grad_shared_in = jnp.concatenate(
        [grad_shared_in[:units], grad_shared_in[lanes : lanes + units]], axis=0
    )
    grad_shared_in = reduced(grad_shared_in, 1).astype(bf16)
    grad_shared_out = dot_tn(shared_hidden, g_all)[:units].astype(bf16)
    grad_shared_out = grad_shared_out.astype(f32) + across(grad_shared_out).astype(f32)
    grad_shared_out = grad_shared_out.astype(bf16)
    shared_grads = jnp.concatenate(
        [grad_shared_in, grad_shared_out[:, :half], grad_shared_out[:, half:]], axis=0
    )
    gate_dot = jnp.concatenate([gate_dot[i : i + 1] for i in spots], axis=0)
    gate_grads = swapped(after(gate_dot, parts)[:, None, :])[:, 0, :].T

    own_down, down_theirs = slot_grads(side, expert_hidden, grad_result)
    own_in, in_theirs = slot_grads(side, dispatched, grad_proj)
    down_theirs = across(after(down_theirs, parts))
    sums, in_theirs, shared_grads, gate_grads = tied(
        sums,
        in_theirs,
        row_major(shared_grads),
        gate_grads,
    )
    split = half * 3 // 8
    in_upper = across(in_theirs[:split])

    sent, cuts, grad_second, layer_out = mix_back(
        spot,
        sums,
        own_gates,
        jnp.pad(gate_grads, ((0, 0), (0, spare - experts))),
        router_pad,
        second,
        scale_two,
        gain_two,
        g,
        w_output,
        output_near,
        output_far,
        spans,
    )
    arrived = swapped(sent).reshape(length, HEAD_DIM)
    arrived, shared_grads, cuts, near[1], down_theirs = tied(
        arrived, shared_grads, cuts, near[1], down_theirs
    )
    cuts = lax.all_to_all(
        cuts, "ctx", split_axis=0, concat_axis=0, tiled=True, axis_index_groups=groups
    )
    extras = cuts[:, :tokens].reshape(length, HEAD_DIM)
    shared_grads = everyone(shared_grads[None])
    grad_heads, grad_heads_ring = attend_back(
        query, key, value, arrived, context, lse, cosine, sine, is_ring
    )
    grad_heads, grad_heads_ring, in_upper = tied(grad_heads, grad_heads_ring, in_upper)
    cut = width // spans
    gain_rows = cuts[:, tokens : tokens + 2, :cut].astype(f32)
    gain_rows = jnp.sum(gain_rows, axis=(0, 1))
    gain_rows = jnp.pad(gain_rows.reshape(1, cut), ((0, 15), (0, HEAD_DIM - cut)))
    grad_router = turned_product(side, normed2_wide, extras, width)[:, cut : cut + experts]
    grad_router = grad_router[:half] + across(grad_router[half:])
    products = turned_product(side, attended_all, extras, width)
    mine, theirs = products[:half], products[half:]
    gain_high = gain_rows.astype(bf16)
    gain_low = jnp.roll((gain_rows - gain_high.astype(f32)).astype(bf16), 1, axis=0)
    theirs = jnp.concatenate([theirs.astype(bf16), gain_high + gain_low], axis=0)
    grad_heads_ring, theirs = tied(grad_heads_ring, theirs)
    theirs = across(theirs).astype(f32)
    grad_output = mine + theirs[:half]
    gain_rows = gain_rows[:1] + theirs[half : half + 1] + theirs[half + 1 : half + 2]
    gain_high = gain_rows.astype(bf16)
    gain_low = (gain_rows - gain_high.astype(f32)).astype(bf16)
    gain_rows = jnp.pad(
        jnp.concatenate([gain_high, gain_low], axis=0), ((0, 14), (3 * HEAD_DIM, 0))
    )
    head_mine, head_theirs = halves(dot_tn(normed1_all, grad_heads_ring))
    head_theirs = head_theirs.astype(bf16)
    got = swapped(grad_heads.reshape(spans, tokens, 3 * HEAD_DIM))
    grad_head_w = (head_mine + across(head_theirs).astype(f32)).astype(bf16)
    part = jnp.sum(grad_head_w.astype(f32) * head_own.astype(f32), axis=1, keepdims=True)
    part_high = part.astype(bf16).astype(f32)
    lane = lax.broadcasted_iota(jnp.int32, (half, HEAD_DIM), 1)
    grad_output = jnp.where(lane < cut, grad_output, 0.0)
    grad_output = jnp.where(lane == cut, part_high, grad_output)
    grad_output = jnp.where(lane == cut + 1, part - part_high, grad_output)
    head_grads = jnp.concatenate([grad_head_w, grad_output.astype(bf16)], axis=1)
    head_grads = jnp.concatenate([head_grads, gain_rows], axis=0)
    in_lower = across(after(in_theirs[split:], head_grads))
    head_grads, got = tied(row_major(head_grads), got)
    head_grads = everyone(head_grads[None])
    near = jnp.concatenate(near, axis=0)
    far = lax.ppermute(near, "ctx", swap_core)

    grad_inputs = inputs_back(
        side, core, got, w_query, w_key, w_value, near, far, x, gain_one, grad_second
    )
    grad_inputs, in_lower = tied(grad_inputs, in_lower)
    grad_query, grad_key, grad_value, grad_output, grad_norm1, grad_norm2 = place_heads(
        side, head_grads, norm1_gain.astype(f32), width
    )
    grad_expert_in = jnp.concatenate(
        [
            own_in[:split] + in_upper.astype(f32),
            own_in[split:] + in_lower.astype(f32),
        ],
        axis=0,
    )
    grad_shared_in, grad_shared_out = place_shared(shared_grads, side)
    return (
        layer_out[None],
        grad_inputs[None],
        grad_norm1.reshape(half),
        grad_query,
        grad_key,
        grad_value,
        grad_output,
        grad_norm2.reshape(half),
        grad_router,
        grad_shared_in,
        grad_shared_out,
        grad_expert_in[None],
        (own_down + down_theirs.astype(f32))[None],
    )


def solution(mesh):
    placed = (
        P("fsdp", "ctx", None),
        P("fsdp"),
        P("fsdp", None),
        P("fsdp", None),
        P("fsdp", None),
        P("fsdp", None),
        P("fsdp"),
        P("fsdp", None),
        P("fsdp", None),
        P("fsdp", None),
        P("ctx", "fsdp", None),
        P("ctx", "fsdp", None),
        P("fsdp", "ctx", None),
        P("fsdp", "ctx", None),
        P("fsdp", "ctx", None),
    )
    return jax.shard_map(
        on_device,
        mesh=mesh,
        in_specs=placed,
        out_specs=(
            P("fsdp", "ctx", None),
            P("fsdp", "ctx", None),
            P("fsdp"),
            P("fsdp", None),
            P("fsdp", None),
            P("fsdp", None),
            P("fsdp", None),
            P("fsdp"),
            P("fsdp", None),
            P("fsdp", None),
            P("fsdp", None),
            P("ctx", "fsdp", None),
            P("ctx", "fsdp", None),
        ),
        check_vma=False,
    )
```

```python
import functools
import math

import jax
import jax.numpy as jnp
from jax import lax
from jax.experimental import pallas as pl
from jax.experimental.layout import Layout, with_layout_constraint
from jax.experimental.pallas import tpu as pltpu
from jax.sharding import PartitionSpec as P

HEADS = 10
HEAD_DIM = 128
EXP_HID = 896
TOP = 7
BLOCK = 256
TILE = 512

epsilon = 1e-06
masked_score = -1000000000.0
score_scale = 1.0 / math.sqrt(HEAD_DIM)
exact = lax.Precision.HIGHEST
f32 = jnp.float32
bf16 = jnp.bfloat16


def dot(a, b):
    return jnp.dot(a, b, preferred_element_type=f32)


def dot_nt(a, b):
    return lax.dot_general(a, b, (((1,), (1,)), ((), ())), preferred_element_type=f32)


def dot_tn(a, b):
    return lax.dot_general(a, b, (((0,), (0,)), ((), ())), preferred_element_type=f32)


def rms_scale(values):
    return lax.rsqrt(jnp.mean(values * values, axis=-1, keepdims=True) + epsilon)


def rotary_tables(starts, count, width):
    half = width // 2
    freqs = jnp.exp(-math.log(10000.0) * jnp.arange(half, dtype=f32) * 2.0 / width)
    freqs = jnp.concatenate([freqs, freqs])
    first = starts.astype(f32)[:, None] * freqs[None, :]
    second = jnp.arange(count, dtype=f32)[:, None] * freqs[None, :]
    angles = jnp.concatenate([first, second], axis=0)
    sign = jnp.where(jnp.arange(width) < half, -1.0, 1.0)
    cosine, sine = lax.optimization_barrier((jnp.cos(angles), jnp.sin(angles) * sign))
    spans = starts.shape[0]
    cos_a, sin_a = cosine[:spans, None], sine[:spans, None]
    cos_b, sin_b = cosine[None, spans:], sine[None, spans:]
    shape = (spans * count, width)
    return (
        (cos_a * cos_b - sin_a * sin_b).reshape(shape),
        (sin_a * cos_b + cos_a * sin_b).reshape(shape),
    )


def allowed_tile(rows, columns):
    key_block = lax.broadcasted_iota(jnp.int32, (rows, columns), 0) // BLOCK
    query_block = lax.broadcasted_iota(jnp.int32, (rows, columns), 1) // BLOCK
    return key_block <= query_block


def ring_of(spans):
    if spans != 16:
        return list(range(spans))
    chips = [0, 2, 4, 6, 7, 5, 3, 1]
    return [2 * chip + core for chip in chips for core in (0, 1)]


def pieces(j, tile, length, ring):
    if ring:
        starts = (j * BLOCK, length - BLOCK - j * BLOCK)
        return [pl.ds(pl.multiple_of(at, BLOCK), BLOCK) for at in starts]
    return [pl.ds(pl.multiple_of(j * tile, tile), tile)]


def load(ref, windows, columns=slice(None)):
    parts = [ref[window, columns] for window in windows]
    return parts[0] if len(parts) == 1 else jnp.concatenate(parts, axis=0)


def store(ref, windows, value, columns=slice(None)):
    size = value.shape[0] // len(windows)
    for i, window in enumerate(windows):
        ref[window, columns] = value[i * size : (i + 1) * size]


def attend_kernel(
    ring, q_ref, k_ref, v_ref, context_ref, lse_ref, low_ref, score_ref
):
    length = k_ref.shape[0]
    tile = context_ref.shape[0]
    here = pl.program_id(0)
    queries = load(q_ref, pieces(here, tile, length, ring))

    def raw_scores(j):
        return dot_nt(load(k_ref, pieces(j, tile, length, ring)), queries) * score_scale

    def fold(j, scores, peak):
        score_ref[pl.ds(pl.multiple_of(j * tile, tile), tile), :] = scores
        return jnp.maximum(peak, jnp.max(scores.reshape(tile // 8, 8, tile), axis=0))

    diagonal = jnp.where(allowed_tile(tile, tile), raw_scores(here), masked_score)
    peak = fold(here, diagonal, jnp.full((8, tile), masked_score, f32))
    peak = lax.fori_loop(0, here, lambda j, p: fold(j, raw_scores(j), p), peak)
    top = jnp.max(peak, axis=0, keepdims=True)

    def gather(j, carry):
        total, numer = carry
        weights = jnp.exp(score_ref[pl.ds(pl.multiple_of(j * tile, tile), tile), :] - top)
        total = total + jnp.sum(weights.reshape(tile // 8, 8, tile), axis=0)
        values = load(v_ref, pieces(j, tile, length, ring))
        return total, numer + dot_tn(values, weights.astype(bf16))

    zero = (jnp.zeros((8, tile), f32), jnp.zeros((HEAD_DIM, tile), f32))
    total, numer = lax.fori_loop(0, here + 1, gather, zero)
    total = jnp.sum(total, axis=0, keepdims=True)
    context = (numer / total).T
    context_ref[...] = context
    low_ref[...] = context.astype(bf16)
    lse_ref[...] = top + jnp.log(total)


def attend(query, key, value, ring):
    length = query.shape[0]
    tile = min(TILE, length)
    whole = pl.BlockSpec((length, HEAD_DIM), lambda i: (0, 0))
    part = pl.BlockSpec((tile, HEAD_DIM), lambda i: (i, 0))
    return pl.pallas_call(
        functools.partial(attend_kernel, ring),
        grid=(length // tile,),
        in_specs=[whole] * 3,
        out_specs=[part, pl.BlockSpec((1, tile), lambda i: (0, i)), part],
        out_shape=[
            jax.ShapeDtypeStruct((length, HEAD_DIM), f32),
            jax.ShapeDtypeStruct((1, length), f32),
            jax.ShapeDtypeStruct((length, HEAD_DIM), bf16),
        ],
        scratch_shapes=[pltpu.VMEM((length, tile), f32)],
        name="attend",
        cost_estimate=pl.CostEstimate(
            flops=2 * length * length * HEAD_DIM,
            bytes_accessed=12 * length * HEAD_DIM,
            transcendentals=length * length // 2,
        ),
    )(query, key, value)


def attend_back_kernel(
    ring,
    q_ref,
    k_ref,
    v_ref,
    grad_ref,
    context_ref,
    lse_ref,
    cos_ref,
    sin_ref,
    out_ref,
    out_ring_ref,
    dq_ref,
    delta_ref,
    dk_ref,
    dv_ref,
):
    length = q_ref.shape[0]
    tile = dk_ref.shape[0]
    steps = length // tile
    here = pl.program_id(0)

    def natural(i):
        return pl.ds(pl.multiple_of(i * tile, tile), tile)

    @pl.when(here == 0)
    def _():
        def prepare(i, carry):
            window = natural(i)
            dq_ref[window, :] = jnp.zeros((tile, HEAD_DIM), f32)
            product = grad_ref[window, :].astype(f32) * context_ref[window, :]
            ones = jnp.ones((8, HEAD_DIM), f32)
            delta = lax.dot_general(
                ones, product, (((1,), (1,)), ((), ())), precision=exact, preferred_element_type=f32
            )
            delta_ref[:, window] = delta
            return carry

        lax.fori_loop(0, steps, prepare, 0)

    keys = load(k_ref, pieces(here, tile, length, ring))
    values = load(v_ref, pieces(here, tile, length, ring))

    dk_ref[...] = jnp.zeros_like(dk_ref)
    dv_ref[...] = jnp.zeros_like(dv_ref)

    def visit(i, carry):
        window = natural(i)
        queries = load(q_ref, pieces(i, tile, length, ring))
        grads = grad_ref[window, :]
        weights = jnp.exp(dot_nt(keys, queries) * score_scale - lse_ref[:, window])
        later = jnp.where(i > here, weights[BLOCK:, :BLOCK], 0.0)
        later = jnp.concatenate([later, weights[BLOCK:, BLOCK:]], axis=1)
        weights = jnp.concatenate([weights[:BLOCK], later], axis=0)
        grad_weights = dot_nt(values, grads)
        grad_raw = (weights * (grad_weights - delta_ref[0:1, window]) * score_scale).astype(bf16)
        dq_ref[window, :] += dot_tn(grad_raw, keys)
        dk_ref[...] += dot(grad_raw, queries)
        dv_ref[...] += dot(weights.astype(bf16), grads)
        return carry

    lax.fori_loop(here, steps, visit, 0)

    def write(i, part, value):
        at = slice(part * HEAD_DIM, (part + 1) * HEAD_DIM)
        out_ref[natural(i), at] = value
        store(out_ring_ref, pieces(i, tile, length, ring), value, at)

    def turned_back(i, value):
        windows = pieces(i, tile, length, ring)
        scaled = pltpu.roll(value * load(sin_ref, windows), HEAD_DIM // 2, 1)
        return (value * load(cos_ref, windows) + scaled).astype(bf16)

    write(here, 1, turned_back(here, dk_ref[...]))
    write(here, 2, dv_ref[...].astype(bf16))

    @pl.when(here == steps - 1)
    def _():
        def finish(i, carry):
            write(i, 0, turned_back(i, dq_ref[natural(i), :]))
            return carry

        lax.fori_loop(0, steps, finish, 0)


def attend_back(query, key, value, grad, context, lse, cosine, sine, ring):
    length = query.shape[0]
    tile = min(TILE, length)
    memory = pl.BlockSpec(memory_space=pltpu.VMEM)
    return pl.pallas_call(
        functools.partial(attend_back_kernel, ring),
        grid=(length // tile,),
        in_specs=[memory] * 8,
        out_specs=[memory] * 2,
        out_shape=[jax.ShapeDtypeStruct((length, 3 * HEAD_DIM), bf16)] * 2,
        scratch_shapes=[
            pltpu.VMEM((length, HEAD_DIM), f32),
            pltpu.VMEM((8, length), f32),
            pltpu.VMEM((tile, HEAD_DIM), f32),
            pltpu.VMEM((tile, HEAD_DIM), f32),
        ],
        name="attend_back",
        cost_estimate=pl.CostEstimate(
            flops=5 * length * length * HEAD_DIM,
            bytes_accessed=20 * length * HEAD_DIM,
            transcendentals=length * length // 2,
        ),
    )(query, key, value, grad, context, lse, cosine, sine)


def project_kernel(
    side_ref, x_ref, gain_ref, own_ref, other_ref, cos_ref, sin_ref, normed_ref, q_ref, k_ref, v_ref
):
    own, other = own_ref[...], other_ref[...]
    weight = jnp.where(
        side_ref[0] == 0,
        jnp.concatenate([own, other], axis=0),
        jnp.concatenate([other, own], axis=0),
    )
    resid = x_ref[...].astype(f32)
    normed = (resid * rms_scale(resid) * gain_ref[...]).astype(bf16)
    normed_ref[...] = normed
    projected = dot(normed, weight)
    for out, at in ((q_ref, 0), (k_ref, HEAD_DIM)):
        part = projected[:, at : at + HEAD_DIM]
        turned = pltpu.roll(part, HEAD_DIM // 2, 1)
        out[...] = (part * cos_ref[...] + turned * sin_ref[...]).astype(bf16)
    v_ref[...] = projected[:, 2 * HEAD_DIM :].astype(bf16)


def project(side, x, gain, own, other, cosine, sine):
    length, width = x.shape
    tile = min(TILE, length)
    part = pl.BlockSpec((tile, HEAD_DIM), lambda i: (i, 0))
    wide = pl.BlockSpec((tile, width), lambda i: (i, 0))
    return pl.pallas_call(
        project_kernel,
        grid=(length // tile,),
        in_specs=[
            pl.BlockSpec(memory_space=pltpu.SMEM),
            wide,
            pl.BlockSpec((1, width), lambda i: (0, 0)),
            pl.BlockSpec(own.shape, lambda i: (0, 0)),
            pl.BlockSpec(own.shape, lambda i: (0, 0)),
            part,
            part,
        ],
        out_specs=[wide, part, part, part],
        out_shape=[jax.ShapeDtypeStruct((length, width), bf16)]
        + [jax.ShapeDtypeStruct((length, HEAD_DIM), bf16)] * 3,
        name="project",
        cost_estimate=pl.CostEstimate(
            flops=6 * length * width * HEAD_DIM,
            bytes_accessed=4 * length * width,
            transcendentals=0,
        ),
    )(side.reshape(1), x, gain, own, other, cosine, sine)


def home(head, spans):
    if spans != 16:
        return head
    chip, core = head // 2, head % 2
    return 2 * jnp.where(chip < 4, 2 * chip, 15 - 2 * chip) + core


def head_pair(side, spans, i):
    count = HEADS // 2
    low, high = home(i, spans), home(count + i, spans)
    mine = jnp.where(side == 0, low, high)
    theirs = jnp.where(side == 0, high, low)
    return mine, theirs, pl.ds(pl.multiple_of(i * HEAD_DIM, HEAD_DIM), HEAD_DIM)


def mix_kernel(
    experts,
    spot_ref,
    got_ref,
    own_ref,
    near_ref,
    far_ref,
    x_ref,
    gain_ref,
    router_ref,
    table_ref,
    second_ref,
    low_ref,
    scale_ref,
    gates_ref,
    attended_ref,
    near_sum_ref,
    far_sum_ref,
):
    ring = ring_of(got_ref.shape[0])
    for h in range(HEADS):
        attended_ref[:, h * HEAD_DIM : (h + 1) * HEAD_DIM] = got_ref[ring[h]]
    second = x_ref[...].astype(f32)
    tokens, width = second.shape
    half = near_ref.shape[1]
    second_ref[...] = second
    near_sum_ref[...] = jnp.zeros((tokens, half), f32)
    far_sum_ref[...] = jnp.zeros((tokens, half), f32)

    def visit(i, carry):
        mine, theirs, at = head_pair(spot_ref[0], got_ref.shape[0], i)
        second_ref[...] += dot(got_ref[mine], own_ref[at, :])
        near_sum_ref[...] += dot(got_ref[theirs], near_ref[at, :])
        far_sum_ref[...] += dot(got_ref[theirs], far_ref[at, :])
        return carry

    lax.fori_loop(0, HEADS // 2, visit, 0, unroll=True)
    second, near, far = second_ref[...], near_sum_ref[...], far_sum_ref[...]
    second += jnp.where(
        spot_ref[1] == 0,
        jnp.concatenate([near, far], axis=1),
        jnp.concatenate([far, near], axis=1),
    )
    scale = rms_scale(second)
    second_ref[...] = second
    scale_ref[...] = scale
    normed = (second * scale * gain_ref[...]).astype(bf16)
    logits = dot_nt(normed, router_ref[...])
    picked = table_ref[...] < tokens
    peak = jnp.max(jnp.where(picked, logits, masked_score), axis=-1, keepdims=True)
    chances = jnp.where(picked, jnp.exp(logits - peak), 0.0)
    gates = chances / jnp.sum(chances, axis=-1, keepdims=True)
    gates_ref[...] = gates
    high = gates.astype(bf16).astype(f32)
    rest = pltpu.roll(gates - high, experts, 1)
    low_ref[:, :width] = normed
    low_ref[:, width:] = (high + rest).astype(bf16)


def mix(spot, got, own, near, far, x, gain, router, table, experts):
    smem = pl.BlockSpec(memory_space=pltpu.SMEM)
    memory = pl.BlockSpec(memory_space=pltpu.VMEM)
    tokens, width = x.shape
    spare = table.shape[1]
    return pl.pallas_call(
        functools.partial(mix_kernel, experts),
        in_specs=[smem] + [memory] * 8,
        out_specs=[memory] * 5,
        out_shape=[
            jax.ShapeDtypeStruct(x.shape, f32),
            jax.ShapeDtypeStruct((tokens, width + spare), bf16),
            jax.ShapeDtypeStruct((tokens, 1), f32),
            jax.ShapeDtypeStruct((tokens, spare), f32),
            jax.ShapeDtypeStruct(x.shape, bf16),
        ],
        scratch_shapes=[pltpu.VMEM((tokens, width // 2), f32)] * 2,
        name="mix",
    )(spot, got, own, near, far, x, gain, router, table)


def mix_back_kernel(
    spot_ref,
    sums_ref,
    gates_ref,
    gate_grads_ref,
    router_ref,
    second_ref,
    scale_ref,
    gain_ref,
    g_ref,
    own_ref,
    near_ref,
    far_ref,
    send_ref,
    cuts_ref,
    grad_second_ref,
    out_ref,
):
    tokens, width = second_ref.shape
    second = second_ref[...]
    scale = scale_ref[...]
    gain = gain_ref[...]
    gates = gates_ref[...]
    gate_grads = gate_grads_ref[...]
    out_ref[...] = (second + sums_ref[:, width:].astype(f32)).astype(bf16)
    weighted = gates * gate_grads
    grad_sel = weighted - gates * jnp.sum(weighted, axis=-1, keepdims=True)
    grad_logits = grad_sel.astype(bf16)
    grad_normed = sums_ref[:, :width].astype(f32) + dot(grad_logits, router_ref[...])
    gain_part = jnp.sum(grad_normed * second * scale, axis=0, keepdims=True)
    hat = grad_normed * gain
    mean = jnp.mean(hat * second, axis=-1, keepdims=True)
    grad_second = g_ref[...].astype(f32) + scale * hat - second * (scale * scale * scale) * mean
    grad_second_ref[...] = grad_second
    grad_mixed = grad_second.astype(bf16)
    spans = send_ref.shape[0]
    cut = width // spans
    lane = lax.broadcasted_iota(jnp.int32, (1, HEAD_DIM), 1)
    high = gain_part.astype(bf16).astype(f32)
    row = lax.broadcasted_iota(jnp.int32, (16, width), 0)
    gain_rows = jnp.where(row == 0, high, jnp.where(row == 1, gain_part - high, 0.0))
    shifted = pltpu.roll(grad_logits.astype(f32), cut, 1)
    for k, c in enumerate(ring_of(spans)):
        start = min(c * cut // HEAD_DIM * HEAD_DIM, width - 2 * HEAD_DIM)
        shift = (start - c * cut) % (2 * HEAD_DIM)
        for value, rest, out_rows in (
            (grad_second, shifted, slice(0, tokens)),
            (gain_rows, 0.0, slice(tokens, tokens + 16)),
        ):
            window = pltpu.roll(value[:, start : start + 2 * HEAD_DIM], shift, 1)[:, :HEAD_DIM]
            window = jnp.where(lane < cut, window, 0.0) + rest
            cuts_ref[k, out_rows, :] = window.astype(bf16)
    left, right = grad_mixed[:, : width // 2], grad_mixed[:, width // 2 :]
    at_near = jnp.where(spot_ref[1] == 0, left, right)
    at_far = jnp.where(spot_ref[1] == 0, right, left)
    def visit(i, carry):
        mine, theirs, at = head_pair(spot_ref[0], spans, i)
        send_ref[mine] = dot_nt(grad_mixed, own_ref[at, :]).astype(bf16)
        other = dot_nt(at_near, near_ref[at, :]) + dot_nt(at_far, far_ref[at, :])
        send_ref[theirs] = other.astype(bf16)
        return carry

    lax.fori_loop(0, HEADS // 2, visit, 0, unroll=True)
    for h in ring_of(spans)[HEADS:]:
        send_ref[h] = jnp.zeros((tokens, HEAD_DIM), bf16)


def mix_back(spot, sums, gates, gate_grads, router, second, scale, gain, g, own, near, far, spans):
    tokens, width = second.shape
    smem = pl.BlockSpec(memory_space=pltpu.SMEM)
    memory = pl.BlockSpec(memory_space=pltpu.VMEM)
    return pl.pallas_call(
        mix_back_kernel,
        in_specs=[smem] + [memory] * 11,
        out_specs=[memory] * 4,
        out_shape=[
            jax.ShapeDtypeStruct((spans, tokens, HEAD_DIM), bf16),
            jax.ShapeDtypeStruct((spans, tokens + 16, HEAD_DIM), bf16),
            jax.ShapeDtypeStruct((tokens, width), f32),
            jax.ShapeDtypeStruct((tokens, width), bf16),
        ],
        name="mix_back",
    )(spot, sums, gates, gate_grads, router, second, scale, gain, g, own, near, far)


def inputs_back_kernel(
    side_ref,
    core_ref,
    got_ref,
    wq_ref,
    wk_ref,
    wv_ref,
    near_q_ref,
    near_rest_ref,
    far_q_ref,
    far_rest_ref,
    x_ref,
    gain_ref,
    grad_second_ref,
    out_ref,
    own_sum_ref,
    other_sum_ref,
):
    tokens, width = x_ref.shape
    half = width // 2
    count = HEADS // 2
    own_sum_ref[...] = jnp.zeros((tokens, half), f32)
    other_sum_ref[...] = jnp.zeros((tokens, half), f32)
    spans = got_ref.shape[0]

    def visit(h, carry):
        low, high = home(h, spans), home(count + h, spans)
        mine = jnp.where(core_ref[0] == 0, low, high)
        theirs = jnp.where(core_ref[0] == 0, high, low)
        window = pl.ds(pl.multiple_of(h * HEAD_DIM, HEAD_DIM), HEAD_DIM)
        upper = pl.ds(pl.multiple_of((count + h) * HEAD_DIM, HEAD_DIM), HEAD_DIM)
        for i, weight in enumerate((wq_ref, wk_ref, wv_ref)):
            at = slice(i * HEAD_DIM, (i + 1) * HEAD_DIM)
            near_ref, far_ref = (near_rest_ref, far_rest_ref) if i else (near_q_ref, far_q_ref)
            rows = slice(max(i - 1, 0) * half, max(i, 1) * half)
            grads = jnp.concatenate([got_ref[low, :, at], got_ref[high, :, at]], axis=1)
            weights = jnp.concatenate([weight[:, window], weight[:, upper]], axis=1)
            own_sum_ref[...] += dot_nt(grads, weights)
            grads = jnp.concatenate([got_ref[mine, :, at], got_ref[theirs, :, at]], axis=1)
            weights = jnp.concatenate([near_ref[rows, window], far_ref[rows, window]], axis=1)
            other_sum_ref[...] += dot_nt(grads, weights)
        return carry

    lax.fori_loop(0, count, visit, 0)
    own_part, other_part = own_sum_ref[...], other_sum_ref[...]
    grad_normed = jnp.where(
        side_ref[0] == 0,
        jnp.concatenate([own_part, other_part], axis=1),
        jnp.concatenate([other_part, own_part], axis=1),
    )
    resid = x_ref[...].astype(f32)
    scale = rms_scale(resid)
    hat = grad_normed * gain_ref[...]
    mean = jnp.mean(hat * resid, axis=-1, keepdims=True)
    out_ref[...] = grad_second_ref[...] + scale * hat - resid * (scale * scale * scale) * mean


def inputs_back(side, core, got, *values):
    x = values[-3]
    smem = pl.BlockSpec(memory_space=pltpu.SMEM)
    memory = pl.BlockSpec(memory_space=pltpu.VMEM)
    return pl.pallas_call(
        inputs_back_kernel,
        in_specs=[smem] * 2 + [memory] * (1 + len(values)),
        out_specs=memory,
        out_shape=jax.ShapeDtypeStruct(x.shape, f32),
        scratch_shapes=[pltpu.VMEM((x.shape[0], x.shape[1] // 2), f32)] * 2,
        name="inputs_back",
    )(
        side.reshape(1),
        core.reshape(1),
        got,
        *values,
    )


def place_heads_kernel(
    cut,
    side_ref,
    heads_ref,
    rest_ref,
    gain_rows_ref,
    gain_ref,
    q_ref,
    k_ref,
    v_ref,
    output_ref,
    norm_ref,
    norm2_ref,
):
    for h in range(HEADS):
        at = slice(h * HEAD_DIM, (h + 1) * HEAD_DIM)
        for i, out in enumerate((q_ref, k_ref, v_ref)):
            out[:, at] = heads_ref[h, :, i * HEAD_DIM : (i + 1) * HEAD_DIM].astype(f32)
    sums = rest_ref[0].astype(f32)
    for h in range(1, HEADS):
        sums += rest_ref[h].astype(f32)
    lane = lax.broadcasted_iota(jnp.int32, (8, HEAD_DIM), 1)
    pair = jnp.where((lane == cut) | (lane == cut + 1), 1.0, 0.0)
    row = lax.dot_general(
        pair, sums, (((1,), (1,)), ((), ())), precision=exact, preferred_element_type=f32
    )
    block = rest_ref.shape[1]
    for i in range(norm_ref.shape[1] // block):

        @pl.when(pl.program_id(0) == i)
        def _(at=slice(i * block, (i + 1) * block)):
            norm_ref[:, at] = row[0:1] / gain_ref[:, at]

    spans = rest_ref.shape[0]

    @pl.when(pl.program_id(0) == 0)
    def _():
        for i in range(spans // 2):
            low, high = ring_position(i, spans), ring_position(spans // 2 + i, spans)
            rows = gain_rows_ref[jnp.where(side_ref[0] == 0, low, high)].astype(f32)
            norm2_ref[:, i * cut : (i + 1) * cut] = (rows[0:1] + rows[1:2])[:, :cut]

    for c in range(spans):
        piece = rest_ref[ring_position(c, spans), :, :cut].astype(f32)
        output_ref[:, c * cut : (c + 1) * cut] = piece


def ring_position(index, spans):
    if spans != 16:
        return index
    chip, core = index // 2, index % 2
    level, column = chip // 2, chip % 2
    return (level + column * (7 - 2 * level)) * 2 + core


def place_heads(side, got, gain, width):
    spans, _, packed = got.shape
    half = width // 2
    cut = width // spans
    block = half // 8
    part = pl.BlockSpec((block, width), lambda r: (r, 0))
    line = pl.BlockSpec((1, half), lambda r: (0, 0))
    return pl.pallas_call(
        functools.partial(place_heads_kernel, cut),
        grid=(8,),
        in_specs=[
            pl.BlockSpec(memory_space=pltpu.SMEM),
            pl.BlockSpec((HEADS, block, 3 * HEAD_DIM), lambda r: (0, r, 0)),
            pl.BlockSpec((spans, block, HEAD_DIM), lambda r: (0, r, 3)),
            pl.BlockSpec((spans, 16, HEAD_DIM), lambda r: (0, half // 16, 3)),
            line,
        ],
        out_specs=[part] * 4 + [line] * 2,
        out_shape=[jax.ShapeDtypeStruct((half, width), f32)] * 4
        + [jax.ShapeDtypeStruct((1, half), f32)] * 2,
        name="place_heads",
    )(side.reshape(1), got, got, got, gain.reshape(1, half))


def place_shared_kernel(side_ref, got_ref, in_ref, out_ref, rows_ref):
    spans = got_ref.shape[0]
    units = got_ref.shape[1] // 4
    half = got_ref.shape[2]
    hidden = spans * units

    for part in range(2):
        for c in range(spans):
            spot = ring_position(c, spans)
            piece = got_ref[spot, part * units : (part + 1) * units, :]
            rows_ref[c * units : (c + 1) * units, :] = piece.astype(f32)

        def turn(i, carry):
            window = pl.ds(pl.multiple_of(i * HEAD_DIM, HEAD_DIM), HEAD_DIM)
            at = pl.ds(pl.multiple_of(part * hidden + i * HEAD_DIM, HEAD_DIM), HEAD_DIM)
            in_ref[:, at] = rows_ref[window, :].T
            return carry

        lax.fori_loop(0, hidden // HEAD_DIM, turn, 0)
    first = side_ref[0] * (spans // 2)
    for c in range(spans // 2):
        spot = ring_position(first + c, spans)
        for part in range(2):
            piece = got_ref[spot, (2 + part) * units : (3 + part) * units, :]
            out_ref[c * units : (c + 1) * units, part * half : (part + 1) * half] = piece.astype(f32)


def place_shared(got, side):
    spans, quad, half = got.shape
    hidden = spans * quad // 4
    memory = pl.BlockSpec(memory_space=pltpu.VMEM)
    return pl.pallas_call(
        place_shared_kernel,
        in_specs=[pl.BlockSpec(memory_space=pltpu.SMEM), memory],
        out_specs=[memory, memory],
        out_shape=[
            jax.ShapeDtypeStruct((half, 2 * hidden), f32),
            jax.ShapeDtypeStruct((hidden // 2, 2 * half), f32),
        ],
        scratch_shapes=[pltpu.VMEM((hidden, half), f32)],
        name="place_shared",
    )(side.reshape(1), got)


def after(value, *others):
    return lax.optimization_barrier((value, *others))[0]


def tied(*values):
    return lax.optimization_barrier(values)


def one_hot_rows(lanes, *targets):
    row = lax.broadcasted_iota(jnp.int32, (8, lanes), 0)
    lane = lax.broadcasted_iota(jnp.int32, (8, lanes), 1)
    rows = jnp.zeros((8, lanes), f32)
    for i, target in enumerate(targets):
        rows = jnp.where((row == i) & (lane == target), 1.0, rows)
    return rows.astype(bf16)


def slot_keys(shape, axis, capacity):
    index = lax.broadcasted_iota(jnp.int32, shape, axis)
    return (index % capacity + 1024 * (index // capacity)).astype(f32)


def run_keys(shape, axis, tokens):
    return (1024 * (lax.broadcasted_iota(jnp.int32, shape, axis) // tokens)).astype(f32)


def group_runs(capacity):
    return min(8, 224 // capacity)


def pick_slots_kernel(capacity, tokens, here_ref, g_ref, out_ref):
    many = g_ref.shape[0]
    width = out_ref.shape[1]
    extras = g_ref[:, width:]
    rows = one_hot_rows(extras.shape[1], here_ref[0])
    slots = dot_nt(rows, extras)[0:1] + run_keys((1, many), 1, tokens)
    takes = slot_keys((out_ref.shape[0], 1), 0, capacity) == slots
    select = jnp.where(takes, 1.0, 0.0).astype(bf16)
    out_ref[...] = dot(select, g_ref[:, :width]).astype(bf16)


def pick_slots(here, g_wide, width, capacity, tokens):
    length, wide = g_wide.shape
    runs = group_runs(capacity)
    steps = length // (runs * tokens)
    return pl.pallas_call(
        functools.partial(pick_slots_kernel, capacity, tokens),
        grid=(steps,),
        in_specs=[
            pl.BlockSpec(memory_space=pltpu.SMEM),
            pl.BlockSpec((runs * tokens, wide), lambda i: (i, 0)),
        ],
        out_specs=pl.BlockSpec((runs * capacity, width), lambda i: (i, 0)),
        out_shape=jax.ShapeDtypeStruct((steps * runs * capacity, width), bf16),
        name="pick_slots",
        cost_estimate=pl.CostEstimate(
            flops=2 * length * runs * capacity * width,
            bytes_accessed=3 * length * wide,
            transcendentals=0,
        ),
    )(here.reshape(1), g_wide)


def sigmoid(value):
    return 1.0 / (1.0 + jnp.exp(-value))


def experts_kernel(
    capacity,
    tokens,
    experts,
    here_ref,
    normed_ref,
    g_ref,
    grad_slots_ref,
    own_in_ref,
    first_in_ref,
    middle_in_ref,
    last_in_ref,
    own_down_ref,
    other_down_ref,
    own_shared_in_ref,
    other_shared_in_ref,
    own_shared_out_ref,
    other_shared_out_ref,
    dispatched_ref,
    hidden_ref,
    grad_result_ref,
    grad_proj_ref,
    shared_hidden_ref,
    shared_grad_ref,
    parts_ref,
    gate_dot_ref,
    in_ref,
    down_ref,
    shared_in_ref,
    shared_out_ref,
    grad_dispatched_ref,
    scaled_ref,
):
    @pl.when(pl.program_id(0) == 0)
    def _():
        side = here_ref[1]
        rows = own_in_ref.shape[0]
        in_ref[pl.ds(pl.multiple_of(side * rows, 64), rows), :] = own_in_ref[...]
        at = (1 - side) * rows
        for ref in (first_in_ref, middle_in_ref, last_in_ref):
            in_ref[pl.ds(pl.multiple_of(at, 16), ref.shape[0]), :] = ref[...]
            at = at + ref.shape[0]
        rows = own_down_ref.shape[0]
        down_ref[pl.ds(pl.multiple_of(side * rows, 64), rows), :] = own_down_ref[...]
        down_ref[pl.ds(pl.multiple_of((1 - side) * rows, 64), rows), :] = other_down_ref[...]
        rows = own_shared_in_ref.shape[0]
        units = own_shared_out_ref.shape[0]
        shared_in_ref[...] = jnp.zeros_like(shared_in_ref)
        shared_out_ref[...] = jnp.zeros_like(shared_out_ref)
        for place, ref in ((side, own_shared_in_ref), (1 - side, other_shared_in_ref)):
            window = pl.ds(pl.multiple_of(place * rows, 64), rows)
            shared_in_ref[window, :units] = ref[:, :units]
            shared_in_ref[window, HEAD_DIM : HEAD_DIM + units] = ref[:, units:]
        shared_out_ref[:units, :] = jnp.where(
            here_ref[2] == side, own_shared_out_ref[...], other_shared_out_ref[...]
        )

    many, slots = normed_ref.shape[0], dispatched_ref.shape[0]
    width = dispatched_ref.shape[1]
    here = here_ref[0]
    spare = normed_ref.shape[1] - width
    gate_rows = dot_nt(one_hot_rows(spare, here, experts + here), normed_ref[:, width:])
    gate_row = gate_rows[0:1] + gate_rows[1:2]
    slot_pick = one_hot_rows(spare, here)
    group = group_runs(capacity)
    chunk, picks = group * tokens, group * capacity
    takes = []
    for at in range(0, many, chunk):
        extras = g_ref[at : at + chunk, width:]
        slot_row = dot_nt(slot_pick, extras)[0:1] + run_keys((1, chunk), 1, tokens)
        hit = slot_keys((picks, 1), 0, capacity) == slot_row
        takes.append(hit)
        select = jnp.where(hit, 1.0, 0.0).astype(bf16)
        at_slots = slice(at // tokens * capacity, (at // tokens + group) * capacity)
        dispatched_ref[at_slots, :] = dot(select, normed_ref[at : at + chunk, :width]).astype(bf16)
    slot_gate = jnp.concatenate(
        [
            jnp.sum(
                jnp.where(hit, gate_row[:, i * chunk : (i + 1) * chunk], 0.0), axis=1, keepdims=True
            )
            for i, hit in enumerate(takes)
        ],
        axis=0,
    )
    dispatched = dispatched_ref[...]
    grad_slots = grad_slots_ref[...].astype(f32)
    grad_result = (grad_slots * slot_gate).astype(bf16)
    grad_result_ref[...] = grad_result

    projected = dot(dispatched, in_ref[...])
    gate, up = projected[:, :EXP_HID], projected[:, EXP_HID:]
    chance = sigmoid(gate)
    silu = gate * chance
    hidden = (silu * up).astype(bf16)
    hidden_ref[...] = hidden
    grad_hidden = dot_nt(grad_result, down_ref[...])
    grad_proj_ref[:, :EXP_HID] = (
        grad_hidden * up * chance * (1.0 + gate * (1.0 - chance))
    ).astype(bf16)
    grad_proj_ref[:, EXP_HID:] = (grad_hidden * silu).astype(bf16)
    result = dot(hidden, down_ref[...]).astype(bf16).astype(f32)
    slot_dot = jnp.sum(grad_slots * result, axis=1, keepdims=True)
    for i, hit in enumerate(takes):
        dots = slot_dot[i * picks : (i + 1) * picks]
        gate_dot = jnp.sum(jnp.where(hit, dots, 0.0), axis=0, keepdims=True)
        gate_dot_ref[:, i * chunk : (i + 1) * chunk] = jnp.broadcast_to(gate_dot, (8, chunk))
    scaled = (result * slot_gate).astype(bf16)
    grad_dispatched = dot_nt(grad_proj_ref[...], in_ref[...]).astype(bf16)

    grad_dispatched_ref[...] = grad_dispatched
    scaled_ref[...] = scaled
    lanes = shared_out_ref.shape[0]
    size = min(4 * HEAD_DIM, chunk)

    def visit(i, carry):
        at = pl.ds(pl.multiple_of(i * size, size), size)
        which = i * size // chunk
        filled = pl.ds(pl.multiple_of(which * picks, 16), picks)
        shared = dot(normed_ref[at, :width], shared_in_ref[...])
        shared_gate, shared_up = shared[:, :lanes], shared[:, lanes:]
        shared_chance = sigmoid(shared_gate)
        shared_silu = shared_gate * shared_chance
        shared_hidden = (shared_silu * shared_up).astype(bf16)
        shared_hidden_ref[at, :] = shared_hidden
        grad_shared = dot_nt(g_ref[at, :width], shared_out_ref[...])
        slope = shared_chance * (1.0 + shared_gate * (1.0 - shared_chance))
        shared_grad = jnp.concatenate(
            [(grad_shared * shared_up * slope).astype(bf16), (grad_shared * shared_silu).astype(bf16)],
            axis=1,
        )
        shared_grad_ref[at, :] = shared_grad
        slot_column = dot_nt(g_ref[at, width:], slot_pick)[:, 0:1]
        run = (i * size - which * chunk + lax.broadcasted_iota(jnp.int32, (size, 1), 0)) // tokens
        key = slot_column + (1024 * run).astype(f32)
        back = jnp.where(key == slot_keys((1, picks), 1, capacity), 1.0, 0.0).astype(bf16)
        parts_ref[at, :width] = (
            dot(back, grad_dispatched_ref[filled, :]) + dot_nt(shared_grad, shared_in_ref[...])
        ).astype(bf16)
        parts_ref[at, width:] = (
            dot(back, scaled_ref[filled, :]) + dot(shared_hidden, shared_out_ref[...])
        ).astype(bf16)
        return carry

    lax.fori_loop(0, many // size, visit, 0)


def run_experts(
    places, normed_wide, g_wide, grad_slots, weights, tokens, capacity
):
    length, wide = normed_wide.shape
    width = grad_slots.shape[1]
    experts = length // tokens
    runs = group_runs(capacity)
    steps = length // (runs * tokens)
    many, slots = runs * tokens, runs * capacity
    lanes = HEAD_DIM

    def block(rows, columns):
        return pl.BlockSpec((rows, columns), lambda i: (i, 0))

    def fixed(value):
        return pl.BlockSpec(value.shape, lambda i: (0, 0), pipeline_mode=pl.Buffered(1))

    def shape(rows, columns, kind=bf16):
        return jax.ShapeDtypeStruct((rows, columns), kind)

    return pl.pallas_call(
        functools.partial(experts_kernel, capacity, tokens, experts),
        grid=(steps,),
        in_specs=[
            pl.BlockSpec(memory_space=pltpu.SMEM),
            block(many, wide),
            block(many, wide),
            block(slots, width),
            *[fixed(weight) for weight in weights],
        ],
        out_specs=[
            block(slots, width),
            block(slots, EXP_HID),
            block(slots, width),
            block(slots, 2 * EXP_HID),
            block(many, lanes),
            block(many, 2 * lanes),
            block(many, 2 * width),
            pl.BlockSpec((8, many), lambda i: (0, i)),
        ],
        out_shape=[
            shape(steps * slots, width),
            shape(steps * slots, EXP_HID),
            shape(steps * slots, width),
            shape(steps * slots, 2 * EXP_HID),
            shape(length, lanes),
            shape(length, 2 * lanes),
            shape(length, 2 * width),
            shape(8, length, f32),
        ],
        scratch_shapes=[
            pltpu.VMEM((width, 2 * EXP_HID), bf16),
            pltpu.VMEM((EXP_HID, width), bf16),
            pltpu.VMEM((width, 2 * lanes), bf16),
            pltpu.VMEM((lanes, width), bf16),
            pltpu.VMEM((slots, width), bf16),
            pltpu.VMEM((slots, width), bf16),
        ],
        name="experts",
        cost_estimate=pl.CostEstimate(
            flops=20 * 10**9, bytes_accessed=40 * 10**6, transcendentals=2 * 10**6
        ),
    )(
        places,
        normed_wide,
        g_wide,
        grad_slots,
        *weights,
    )


def slot_grads_kernel(side_ref, left_ref, right_ref, own_ref, other_ref, turned_ref):
    @pl.when(pl.program_id(0) == 0)
    def _():
        turned_ref[...] = left_ref[...].T

    rows = own_ref.shape[0]
    size = rows // 5 if rows % 80 == 0 else rows // 4
    side = side_ref[0]

    def visit(i, carry):
        def part(place):
            at = pl.ds(pl.multiple_of(place * rows + i * size, 16), size)
            return dot(turned_ref[at, :], right_ref[...])

        at = pl.ds(pl.multiple_of(i * size, 16), size)
        own_ref[at, :] = part(side)
        other_ref[at, :] = part(1 - side).astype(bf16)
        return carry

    lax.fori_loop(0, rows // size, visit, 0)


def slot_grads(side, left, right):
    slots, tall = left.shape
    wide = right.shape[1]
    block = pl.BlockSpec((tall // 2, 2 * HEAD_DIM), lambda i: (0, i))
    return pl.pallas_call(
        slot_grads_kernel,
        grid=(wide // (2 * HEAD_DIM),),
        in_specs=[
            pl.BlockSpec(memory_space=pltpu.SMEM),
            pl.BlockSpec((slots, tall), lambda i: (0, 0), pipeline_mode=pl.Buffered(1)),
            pl.BlockSpec((slots, 2 * HEAD_DIM), lambda i: (0, i)),
        ],
        out_specs=[block, block],
        out_shape=[
            jax.ShapeDtypeStruct((tall // 2, wide), f32),
            jax.ShapeDtypeStruct((tall // 2, wide), bf16),
        ],
        scratch_shapes=[pltpu.VMEM((tall, slots), bf16)],
        name="slot_grads",
        cost_estimate=pl.CostEstimate(
            flops=2 * slots * tall * wide,
            bytes_accessed=2 * slots * (tall + wide) + 3 * tall * wide,
            transcendentals=0,
        ),
    )(side.reshape(1), left, right)


def shared_grads_kernel(grad_ref, normed_ref, hidden_ref, g_ref, in_ref, out_ref):
    @pl.when(pl.program_id(0) == 0)
    def _():
        in_ref[...] = jnp.zeros_like(in_ref)
        out_ref[...] = jnp.zeros_like(out_ref)

    in_ref[...] += dot_tn(grad_ref[...], normed_ref[...])
    out_ref[...] += dot_tn(hidden_ref[...], g_ref[...])


def shared_products(grad, normed_wide, hidden, g_wide, width):
    length, lanes = hidden.shape
    tile = 4 * HEAD_DIM

    def block(columns):
        return pl.BlockSpec((tile, columns), lambda i: (i, 0))

    def whole(rows):
        return pl.BlockSpec((rows, width), lambda i: (0, 0))

    return pl.pallas_call(
        shared_grads_kernel,
        grid=(length // tile,),
        in_specs=[block(2 * lanes), block(width), block(lanes), block(width)],
        out_specs=[whole(2 * lanes), whole(lanes)],
        out_shape=[
            jax.ShapeDtypeStruct((2 * lanes, width), f32),
            jax.ShapeDtypeStruct((lanes, width), f32),
        ],
        name="shared_products",
        cost_estimate=pl.CostEstimate(
            flops=6 * length * lanes * width, bytes_accessed=6 * length * width, transcendentals=0
        ),
    )(grad, normed_wide, hidden, g_wide)


def turned_product_kernel(side_ref, left_ref, right_ref, out_ref, sum_ref):
    step = pl.program_id(0)

    @pl.when(step == 0)
    def _():
        sum_ref[...] = jnp.zeros_like(sum_ref)

    sum_ref[...] += dot_tn(right_ref[...], left_ref[...])

    @pl.when(step == pl.num_programs(0) - 1)
    def _():
        count = out_ref.shape[0] // HEAD_DIM
        near = count // 2

        def turn(i, carry):
            window = pl.ds(pl.multiple_of(i * HEAD_DIM, HEAD_DIM), HEAD_DIM)
            place = jnp.where(i // near == side_ref[0], 0, near) + i % near
            at = pl.ds(pl.multiple_of(place * HEAD_DIM, HEAD_DIM), HEAD_DIM)
            out_ref[at, :] = sum_ref[:, window].T
            return carry

        lax.fori_loop(0, count, turn, 0)


def turned_product(side, left, right, wide):
    length, lanes = right.shape
    tile = 4 * HEAD_DIM
    return pl.pallas_call(
        turned_product_kernel,
        grid=(length // tile,),
        in_specs=[
            pl.BlockSpec(memory_space=pltpu.SMEM),
            pl.BlockSpec((tile, wide), lambda i: (i, 0)),
            pl.BlockSpec((tile, lanes), lambda i: (i, 0)),
        ],
        out_specs=pl.BlockSpec((wide, lanes), lambda i: (0, 0)),
        out_shape=jax.ShapeDtypeStruct((wide, lanes), f32),
        scratch_shapes=[pltpu.VMEM((lanes, wide), f32)],
        name="turned_product",
        cost_estimate=pl.CostEstimate(
            flops=2 * length * lanes * wide,
            bytes_accessed=2 * length * wide,
            transcendentals=0,
        ),
    )(side.reshape(1), left, right)


def slot_table(span_picks, span_order, experts):
    tokens = span_picks.shape[0]
    order = span_order.reshape(tokens, TOP)
    onehot = span_picks[:, :, None] == jnp.arange(experts, dtype=jnp.int32)
    picked = jnp.any(onehot, axis=1)
    rank_key = jnp.sum(jnp.where(onehot, order[:, :, None], 0), axis=1)
    rank_key = jnp.where(picked, rank_key, tokens * TOP)
    before = rank_key[:, None, :] < rank_key[None, :, :]
    slots = jnp.sum(before.astype(jnp.int32), axis=0)
    return jnp.where(picked, slots, 2 * tokens)


def on_device(
    inputs,
    norm1_gain,
    w_query,
    w_key,
    w_value,
    w_output,
    norm2_gain,
    router,
    shared_gate_up_weight,
    shared_down_weight,
    expert_in,
    expert_out,
    picks,
    fill_order,
    grad_out,
):
    spans = lax.axis_size("ctx")
    here = lax.axis_index("ctx")
    side = lax.axis_index("fsdp")
    core = here % 2
    tokens, width = inputs.shape[1:]
    half = width // 2
    length = spans * tokens
    experts = spans * expert_in.shape[0]
    capacity = tokens * TOP // experts
    head = jnp.minimum(ring_position(here, spans), HEADS - 1)
    units = EXP_HID // spans
    ring = ring_of(spans)
    is_ring = spans == 16
    groups = [ring] if is_ring else None
    swap_core = [(i, i ^ 1) for i in range(spans)]

    def across(value):
        return lax.ppermute(value, "fsdp", [(0, 1), (1, 0)])

    def ordered(own, other, axis):
        return jnp.where(
            side == 0,
            jnp.concatenate([own, other], axis=axis),
            jnp.concatenate([other, own], axis=axis),
        )

    def everyone(value):
        return lax.all_gather(value, "ctx", axis=0, tiled=True, axis_index_groups=groups)

    def columns(value, start, count):
        return lax.dynamic_slice_in_dim(value, start, count, 1)

    def rows(value, start, count):
        return lax.dynamic_slice_in_dim(value, start, count, 0)

    def halves(value, axis=0):
        size = value.shape[axis] // 2
        mine = lax.dynamic_slice_in_dim(value, side * size, size, axis)
        theirs = lax.dynamic_slice_in_dim(value, (1 - side) * size, size, axis)
        return mine, theirs

    def reduced(value, axis=0):
        mine, theirs = halves(value, axis)
        return mine + across(theirs.astype(bf16)).astype(f32)

    def swapped(value):
        return lax.all_to_all(value, "ctx", split_axis=0, concat_axis=0, tiled=True)

    def row_major(value):
        return with_layout_constraint(value, Layout(tuple(range(value.ndim))))

    x = inputs[0]
    g = grad_out[0]
    x_all = everyone(x)
    spare = -(-2 * experts // HEAD_DIM) * HEAD_DIM
    own_table = slot_table(picks[0], fill_order[0, 0], experts)
    own_table = jnp.pad(
        own_table.astype(f32), ((0, 0), (0, spare - experts)), constant_values=2.0 * tokens
    )
    g_wide = jnp.concatenate([g, own_table.astype(bf16)], axis=1)
    head_own = jnp.concatenate(
        [columns(w, head * HEAD_DIM, HEAD_DIM) for w in (w_query, w_key, w_value)], axis=1
    )
    head_other = across(head_own)
    small = jnp.concatenate([router.T, norm1_gain[None], norm2_gain[None]], axis=0)
    small_other = across(small)
    output_near = across(columns(w_output, core * half, half))
    lanes = HEAD_DIM
    shared_in_own = jnp.concatenate(
        [columns(shared_gate_up_weight, at + here * units, units) for at in (0, EXP_HID)], axis=1
    )
    shared_rows = shared_down_weight.shape[0]
    shared_out_own = rows(shared_down_weight, here * units % shared_rows, units)
    cosine, sine = rotary_tables(jnp.asarray(ring, jnp.int32) * tokens, tokens, HEAD_DIM)
    small = ordered(small, small_other, 1)
    router_w = small[:experts]
    gain_one = small[experts : experts + 1].astype(f32)
    gain_two = small[experts + 1 :].astype(f32)
    quarter = half // 4
    chunks = [expert_in[0, :quarter], expert_in[0, quarter:-quarter], expert_in[0, -quarter:]]
    head_other, *chunks = tied(head_other, *chunks)
    chunks = [across(chunk) for chunk in chunks]
    x_all, cosine, sine, head_other, gain_one, output_near = tied(
        x_all, cosine, sine, head_other, gain_one, output_near
    )
    output_far = lax.ppermute(output_near, "ctx", swap_core)
    g_wide_all = everyone(after(g_wide, x_all))
    g_all = g_wide_all[:, :width]
    table = g_wide_all[:, width : width + experts]

    normed1_all, query, key, value = project(
        side, x_all, gain_one, head_own, head_other, cosine, sine
    )
    context, lse, attended = attend(query, key, value, is_ring)
    attended, output_far, chunks[0] = tied(attended, output_far, chunks[0])
    down_other = across(after(expert_out[0], attended))
    got = swapped(attended.reshape(spans, tokens, HEAD_DIM))
    got, chunks[1] = tied(got, chunks[1])
    spot = jnp.stack([side, core]).astype(jnp.int32)
    router_pad = jnp.pad(router_w, ((0, spare - experts), (0, 0)))
    second, normed2_wide, scale_two, own_gates, attended = mix(
        spot,
        got,
        w_output,
        output_near,
        output_far,
        x,
        gain_two,
        router_pad,
        own_table,
        experts,
    )
    normed2_wide, g_wide_all, chunks[2] = tied(normed2_wide, g_wide_all, chunks[2])
    normed2_wide = everyone(normed2_wide)
    grad_slots = pick_slots(here, g_wide_all, width, capacity, tokens)
    shared_in_other = across(after(shared_in_own, grad_slots))
    shared_out_other = across(after(shared_out_own, grad_slots))
    normed2_wide, grad_slots, down_other, shared_in_other, shared_out_other = tied(
        normed2_wide, grad_slots, down_other, shared_in_other, shared_out_other
    )
    normed2_all = normed2_wide[:, :width]
    attended_all = everyone(after(attended, normed2_wide))
    dense = [
        columns(after(w, grad_slots), core * half, half) for w in (w_query, w_key, w_value)
    ]
    near = [across(dense[0]), across(jnp.concatenate(dense[1:], axis=0))]
    spots = [ring_position(i, spans) for i in range(spans)]
    (
        dispatched,
        expert_hidden,
        grad_result,
        grad_proj,
        shared_hidden,
        grad_sproj,
        parts,
        gate_dot,
    ) = run_experts(
        jnp.stack([here, side, here * units // shared_rows]).astype(jnp.int32),
        normed2_wide,
        g_wide_all,
        grad_slots,
        (
            expert_in[0],
            *chunks,
            expert_out[0],
            down_other,
            shared_in_own,
            shared_in_other,
            shared_out_own,
            shared_out_other,
        ),
        tokens,
        capacity,
    )
    parts, near[0], attended_all = tied(parts, near[0], attended_all)
    sums = lax.psum_scatter(
        parts, "ctx", scatter_dimension=0, tiled=True, axis_index_groups=groups
    )
    gate_dot = gate_dot[0].reshape(spans, tokens)
    grad_shared_in, grad_shared_out = shared_products(
        grad_sproj, normed2_wide, shared_hidden, g_wide_all, width
    )
    grad_shared_in = jnp.concatenate(
        [grad_shared_in[:units], grad_shared_in[lanes : lanes + units]], axis=0
    )
    grad_shared_in = reduced(grad_shared_in, 1).astype(bf16)
    grad_shared_out = grad_shared_out[:units].astype(bf16)
    grad_shared_out = grad_shared_out.astype(f32) + across(grad_shared_out).astype(f32)
    grad_shared_out = grad_shared_out.astype(bf16)
    shared_grads = jnp.concatenate(
        [grad_shared_in, grad_shared_out[:, :half], grad_shared_out[:, half:]], axis=0
    )
    gate_dot = jnp.concatenate([gate_dot[i : i + 1] for i in spots], axis=0)
    gate_grads = swapped(after(gate_dot, parts)[:, None, :])[:, 0, :].T

    own_down, down_theirs = slot_grads(side, expert_hidden, grad_result)
    own_in, in_theirs = slot_grads(side, dispatched, grad_proj)
    down_theirs = across(after(down_theirs, parts))
    cuts_at = [0, half // 4, half * 9 // 16, half]
    sums, in_theirs, shared_grads, gate_grads = tied(
        sums,
        in_theirs,
        row_major(shared_grads),
        gate_grads,
    )
    split = half * 5 // 16
    in_parts = [in_theirs[a:b] for a, b in zip(cuts_at, cuts_at[1:])]
    in_parts[0], in_parts[1] = across(in_parts[0]), across(in_parts[1])

    sent, cuts, grad_second, layer_out = mix_back(
        spot,
        sums,
        own_gates,
        jnp.pad(gate_grads, ((0, 0), (0, spare - experts))),
        router_pad,
        second,
        scale_two,
        gain_two,
        g,
        w_output,
        output_near,
        output_far,
        spans,
    )
    arrived = swapped(sent).reshape(length, HEAD_DIM)
    arrived, shared_grads, cuts, near[1], down_theirs, in_parts[0] = tied(
        arrived, shared_grads, cuts, near[1], down_theirs, in_parts[0]
    )
    cuts = lax.all_to_all(
        cuts, "ctx", split_axis=0, concat_axis=0, tiled=True, axis_index_groups=groups
    )
    extras = cuts[:, :tokens].reshape(length, HEAD_DIM)
    shared_grads = everyone(shared_grads[None])
    grad_heads, grad_heads_ring = attend_back(
        query, key, value, arrived, context, lse, cosine, sine, is_ring
    )
    grad_heads, grad_heads_ring, in_parts[1] = tied(grad_heads, grad_heads_ring, in_parts[1])
    cut = width // spans
    gain_rows = cuts[:, tokens : tokens + 2, :cut].astype(f32)
    gain_rows = jnp.sum(gain_rows, axis=(0, 1))
    gain_rows = jnp.pad(gain_rows.reshape(1, cut), ((0, 15), (0, HEAD_DIM - cut)))
    grad_router = turned_product(side, normed2_wide, extras, width)[:, cut : cut + experts]
    grad_router = grad_router[:half] + across(grad_router[half:])
    products = turned_product(side, attended_all, extras, width)
    mine, theirs = products[:half], products[half:]
    gain_high = gain_rows.astype(bf16)
    gain_low = jnp.roll((gain_rows - gain_high.astype(f32)).astype(bf16), 1, axis=0)
    theirs = jnp.concatenate([theirs.astype(bf16), gain_high + gain_low], axis=0)
    grad_heads_ring, theirs = tied(grad_heads_ring, theirs)
    head_mine, head_theirs = halves(dot_tn(normed1_all, grad_heads_ring))
    head_theirs = head_theirs.astype(bf16)
    theirs = across(theirs).astype(f32)
    grad_output = mine + theirs[:half]
    gain_rows = gain_rows[:1] + theirs[half : half + 1] + theirs[half + 1 : half + 2]
    gain_high = gain_rows.astype(bf16)
    gain_low = (gain_rows - gain_high.astype(f32)).astype(bf16)
    gain_rows = jnp.pad(
        jnp.concatenate([gain_high, gain_low], axis=0), ((0, 14), (3 * HEAD_DIM, 0))
    )
    got = swapped(grad_heads.reshape(spans, tokens, 3 * HEAD_DIM))
    grad_head_w = (head_mine + across(head_theirs).astype(f32)).astype(bf16)
    part = jnp.sum(grad_head_w.astype(f32) * head_own.astype(f32), axis=1, keepdims=True)
    part_high = part.astype(bf16).astype(f32)
    lane = lax.broadcasted_iota(jnp.int32, (half, HEAD_DIM), 1)
    grad_output = jnp.where(lane < cut, grad_output, 0.0)
    grad_output = jnp.where(lane == cut, part_high, grad_output)
    grad_output = jnp.where(lane == cut + 1, part - part_high, grad_output)
    head_grads = jnp.concatenate([grad_head_w, grad_output.astype(bf16)], axis=1)
    head_grads = jnp.concatenate([head_grads, gain_rows], axis=0)
    head_pack = head_grads
    head_grads, got = tied(row_major(head_grads), got)
    head_grads = everyone(head_grads[None])
    in_parts[2] = across(after(in_parts[2], head_pack))
    far = [lax.ppermute(part, "ctx", swap_core) for part in near]

    grad_inputs = inputs_back(
        side, core, got, w_query, w_key, w_value, *near, *far, x, gain_one, grad_second
    )
    grad_query, grad_key, grad_value, grad_output, grad_norm1, grad_norm2 = place_heads(
        side, head_grads, norm1_gain.astype(f32), width
    )
    grad_expert_in = jnp.concatenate(
        [
            own_in[a:b] + part.astype(f32)
            for a, b, part in zip(cuts_at, cuts_at[1:], in_parts)
        ],
        axis=0,
    )
    grad_shared_in, grad_shared_out = place_shared(shared_grads, side)
    return (
        layer_out[None],
        grad_inputs[None],
        grad_norm1.reshape(half),
        grad_query,
        grad_key,
        grad_value,
        grad_output,
        grad_norm2.reshape(half),
        grad_router,
        grad_shared_in,
        grad_shared_out,
        grad_expert_in[None],
        (own_down + down_theirs.astype(f32))[None],
    )


def solution(mesh):
    placed = (
        P("fsdp", "ctx", None),
        P("fsdp"),
        P("fsdp", None),
        P("fsdp", None),
        P("fsdp", None),
        P("fsdp", None),
        P("fsdp"),
        P("fsdp", None),
        P("fsdp", None),
        P("fsdp", None),
        P("ctx", "fsdp", None),
        P("ctx", "fsdp", None),
        P("fsdp", "ctx", None),
        P("fsdp", "ctx", None),
        P("fsdp", "ctx", None),
    )
    return jax.shard_map(
        on_device,
        mesh=mesh,
        in_specs=placed,
        out_specs=(
            P("fsdp", "ctx", None),
            P("fsdp", "ctx", None),
            P("fsdp"),
            P("fsdp", None),
            P("fsdp", None),
            P("fsdp", None),
            P("fsdp", None),
            P("fsdp"),
            P("fsdp", None),
            P("fsdp", None),
            P("fsdp", None),
            P("ctx", "fsdp", None),
            P("ctx", "fsdp", None),
        ),
        check_vma=False,
    )
```

```python
import functools
import math

import jax
import jax.numpy as jnp
from jax import lax
from jax.experimental import pallas as pl
from jax.experimental.layout import Layout, with_layout_constraint
from jax.experimental.pallas import tpu as pltpu
from jax.sharding import PartitionSpec as P

HEADS = 10
HEAD_DIM = 128
EXP_HID = 896
TOP = 7
BLOCK = 256
TILE = 512

epsilon = 1e-06
masked_score = -1000000000.0
score_scale = 1.0 / math.sqrt(HEAD_DIM)
exact = lax.Precision.HIGHEST
f32 = jnp.float32
bf16 = jnp.bfloat16


def dot(a, b):
    return jnp.dot(a, b, preferred_element_type=f32)


def dot_nt(a, b):
    return lax.dot_general(a, b, (((1,), (1,)), ((), ())), preferred_element_type=f32)


def dot_tn(a, b):
    return lax.dot_general(a, b, (((0,), (0,)), ((), ())), preferred_element_type=f32)


def rms_scale(values):
    return lax.rsqrt(jnp.mean(values * values, axis=-1, keepdims=True) + epsilon)


def rotary_tables(starts, count, width):
    half = width // 2
    freqs = jnp.exp(-math.log(10000.0) * jnp.arange(half, dtype=f32) * 2.0 / width)
    freqs = jnp.concatenate([freqs, freqs])
    first = starts.astype(f32)[:, None] * freqs[None, :]
    second = jnp.arange(count, dtype=f32)[:, None] * freqs[None, :]
    angles = jnp.concatenate([first, second], axis=0)
    sign = jnp.where(jnp.arange(width) < half, -1.0, 1.0)
    cosine, sine = lax.optimization_barrier((jnp.cos(angles), jnp.sin(angles) * sign))
    spans = starts.shape[0]
    cos_a, sin_a = cosine[:spans, None], sine[:spans, None]
    cos_b, sin_b = cosine[None, spans:], sine[None, spans:]
    shape = (spans * count, width)
    return (
        (cos_a * cos_b - sin_a * sin_b).reshape(shape),
        (sin_a * cos_b + cos_a * sin_b).reshape(shape),
    )


def allowed_tile(rows, columns):
    key_block = lax.broadcasted_iota(jnp.int32, (rows, columns), 0) // BLOCK
    query_block = lax.broadcasted_iota(jnp.int32, (rows, columns), 1) // BLOCK
    return key_block <= query_block


def ring_of(spans):
    if spans != 16:
        return list(range(spans))
    chips = [0, 2, 4, 6, 7, 5, 3, 1]
    return [2 * chip + core for chip in chips for core in (0, 1)]


def pieces(j, tile, length, ring):
    if ring:
        starts = (j * BLOCK, length - BLOCK - j * BLOCK)
        return [pl.ds(pl.multiple_of(at, BLOCK), BLOCK) for at in starts]
    return [pl.ds(pl.multiple_of(j * tile, tile), tile)]


def load(ref, windows, columns=slice(None)):
    parts = [ref[window, columns] for window in windows]
    return parts[0] if len(parts) == 1 else jnp.concatenate(parts, axis=0)


def store(ref, windows, value, columns=slice(None)):
    size = value.shape[0] // len(windows)
    for i, window in enumerate(windows):
        ref[window, columns] = value[i * size : (i + 1) * size]


def attend_kernel(
    ring, q_ref, k_ref, v_ref, context_ref, lse_ref, low_ref, score_ref
):
    length = k_ref.shape[0]
    tile = context_ref.shape[0]
    here = pl.program_id(0)
    queries = load(q_ref, pieces(here, tile, length, ring))

    def raw_scores(j):
        return dot_nt(load(k_ref, pieces(j, tile, length, ring)), queries) * score_scale

    def fold(j, scores, peak):
        score_ref[pl.ds(pl.multiple_of(j * tile, tile), tile), :] = scores
        return jnp.maximum(peak, jnp.max(scores.reshape(tile // 8, 8, tile), axis=0))

    diagonal = jnp.where(allowed_tile(tile, tile), raw_scores(here), masked_score)
    peak = fold(here, diagonal, jnp.full((8, tile), masked_score, f32))
    peak = lax.fori_loop(0, here, lambda j, p: fold(j, raw_scores(j), p), peak)
    top = jnp.max(peak, axis=0, keepdims=True)

    def gather(j, carry):
        total, numer = carry
        weights = jnp.exp(score_ref[pl.ds(pl.multiple_of(j * tile, tile), tile), :] - top)
        total = total + jnp.sum(weights.reshape(tile // 8, 8, tile), axis=0)
        values = load(v_ref, pieces(j, tile, length, ring))
        return total, numer + dot_tn(values, weights.astype(bf16))

    zero = (jnp.zeros((8, tile), f32), jnp.zeros((HEAD_DIM, tile), f32))
    total, numer = lax.fori_loop(0, here + 1, gather, zero)
    total = jnp.sum(total, axis=0, keepdims=True)
    context = (numer / total).T
    context_ref[...] = context
    low_ref[...] = context.astype(bf16)
    lse_ref[...] = top + jnp.log(total)


def attend(query, key, value, ring):
    length = query.shape[0]
    tile = min(TILE, length)
    whole = pl.BlockSpec((length, HEAD_DIM), lambda i: (0, 0))
    part = pl.BlockSpec((tile, HEAD_DIM), lambda i: (i, 0))
    return pl.pallas_call(
        functools.partial(attend_kernel, ring),
        grid=(length // tile,),
        in_specs=[whole] * 3,
        out_specs=[part, pl.BlockSpec((1, tile), lambda i: (0, i)), part],
        out_shape=[
            jax.ShapeDtypeStruct((length, HEAD_DIM), f32),
            jax.ShapeDtypeStruct((1, length), f32),
            jax.ShapeDtypeStruct((length, HEAD_DIM), bf16),
        ],
        scratch_shapes=[pltpu.VMEM((length, tile), f32)],
        name="attend",
        cost_estimate=pl.CostEstimate(
            flops=2 * length * length * HEAD_DIM,
            bytes_accessed=12 * length * HEAD_DIM,
            transcendentals=length * length // 2,
        ),
    )(query, key, value)


def attend_back_kernel(
    ring,
    q_ref,
    k_ref,
    v_ref,
    grad_ref,
    context_ref,
    lse_ref,
    cos_ref,
    sin_ref,
    out_ref,
    out_ring_ref,
    dq_ref,
    delta_ref,
    dk_ref,
    dv_ref,
):
    length = q_ref.shape[0]
    tile = dk_ref.shape[0]
    steps = length // tile
    here = pl.program_id(0)

    def natural(i):
        return pl.ds(pl.multiple_of(i * tile, tile), tile)

    @pl.when(here == 0)
    def _():
        def prepare(i, carry):
            window = natural(i)
            dq_ref[window, :] = jnp.zeros((tile, HEAD_DIM), f32)
            product = grad_ref[window, :].astype(f32) * context_ref[window, :]
            ones = jnp.ones((8, HEAD_DIM), f32)
            delta = lax.dot_general(
                ones, product, (((1,), (1,)), ((), ())), precision=exact, preferred_element_type=f32
            )
            delta_ref[:, window] = delta
            return carry

        lax.fori_loop(0, steps, prepare, 0)

    keys = load(k_ref, pieces(here, tile, length, ring))
    values = load(v_ref, pieces(here, tile, length, ring))

    dk_ref[...] = jnp.zeros_like(dk_ref)
    dv_ref[...] = jnp.zeros_like(dv_ref)

    def visit(i, carry):
        window = natural(i)
        queries = load(q_ref, pieces(i, tile, length, ring))
        grads = grad_ref[window, :]
        weights = jnp.exp(dot_nt(keys, queries) * score_scale - lse_ref[:, window])
        later = jnp.where(i > here, weights[BLOCK:, :BLOCK], 0.0)
        later = jnp.concatenate([later, weights[BLOCK:, BLOCK:]], axis=1)
        weights = jnp.concatenate([weights[:BLOCK], later], axis=0)
        grad_weights = dot_nt(values, grads)
        grad_raw = (weights * (grad_weights - delta_ref[0:1, window]) * score_scale).astype(bf16)
        dq_ref[window, :] += dot_tn(grad_raw, keys)
        dk_ref[...] += dot(grad_raw, queries)
        dv_ref[...] += dot(weights.astype(bf16), grads)
        return carry

    lax.fori_loop(here, steps, visit, 0)

    def write(i, part, value):
        at = slice(part * HEAD_DIM, (part + 1) * HEAD_DIM)
        out_ref[natural(i), at] = value
        store(out_ring_ref, pieces(i, tile, length, ring), value, at)

    def turned_back(i, value):
        windows = pieces(i, tile, length, ring)
        scaled = pltpu.roll(value * load(sin_ref, windows), HEAD_DIM // 2, 1)
        return (value * load(cos_ref, windows) + scaled).astype(bf16)

    write(here, 1, turned_back(here, dk_ref[...]))
    write(here, 2, dv_ref[...].astype(bf16))

    @pl.when(here == steps - 1)
    def _():
        def finish(i, carry):
            write(i, 0, turned_back(i, dq_ref[natural(i), :]))
            return carry

        lax.fori_loop(0, steps, finish, 0)


def attend_back(query, key, value, grad, context, lse, cosine, sine, ring):
    length = query.shape[0]
    tile = min(TILE, length)
    memory = pl.BlockSpec(memory_space=pltpu.VMEM)
    return pl.pallas_call(
        functools.partial(attend_back_kernel, ring),
        grid=(length // tile,),
        in_specs=[memory] * 8,
        out_specs=[memory] * 2,
        out_shape=[jax.ShapeDtypeStruct((length, 3 * HEAD_DIM), bf16)] * 2,
        scratch_shapes=[
            pltpu.VMEM((length, HEAD_DIM), f32),
            pltpu.VMEM((8, length), f32),
            pltpu.VMEM((tile, HEAD_DIM), f32),
            pltpu.VMEM((tile, HEAD_DIM), f32),
        ],
        name="attend_back",
        cost_estimate=pl.CostEstimate(
            flops=5 * length * length * HEAD_DIM,
            bytes_accessed=20 * length * HEAD_DIM,
            transcendentals=length * length // 2,
        ),
    )(query, key, value, grad, context, lse, cosine, sine)


def project_kernel(
    side_ref, x_ref, gain_ref, own_ref, other_ref, cos_ref, sin_ref, normed_ref, q_ref, k_ref, v_ref
):
    own, other = own_ref[...], other_ref[...]
    weight = jnp.where(
        side_ref[0] == 0,
        jnp.concatenate([own, other], axis=0),
        jnp.concatenate([other, own], axis=0),
    )
    resid = x_ref[...].astype(f32)
    normed = (resid * rms_scale(resid) * gain_ref[...]).astype(bf16)
    normed_ref[...] = normed
    projected = dot(normed, weight)
    for out, at in ((q_ref, 0), (k_ref, HEAD_DIM)):
        part = projected[:, at : at + HEAD_DIM]
        turned = pltpu.roll(part, HEAD_DIM // 2, 1)
        out[...] = (part * cos_ref[...] + turned * sin_ref[...]).astype(bf16)
    v_ref[...] = projected[:, 2 * HEAD_DIM :].astype(bf16)


def project(side, x, gain, own, other, cosine, sine):
    length, width = x.shape
    tile = min(TILE, length)
    part = pl.BlockSpec((tile, HEAD_DIM), lambda i: (i, 0))
    wide = pl.BlockSpec((tile, width), lambda i: (i, 0))
    return pl.pallas_call(
        project_kernel,
        grid=(length // tile,),
        in_specs=[
            pl.BlockSpec(memory_space=pltpu.SMEM),
            wide,
            pl.BlockSpec((1, width), lambda i: (0, 0)),
            pl.BlockSpec(own.shape, lambda i: (0, 0)),
            pl.BlockSpec(own.shape, lambda i: (0, 0)),
            part,
            part,
        ],
        out_specs=[wide, part, part, part],
        out_shape=[jax.ShapeDtypeStruct((length, width), bf16)]
        + [jax.ShapeDtypeStruct((length, HEAD_DIM), bf16)] * 3,
        name="project",
        cost_estimate=pl.CostEstimate(
            flops=6 * length * width * HEAD_DIM,
            bytes_accessed=4 * length * width,
            transcendentals=0,
        ),
    )(side.reshape(1), x, gain, own, other, cosine, sine)


def home(head, spans):
    if spans != 16:
        return head
    chip, core = head // 2, head % 2
    return 2 * jnp.where(chip < 4, 2 * chip, 15 - 2 * chip) + core


def head_pair(side, spans, i):
    count = HEADS // 2
    low, high = home(i, spans), home(count + i, spans)
    mine = jnp.where(side == 0, low, high)
    theirs = jnp.where(side == 0, high, low)
    return mine, theirs, pl.ds(pl.multiple_of(i * HEAD_DIM, HEAD_DIM), HEAD_DIM)


def mix_kernel(
    experts,
    spot_ref,
    got_ref,
    own_ref,
    near_ref,
    far_ref,
    x_ref,
    gain_ref,
    router_ref,
    table_ref,
    second_ref,
    low_ref,
    scale_ref,
    gates_ref,
    attended_ref,
    near_sum_ref,
    far_sum_ref,
):
    ring = ring_of(got_ref.shape[0])
    for h in range(HEADS):
        attended_ref[:, h * HEAD_DIM : (h + 1) * HEAD_DIM] = got_ref[ring[h]]
    second = x_ref[...].astype(f32)
    tokens, width = second.shape
    half = near_ref.shape[1]
    second_ref[...] = second
    near_sum_ref[...] = jnp.zeros((tokens, half), f32)
    far_sum_ref[...] = jnp.zeros((tokens, half), f32)

    def visit(i, carry):
        mine, theirs, at = head_pair(spot_ref[0], got_ref.shape[0], i)
        second_ref[...] += dot(got_ref[mine], own_ref[at, :])
        near_sum_ref[...] += dot(got_ref[theirs], near_ref[at, :])
        far_sum_ref[...] += dot(got_ref[theirs], far_ref[at, :])
        return carry

    lax.fori_loop(0, HEADS // 2, visit, 0, unroll=True)
    second, near, far = second_ref[...], near_sum_ref[...], far_sum_ref[...]
    second += jnp.where(
        spot_ref[1] == 0,
        jnp.concatenate([near, far], axis=1),
        jnp.concatenate([far, near], axis=1),
    )
    scale = rms_scale(second)
    second_ref[...] = second
    scale_ref[...] = scale
    normed = (second * scale * gain_ref[...]).astype(bf16)
    logits = dot_nt(normed, router_ref[...])
    picked = table_ref[...] < tokens
    peak = jnp.max(jnp.where(picked, logits, masked_score), axis=-1, keepdims=True)
    chances = jnp.where(picked, jnp.exp(logits - peak), 0.0)
    gates = chances / jnp.sum(chances, axis=-1, keepdims=True)
    gates_ref[...] = gates
    high = gates.astype(bf16).astype(f32)
    rest = pltpu.roll(gates - high, experts, 1)
    low_ref[:, :width] = normed
    low_ref[:, width:] = (high + rest).astype(bf16)


def mix(spot, got, own, near, far, x, gain, router, table, experts):
    smem = pl.BlockSpec(memory_space=pltpu.SMEM)
    memory = pl.BlockSpec(memory_space=pltpu.VMEM)
    tokens, width = x.shape
    spare = table.shape[1]
    return pl.pallas_call(
        functools.partial(mix_kernel, experts),
        in_specs=[smem] + [memory] * 8,
        out_specs=[memory] * 5,
        out_shape=[
            jax.ShapeDtypeStruct(x.shape, f32),
            jax.ShapeDtypeStruct((tokens, width + spare), bf16),
            jax.ShapeDtypeStruct((tokens, 1), f32),
            jax.ShapeDtypeStruct((tokens, spare), f32),
            jax.ShapeDtypeStruct(x.shape, bf16),
        ],
        scratch_shapes=[pltpu.VMEM((tokens, width // 2), f32)] * 2,
        name="mix",
    )(spot, got, own, near, far, x, gain, router, table)


def mix_back_kernel(
    spot_ref,
    sums_ref,
    gates_ref,
    gate_grads_ref,
    router_ref,
    second_ref,
    scale_ref,
    gain_ref,
    g_ref,
    own_ref,
    near_ref,
    far_ref,
    send_ref,
    cuts_ref,
    grad_second_ref,
    out_ref,
):
    tokens, width = second_ref.shape
    second = second_ref[...]
    scale = scale_ref[...]
    gain = gain_ref[...]
    gates = gates_ref[...]
    gate_grads = gate_grads_ref[...]
    out_ref[...] = (second + sums_ref[:, width:].astype(f32)).astype(bf16)
    weighted = gates * gate_grads
    grad_sel = weighted - gates * jnp.sum(weighted, axis=-1, keepdims=True)
    grad_logits = grad_sel.astype(bf16)
    grad_normed = sums_ref[:, :width].astype(f32) + dot(grad_logits, router_ref[...])
    gain_part = jnp.sum(grad_normed * second * scale, axis=0, keepdims=True)
    hat = grad_normed * gain
    mean = jnp.mean(hat * second, axis=-1, keepdims=True)
    grad_second = g_ref[...].astype(f32) + scale * hat - second * (scale * scale * scale) * mean
    grad_second_ref[...] = grad_second
    grad_mixed = grad_second.astype(bf16)
    spans = send_ref.shape[0]
    cut = width // spans
    lane = lax.broadcasted_iota(jnp.int32, (1, HEAD_DIM), 1)
    high = gain_part.astype(bf16).astype(f32)
    row = lax.broadcasted_iota(jnp.int32, (16, width), 0)
    gain_rows = jnp.where(row == 0, high, jnp.where(row == 1, gain_part - high, 0.0))
    shifted = pltpu.roll(grad_logits.astype(f32), cut, 1)
    for k, c in enumerate(ring_of(spans)):
        start = min(c * cut // HEAD_DIM * HEAD_DIM, width - 2 * HEAD_DIM)
        shift = (start - c * cut) % (2 * HEAD_DIM)
        for value, rest, out_rows in (
            (grad_second, shifted, slice(0, tokens)),
            (gain_rows, 0.0, slice(tokens, tokens + 16)),
        ):
            window = pltpu.roll(value[:, start : start + 2 * HEAD_DIM], shift, 1)[:, :HEAD_DIM]
            window = jnp.where(lane < cut, window, 0.0) + rest
            cuts_ref[k, out_rows, :] = window.astype(bf16)
    left, right = grad_mixed[:, : width // 2], grad_mixed[:, width // 2 :]
    at_near = jnp.where(spot_ref[1] == 0, left, right)
    at_far = jnp.where(spot_ref[1] == 0, right, left)
    def visit(i, carry):
        mine, theirs, at = head_pair(spot_ref[0], spans, i)
        send_ref[mine] = dot_nt(grad_mixed, own_ref[at, :]).astype(bf16)
        other = dot_nt(at_near, near_ref[at, :]) + dot_nt(at_far, far_ref[at, :])
        send_ref[theirs] = other.astype(bf16)
        return carry

    lax.fori_loop(0, HEADS // 2, visit, 0, unroll=True)
    for h in ring_of(spans)[HEADS:]:
        send_ref[h] = jnp.zeros((tokens, HEAD_DIM), bf16)


def mix_back(spot, sums, gates, gate_grads, router, second, scale, gain, g, own, near, far, spans):
    tokens, width = second.shape
    smem = pl.BlockSpec(memory_space=pltpu.SMEM)
    memory = pl.BlockSpec(memory_space=pltpu.VMEM)
    return pl.pallas_call(
        mix_back_kernel,
        in_specs=[smem] + [memory] * 11,
        out_specs=[memory] * 4,
        out_shape=[
            jax.ShapeDtypeStruct((spans, tokens, HEAD_DIM), bf16),
            jax.ShapeDtypeStruct((spans, tokens + 16, HEAD_DIM), bf16),
            jax.ShapeDtypeStruct((tokens, width), f32),
            jax.ShapeDtypeStruct((tokens, width), bf16),
        ],
        name="mix_back",
    )(spot, sums, gates, gate_grads, router, second, scale, gain, g, own, near, far)


def inputs_back_kernel(
    side_ref,
    core_ref,
    got_ref,
    wq_ref,
    wk_ref,
    wv_ref,
    near_q_ref,
    near_rest_ref,
    far_q_ref,
    far_rest_ref,
    x_ref,
    gain_ref,
    grad_second_ref,
    out_ref,
    own_sum_ref,
    other_sum_ref,
):
    tokens, width = x_ref.shape
    half = width // 2
    count = HEADS // 2
    own_sum_ref[...] = jnp.zeros((tokens, half), f32)
    other_sum_ref[...] = jnp.zeros((tokens, half), f32)
    spans = got_ref.shape[0]

    def visit(h, carry):
        low, high = home(h, spans), home(count + h, spans)
        mine = jnp.where(core_ref[0] == 0, low, high)
        theirs = jnp.where(core_ref[0] == 0, high, low)
        window = pl.ds(pl.multiple_of(h * HEAD_DIM, HEAD_DIM), HEAD_DIM)
        upper = pl.ds(pl.multiple_of((count + h) * HEAD_DIM, HEAD_DIM), HEAD_DIM)
        for i, weight in enumerate((wq_ref, wk_ref, wv_ref)):
            at = slice(i * HEAD_DIM, (i + 1) * HEAD_DIM)
            near_ref, far_ref = (near_rest_ref, far_rest_ref) if i else (near_q_ref, far_q_ref)
            rows = slice(max(i - 1, 0) * half, max(i, 1) * half)
            grads = jnp.concatenate([got_ref[low, :, at], got_ref[high, :, at]], axis=1)
            weights = jnp.concatenate([weight[:, window], weight[:, upper]], axis=1)
            own_sum_ref[...] += dot_nt(grads, weights)
            grads = jnp.concatenate([got_ref[mine, :, at], got_ref[theirs, :, at]], axis=1)
            weights = jnp.concatenate([near_ref[rows, window], far_ref[rows, window]], axis=1)
            other_sum_ref[...] += dot_nt(grads, weights)
        return carry

    lax.fori_loop(0, count, visit, 0)
    own_part, other_part = own_sum_ref[...], other_sum_ref[...]
    grad_normed = jnp.where(
        side_ref[0] == 0,
        jnp.concatenate([own_part, other_part], axis=1),
        jnp.concatenate([other_part, own_part], axis=1),
    )
    resid = x_ref[...].astype(f32)
    scale = rms_scale(resid)
    hat = grad_normed * gain_ref[...]
    mean = jnp.mean(hat * resid, axis=-1, keepdims=True)
    out_ref[...] = grad_second_ref[...] + scale * hat - resid * (scale * scale * scale) * mean


def inputs_back(side, core, got, *values):
    x = values[-3]
    smem = pl.BlockSpec(memory_space=pltpu.SMEM)
    memory = pl.BlockSpec(memory_space=pltpu.VMEM)
    return pl.pallas_call(
        inputs_back_kernel,
        in_specs=[smem] * 2 + [memory] * (1 + len(values)),
        out_specs=memory,
        out_shape=jax.ShapeDtypeStruct(x.shape, f32),
        scratch_shapes=[pltpu.VMEM((x.shape[0], x.shape[1] // 2), f32)] * 2,
        name="inputs_back",
    )(
        side.reshape(1),
        core.reshape(1),
        got,
        *values,
    )


def place_heads_kernel(
    cut,
    side_ref,
    heads_ref,
    rest_ref,
    gain_rows_ref,
    gain_ref,
    q_ref,
    k_ref,
    v_ref,
    output_ref,
    norm_ref,
    norm2_ref,
    line_ref,
    line2_ref,
):
    for h in range(HEADS):
        at = slice(h * HEAD_DIM, (h + 1) * HEAD_DIM)
        for i, out in enumerate((q_ref, k_ref, v_ref)):
            out[:, at] = heads_ref[h, :, i * HEAD_DIM : (i + 1) * HEAD_DIM].astype(f32)
    sums = rest_ref[0].astype(f32)
    for h in range(1, HEADS):
        sums += rest_ref[h].astype(f32)
    lane = lax.broadcasted_iota(jnp.int32, (8, HEAD_DIM), 1)
    pair = jnp.where((lane == cut) | (lane == cut + 1), 1.0, 0.0)
    row = lax.dot_general(
        pair, sums, (((1,), (1,)), ((), ())), precision=exact, preferred_element_type=f32
    )
    block = rest_ref.shape[1]
    for i in range(line_ref.shape[1] // block):

        @pl.when(pl.program_id(0) == i)
        def _(at=slice(i * block, (i + 1) * block)):
            line_ref[:, at] = row[0:1] / gain_ref[:, at]

    spans = rest_ref.shape[0]

    @pl.when(pl.program_id(0) == 0)
    def _():
        for i in range(spans // 2):
            low, high = ring_position(i, spans), ring_position(spans // 2 + i, spans)
            rows = gain_rows_ref[jnp.where(side_ref[0] == 0, low, high)].astype(f32)
            line2_ref[:, i * cut : (i + 1) * cut] = (rows[0:1] + rows[1:2])[:, :cut]

    for c in range(spans):
        piece = rest_ref[ring_position(c, spans), :, :cut].astype(f32)
        output_ref[:, c * cut : (c + 1) * cut] = piece

    @pl.when(pl.program_id(0) == pl.num_programs(0) - 1)
    def _():
        for i in range(norm_ref.shape[0]):
            at = slice(i * HEAD_DIM, (i + 1) * HEAD_DIM)
            norm_ref[i : i + 1, :] = line_ref[:, at]
            norm2_ref[i : i + 1, :] = line2_ref[:, at]


def ring_position(index, spans):
    if spans != 16:
        return index
    chip, core = index // 2, index % 2
    level, column = chip // 2, chip % 2
    return (level + column * (7 - 2 * level)) * 2 + core


def place_heads(side, got, gain, width):
    spans, _, packed = got.shape
    half = width // 2
    cut = width // spans
    block = half // 8
    part = pl.BlockSpec((block, width), lambda r: (r, 0))
    line = pl.BlockSpec((1, half), lambda r: (0, 0))
    return pl.pallas_call(
        functools.partial(place_heads_kernel, cut),
        grid=(8,),
        in_specs=[
            pl.BlockSpec(memory_space=pltpu.SMEM),
            pl.BlockSpec((HEADS, block, 3 * HEAD_DIM), lambda r: (0, r, 0)),
            pl.BlockSpec((spans, block, HEAD_DIM), lambda r: (0, r, 3)),
            pl.BlockSpec((spans, 16, HEAD_DIM), lambda r: (0, half // 16, 3)),
            line,
        ],
        out_specs=[part] * 4 + [pl.BlockSpec((half // HEAD_DIM, HEAD_DIM), lambda r: (0, 0))] * 2,
        out_shape=[jax.ShapeDtypeStruct((half, width), f32)] * 4
        + [jax.ShapeDtypeStruct((half // HEAD_DIM, HEAD_DIM), f32)] * 2,
        scratch_shapes=[pltpu.VMEM((1, half), f32)] * 2,
        name="place_heads",
    )(side.reshape(1), got, got, got, gain.reshape(1, half))


def place_shared_kernel(side_ref, got_ref, in_ref, out_ref, rows_ref):
    spans = got_ref.shape[0]
    units = got_ref.shape[1] // 4
    half = got_ref.shape[2]
    hidden = spans * units

    for part in range(2):
        for c in range(spans):
            spot = ring_position(c, spans)
            piece = got_ref[spot, part * units : (part + 1) * units, :]
            rows_ref[c * units : (c + 1) * units, :] = piece.astype(f32)

        def turn(i, carry):
            window = pl.ds(pl.multiple_of(i * HEAD_DIM, HEAD_DIM), HEAD_DIM)
            at = pl.ds(pl.multiple_of(part * hidden + i * HEAD_DIM, HEAD_DIM), HEAD_DIM)
            in_ref[:, at] = rows_ref[window, :].T
            return carry

        lax.fori_loop(0, hidden // HEAD_DIM, turn, 0)
    first = side_ref[0] * (spans // 2)
    for c in range(spans // 2):
        spot = ring_position(first + c, spans)
        for part in range(2):
            piece = got_ref[spot, (2 + part) * units : (3 + part) * units, :]
            out_ref[c * units : (c + 1) * units, part * half : (part + 1) * half] = piece.astype(f32)


def place_shared(got, side):
    spans, quad, half = got.shape
    hidden = spans * quad // 4
    memory = pl.BlockSpec(memory_space=pltpu.VMEM)
    return pl.pallas_call(
        place_shared_kernel,
        in_specs=[pl.BlockSpec(memory_space=pltpu.SMEM), memory],
        out_specs=[memory, memory],
        out_shape=[
            jax.ShapeDtypeStruct((half, 2 * hidden), f32),
            jax.ShapeDtypeStruct((hidden // 2, 2 * half), f32),
        ],
        scratch_shapes=[pltpu.VMEM((hidden, half), f32)],
        name="place_shared",
    )(side.reshape(1), got)


def after(value, *others):
    return lax.optimization_barrier((value, *others))[0]


def tied(*values):
    return lax.optimization_barrier(values)


def one_hot_rows(lanes, *targets):
    row = lax.broadcasted_iota(jnp.int32, (8, lanes), 0)
    lane = lax.broadcasted_iota(jnp.int32, (8, lanes), 1)
    rows = jnp.zeros((8, lanes), f32)
    for i, target in enumerate(targets):
        rows = jnp.where((row == i) & (lane == target), 1.0, rows)
    return rows.astype(bf16)


def slot_keys(shape, axis, capacity):
    index = lax.broadcasted_iota(jnp.int32, shape, axis)
    return (index % capacity + 1024 * (index // capacity)).astype(f32)


def run_keys(shape, axis, tokens):
    return (1024 * (lax.broadcasted_iota(jnp.int32, shape, axis) // tokens)).astype(f32)


def group_runs(capacity):
    return min(8, 224 // capacity)


def pick_slots_kernel(capacity, tokens, here_ref, g_ref, out_ref):
    many = g_ref.shape[0]
    width = out_ref.shape[1]
    extras = g_ref[:, width:]
    rows = one_hot_rows(extras.shape[1], here_ref[0])
    slots = dot_nt(rows, extras)[0:1] + run_keys((1, many), 1, tokens)
    takes = slot_keys((out_ref.shape[0], 1), 0, capacity) == slots
    select = jnp.where(takes, 1.0, 0.0).astype(bf16)
    out_ref[...] = dot(select, g_ref[:, :width]).astype(bf16)


def pick_slots(here, g_wide, width, capacity, tokens):
    length, wide = g_wide.shape
    runs = group_runs(capacity)
    steps = length // (runs * tokens)
    return pl.pallas_call(
        functools.partial(pick_slots_kernel, capacity, tokens),
        grid=(steps,),
        in_specs=[
            pl.BlockSpec(memory_space=pltpu.SMEM),
            pl.BlockSpec((runs * tokens, wide), lambda i: (i, 0)),
        ],
        out_specs=pl.BlockSpec((runs * capacity, width), lambda i: (i, 0)),
        out_shape=jax.ShapeDtypeStruct((steps * runs * capacity, width), bf16),
        name="pick_slots",
        cost_estimate=pl.CostEstimate(
            flops=2 * length * runs * capacity * width,
            bytes_accessed=3 * length * wide,
            transcendentals=0,
        ),
    )(here.reshape(1), g_wide)


def sigmoid(value):
    return 1.0 / (1.0 + jnp.exp(-value))


def experts_kernel(
    capacity,
    tokens,
    experts,
    here_ref,
    normed_ref,
    g_ref,
    grad_slots_ref,
    own_in_ref,
    first_in_ref,
    middle_in_ref,
    last_in_ref,
    own_down_ref,
    other_down_ref,
    own_shared_in_ref,
    other_shared_in_ref,
    own_shared_out_ref,
    other_shared_out_ref,
    dispatched_ref,
    hidden_ref,
    grad_result_ref,
    grad_proj_ref,
    shared_hidden_ref,
    shared_grad_ref,
    parts_ref,
    gate_dot_ref,
    in_ref,
    down_ref,
    shared_in_ref,
    shared_out_ref,
    grad_dispatched_ref,
    scaled_ref,
):
    @pl.when(pl.program_id(0) == 0)
    def _():
        side = here_ref[1]
        rows = own_in_ref.shape[0]
        in_ref[pl.ds(pl.multiple_of(side * rows, 64), rows), :] = own_in_ref[...]
        at = (1 - side) * rows
        for ref in (first_in_ref, middle_in_ref, last_in_ref):
            in_ref[pl.ds(pl.multiple_of(at, 16), ref.shape[0]), :] = ref[...]
            at = at + ref.shape[0]
        rows = own_down_ref.shape[0]
        down_ref[pl.ds(pl.multiple_of(side * rows, 64), rows), :] = own_down_ref[...]
        down_ref[pl.ds(pl.multiple_of((1 - side) * rows, 64), rows), :] = other_down_ref[...]
        rows = own_shared_in_ref.shape[0]
        units = own_shared_out_ref.shape[0]
        shared_in_ref[...] = jnp.zeros_like(shared_in_ref)
        shared_out_ref[...] = jnp.zeros_like(shared_out_ref)
        for place, ref in ((side, own_shared_in_ref), (1 - side, other_shared_in_ref)):
            window = pl.ds(pl.multiple_of(place * rows, 64), rows)
            shared_in_ref[window, :units] = ref[:, :units]
            shared_in_ref[window, HEAD_DIM : HEAD_DIM + units] = ref[:, units:]
        shared_out_ref[:units, :] = jnp.where(
            here_ref[2] == side, own_shared_out_ref[...], other_shared_out_ref[...]
        )

    many, slots = normed_ref.shape[0], dispatched_ref.shape[0]
    width = dispatched_ref.shape[1]
    here = here_ref[0]
    spare = normed_ref.shape[1] - width
    gate_rows = dot_nt(one_hot_rows(spare, here, experts + here), normed_ref[:, width:])
    gate_row = gate_rows[0:1] + gate_rows[1:2]
    slot_pick = one_hot_rows(spare, here)
    group = group_runs(capacity)
    chunk, picks = group * tokens, group * capacity
    takes = []
    for at in range(0, many, chunk):
        extras = g_ref[at : at + chunk, width:]
        slot_row = dot_nt(slot_pick, extras)[0:1] + run_keys((1, chunk), 1, tokens)
        hit = slot_keys((picks, 1), 0, capacity) == slot_row
        takes.append(hit)
        select = jnp.where(hit, 1.0, 0.0).astype(bf16)
        at_slots = slice(at // tokens * capacity, (at // tokens + group) * capacity)
        dispatched_ref[at_slots, :] = dot(select, normed_ref[at : at + chunk, :width]).astype(bf16)
    slot_gate = jnp.concatenate(
        [
            jnp.sum(
                jnp.where(hit, gate_row[:, i * chunk : (i + 1) * chunk], 0.0), axis=1, keepdims=True
            )
            for i, hit in enumerate(takes)
        ],
        axis=0,
    )
    dispatched = dispatched_ref[...]
    grad_slots = grad_slots_ref[...].astype(f32)
    grad_result = (grad_slots * slot_gate).astype(bf16)
    grad_result_ref[...] = grad_result

    projected = dot(dispatched, in_ref[...])
    gate, up = projected[:, :EXP_HID], projected[:, EXP_HID:]
    chance = sigmoid(gate)
    silu = gate * chance
    hidden = (silu * up).astype(bf16)
    hidden_ref[...] = hidden
    grad_hidden = dot_nt(grad_result, down_ref[...])
    grad_proj_ref[:, :EXP_HID] = (
        grad_hidden * up * chance * (1.0 + gate * (1.0 - chance))
    ).astype(bf16)
    grad_proj_ref[:, EXP_HID:] = (grad_hidden * silu).astype(bf16)
    result = dot(hidden, down_ref[...]).astype(bf16).astype(f32)
    slot_dot = jnp.sum(grad_slots * result, axis=1, keepdims=True)
    for i, hit in enumerate(takes):
        dots = slot_dot[i * picks : (i + 1) * picks]
        gate_dot = jnp.sum(jnp.where(hit, dots, 0.0), axis=0, keepdims=True)
        gate_dot_ref[:, i * chunk : (i + 1) * chunk] = jnp.broadcast_to(gate_dot, (8, chunk))
    scaled = (result * slot_gate).astype(bf16)
    grad_dispatched = dot_nt(grad_proj_ref[...], in_ref[...]).astype(bf16)

    grad_dispatched_ref[...] = grad_dispatched
    scaled_ref[...] = scaled
    lanes = shared_out_ref.shape[0]
    size = min(4 * HEAD_DIM, chunk)

    def visit(i, carry):
        at = pl.ds(pl.multiple_of(i * size, size), size)
        which = i * size // chunk
        filled = pl.ds(pl.multiple_of(which * picks, 16), picks)
        shared = dot(normed_ref[at, :width], shared_in_ref[...])
        shared_gate, shared_up = shared[:, :lanes], shared[:, lanes:]
        shared_chance = sigmoid(shared_gate)
        shared_silu = shared_gate * shared_chance
        shared_hidden = (shared_silu * shared_up).astype(bf16)
        shared_hidden_ref[at, :] = shared_hidden
        grad_shared = dot_nt(g_ref[at, :width], shared_out_ref[...])
        slope = shared_chance * (1.0 + shared_gate * (1.0 - shared_chance))
        shared_grad = jnp.concatenate(
            [(grad_shared * shared_up * slope).astype(bf16), (grad_shared * shared_silu).astype(bf16)],
            axis=1,
        )
        shared_grad_ref[at, :] = shared_grad
        slot_column = dot_nt(g_ref[at, width:], slot_pick)[:, 0:1]
        run = (i * size - which * chunk + lax.broadcasted_iota(jnp.int32, (size, 1), 0)) // tokens
        key = slot_column + (1024 * run).astype(f32)
        back = jnp.where(key == slot_keys((1, picks), 1, capacity), 1.0, 0.0).astype(bf16)
        parts_ref[at, :width] = (
            dot(back, grad_dispatched_ref[filled, :]) + dot_nt(shared_grad, shared_in_ref[...])
        ).astype(bf16)
        parts_ref[at, width:] = (
            dot(back, scaled_ref[filled, :]) + dot(shared_hidden, shared_out_ref[...])
        ).astype(bf16)
        return carry

    lax.fori_loop(0, many // size, visit, 0)


def run_experts(
    places, normed_wide, g_wide, grad_slots, weights, tokens, capacity
):
    length, wide = normed_wide.shape
    width = grad_slots.shape[1]
    experts = length // tokens
    runs = group_runs(capacity)
    steps = length // (runs * tokens)
    many, slots = runs * tokens, runs * capacity
    lanes = HEAD_DIM

    def block(rows, columns):
        return pl.BlockSpec((rows, columns), lambda i: (i, 0))

    def fixed(value):
        return pl.BlockSpec(value.shape, lambda i: (0, 0), pipeline_mode=pl.Buffered(1))

    def shape(rows, columns, kind=bf16):
        return jax.ShapeDtypeStruct((rows, columns), kind)

    return pl.pallas_call(
        functools.partial(experts_kernel, capacity, tokens, experts),
        grid=(steps,),
        in_specs=[
            pl.BlockSpec(memory_space=pltpu.SMEM),
            block(many, wide),
            block(many, wide),
            block(slots, width),
            *[fixed(weight) for weight in weights],
        ],
        out_specs=[
            block(slots, width),
            block(slots, EXP_HID),
            block(slots, width),
            block(slots, 2 * EXP_HID),
            block(many, lanes),
            block(many, 2 * lanes),
            block(many, 2 * width),
            pl.BlockSpec((8, many), lambda i: (0, i)),
        ],
        out_shape=[
            shape(steps * slots, width),
            shape(steps * slots, EXP_HID),
            shape(steps * slots, width),
            shape(steps * slots, 2 * EXP_HID),
            shape(length, lanes),
            shape(length, 2 * lanes),
            shape(length, 2 * width),
            shape(8, length, f32),
        ],
        scratch_shapes=[
            pltpu.VMEM((width, 2 * EXP_HID), bf16),
            pltpu.VMEM((EXP_HID, width), bf16),
            pltpu.VMEM((width, 2 * lanes), bf16),
            pltpu.VMEM((lanes, width), bf16),
            pltpu.VMEM((slots, width), bf16),
            pltpu.VMEM((slots, width), bf16),
        ],
        name="experts",
        cost_estimate=pl.CostEstimate(
            flops=20 * 10**9, bytes_accessed=40 * 10**6, transcendentals=2 * 10**6
        ),
    )(
        places,
        normed_wide,
        g_wide,
        grad_slots,
        *weights,
    )


def slot_grads_kernel(side_ref, left_ref, right_ref, own_ref, other_ref, turned_ref):
    @pl.when(pl.program_id(0) == 0)
    def _():
        turned_ref[...] = left_ref[...].T

    rows = own_ref.shape[0]
    size = rows // 5 if rows % 80 == 0 else rows // 4
    side = side_ref[0]

    def visit(i, carry):
        def part(place):
            at = pl.ds(pl.multiple_of(place * rows + i * size, 16), size)
            return dot(turned_ref[at, :], right_ref[...])

        at = pl.ds(pl.multiple_of(i * size, 16), size)
        own_ref[at, :] = part(side)
        other_ref[at, :] = part(1 - side).astype(bf16)
        return carry

    lax.fori_loop(0, rows // size, visit, 0)


def slot_grads(side, left, right):
    slots, tall = left.shape
    wide = right.shape[1]
    block = pl.BlockSpec((tall // 2, 2 * HEAD_DIM), lambda i: (0, i))
    return pl.pallas_call(
        slot_grads_kernel,
        grid=(wide // (2 * HEAD_DIM),),
        in_specs=[
            pl.BlockSpec(memory_space=pltpu.SMEM),
            pl.BlockSpec((slots, tall), lambda i: (0, 0), pipeline_mode=pl.Buffered(1)),
            pl.BlockSpec((slots, 2 * HEAD_DIM), lambda i: (0, i)),
        ],
        out_specs=[block, block],
        out_shape=[
            jax.ShapeDtypeStruct((tall // 2, wide), f32),
            jax.ShapeDtypeStruct((tall // 2, wide), bf16),
        ],
        scratch_shapes=[pltpu.VMEM((tall, slots), bf16)],
        name="slot_grads",
        cost_estimate=pl.CostEstimate(
            flops=2 * slots * tall * wide,
            bytes_accessed=2 * slots * (tall + wide) + 3 * tall * wide,
            transcendentals=0,
        ),
    )(side.reshape(1), left, right)


def shared_grads_kernel(grad_ref, normed_ref, hidden_ref, g_ref, in_ref, out_ref):
    @pl.when(pl.program_id(0) == 0)
    def _():
        in_ref[...] = jnp.zeros_like(in_ref)
        out_ref[...] = jnp.zeros_like(out_ref)

    in_ref[...] += dot_tn(grad_ref[...], normed_ref[...])
    out_ref[...] += dot_tn(hidden_ref[...], g_ref[...])


def shared_products(grad, normed_wide, hidden, g_wide, width):
    length, lanes = hidden.shape
    tile = 4 * HEAD_DIM

    def block(columns):
        return pl.BlockSpec((tile, columns), lambda i: (i, 0))

    def whole(rows):
        return pl.BlockSpec((rows, width), lambda i: (0, 0))

    return pl.pallas_call(
        shared_grads_kernel,
        grid=(length // tile,),
        in_specs=[block(2 * lanes), block(width), block(lanes), block(width)],
        out_specs=[whole(2 * lanes), whole(lanes)],
        out_shape=[
            jax.ShapeDtypeStruct((2 * lanes, width), f32),
            jax.ShapeDtypeStruct((lanes, width), f32),
        ],
        name="shared_products",
        cost_estimate=pl.CostEstimate(
            flops=6 * length * lanes * width, bytes_accessed=6 * length * width, transcendentals=0
        ),
    )(grad, normed_wide, hidden, g_wide)


def turned_product_kernel(side_ref, left_ref, right_ref, out_ref, sum_ref):
    step = pl.program_id(0)

    @pl.when(step == 0)
    def _():
        sum_ref[...] = jnp.zeros_like(sum_ref)

    sum_ref[...] += dot_tn(right_ref[...], left_ref[...])

    @pl.when(step == pl.num_programs(0) - 1)
    def _():
        count = out_ref.shape[0] // HEAD_DIM
        near = count // 2

        def turn(i, carry):
            window = pl.ds(pl.multiple_of(i * HEAD_DIM, HEAD_DIM), HEAD_DIM)
            place = jnp.where(i // near == side_ref[0], 0, near) + i % near
            at = pl.ds(pl.multiple_of(place * HEAD_DIM, HEAD_DIM), HEAD_DIM)
            out_ref[at, :] = sum_ref[:, window].T
            return carry

        lax.fori_loop(0, count, turn, 0)


def turned_product(side, left, right, wide):
    length, lanes = right.shape
    tile = 4 * HEAD_DIM
    return pl.pallas_call(
        turned_product_kernel,
        grid=(length // tile,),
        in_specs=[
            pl.BlockSpec(memory_space=pltpu.SMEM),
            pl.BlockSpec((tile, wide), lambda i: (i, 0)),
            pl.BlockSpec((tile, lanes), lambda i: (i, 0)),
        ],
        out_specs=pl.BlockSpec((wide, lanes), lambda i: (0, 0)),
        out_shape=jax.ShapeDtypeStruct((wide, lanes), f32),
        scratch_shapes=[pltpu.VMEM((lanes, wide), f32)],
        name="turned_product",
        cost_estimate=pl.CostEstimate(
            flops=2 * length * lanes * wide,
            bytes_accessed=2 * length * wide,
            transcendentals=0,
        ),
    )(side.reshape(1), left, right)


def slot_table(span_picks, span_order, experts):
    tokens = span_picks.shape[0]
    order = span_order.reshape(tokens, TOP)
    onehot = span_picks[:, :, None] == jnp.arange(experts, dtype=jnp.int32)
    picked = jnp.any(onehot, axis=1)
    rank_key = jnp.sum(jnp.where(onehot, order[:, :, None], 0), axis=1)
    rank_key = jnp.where(picked, rank_key, tokens * TOP)
    before = rank_key[:, None, :] < rank_key[None, :, :]
    slots = jnp.sum(before.astype(jnp.int32), axis=0)
    return jnp.where(picked, slots, 2 * tokens)


def on_device(
    inputs,
    norm1_gain,
    w_query,
    w_key,
    w_value,
    w_output,
    norm2_gain,
    router,
    shared_gate_up_weight,
    shared_down_weight,
    expert_in,
    expert_out,
    picks,
    fill_order,
    grad_out,
):
    spans = lax.axis_size("ctx")
    here = lax.axis_index("ctx")
    side = lax.axis_index("fsdp")
    core = here % 2
    tokens, width = inputs.shape[1:]
    half = width // 2
    length = spans * tokens
    experts = spans * expert_in.shape[0]
    capacity = tokens * TOP // experts
    head = jnp.minimum(ring_position(here, spans), HEADS - 1)
    units = EXP_HID // spans
    ring = ring_of(spans)
    is_ring = spans == 16
    groups = [ring] if is_ring else None
    swap_core = [(i, i ^ 1) for i in range(spans)]

    def across(value):
        return lax.ppermute(value, "fsdp", [(0, 1), (1, 0)])

    def ordered(own, other, axis):
        return jnp.where(
            side == 0,
            jnp.concatenate([own, other], axis=axis),
            jnp.concatenate([other, own], axis=axis),
        )

    def everyone(value):
        return lax.all_gather(value, "ctx", axis=0, tiled=True, axis_index_groups=groups)

    def columns(value, start, count):
        return lax.dynamic_slice_in_dim(value, start, count, 1)

    def rows(value, start, count):
        return lax.dynamic_slice_in_dim(value, start, count, 0)

    def halves(value, axis=0):
        size = value.shape[axis] // 2
        mine = lax.dynamic_slice_in_dim(value, side * size, size, axis)
        theirs = lax.dynamic_slice_in_dim(value, (1 - side) * size, size, axis)
        return mine, theirs

    def reduced(value, axis=0):
        mine, theirs = halves(value, axis)
        return mine + across(theirs.astype(bf16)).astype(f32)

    def swapped(value):
        return lax.all_to_all(value, "ctx", split_axis=0, concat_axis=0, tiled=True)

    def row_major(value):
        return with_layout_constraint(value, Layout(tuple(range(value.ndim))))

    x = inputs[0]
    g = grad_out[0]
    x_all = everyone(x)
    spare = -(-2 * experts // HEAD_DIM) * HEAD_DIM
    own_table = slot_table(picks[0], fill_order[0, 0], experts)
    own_table = jnp.pad(
        own_table.astype(f32), ((0, 0), (0, spare - experts)), constant_values=2.0 * tokens
    )
    g_wide = jnp.concatenate([g, own_table.astype(bf16)], axis=1)
    head_own = jnp.concatenate(
        [columns(w, head * HEAD_DIM, HEAD_DIM) for w in (w_query, w_key, w_value)], axis=1
    )
    head_other = across(head_own)
    small = jnp.concatenate([router.T, norm1_gain[None], norm2_gain[None]], axis=0)
    small_other = across(small)
    output_near = across(columns(w_output, core * half, half))
    lanes = HEAD_DIM
    shared_in_own = jnp.concatenate(
        [columns(shared_gate_up_weight, at + here * units, units) for at in (0, EXP_HID)], axis=1
    )
    shared_rows = shared_down_weight.shape[0]
    shared_out_own = rows(shared_down_weight, here * units % shared_rows, units)
    cosine, sine = rotary_tables(jnp.asarray(ring, jnp.int32) * tokens, tokens, HEAD_DIM)
    small = ordered(small, small_other, 1)
    router_w = small[:experts]
    gain_one = small[experts : experts + 1].astype(f32)
    gain_two = small[experts + 1 :].astype(f32)
    quarter = half // 4
    chunks = [expert_in[0, :quarter], expert_in[0, quarter:-quarter], expert_in[0, -quarter:]]
    head_other, *chunks = tied(head_other, *chunks)
    chunks = [across(chunk) for chunk in chunks]
    x_all, cosine, sine, head_other, gain_one, output_near = tied(
        x_all, cosine, sine, head_other, gain_one, output_near
    )
    output_far = lax.ppermute(output_near, "ctx", swap_core)
    g_wide_all = everyone(after(g_wide, x_all))
    g_all = g_wide_all[:, :width]
    table = g_wide_all[:, width : width + experts]

    normed1_all, query, key, value = project(
        side, x_all, gain_one, head_own, head_other, cosine, sine
    )
    context, lse, attended = attend(query, key, value, is_ring)
    attended, output_far, chunks[0] = tied(attended, output_far, chunks[0])
    down_other = across(after(expert_out[0], attended))
    got = swapped(attended.reshape(spans, tokens, HEAD_DIM))
    got, chunks[1] = tied(got, chunks[1])
    spot = jnp.stack([side, core]).astype(jnp.int32)
    router_pad = jnp.pad(router_w, ((0, spare - experts), (0, 0)))
    second, normed2_wide, scale_two, own_gates, attended = mix(
        spot,
        got,
        w_output,
        output_near,
        output_far,
        x,
        gain_two,
        router_pad,
        own_table,
        experts,
    )
    normed2_wide, g_wide_all, chunks[2] = tied(normed2_wide, g_wide_all, chunks[2])
    normed2_wide = everyone(normed2_wide)
    grad_slots = pick_slots(here, g_wide_all, width, capacity, tokens)
    shared_in_other = across(after(shared_in_own, grad_slots))
    shared_out_other = across(after(shared_out_own, grad_slots))
    normed2_wide, grad_slots, down_other, shared_in_other, shared_out_other = tied(
        normed2_wide, grad_slots, down_other, shared_in_other, shared_out_other
    )
    normed2_all = normed2_wide[:, :width]
    attended_all = everyone(after(attended, normed2_wide))
    dense = [
        columns(after(w, grad_slots), core * half, half) for w in (w_query, w_key, w_value)
    ]
    near = [across(dense[0]), across(jnp.concatenate(dense[1:], axis=0))]
    spots = [ring_position(i, spans) for i in range(spans)]
    (
        dispatched,
        expert_hidden,
        grad_result,
        grad_proj,
        shared_hidden,
        grad_sproj,
        parts,
        gate_dot,
    ) = run_experts(
        jnp.stack([here, side, here * units // shared_rows]).astype(jnp.int32),
        normed2_wide,
        g_wide_all,
        grad_slots,
        (
            expert_in[0],
            *chunks,
            expert_out[0],
            down_other,
            shared_in_own,
            shared_in_other,
            shared_out_own,
            shared_out_other,
        ),
        tokens,
        capacity,
    )
    parts, near[0], attended_all = tied(parts, near[0], attended_all)
    sums = lax.psum_scatter(
        parts, "ctx", scatter_dimension=0, tiled=True, axis_index_groups=groups
    )
    gate_dot = gate_dot[0].reshape(spans, tokens)
    grad_shared_in, grad_shared_out = shared_products(
        grad_sproj, normed2_wide, shared_hidden, g_wide_all, width
    )
    grad_shared_in = jnp.concatenate(
        [grad_shared_in[:units], grad_shared_in[lanes : lanes + units]], axis=0
    )
    grad_shared_in = reduced(grad_shared_in, 1).astype(bf16)
    grad_shared_out = grad_shared_out[:units].astype(bf16)
    grad_shared_out = grad_shared_out.astype(f32) + across(grad_shared_out).astype(f32)
    grad_shared_out = grad_shared_out.astype(bf16)
    shared_grads = jnp.concatenate(
        [grad_shared_in, grad_shared_out[:, :half], grad_shared_out[:, half:]], axis=0
    )
    gate_dot = jnp.concatenate([gate_dot[i : i + 1] for i in spots], axis=0)
    gate_grads = swapped(after(gate_dot, parts)[:, None, :])[:, 0, :].T

    own_down, down_theirs = slot_grads(side, expert_hidden, grad_result)
    own_in, in_theirs = slot_grads(side, dispatched, grad_proj)
    down_theirs = across(after(down_theirs, parts))
    cuts_at = [0, half // 4, half * 9 // 16, half]
    sums, in_theirs, shared_grads, gate_grads = tied(
        sums,
        in_theirs,
        row_major(shared_grads),
        gate_grads,
    )
    split = half * 5 // 16
    in_parts = [in_theirs[a:b] for a, b in zip(cuts_at, cuts_at[1:])]
    in_parts[0], in_parts[1] = across(in_parts[0]), across(in_parts[1])

    sent, cuts, grad_second, layer_out = mix_back(
        spot,
        sums,
        own_gates,
        jnp.pad(gate_grads, ((0, 0), (0, spare - experts))),
        router_pad,
        second,
        scale_two,
        gain_two,
        g,
        w_output,
        output_near,
        output_far,
        spans,
    )
    arrived = swapped(sent).reshape(length, HEAD_DIM)
    arrived, shared_grads, cuts, near[1], down_theirs, in_parts[0] = tied(
        arrived, shared_grads, cuts, near[1], down_theirs, in_parts[0]
    )
    cuts = lax.all_to_all(
        cuts, "ctx", split_axis=0, concat_axis=0, tiled=True, axis_index_groups=groups
    )
    extras = cuts[:, :tokens].reshape(length, HEAD_DIM)
    shared_grads = everyone(shared_grads[None])
    grad_heads, grad_heads_ring = attend_back(
        query, key, value, arrived, context, lse, cosine, sine, is_ring
    )
    grad_heads, grad_heads_ring, in_parts[1] = tied(grad_heads, grad_heads_ring, in_parts[1])
    cut = width // spans
    gain_rows = cuts[:, tokens : tokens + 2, :cut].astype(f32)
    gain_rows = jnp.sum(gain_rows, axis=(0, 1))
    gain_rows = jnp.pad(gain_rows.reshape(1, cut), ((0, 15), (0, HEAD_DIM - cut)))
    grad_router = turned_product(side, normed2_wide, extras, width)[:, cut : cut + experts]
    grad_router = grad_router[:half] + across(grad_router[half:])
    products = turned_product(side, attended_all, extras, width)
    mine, theirs = products[:half], products[half:]
    gain_high = gain_rows.astype(bf16)
    gain_low = jnp.roll((gain_rows - gain_high.astype(f32)).astype(bf16), 1, axis=0)
    theirs = jnp.concatenate([theirs.astype(bf16), gain_high + gain_low], axis=0)
    grad_heads_ring, theirs = tied(grad_heads_ring, theirs)
    head_mine, head_theirs = halves(dot_tn(normed1_all, grad_heads_ring))
    head_theirs = head_theirs.astype(bf16)
    theirs = across(theirs).astype(f32)
    grad_output = mine + theirs[:half]
    gain_rows = gain_rows[:1] + theirs[half : half + 1] + theirs[half + 1 : half + 2]
    gain_high = gain_rows.astype(bf16)
    gain_low = (gain_rows - gain_high.astype(f32)).astype(bf16)
    gain_rows = jnp.pad(
        jnp.concatenate([gain_high, gain_low], axis=0), ((0, 14), (3 * HEAD_DIM, 0))
    )
    got = swapped(grad_heads.reshape(spans, tokens, 3 * HEAD_DIM))
    grad_head_w = (head_mine + across(head_theirs).astype(f32)).astype(bf16)
    part = jnp.sum(grad_head_w.astype(f32) * head_own.astype(f32), axis=1, keepdims=True)
    part_high = part.astype(bf16).astype(f32)
    lane = lax.broadcasted_iota(jnp.int32, (half, HEAD_DIM), 1)
    grad_output = jnp.where(lane < cut, grad_output, 0.0)
    grad_output = jnp.where(lane == cut, part_high, grad_output)
    grad_output = jnp.where(lane == cut + 1, part - part_high, grad_output)
    head_grads = jnp.concatenate([grad_head_w, grad_output.astype(bf16)], axis=1)
    head_grads = jnp.concatenate([head_grads, gain_rows], axis=0)
    head_pack = head_grads
    head_grads, got = tied(row_major(head_grads), got)
    head_grads = everyone(head_grads[None])
    in_parts[2] = across(after(in_parts[2], head_pack))
    far = [lax.ppermute(part, "ctx", swap_core) for part in near]

    grad_inputs = inputs_back(
        side, core, got, w_query, w_key, w_value, *near, *far, x, gain_one, grad_second
    )
    grad_query, grad_key, grad_value, grad_output, grad_norm1, grad_norm2 = place_heads(
        side, head_grads, norm1_gain.astype(f32), width
    )
    grad_expert_in = jnp.concatenate(
        [
            own_in[a:b] + part.astype(f32)
            for a, b, part in zip(cuts_at, cuts_at[1:], in_parts)
        ],
        axis=0,
    )
    grad_shared_in, grad_shared_out = place_shared(shared_grads, side)
    return (
        layer_out[None],
        grad_inputs[None],
        grad_norm1.reshape(half),
        grad_query,
        grad_key,
        grad_value,
        grad_output,
        grad_norm2.reshape(half),
        grad_router,
        grad_shared_in,
        grad_shared_out,
        grad_expert_in[None],
        (own_down + down_theirs.astype(f32))[None],
    )


def solution(mesh):
    placed = (
        P("fsdp", "ctx", None),
        P("fsdp"),
        P("fsdp", None),
        P("fsdp", None),
        P("fsdp", None),
        P("fsdp", None),
        P("fsdp"),
        P("fsdp", None),
        P("fsdp", None),
        P("fsdp", None),
        P("ctx", "fsdp", None),
        P("ctx", "fsdp", None),
        P("fsdp", "ctx", None),
        P("fsdp", "ctx", None),
        P("fsdp", "ctx", None),
    )
    return jax.shard_map(
        on_device,
        mesh=mesh,
        in_specs=placed,
        out_specs=(
            P("fsdp", "ctx", None),
            P("fsdp", "ctx", None),
            P("fsdp"),
            P("fsdp", None),
            P("fsdp", None),
            P("fsdp", None),
            P("fsdp", None),
            P("fsdp"),
            P("fsdp", None),
            P("fsdp", None),
            P("fsdp", None),
            P("ctx", "fsdp", None),
            P("ctx", "fsdp", None),
        ),
        check_vma=False,
    )
```

```python
import functools
import math

import jax
import jax.numpy as jnp
from jax import lax
from jax.experimental import pallas as pl
from jax.experimental.layout import Layout, with_layout_constraint
from jax.experimental.pallas import tpu as pltpu
from jax.sharding import PartitionSpec as P

HEADS = 10
HEAD_DIM = 128
EXP_HID = 896
TOP = 7
BLOCK = 256
TILE = 512

epsilon = 1e-06
masked_score = -1000000000.0
score_scale = 1.0 / math.sqrt(HEAD_DIM)
exact = lax.Precision.HIGHEST
f32 = jnp.float32
bf16 = jnp.bfloat16


def dot(a, b):
    return jnp.dot(a, b, preferred_element_type=f32)


def dot_nt(a, b):
    return lax.dot_general(a, b, (((1,), (1,)), ((), ())), preferred_element_type=f32)


def dot_tn(a, b):
    return lax.dot_general(a, b, (((0,), (0,)), ((), ())), preferred_element_type=f32)


def rms_scale(values):
    return lax.rsqrt(jnp.mean(values * values, axis=-1, keepdims=True) + epsilon)


def rotary_tables(starts, count, width):
    half = width // 2
    freqs = jnp.exp(-math.log(10000.0) * jnp.arange(half, dtype=f32) * 2.0 / width)
    freqs = jnp.concatenate([freqs, freqs])
    first = starts.astype(f32)[:, None] * freqs[None, :]
    second = jnp.arange(count, dtype=f32)[:, None] * freqs[None, :]
    angles = jnp.concatenate([first, second], axis=0)
    sign = jnp.where(jnp.arange(width) < half, -1.0, 1.0)
    cosine, sine = lax.optimization_barrier((jnp.cos(angles), jnp.sin(angles) * sign))
    spans = starts.shape[0]
    cos_a, sin_a = cosine[:spans, None], sine[:spans, None]
    cos_b, sin_b = cosine[None, spans:], sine[None, spans:]
    shape = (spans * count, width)
    return (
        (cos_a * cos_b - sin_a * sin_b).reshape(shape),
        (sin_a * cos_b + cos_a * sin_b).reshape(shape),
    )


def allowed_tile(rows, columns):
    key_block = lax.broadcasted_iota(jnp.int32, (rows, columns), 0) // BLOCK
    query_block = lax.broadcasted_iota(jnp.int32, (rows, columns), 1) // BLOCK
    return key_block <= query_block


def ring_of(spans):
    if spans != 16:
        return list(range(spans))
    chips = [0, 2, 4, 6, 7, 5, 3, 1]
    return [2 * chip + core for chip in chips for core in (0, 1)]


def pieces(j, tile, length, ring):
    if ring:
        starts = (j * BLOCK, length - BLOCK - j * BLOCK)
        return [pl.ds(pl.multiple_of(at, BLOCK), BLOCK) for at in starts]
    return [pl.ds(pl.multiple_of(j * tile, tile), tile)]


def load(ref, windows, columns=slice(None)):
    parts = [ref[window, columns] for window in windows]
    return parts[0] if len(parts) == 1 else jnp.concatenate(parts, axis=0)


def store(ref, windows, value, columns=slice(None)):
    size = value.shape[0] // len(windows)
    for i, window in enumerate(windows):
        ref[window, columns] = value[i * size : (i + 1) * size]


def attend_kernel(
    ring, q_ref, k_ref, v_ref, context_ref, lse_ref, low_ref, score_ref
):
    length = k_ref.shape[0]
    tile = context_ref.shape[0]
    here = pl.program_id(0)
    queries = load(q_ref, pieces(here, tile, length, ring))

    def raw_scores(j):
        return dot_nt(load(k_ref, pieces(j, tile, length, ring)), queries) * score_scale

    def fold(j, scores, peak):
        score_ref[pl.ds(pl.multiple_of(j * tile, tile), tile), :] = scores
        return jnp.maximum(peak, jnp.max(scores.reshape(tile // 8, 8, tile), axis=0))

    diagonal = jnp.where(allowed_tile(tile, tile), raw_scores(here), masked_score)
    peak = fold(here, diagonal, jnp.full((8, tile), masked_score, f32))
    peak = lax.fori_loop(0, here, lambda j, p: fold(j, raw_scores(j), p), peak)
    top = jnp.max(peak, axis=0, keepdims=True)

    def gather(j, carry):
        total, numer = carry
        weights = jnp.exp(score_ref[pl.ds(pl.multiple_of(j * tile, tile), tile), :] - top)
        total = total + jnp.sum(weights.reshape(tile // 8, 8, tile), axis=0)
        values = load(v_ref, pieces(j, tile, length, ring))
        return total, numer + dot_tn(values, weights.astype(bf16))

    zero = (jnp.zeros((8, tile), f32), jnp.zeros((HEAD_DIM, tile), f32))
    total, numer = lax.fori_loop(0, here + 1, gather, zero)
    total = jnp.sum(total, axis=0, keepdims=True)
    context = (numer / total).T
    context_ref[...] = context
    low_ref[...] = context.astype(bf16)
    lse_ref[...] = top + jnp.log(total)


def attend(query, key, value, ring):
    length = query.shape[0]
    tile = min(TILE, length)
    whole = pl.BlockSpec((length, HEAD_DIM), lambda i: (0, 0))
    part = pl.BlockSpec((tile, HEAD_DIM), lambda i: (i, 0))
    return pl.pallas_call(
        functools.partial(attend_kernel, ring),
        grid=(length // tile,),
        in_specs=[whole] * 3,
        out_specs=[part, pl.BlockSpec((1, tile), lambda i: (0, i)), part],
        out_shape=[
            jax.ShapeDtypeStruct((length, HEAD_DIM), f32),
            jax.ShapeDtypeStruct((1, length), f32),
            jax.ShapeDtypeStruct((length, HEAD_DIM), bf16),
        ],
        scratch_shapes=[pltpu.VMEM((length, tile), f32)],
        name="attend",
        cost_estimate=pl.CostEstimate(
            flops=2 * length * length * HEAD_DIM,
            bytes_accessed=12 * length * HEAD_DIM,
            transcendentals=length * length // 2,
        ),
    )(query, key, value)


def attend_back_kernel(
    ring,
    q_ref,
    k_ref,
    v_ref,
    grad_ref,
    context_ref,
    lse_ref,
    cos_ref,
    sin_ref,
    out_ref,
    out_ring_ref,
    dq_ref,
    delta_ref,
    dk_ref,
    dv_ref,
):
    length = q_ref.shape[0]
    tile = dk_ref.shape[0]
    steps = length // tile
    here = pl.program_id(0)

    def natural(i):
        return pl.ds(pl.multiple_of(i * tile, tile), tile)

    @pl.when(here == 0)
    def _():
        def prepare(i, carry):
            window = natural(i)
            dq_ref[window, :] = jnp.zeros((tile, HEAD_DIM), f32)
            product = grad_ref[window, :].astype(f32) * context_ref[window, :]
            ones = jnp.ones((8, HEAD_DIM), f32)
            delta = lax.dot_general(
                ones, product, (((1,), (1,)), ((), ())), precision=exact, preferred_element_type=f32
            )
            delta_ref[:, window] = delta
            return carry

        lax.fori_loop(0, steps, prepare, 0)

    keys = load(k_ref, pieces(here, tile, length, ring))
    values = load(v_ref, pieces(here, tile, length, ring))

    dk_ref[...] = jnp.zeros_like(dk_ref)
    dv_ref[...] = jnp.zeros_like(dv_ref)

    def visit(i, carry):
        window = natural(i)
        queries = load(q_ref, pieces(i, tile, length, ring))
        grads = grad_ref[window, :]
        weights = jnp.exp(dot_nt(keys, queries) * score_scale - lse_ref[:, window])
        later = jnp.where(i > here, weights[BLOCK:, :BLOCK], 0.0)
        later = jnp.concatenate([later, weights[BLOCK:, BLOCK:]], axis=1)
        weights = jnp.concatenate([weights[:BLOCK], later], axis=0)
        grad_weights = dot_nt(values, grads)
        grad_raw = (weights * (grad_weights - delta_ref[0:1, window]) * score_scale).astype(bf16)
        dq_ref[window, :] += dot_tn(grad_raw, keys)
        dk_ref[...] += dot(grad_raw, queries)
        dv_ref[...] += dot(weights.astype(bf16), grads)
        return carry

    lax.fori_loop(here, steps, visit, 0)

    def write(i, part, value):
        at = slice(part * HEAD_DIM, (part + 1) * HEAD_DIM)
        out_ref[natural(i), at] = value
        store(out_ring_ref, pieces(i, tile, length, ring), value, at)

    def turned_back(i, value):
        windows = pieces(i, tile, length, ring)
        scaled = pltpu.roll(value * load(sin_ref, windows), HEAD_DIM // 2, 1)
        return (value * load(cos_ref, windows) + scaled).astype(bf16)

    write(here, 1, turned_back(here, dk_ref[...]))
    write(here, 2, dv_ref[...].astype(bf16))

    @pl.when(here == steps - 1)
    def _():
        def finish(i, carry):
            write(i, 0, turned_back(i, dq_ref[natural(i), :]))
            return carry

        lax.fori_loop(0, steps, finish, 0)


def attend_back(query, key, value, grad, context, lse, cosine, sine, ring):
    length = query.shape[0]
    tile = min(TILE, length)
    memory = pl.BlockSpec(memory_space=pltpu.VMEM)
    return pl.pallas_call(
        functools.partial(attend_back_kernel, ring),
        grid=(length // tile,),
        in_specs=[memory] * 8,
        out_specs=[memory] * 2,
        out_shape=[jax.ShapeDtypeStruct((length, 3 * HEAD_DIM), bf16)] * 2,
        scratch_shapes=[
            pltpu.VMEM((length, HEAD_DIM), f32),
            pltpu.VMEM((8, length), f32),
            pltpu.VMEM((tile, HEAD_DIM), f32),
            pltpu.VMEM((tile, HEAD_DIM), f32),
        ],
        name="attend_back",
        cost_estimate=pl.CostEstimate(
            flops=5 * length * length * HEAD_DIM,
            bytes_accessed=20 * length * HEAD_DIM,
            transcendentals=length * length // 2,
        ),
    )(query, key, value, grad, context, lse, cosine, sine)


def project_kernel(
    side_ref, x_ref, gain_ref, own_ref, other_ref, cos_ref, sin_ref, normed_ref, q_ref, k_ref, v_ref
):
    own, other = own_ref[...], other_ref[...]
    weight = jnp.where(
        side_ref[0] == 0,
        jnp.concatenate([own, other], axis=0),
        jnp.concatenate([other, own], axis=0),
    )
    resid = x_ref[...].astype(f32)
    normed = (resid * rms_scale(resid) * gain_ref[...]).astype(bf16)
    normed_ref[...] = normed
    projected = dot(normed, weight)
    for out, at in ((q_ref, 0), (k_ref, HEAD_DIM)):
        part = projected[:, at : at + HEAD_DIM]
        turned = pltpu.roll(part, HEAD_DIM // 2, 1)
        out[...] = (part * cos_ref[...] + turned * sin_ref[...]).astype(bf16)
    v_ref[...] = projected[:, 2 * HEAD_DIM :].astype(bf16)


def project(side, x, gain, own, other, cosine, sine):
    length, width = x.shape
    tile = min(TILE, length)
    part = pl.BlockSpec((tile, HEAD_DIM), lambda i: (i, 0))
    wide = pl.BlockSpec((tile, width), lambda i: (i, 0))
    return pl.pallas_call(
        project_kernel,
        grid=(length // tile,),
        in_specs=[
            pl.BlockSpec(memory_space=pltpu.SMEM),
            wide,
            pl.BlockSpec((1, width), lambda i: (0, 0)),
            pl.BlockSpec(own.shape, lambda i: (0, 0)),
            pl.BlockSpec(own.shape, lambda i: (0, 0)),
            part,
            part,
        ],
        out_specs=[wide, part, part, part],
        out_shape=[jax.ShapeDtypeStruct((length, width), bf16)]
        + [jax.ShapeDtypeStruct((length, HEAD_DIM), bf16)] * 3,
        name="project",
        cost_estimate=pl.CostEstimate(
            flops=6 * length * width * HEAD_DIM,
            bytes_accessed=4 * length * width,
            transcendentals=0,
        ),
    )(side.reshape(1), x, gain, own, other, cosine, sine)


def home(head, spans):
    if spans != 16:
        return head
    chip, core = head // 2, head % 2
    return 2 * jnp.where(chip < 4, 2 * chip, 15 - 2 * chip) + core


def head_pair(side, spans, i):
    count = HEADS // 2
    low, high = home(i, spans), home(count + i, spans)
    mine = jnp.where(side == 0, low, high)
    theirs = jnp.where(side == 0, high, low)
    return mine, theirs, pl.ds(pl.multiple_of(i * HEAD_DIM, HEAD_DIM), HEAD_DIM)


def mix_kernel(
    experts,
    spot_ref,
    got_ref,
    own_ref,
    near_ref,
    far_ref,
    x_ref,
    gain_ref,
    router_ref,
    table_ref,
    second_ref,
    low_ref,
    scale_ref,
    gates_ref,
    attended_ref,
    near_sum_ref,
    far_sum_ref,
):
    ring = ring_of(got_ref.shape[0])
    for h in range(HEADS):
        attended_ref[:, h * HEAD_DIM : (h + 1) * HEAD_DIM] = got_ref[ring[h]]
    second = x_ref[...].astype(f32)
    tokens, width = second.shape
    half = near_ref.shape[1]
    second_ref[...] = second
    near_sum_ref[...] = jnp.zeros((tokens, half), f32)
    far_sum_ref[...] = jnp.zeros((tokens, half), f32)

    def visit(i, carry):
        mine, theirs, at = head_pair(spot_ref[0], got_ref.shape[0], i)
        second_ref[...] += dot(got_ref[mine], own_ref[at, :])
        near_sum_ref[...] += dot(got_ref[theirs], near_ref[at, :])
        far_sum_ref[...] += dot(got_ref[theirs], far_ref[at, :])
        return carry

    lax.fori_loop(0, HEADS // 2, visit, 0, unroll=True)
    second, near, far = second_ref[...], near_sum_ref[...], far_sum_ref[...]
    second += jnp.where(
        spot_ref[1] == 0,
        jnp.concatenate([near, far], axis=1),
        jnp.concatenate([far, near], axis=1),
    )
    scale = rms_scale(second)
    second_ref[...] = second
    scale_ref[...] = scale
    normed = (second * scale * gain_ref[...]).astype(bf16)
    logits = dot_nt(normed, router_ref[...])
    picked = table_ref[...] < tokens
    peak = jnp.max(jnp.where(picked, logits, masked_score), axis=-1, keepdims=True)
    chances = jnp.where(picked, jnp.exp(logits - peak), 0.0)
    gates = chances / jnp.sum(chances, axis=-1, keepdims=True)
    gates_ref[...] = gates
    high = gates.astype(bf16).astype(f32)
    rest = pltpu.roll(gates - high, experts, 1)
    low_ref[:, :width] = normed
    low_ref[:, width:] = (high + rest).astype(bf16)


def mix(spot, got, own, near, far, x, gain, router, table, experts):
    smem = pl.BlockSpec(memory_space=pltpu.SMEM)
    memory = pl.BlockSpec(memory_space=pltpu.VMEM)
    tokens, width = x.shape
    spare = table.shape[1]
    return pl.pallas_call(
        functools.partial(mix_kernel, experts),
        in_specs=[smem] + [memory] * 8,
        out_specs=[memory] * 5,
        out_shape=[
            jax.ShapeDtypeStruct(x.shape, f32),
            jax.ShapeDtypeStruct((tokens, width + spare), bf16),
            jax.ShapeDtypeStruct((tokens, 1), f32),
            jax.ShapeDtypeStruct((tokens, spare), f32),
            jax.ShapeDtypeStruct(x.shape, bf16),
        ],
        scratch_shapes=[pltpu.VMEM((tokens, width // 2), f32)] * 2,
        name="mix",
    )(spot, got, own, near, far, x, gain, router, table)


def mix_back_kernel(
    spot_ref,
    sums_ref,
    gates_ref,
    gate_grads_ref,
    router_ref,
    second_ref,
    scale_ref,
    gain_ref,
    g_ref,
    own_ref,
    near_ref,
    far_ref,
    send_ref,
    cuts_ref,
    grad_second_ref,
    out_ref,
):
    tokens, width = second_ref.shape
    second = second_ref[...]
    scale = scale_ref[...]
    gain = gain_ref[...]
    gates = gates_ref[...]
    gate_grads = gate_grads_ref[...]
    out_ref[...] = (second + sums_ref[:, width:].astype(f32)).astype(bf16)
    weighted = gates * gate_grads
    grad_sel = weighted - gates * jnp.sum(weighted, axis=-1, keepdims=True)
    grad_logits = grad_sel.astype(bf16)
    grad_normed = sums_ref[:, :width].astype(f32) + dot(grad_logits, router_ref[...])
    gain_part = jnp.sum(grad_normed * second * scale, axis=0, keepdims=True)
    hat = grad_normed * gain
    mean = jnp.mean(hat * second, axis=-1, keepdims=True)
    grad_second = g_ref[...].astype(f32) + scale * hat - second * (scale * scale * scale) * mean
    grad_second_ref[...] = grad_second
    grad_mixed = grad_second.astype(bf16)
    spans = send_ref.shape[0]
    cut = width // spans
    lane = lax.broadcasted_iota(jnp.int32, (1, HEAD_DIM), 1)
    high = gain_part.astype(bf16).astype(f32)
    row = lax.broadcasted_iota(jnp.int32, (16, width), 0)
    gain_rows = jnp.where(row == 0, high, jnp.where(row == 1, gain_part - high, 0.0))
    shifted = pltpu.roll(grad_logits.astype(f32), cut, 1)
    for k, c in enumerate(ring_of(spans)):
        start = min(c * cut // HEAD_DIM * HEAD_DIM, width - 2 * HEAD_DIM)
        shift = (start - c * cut) % (2 * HEAD_DIM)
        for value, rest, out_rows in (
            (grad_second, shifted, slice(0, tokens)),
            (gain_rows, 0.0, slice(tokens, tokens + 16)),
        ):
            window = pltpu.roll(value[:, start : start + 2 * HEAD_DIM], shift, 1)[:, :HEAD_DIM]
            window = jnp.where(lane < cut, window, 0.0) + rest
            cuts_ref[k, out_rows, :] = window.astype(bf16)
    left, right = grad_mixed[:, : width // 2], grad_mixed[:, width // 2 :]
    at_near = jnp.where(spot_ref[1] == 0, left, right)
    at_far = jnp.where(spot_ref[1] == 0, right, left)
    def visit(i, carry):
        mine, theirs, at = head_pair(spot_ref[0], spans, i)
        send_ref[mine] = dot_nt(grad_mixed, own_ref[at, :]).astype(bf16)
        other = dot_nt(at_near, near_ref[at, :]) + dot_nt(at_far, far_ref[at, :])
        send_ref[theirs] = other.astype(bf16)
        return carry

    lax.fori_loop(0, HEADS // 2, visit, 0, unroll=True)
    for h in ring_of(spans)[HEADS:]:
        send_ref[h] = jnp.zeros((tokens, HEAD_DIM), bf16)


def mix_back(spot, sums, gates, gate_grads, router, second, scale, gain, g, own, near, far, spans):
    tokens, width = second.shape
    smem = pl.BlockSpec(memory_space=pltpu.SMEM)
    memory = pl.BlockSpec(memory_space=pltpu.VMEM)
    return pl.pallas_call(
        mix_back_kernel,
        in_specs=[smem] + [memory] * 11,
        out_specs=[memory] * 4,
        out_shape=[
            jax.ShapeDtypeStruct((spans, tokens, HEAD_DIM), bf16),
            jax.ShapeDtypeStruct((spans, tokens + 16, HEAD_DIM), bf16),
            jax.ShapeDtypeStruct((tokens, width), f32),
            jax.ShapeDtypeStruct((tokens, width), bf16),
        ],
        name="mix_back",
    )(spot, sums, gates, gate_grads, router, second, scale, gain, g, own, near, far)


def inputs_back_kernel(
    side_ref,
    core_ref,
    got_ref,
    wq_ref,
    wk_ref,
    wv_ref,
    near_q_ref,
    near_rest_ref,
    far_q_ref,
    far_rest_ref,
    x_ref,
    gain_ref,
    grad_second_ref,
    out_ref,
    own_sum_ref,
    other_sum_ref,
):
    tokens, width = x_ref.shape
    half = width // 2
    count = HEADS // 2
    own_sum_ref[...] = jnp.zeros((tokens, half), f32)
    other_sum_ref[...] = jnp.zeros((tokens, half), f32)
    spans = got_ref.shape[0]

    def visit(h, carry):
        low, high = home(h, spans), home(count + h, spans)
        mine = jnp.where(core_ref[0] == 0, low, high)
        theirs = jnp.where(core_ref[0] == 0, high, low)
        window = pl.ds(pl.multiple_of(h * HEAD_DIM, HEAD_DIM), HEAD_DIM)
        upper = pl.ds(pl.multiple_of((count + h) * HEAD_DIM, HEAD_DIM), HEAD_DIM)
        for i, weight in enumerate((wq_ref, wk_ref, wv_ref)):
            at = slice(i * HEAD_DIM, (i + 1) * HEAD_DIM)
            near_ref, far_ref = (near_rest_ref, far_rest_ref) if i else (near_q_ref, far_q_ref)
            rows = slice(max(i - 1, 0) * half, max(i, 1) * half)
            grads = jnp.concatenate([got_ref[low, :, at], got_ref[high, :, at]], axis=1)
            weights = jnp.concatenate([weight[:, window], weight[:, upper]], axis=1)
            own_sum_ref[...] += dot_nt(grads, weights)
            grads = jnp.concatenate([got_ref[mine, :, at], got_ref[theirs, :, at]], axis=1)
            weights = jnp.concatenate([near_ref[rows, window], far_ref[rows, window]], axis=1)
            other_sum_ref[...] += dot_nt(grads, weights)
        return carry

    lax.fori_loop(0, count, visit, 0)
    own_part, other_part = own_sum_ref[...], other_sum_ref[...]
    grad_normed = jnp.where(
        side_ref[0] == 0,
        jnp.concatenate([own_part, other_part], axis=1),
        jnp.concatenate([other_part, own_part], axis=1),
    )
    resid = x_ref[...].astype(f32)
    scale = rms_scale(resid)
    hat = grad_normed * gain_ref[...]
    mean = jnp.mean(hat * resid, axis=-1, keepdims=True)
    out_ref[...] = grad_second_ref[...] + scale * hat - resid * (scale * scale * scale) * mean


def inputs_back(side, core, got, *values):
    x = values[-3]
    smem = pl.BlockSpec(memory_space=pltpu.SMEM)
    memory = pl.BlockSpec(memory_space=pltpu.VMEM)
    return pl.pallas_call(
        inputs_back_kernel,
        in_specs=[smem] * 2 + [memory] * (1 + len(values)),
        out_specs=memory,
        out_shape=jax.ShapeDtypeStruct(x.shape, f32),
        scratch_shapes=[pltpu.VMEM((x.shape[0], x.shape[1] // 2), f32)] * 2,
        name="inputs_back",
    )(
        side.reshape(1),
        core.reshape(1),
        got,
        *values,
    )


def place_heads_kernel(
    cut,
    side_ref,
    heads_ref,
    rest_ref,
    gain_rows_ref,
    gain_ref,
    q_ref,
    k_ref,
    v_ref,
    output_ref,
    norm_ref,
    norm2_ref,
    line_ref,
    line2_ref,
):
    for h in range(HEADS):
        at = slice(h * HEAD_DIM, (h + 1) * HEAD_DIM)
        for i, out in enumerate((q_ref, k_ref, v_ref)):
            out[:, at] = heads_ref[h, :, i * HEAD_DIM : (i + 1) * HEAD_DIM].astype(f32)
    sums = rest_ref[0].astype(f32)
    for h in range(1, HEADS):
        sums += rest_ref[h].astype(f32)
    lane = lax.broadcasted_iota(jnp.int32, (8, HEAD_DIM), 1)
    pair = jnp.where((lane == cut) | (lane == cut + 1), 1.0, 0.0)
    row = lax.dot_general(
        pair, sums, (((1,), (1,)), ((), ())), precision=exact, preferred_element_type=f32
    )
    block = rest_ref.shape[1]
    for i in range(line_ref.shape[1] // block):

        @pl.when(pl.program_id(0) == i)
        def _(at=slice(i * block, (i + 1) * block)):
            line_ref[:, at] = row[0:1] / gain_ref[:, at]

    spans = rest_ref.shape[0]

    @pl.when(pl.program_id(0) == 0)
    def _():
        for i in range(spans // 2):
            low, high = ring_position(i, spans), ring_position(spans // 2 + i, spans)
            rows = gain_rows_ref[jnp.where(side_ref[0] == 0, low, high)].astype(f32)
            line2_ref[:, i * cut : (i + 1) * cut] = (rows[0:1] + rows[1:2])[:, :cut]

    for c in range(spans):
        piece = rest_ref[ring_position(c, spans), :, :cut].astype(f32)
        output_ref[:, c * cut : (c + 1) * cut] = piece

    @pl.when(pl.program_id(0) == pl.num_programs(0) - 1)
    def _():
        for i in range(norm_ref.shape[0]):
            at = slice(i * HEAD_DIM, (i + 1) * HEAD_DIM)
            norm_ref[i : i + 1, :] = line_ref[:, at]
            norm2_ref[i : i + 1, :] = line2_ref[:, at]


def ring_position(index, spans):
    if spans != 16:
        return index
    chip, core = index // 2, index % 2
    level, column = chip // 2, chip % 2
    return (level + column * (7 - 2 * level)) * 2 + core


def place_heads(side, got, gain, width):
    spans, _, packed = got.shape
    half = width // 2
    cut = width // spans
    block = half // 5
    part = pl.BlockSpec((block, width), lambda r: (r, 0))
    line = pl.BlockSpec((1, half), lambda r: (0, 0))
    return pl.pallas_call(
        functools.partial(place_heads_kernel, cut),
        grid=(5,),
        in_specs=[
            pl.BlockSpec(memory_space=pltpu.SMEM),
            pl.BlockSpec((HEADS, block, 3 * HEAD_DIM), lambda r: (0, r, 0)),
            pl.BlockSpec((spans, block, HEAD_DIM), lambda r: (0, r, 3)),
            pl.BlockSpec((spans, 16, HEAD_DIM), lambda r: (0, half // 16, 3)),
            line,
        ],
        out_specs=[part] * 4 + [pl.BlockSpec((half // HEAD_DIM, HEAD_DIM), lambda r: (0, 0))] * 2,
        out_shape=[jax.ShapeDtypeStruct((half, width), f32)] * 4
        + [jax.ShapeDtypeStruct((half // HEAD_DIM, HEAD_DIM), f32)] * 2,
        scratch_shapes=[pltpu.VMEM((1, half), f32)] * 2,
        name="place_heads",
    )(side.reshape(1), got, got, got, gain.reshape(1, half))


def place_shared_kernel(side_ref, got_ref, in_ref, out_ref, rows_ref):
    spans = got_ref.shape[0]
    units = got_ref.shape[1] // 4
    half = got_ref.shape[2]
    hidden = spans * units

    for part in range(2):
        for c in range(spans):
            spot = ring_position(c, spans)
            piece = got_ref[spot, part * units : (part + 1) * units, :]
            rows_ref[c * units : (c + 1) * units, :] = piece.astype(f32)

        def turn(i, carry):
            window = pl.ds(pl.multiple_of(i * HEAD_DIM, HEAD_DIM), HEAD_DIM)
            at = pl.ds(pl.multiple_of(part * hidden + i * HEAD_DIM, HEAD_DIM), HEAD_DIM)
            in_ref[:, at] = rows_ref[window, :].T
            return carry

        lax.fori_loop(0, hidden // HEAD_DIM, turn, 0)
    first = side_ref[0] * (spans // 2)
    for c in range(spans // 2):
        spot = ring_position(first + c, spans)
        for part in range(2):
            piece = got_ref[spot, (2 + part) * units : (3 + part) * units, :]
            out_ref[c * units : (c + 1) * units, part * half : (part + 1) * half] = piece.astype(f32)


def place_shared(got, side):
    spans, quad, half = got.shape
    hidden = spans * quad // 4
    memory = pl.BlockSpec(memory_space=pltpu.VMEM)
    return pl.pallas_call(
        place_shared_kernel,
        in_specs=[pl.BlockSpec(memory_space=pltpu.SMEM), memory],
        out_specs=[memory, memory],
        out_shape=[
            jax.ShapeDtypeStruct((half, 2 * hidden), f32),
            jax.ShapeDtypeStruct((hidden // 2, 2 * half), f32),
        ],
        scratch_shapes=[pltpu.VMEM((hidden, half), f32)],
        name="place_shared",
    )(side.reshape(1), got)


def after(value, *others):
    return lax.optimization_barrier((value, *others))[0]


def tied(*values):
    return lax.optimization_barrier(values)


def one_hot_rows(lanes, *targets):
    row = lax.broadcasted_iota(jnp.int32, (8, lanes), 0)
    lane = lax.broadcasted_iota(jnp.int32, (8, lanes), 1)
    rows = jnp.zeros((8, lanes), f32)
    for i, target in enumerate(targets):
        rows = jnp.where((row == i) & (lane == target), 1.0, rows)
    return rows.astype(bf16)


def slot_keys(shape, axis, capacity):
    index = lax.broadcasted_iota(jnp.int32, shape, axis)
    return (index % capacity + 1024 * (index // capacity)).astype(f32)


def run_keys(shape, axis, tokens):
    return (1024 * (lax.broadcasted_iota(jnp.int32, shape, axis) // tokens)).astype(f32)


def group_runs(capacity):
    return min(8, 224 // capacity)


def pick_slots_kernel(capacity, tokens, here_ref, g_ref, out_ref):
    many = g_ref.shape[0]
    width = out_ref.shape[1]
    extras = g_ref[:, width:]
    rows = one_hot_rows(extras.shape[1], here_ref[0])
    slots = dot_nt(rows, extras)[0:1] + run_keys((1, many), 1, tokens)
    takes = slot_keys((out_ref.shape[0], 1), 0, capacity) == slots
    select = jnp.where(takes, 1.0, 0.0).astype(bf16)
    out_ref[...] = dot(select, g_ref[:, :width]).astype(bf16)


def pick_slots(here, g_wide, width, capacity, tokens):
    length, wide = g_wide.shape
    runs = group_runs(capacity)
    steps = length // (runs * tokens)
    return pl.pallas_call(
        functools.partial(pick_slots_kernel, capacity, tokens),
        grid=(steps,),
        in_specs=[
            pl.BlockSpec(memory_space=pltpu.SMEM),
            pl.BlockSpec((runs * tokens, wide), lambda i: (i, 0)),
        ],
        out_specs=pl.BlockSpec((runs * capacity, width), lambda i: (i, 0)),
        out_shape=jax.ShapeDtypeStruct((steps * runs * capacity, width), bf16),
        name="pick_slots",
        cost_estimate=pl.CostEstimate(
            flops=2 * length * runs * capacity * width,
            bytes_accessed=3 * length * wide,
            transcendentals=0,
        ),
    )(here.reshape(1), g_wide)


def sigmoid(value):
    return 1.0 / (1.0 + jnp.exp(-value))


def experts_kernel(
    capacity,
    tokens,
    experts,
    here_ref,
    normed_ref,
    g_ref,
    grad_slots_ref,
    own_in_ref,
    first_in_ref,
    middle_in_ref,
    last_in_ref,
    own_down_ref,
    other_down_ref,
    own_shared_in_ref,
    other_shared_in_ref,
    own_shared_out_ref,
    other_shared_out_ref,
    dispatched_ref,
    hidden_ref,
    grad_result_ref,
    grad_proj_ref,
    shared_hidden_ref,
    shared_grad_ref,
    parts_ref,
    gate_dot_ref,
    in_ref,
    down_ref,
    shared_in_ref,
    shared_out_ref,
    grad_dispatched_ref,
    scaled_ref,
):
    @pl.when(pl.program_id(0) == 0)
    def _():
        side = here_ref[1]
        rows = own_in_ref.shape[0]
        in_ref[pl.ds(pl.multiple_of(side * rows, 64), rows), :] = own_in_ref[...]
        at = (1 - side) * rows
        for ref in (first_in_ref, middle_in_ref, last_in_ref):
            in_ref[pl.ds(pl.multiple_of(at, 16), ref.shape[0]), :] = ref[...]
            at = at + ref.shape[0]
        rows = own_down_ref.shape[0]
        down_ref[pl.ds(pl.multiple_of(side * rows, 64), rows), :] = own_down_ref[...]
        down_ref[pl.ds(pl.multiple_of((1 - side) * rows, 64), rows), :] = other_down_ref[...]
        rows = own_shared_in_ref.shape[0]
        units = own_shared_out_ref.shape[0]
        shared_in_ref[...] = jnp.zeros_like(shared_in_ref)
        shared_out_ref[...] = jnp.zeros_like(shared_out_ref)
        for place, ref in ((side, own_shared_in_ref), (1 - side, other_shared_in_ref)):
            window = pl.ds(pl.multiple_of(place * rows, 64), rows)
            shared_in_ref[window, :units] = ref[:, :units]
            shared_in_ref[window, HEAD_DIM : HEAD_DIM + units] = ref[:, units:]
        shared_out_ref[:units, :] = jnp.where(
            here_ref[2] == side, own_shared_out_ref[...], other_shared_out_ref[...]
        )

    many, slots = normed_ref.shape[0], dispatched_ref.shape[0]
    width = dispatched_ref.shape[1]
    here = here_ref[0]
    spare = normed_ref.shape[1] - width
    gate_rows = dot_nt(one_hot_rows(spare, here, experts + here), normed_ref[:, width:])
    gate_row = gate_rows[0:1] + gate_rows[1:2]
    slot_pick = one_hot_rows(spare, here)
    group = group_runs(capacity)
    chunk, picks = group * tokens, group * capacity
    takes = []
    for at in range(0, many, chunk):
        extras = g_ref[at : at + chunk, width:]
        slot_row = dot_nt(slot_pick, extras)[0:1] + run_keys((1, chunk), 1, tokens)
        hit = slot_keys((picks, 1), 0, capacity) == slot_row
        takes.append(hit)
        select = jnp.where(hit, 1.0, 0.0).astype(bf16)
        at_slots = slice(at // tokens * capacity, (at // tokens + group) * capacity)
        dispatched_ref[at_slots, :] = dot(select, normed_ref[at : at + chunk, :width]).astype(bf16)
    slot_gate = jnp.concatenate(
        [
            jnp.sum(
                jnp.where(hit, gate_row[:, i * chunk : (i + 1) * chunk], 0.0), axis=1, keepdims=True
            )
            for i, hit in enumerate(takes)
        ],
        axis=0,
    )
    dispatched = dispatched_ref[...]
    grad_slots = grad_slots_ref[...].astype(f32)
    grad_result = (grad_slots * slot_gate).astype(bf16)
    grad_result_ref[...] = grad_result

    projected = dot(dispatched, in_ref[...])
    gate, up = projected[:, :EXP_HID], projected[:, EXP_HID:]
    chance = sigmoid(gate)
    silu = gate * chance
    hidden = (silu * up).astype(bf16)
    hidden_ref[...] = hidden
    grad_hidden = dot_nt(grad_result, down_ref[...])
    grad_proj_ref[:, :EXP_HID] = (
        grad_hidden * up * chance * (1.0 + gate * (1.0 - chance))
    ).astype(bf16)
    grad_proj_ref[:, EXP_HID:] = (grad_hidden * silu).astype(bf16)
    result = dot(hidden, down_ref[...]).astype(bf16).astype(f32)
    slot_dot = jnp.sum(grad_slots * result, axis=1, keepdims=True)
    for i, hit in enumerate(takes):
        dots = slot_dot[i * picks : (i + 1) * picks]
        gate_dot = jnp.sum(jnp.where(hit, dots, 0.0), axis=0, keepdims=True)
        gate_dot_ref[:, i * chunk : (i + 1) * chunk] = jnp.broadcast_to(gate_dot, (8, chunk))
    scaled = (result * slot_gate).astype(bf16)
    grad_dispatched = dot_nt(grad_proj_ref[...], in_ref[...]).astype(bf16)

    grad_dispatched_ref[...] = grad_dispatched
    scaled_ref[...] = scaled
    lanes = shared_out_ref.shape[0]
    size = min(4 * HEAD_DIM, chunk)

    def visit(i, carry):
        at = pl.ds(pl.multiple_of(i * size, size), size)
        which = i * size // chunk
        filled = pl.ds(pl.multiple_of(which * picks, 16), picks)
        shared = dot(normed_ref[at, :width], shared_in_ref[...])
        shared_gate, shared_up = shared[:, :lanes], shared[:, lanes:]
        shared_chance = sigmoid(shared_gate)
        shared_silu = shared_gate * shared_chance
        shared_hidden = (shared_silu * shared_up).astype(bf16)
        shared_hidden_ref[at, :] = shared_hidden
        grad_shared = dot_nt(g_ref[at, :width], shared_out_ref[...])
        slope = shared_chance * (1.0 + shared_gate * (1.0 - shared_chance))
        shared_grad = jnp.concatenate(
            [(grad_shared * shared_up * slope).astype(bf16), (grad_shared * shared_silu).astype(bf16)],
            axis=1,
        )
        shared_grad_ref[at, :] = shared_grad
        slot_column = dot_nt(g_ref[at, width:], slot_pick)[:, 0:1]
        run = (i * size - which * chunk + lax.broadcasted_iota(jnp.int32, (size, 1), 0)) // tokens
        key = slot_column + (1024 * run).astype(f32)
        back = jnp.where(key == slot_keys((1, picks), 1, capacity), 1.0, 0.0).astype(bf16)
        parts_ref[at, :width] = (
            dot(back, grad_dispatched_ref[filled, :]) + dot_nt(shared_grad, shared_in_ref[...])
        ).astype(bf16)
        parts_ref[at, width:] = (
            dot(back, scaled_ref[filled, :]) + dot(shared_hidden, shared_out_ref[...])
        ).astype(bf16)
        return carry

    lax.fori_loop(0, many // size, visit, 0)


def run_experts(
    places, normed_wide, g_wide, grad_slots, weights, tokens, capacity
):
    length, wide = normed_wide.shape
    width = grad_slots.shape[1]
    experts = length // tokens
    runs = group_runs(capacity)
    steps = length // (runs * tokens)
    many, slots = runs * tokens, runs * capacity
    lanes = HEAD_DIM

    def block(rows, columns):
        return pl.BlockSpec((rows, columns), lambda i: (i, 0))

    def fixed(value):
        return pl.BlockSpec(value.shape, lambda i: (0, 0), pipeline_mode=pl.Buffered(1))

    def shape(rows, columns, kind=bf16):
        return jax.ShapeDtypeStruct((rows, columns), kind)

    return pl.pallas_call(
        functools.partial(experts_kernel, capacity, tokens, experts),
        grid=(steps,),
        in_specs=[
            pl.BlockSpec(memory_space=pltpu.SMEM),
            block(many, wide),
            block(many, wide),
            block(slots, width),
            *[fixed(weight) for weight in weights],
        ],
        out_specs=[
            block(slots, width),
            block(slots, EXP_HID),
            block(slots, width),
            block(slots, 2 * EXP_HID),
            block(many, lanes),
            block(many, 2 * lanes),
            block(many, 2 * width),
            pl.BlockSpec((8, many), lambda i: (0, i)),
        ],
        out_shape=[
            shape(steps * slots, width),
            shape(steps * slots, EXP_HID),
            shape(steps * slots, width),
            shape(steps * slots, 2 * EXP_HID),
            shape(length, lanes),
            shape(length, 2 * lanes),
            shape(length, 2 * width),
            shape(8, length, f32),
        ],
        scratch_shapes=[
            pltpu.VMEM((width, 2 * EXP_HID), bf16),
            pltpu.VMEM((EXP_HID, width), bf16),
            pltpu.VMEM((width, 2 * lanes), bf16),
            pltpu.VMEM((lanes, width), bf16),
            pltpu.VMEM((slots, width), bf16),
            pltpu.VMEM((slots, width), bf16),
        ],
        name="experts",
        cost_estimate=pl.CostEstimate(
            flops=20 * 10**9, bytes_accessed=40 * 10**6, transcendentals=2 * 10**6
        ),
    )(
        places,
        normed_wide,
        g_wide,
        grad_slots,
        *weights,
    )


def slot_grads_kernel(side_ref, left_ref, right_ref, own_ref, other_ref, turned_ref):
    @pl.when(pl.program_id(0) == 0)
    def _():
        turned_ref[...] = left_ref[...].T

    rows = own_ref.shape[0]
    size = rows // 5 if rows % 80 == 0 else rows // 4
    side = side_ref[0]

    def visit(i, carry):
        def part(place):
            at = pl.ds(pl.multiple_of(place * rows + i * size, 16), size)
            return dot(turned_ref[at, :], right_ref[...])

        at = pl.ds(pl.multiple_of(i * size, 16), size)
        own_ref[at, :] = part(side)
        other_ref[at, :] = part(1 - side).astype(bf16)
        return carry

    lax.fori_loop(0, rows // size, visit, 0)


def slot_grads(side, left, right):
    slots, tall = left.shape
    wide = right.shape[1]
    block = pl.BlockSpec((tall // 2, 2 * HEAD_DIM), lambda i: (0, i))
    return pl.pallas_call(
        slot_grads_kernel,
        grid=(wide // (2 * HEAD_DIM),),
        in_specs=[
            pl.BlockSpec(memory_space=pltpu.SMEM),
            pl.BlockSpec((slots, tall), lambda i: (0, 0), pipeline_mode=pl.Buffered(1)),
            pl.BlockSpec((slots, 2 * HEAD_DIM), lambda i: (0, i)),
        ],
        out_specs=[block, block],
        out_shape=[
            jax.ShapeDtypeStruct((tall // 2, wide), f32),
            jax.ShapeDtypeStruct((tall // 2, wide), bf16),
        ],
        scratch_shapes=[pltpu.VMEM((tall, slots), bf16)],
        name="slot_grads",
        cost_estimate=pl.CostEstimate(
            flops=2 * slots * tall * wide,
            bytes_accessed=2 * slots * (tall + wide) + 3 * tall * wide,
            transcendentals=0,
        ),
    )(side.reshape(1), left, right)


def shared_grads_kernel(grad_ref, normed_ref, hidden_ref, g_ref, in_ref, out_ref):
    @pl.when(pl.program_id(0) == 0)
    def _():
        in_ref[...] = jnp.zeros_like(in_ref)
        out_ref[...] = jnp.zeros_like(out_ref)

    in_ref[...] += dot_tn(grad_ref[...], normed_ref[...])
    out_ref[...] += dot_tn(hidden_ref[...], g_ref[...])


def shared_products(grad, normed_wide, hidden, g_wide, width):
    length, lanes = hidden.shape
    tile = 4 * HEAD_DIM

    def block(columns):
        return pl.BlockSpec((tile, columns), lambda i: (i, 0))

    def whole(rows):
        return pl.BlockSpec((rows, width), lambda i: (0, 0))

    return pl.pallas_call(
        shared_grads_kernel,
        grid=(length // tile,),
        in_specs=[block(2 * lanes), block(width), block(lanes), block(width)],
        out_specs=[whole(2 * lanes), whole(lanes)],
        out_shape=[
            jax.ShapeDtypeStruct((2 * lanes, width), f32),
            jax.ShapeDtypeStruct((lanes, width), f32),
        ],
        name="shared_products",
        cost_estimate=pl.CostEstimate(
            flops=6 * length * lanes * width, bytes_accessed=6 * length * width, transcendentals=0
        ),
    )(grad, normed_wide, hidden, g_wide)


def turned_product_kernel(side_ref, left_ref, right_ref, out_ref, sum_ref):
    step = pl.program_id(0)

    @pl.when(step == 0)
    def _():
        sum_ref[...] = jnp.zeros_like(sum_ref)

    sum_ref[...] += dot_tn(right_ref[...], left_ref[...])

    @pl.when(step == pl.num_programs(0) - 1)
    def _():
        count = out_ref.shape[0] // HEAD_DIM
        near = count // 2

        def turn(i, carry):
            window = pl.ds(pl.multiple_of(i * HEAD_DIM, HEAD_DIM), HEAD_DIM)
            place = jnp.where(i // near == side_ref[0], 0, near) + i % near
            at = pl.ds(pl.multiple_of(place * HEAD_DIM, HEAD_DIM), HEAD_DIM)
            out_ref[at, :] = sum_ref[:, window].T
            return carry

        lax.fori_loop(0, count, turn, 0)


def turned_product(side, left, right, wide):
    length, lanes = right.shape
    tile = 4 * HEAD_DIM
    return pl.pallas_call(
        turned_product_kernel,
        grid=(length // tile,),
        in_specs=[
            pl.BlockSpec(memory_space=pltpu.SMEM),
            pl.BlockSpec((tile, wide), lambda i: (i, 0)),
            pl.BlockSpec((tile, lanes), lambda i: (i, 0)),
        ],
        out_specs=pl.BlockSpec((wide, lanes), lambda i: (0, 0)),
        out_shape=jax.ShapeDtypeStruct((wide, lanes), f32),
        scratch_shapes=[pltpu.VMEM((lanes, wide), f32)],
        name="turned_product",
        cost_estimate=pl.CostEstimate(
            flops=2 * length * lanes * wide,
            bytes_accessed=2 * length * wide,
            transcendentals=0,
        ),
    )(side.reshape(1), left, right)


def slot_table(span_picks, span_order, experts):
    tokens = span_picks.shape[0]
    order = span_order.reshape(tokens, TOP)
    onehot = span_picks[:, :, None] == jnp.arange(experts, dtype=jnp.int32)
    picked = jnp.any(onehot, axis=1)
    rank_key = jnp.sum(jnp.where(onehot, order[:, :, None], 0), axis=1)
    rank_key = jnp.where(picked, rank_key, tokens * TOP)
    before = rank_key[:, None, :] < rank_key[None, :, :]
    slots = jnp.sum(before.astype(jnp.int32), axis=0)
    return jnp.where(picked, slots, 2 * tokens)


def on_device(
    inputs,
    norm1_gain,
    w_query,
    w_key,
    w_value,
    w_output,
    norm2_gain,
    router,
    shared_gate_up_weight,
    shared_down_weight,
    expert_in,
    expert_out,
    picks,
    fill_order,
    grad_out,
):
    spans = lax.axis_size("ctx")
    here = lax.axis_index("ctx")
    side = lax.axis_index("fsdp")
    core = here % 2
    tokens, width = inputs.shape[1:]
    half = width // 2
    length = spans * tokens
    experts = spans * expert_in.shape[0]
    capacity = tokens * TOP // experts
    head = jnp.minimum(ring_position(here, spans), HEADS - 1)
    units = EXP_HID // spans
    ring = ring_of(spans)
    is_ring = spans == 16
    groups = [ring] if is_ring else None
    swap_core = [(i, i ^ 1) for i in range(spans)]

    def across(value):
        return lax.ppermute(value, "fsdp", [(0, 1), (1, 0)])

    def ordered(own, other, axis):
        return jnp.where(
            side == 0,
            jnp.concatenate([own, other], axis=axis),
            jnp.concatenate([other, own], axis=axis),
        )

    def everyone(value):
        return lax.all_gather(value, "ctx", axis=0, tiled=True, axis_index_groups=groups)

    def columns(value, start, count):
        return lax.dynamic_slice_in_dim(value, start, count, 1)

    def rows(value, start, count):
        return lax.dynamic_slice_in_dim(value, start, count, 0)

    def halves(value, axis=0):
        size = value.shape[axis] // 2
        mine = lax.dynamic_slice_in_dim(value, side * size, size, axis)
        theirs = lax.dynamic_slice_in_dim(value, (1 - side) * size, size, axis)
        return mine, theirs

    def reduced(value, axis=0):
        mine, theirs = halves(value, axis)
        return mine + across(theirs.astype(bf16)).astype(f32)

    def swapped(value):
        return lax.all_to_all(value, "ctx", split_axis=0, concat_axis=0, tiled=True)

    def row_major(value):
        return with_layout_constraint(value, Layout(tuple(range(value.ndim))))

    x = inputs[0]
    g = grad_out[0]
    x_all = everyone(x)
    spare = -(-2 * experts // HEAD_DIM) * HEAD_DIM
    own_table = slot_table(picks[0], fill_order[0, 0], experts)
    own_table = jnp.pad(
        own_table.astype(f32), ((0, 0), (0, spare - experts)), constant_values=2.0 * tokens
    )
    g_wide = jnp.concatenate([g, own_table.astype(bf16)], axis=1)
    head_own = jnp.concatenate(
        [columns(w, head * HEAD_DIM, HEAD_DIM) for w in (w_query, w_key, w_value)], axis=1
    )
    head_other = across(head_own)
    small = jnp.concatenate([router.T, norm1_gain[None], norm2_gain[None]], axis=0)
    small_other = across(small)
    output_near = across(columns(w_output, core * half, half))
    lanes = HEAD_DIM
    shared_in_own = jnp.concatenate(
        [columns(shared_gate_up_weight, at + here * units, units) for at in (0, EXP_HID)], axis=1
    )
    shared_rows = shared_down_weight.shape[0]
    shared_out_own = rows(shared_down_weight, here * units % shared_rows, units)
    cosine, sine = rotary_tables(jnp.asarray(ring, jnp.int32) * tokens, tokens, HEAD_DIM)
    small = ordered(small, small_other, 1)
    router_w = small[:experts]
    gain_one = small[experts : experts + 1].astype(f32)
    gain_two = small[experts + 1 :].astype(f32)
    quarter = half // 4
    chunks = [expert_in[0, :quarter], expert_in[0, quarter:-quarter], expert_in[0, -quarter:]]
    head_other, *chunks = tied(head_other, *chunks)
    chunks = [across(chunk) for chunk in chunks]
    x_all, cosine, sine, head_other, gain_one, output_near = tied(
        x_all, cosine, sine, head_other, gain_one, output_near
    )
    output_far = lax.ppermute(output_near, "ctx", swap_core)
    g_wide_all = everyone(after(g_wide, x_all))
    g_all = g_wide_all[:, :width]
    table = g_wide_all[:, width : width + experts]

    normed1_all, query, key, value = project(
        side, x_all, gain_one, head_own, head_other, cosine, sine
    )
    context, lse, attended = attend(query, key, value, is_ring)
    attended, output_far, chunks[0] = tied(attended, output_far, chunks[0])
    down_other = across(after(expert_out[0], attended))
    got = swapped(attended.reshape(spans, tokens, HEAD_DIM))
    got, chunks[1] = tied(got, chunks[1])
    spot = jnp.stack([side, core]).astype(jnp.int32)
    router_pad = jnp.pad(router_w, ((0, spare - experts), (0, 0)))
    second, normed2_wide, scale_two, own_gates, attended = mix(
        spot,
        got,
        w_output,
        output_near,
        output_far,
        x,
        gain_two,
        router_pad,
        own_table,
        experts,
    )
    normed2_wide, g_wide_all, chunks[2] = tied(normed2_wide, g_wide_all, chunks[2])
    normed2_wide = everyone(normed2_wide)
    grad_slots = pick_slots(here, g_wide_all, width, capacity, tokens)
    shared_in_other = across(after(shared_in_own, grad_slots))
    shared_out_other = across(after(shared_out_own, grad_slots))
    normed2_wide, grad_slots, down_other, shared_in_other, shared_out_other = tied(
        normed2_wide, grad_slots, down_other, shared_in_other, shared_out_other
    )
    normed2_all = normed2_wide[:, :width]
    attended_all = everyone(after(attended, normed2_wide))
    dense = [
        columns(after(w, grad_slots), core * half, half) for w in (w_query, w_key, w_value)
    ]
    near = [across(dense[0]), across(jnp.concatenate(dense[1:], axis=0))]
    spots = [ring_position(i, spans) for i in range(spans)]
    (
        dispatched,
        expert_hidden,
        grad_result,
        grad_proj,
        shared_hidden,
        grad_sproj,
        parts,
        gate_dot,
    ) = run_experts(
        jnp.stack([here, side, here * units // shared_rows]).astype(jnp.int32),
        normed2_wide,
        g_wide_all,
        grad_slots,
        (
            expert_in[0],
            *chunks,
            expert_out[0],
            down_other,
            shared_in_own,
            shared_in_other,
            shared_out_own,
            shared_out_other,
        ),
        tokens,
        capacity,
    )
    parts, near[0], attended_all = tied(parts, near[0], attended_all)
    sums = lax.psum_scatter(
        parts, "ctx", scatter_dimension=0, tiled=True, axis_index_groups=groups
    )
    gate_dot = gate_dot[0].reshape(spans, tokens)
    grad_shared_in, grad_shared_out = shared_products(
        grad_sproj, normed2_wide, shared_hidden, g_wide_all, width
    )
    grad_shared_in = jnp.concatenate(
        [grad_shared_in[:units], grad_shared_in[lanes : lanes + units]], axis=0
    )
    grad_shared_in = reduced(grad_shared_in, 1).astype(bf16)
    grad_shared_out = grad_shared_out[:units].astype(bf16)
    grad_shared_out = grad_shared_out.astype(f32) + across(grad_shared_out).astype(f32)
    grad_shared_out = grad_shared_out.astype(bf16)
    shared_grads = jnp.concatenate(
        [grad_shared_in, grad_shared_out[:, :half], grad_shared_out[:, half:]], axis=0
    )
    gate_dot = jnp.concatenate([gate_dot[i : i + 1] for i in spots], axis=0)
    gate_grads = swapped(after(gate_dot, parts)[:, None, :])[:, 0, :].T

    own_down, down_theirs = slot_grads(side, expert_hidden, grad_result)
    own_in, in_theirs = slot_grads(side, dispatched, grad_proj)
    down_theirs = across(after(down_theirs, parts))
    cuts_at = [0, half // 4, half * 9 // 16, half]
    sums, in_theirs, shared_grads, gate_grads = tied(
        sums,
        in_theirs,
        row_major(shared_grads),
        gate_grads,
    )
    split = half * 5 // 16
    in_parts = [in_theirs[a:b] for a, b in zip(cuts_at, cuts_at[1:])]
    in_parts[0], in_parts[1] = across(in_parts[0]), across(in_parts[1])

    sent, cuts, grad_second, layer_out = mix_back(
        spot,
        sums,
        own_gates,
        jnp.pad(gate_grads, ((0, 0), (0, spare - experts))),
        router_pad,
        second,
        scale_two,
        gain_two,
        g,
        w_output,
        output_near,
        output_far,
        spans,
    )
    arrived = swapped(sent).reshape(length, HEAD_DIM)
    arrived, shared_grads, near[1], down_theirs, in_parts[0] = tied(
        arrived, shared_grads, near[1], down_theirs, in_parts[0]
    )
    cuts = lax.all_to_all(
        cuts, "ctx", split_axis=0, concat_axis=0, tiled=True, axis_index_groups=groups
    )
    extras = cuts[:, :tokens].reshape(length, HEAD_DIM)
    shared_grads = everyone(shared_grads[None])
    grad_heads, grad_heads_ring = attend_back(
        query, key, value, arrived, context, lse, cosine, sine, is_ring
    )
    grad_heads, grad_heads_ring, in_parts[1] = tied(grad_heads, grad_heads_ring, in_parts[1])
    cut = width // spans
    gain_rows = cuts[:, tokens : tokens + 2, :cut].astype(f32)
    gain_rows = jnp.sum(gain_rows, axis=(0, 1))
    gain_rows = jnp.pad(gain_rows.reshape(1, cut), ((0, 15), (0, HEAD_DIM - cut)))
    grad_router = turned_product(side, normed2_wide, extras, width)[:, cut : cut + experts]
    grad_router = grad_router[:half] + across(grad_router[half:])
    products = turned_product(side, attended_all, extras, width)
    mine, theirs = products[:half], products[half:]
    gain_high = gain_rows.astype(bf16)
    gain_low = jnp.roll((gain_rows - gain_high.astype(f32)).astype(bf16), 1, axis=0)
    theirs = jnp.concatenate([theirs.astype(bf16), gain_high + gain_low], axis=0)
    grad_heads_ring, theirs = tied(grad_heads_ring, theirs)
    head_mine, head_theirs = halves(dot_tn(normed1_all, grad_heads_ring))
    head_theirs = head_theirs.astype(bf16)
    theirs = across(theirs).astype(f32)
    grad_output = mine + theirs[:half]
    gain_rows = gain_rows[:1] + theirs[half : half + 1] + theirs[half + 1 : half + 2]
    gain_high = gain_rows.astype(bf16)
    gain_low = (gain_rows - gain_high.astype(f32)).astype(bf16)
    gain_rows = jnp.pad(
        jnp.concatenate([gain_high, gain_low], axis=0), ((0, 14), (3 * HEAD_DIM, 0))
    )
    got = swapped(grad_heads.reshape(spans, tokens, 3 * HEAD_DIM))
    grad_head_w = (head_mine + across(head_theirs).astype(f32)).astype(bf16)
    part = jnp.sum(grad_head_w.astype(f32) * head_own.astype(f32), axis=1, keepdims=True)
    part_high = part.astype(bf16).astype(f32)
    lane = lax.broadcasted_iota(jnp.int32, (half, HEAD_DIM), 1)
    grad_output = jnp.where(lane < cut, grad_output, 0.0)
    grad_output = jnp.where(lane == cut, part_high, grad_output)
    grad_output = jnp.where(lane == cut + 1, part - part_high, grad_output)
    head_grads = jnp.concatenate([grad_head_w, grad_output.astype(bf16)], axis=1)
    head_grads = jnp.concatenate([head_grads, gain_rows], axis=0)
    head_pack = head_grads
    head_grads, got = tied(row_major(head_grads), got)
    head_grads = everyone(head_grads[None])
    in_parts[2] = across(after(in_parts[2], head_pack))
    far = [lax.ppermute(part, "ctx", swap_core) for part in near]

    grad_inputs = inputs_back(
        side, core, got, w_query, w_key, w_value, *near, *far, x, gain_one, grad_second
    )
    grad_query, grad_key, grad_value, grad_output, grad_norm1, grad_norm2 = place_heads(
        side, head_grads, norm1_gain.astype(f32), width
    )
    grad_expert_in = jnp.concatenate(
        [
            own_in[a:b] + part.astype(f32)
            for a, b, part in zip(cuts_at, cuts_at[1:], in_parts)
        ],
        axis=0,
    )
    grad_shared_in, grad_shared_out = place_shared(shared_grads, side)
    return (
        layer_out[None],
        grad_inputs[None],
        grad_norm1.reshape(half),
        grad_query,
        grad_key,
        grad_value,
        grad_output,
        grad_norm2.reshape(half),
        grad_router,
        grad_shared_in,
        grad_shared_out,
        grad_expert_in[None],
        (own_down + down_theirs.astype(f32))[None],
    )


def solution(mesh):
    placed = (
        P("fsdp", "ctx", None),
        P("fsdp"),
        P("fsdp", None),
        P("fsdp", None),
        P("fsdp", None),
        P("fsdp", None),
        P("fsdp"),
        P("fsdp", None),
        P("fsdp", None),
        P("fsdp", None),
        P("ctx", "fsdp", None),
        P("ctx", "fsdp", None),
        P("fsdp", "ctx", None),
        P("fsdp", "ctx", None),
        P("fsdp", "ctx", None),
    )
    return jax.shard_map(
        on_device,
        mesh=mesh,
        in_specs=placed,
        out_specs=(
            P("fsdp", "ctx", None),
            P("fsdp", "ctx", None),
            P("fsdp"),
            P("fsdp", None),
            P("fsdp", None),
            P("fsdp", None),
            P("fsdp", None),
            P("fsdp"),
            P("fsdp", None),
            P("fsdp", None),
            P("fsdp", None),
            P("ctx", "fsdp", None),
            P("ctx", "fsdp", None),
        ),
        check_vma=False,
    )
```
